32 devices in a mesh: rep: 2 (over y), shard: 16 (over z, x, core).
Axes of the slice: x: 2, y: 2, z: 4, core: 2. Of those that a mesh axis runs over, the one named last changes fastest.
Arguments:
- tokens: bfloat16 [16384, 1024], P(('rep', 'shard')), may hold values from -6 to 6
- cotangent: bfloat16 [16384, 1024], P(('rep', 'shard')), may hold values from -6 to 6
- send_slot: int32 [16384], P(('rep', 'shard')), may hold values from 0 to 1023, as said below
- recv_slot: int32 [16384], P(('rep', 'shard')), may hold values from 0 to 1023, as said below
- lengths: int32 [32, 4], P(('rep', 'shard')), may hold values from 1 to 384, 512 in all within a row
- variate: int32 [16384], P(('rep', 'shard')), may hold values from 0 to 3
- valid_mask: int32 [16384], P(('rep', 'shard')), may hold values from 0 to 1, as said below
- norm_attn: bfloat16 [1024], P('shard'), may hold values from 0.5 to 1.5
- w_query: bfloat16 [1024, 1024], P('shard'), may hold values from -0.1875 to 0.1875
- w_key: bfloat16 [1024, 1024], P('shard'), may hold values from -0.1875 to 0.1875
- w_value: bfloat16 [1024, 1024], P('shard'), may hold values from -0.1875 to 0.1875
- w_out: bfloat16 [1024, 1024], P('shard'), may hold values from -0.75 to 0.75
- variate_bias: float32 [2, 16], replicated, may hold values from -3 to 3
- norm_mlp: bfloat16 [1024], P('shard'), may hold values from 0.5 to 1.5
- w_gate: bfloat16 [1024, 4096], P('shard'), may hold values from -0.1875 to 0.1875
- w_up: bfloat16 [1024, 4096], P('shard'), may hold values from -0.1875 to 0.1875
- w_down: bfloat16 [4096, 1024], P('shard'), may hold values from -0.1875 to 0.1875
Outputs:
- output: bfloat16 [16384, 1024], P(('rep', 'shard'))
- input_grad: bfloat16 [16384, 1024], P(('rep', 'shard'))
- grad_norm_attn: float32 [1024], P('shard')
- grad_query: float32 [1024, 1024], P('shard')
- grad_key: float32 [1024, 1024], P('shard')
- grad_value: float32 [1024, 1024], P('shard')
- grad_out: float32 [1024, 1024], P('shard')
- grad_bias: float32 [2, 16], replicated
- grad_norm_mlp: float32 [1024], P('shard')
- grad_gate: float32 [1024, 4096], P('shard')
- grad_up: float32 [1024, 4096], P('shard')
- grad_down: float32 [4096, 1024], P('shard')
- root_means: float32 [5], replicated
The draws below stay inside these ranges and needn't reach their ends.
Inputs may be any that keep to these rules, and one draw needn't show every extreme that they name: send_slot[i] = (index in the rep group of the device that gets token i) * 64 + the token's rank among its device's tokens going there. The values on one device are distinct; a device sends to each device of its group a multiple of 16 tokens and at most 64, and some device sends exactly 64 to the last device of its group. recv_slot[t] = (index in the group of the sending device) * 64 + the token's rank there; the values on one device are distinct. With send_slot it describes one permutation of the tokens of each rep group, every device receives exactly 512 tokens, and the last device of some group sends exactly 64 to some device. `valid_mask`: the first row of every device's block is 1.
All inputs are finite; a program needn't handle non-finite values.
Results may differ from the reference program's by a relative error of at most 0.017.
Values may be sent and summed in bfloat16 or wider, within the bound.
A program may use at most 256 MiB of HBM per device.

```python
import math
import jax
import jax.numpy as jnp
import numpy as np
from jax import lax

D = 1024
HEADS = 16
HD = 64
FF = 4096
TOK_DEV = 512
SEQS = 4
LONGEST = 384
CAP = 64
BLOCKS = 32
TOKENS = 16384
N_REP = 2
N_SHARD = 16


def band_counts(key):
    shards = N_SHARD
    quarter = CAP // 4

    def one_group(group_key, group_index):
        anchor_key, band_key = jax.random.split(group_key)
        drawn = jax.random.randint(anchor_key, (2,), 0, shards).astype(jnp.int32)
        last = jnp.int32(shards - 1)
        even = group_index % 2 == 0
        anchor_row = jnp.where(even, drawn[0], last)
        anchor_col = jnp.where(even, last, drawn[1])
        band_keys = jax.random.split(band_key, 4)

        def one_band(single_key):
            pair_keys = jax.random.split(single_key)
            row_order = jax.random.permutation(pair_keys[0], shards).astype(jnp.int32)
            col_order = jax.random.permutation(pair_keys[1], shards).astype(jnp.int32)
            shifted = row_order[:, None] + col_order[None, :] - row_order[anchor_row] - col_order[anchor_col]
            return (jnp.mod(shifted, shards) < shards // 2).astype(jnp.int32)
        return quarter * jnp.sum(jax.vmap(one_band)(band_keys), axis=0)
    group_keys = jax.random.split(jax.random.fold_in(key, 17), N_REP)
    group_ids = jnp.arange(N_REP, dtype=jnp.int32)
    return jax.vmap(one_group)(group_keys, group_ids).astype(jnp.int32)


def slot_lists(counts, key):
    ends_all = jnp.cumsum(counts, axis=1).astype(jnp.int32)
    positions = jnp.arange(TOK_DEV, dtype=jnp.int32)

    def one_row(row_counts, row_ends, row_key):
        target = jnp.sum((row_ends[None, :] <= positions[:, None]).astype(jnp.int32), axis=1)
        before = jnp.take(row_ends - row_counts, target)
        listed = target * CAP + positions - before
        return jnp.take(listed, jax.random.permutation(row_key, TOK_DEV))
    row_keys = jax.random.split(key, counts.shape[0])
    return jax.vmap(one_row)(counts, ends_all, row_keys)


def draw_send_slot(key, part):
    counts = band_counts(key)
    sender_rows = counts.reshape(N_REP * N_SHARD, N_SHARD)
    return slot_lists(sender_rows, jax.random.fold_in(key, 23)).reshape(-1).astype(jnp.int32)


def draw_recv_slot(key, part):
    counts = band_counts(key)
    receiver_rows = jnp.swapaxes(counts, 1, 2).reshape(N_REP * N_SHARD, N_SHARD)
    return slot_lists(receiver_rows, jax.random.fold_in(key, 29)).reshape(-1).astype(jnp.int32)


def draw_valid_mask(key, part):
    blocks = N_REP * N_SHARD
    levels = 25 + 60 * jnp.arange(blocks, dtype=jnp.int32) // max(blocks - 1, 1)
    rolled = jax.random.randint(key, (blocks, TOK_DEV), 0, 100)
    leading = jnp.arange(TOK_DEV, dtype=jnp.int32)[None, :] == 0
    return ((rolled < levels[:, None]) | leading).astype(jnp.int32).reshape(-1)


def plant(entries, own_key, least, largest):
    index_at = [jax.random.randint(jax.random.fold_in(own_key, axis), (), 0, length) for axis, length in enumerate(entries.shape)]
    widest = entries.shape.index(max(entries.shape))
    next_to = index_at[:widest] + [(index_at[widest] + 1) % entries.shape[widest]] + index_at[widest + 1:]
    return entries.at[tuple(index_at)].set(least).at[tuple(next_to)].set(largest)


def level_of(key, dims, cuts, smallest, largest):
    level = 1.0
    for axis_at, parts in cuts:
        draws = jax.random.uniform(jax.random.fold_in(jax.random.fold_in(key, 6), axis_at), (parts,), jnp.float32, smallest / len(cuts), largest / len(cuts))
        level = level * jnp.repeat(jnp.exp(draws), dims[axis_at] // parts).reshape((-1,) + (1,) * (len(dims) - 1 - axis_at))
    return level


def length_profile(number_of, total, bound, lean):
    portions = [(1 << 20) // math.isqrt(rank ** lean) + 1 for rank in range(2, number_of + 1)]
    spare, given = total - bound - (number_of - 1), [1] * (number_of - 1)
    while spare > 0:
        candidates = [i for i in range(number_of - 1) if given[i] < bound]
        pool, left = sum([portions[i] for i in candidates]), spare
        for i in candidates:
            extra = min(bound - given[i], max(1, left * portions[i] // pool), spare)
            given[i] = given[i] + extra
            spare = spare - extra
    return np.array([bound] + given)


def ragged(key, number_of, total, limit, lean):
    if number_of == 2:
        one = jax.random.randint(key, (), max(1, total - limit), min(limit, total - 1) + 1)
        return jnp.stack([one, total - one])
    sizes = jnp.asarray(length_profile(number_of, total, limit, lean), jnp.int32)
    couples = (number_of - 1) // 2
    source_of, sink = sizes[1:1 + 2 * couples:2], sizes[2:2 + 2 * couples:2]
    margin = jnp.minimum(source_of - 1, limit - sink)
    moved = jax.random.randint(jax.random.fold_in(key, 1), (couples,), 0, 1 << 20) % (margin + 1)
    sizes = sizes.at[1:1 + 2 * couples:2].set(source_of - moved).at[2:2 + 2 * couples:2].set(sink + moved)
    return sizes[jax.random.permutation(jax.random.fold_in(key, 2), number_of)]


def scatter_about(stream_key, shape, deviation, bound, cuts=(), held_as=jnp.bfloat16):
    values = deviation * jax.random.normal(stream_key, shape, jnp.float32)
    if cuts:
        values = values * level_of(stream_key, shape, cuts, -0.22, 0.18)
    return jnp.clip(values, -bound, bound).astype(held_as)


def setup_inputs(seed: int = 0) -> dict:
    streams_of = jax.random.split(jax.random.key(seed), 18)
    return {
        "tokens": scatter_about(streams_of[0], (TOKENS, D), 1.0, 6.0, ((0, 32),)),
        "cotangent": scatter_about(streams_of[1], (TOKENS, D), 1.0, 6.0, ((0, 32),)),
        "send_slot": draw_send_slot(jax.random.fold_in(streams_of[17], 71), 0),
        "recv_slot": draw_recv_slot(jax.random.fold_in(streams_of[17], 71), 0),
        "lengths": jax.vmap(lambda own: ragged(own, SEQS, TOK_DEV, LONGEST, 2))(jax.random.split(streams_of[4], BLOCKS)).reshape((BLOCKS, SEQS)).astype(jnp.int32),
        "variate": plant(jax.random.randint(streams_of[5], (TOKENS,), 0, 4), jax.random.fold_in(streams_of[5], 1), 0, 3).astype(jnp.int32),
        "valid_mask": draw_valid_mask(jax.random.fold_in(streams_of[17], 71), 0),
        "norm_attn": jnp.clip(1.0 + 0.1 * jax.random.normal(streams_of[7], (D,), jnp.float32), 0.5, 1.5).astype(jnp.bfloat16),
        "w_query": scatter_about(streams_of[8], (D, D), D ** -0.5, 0.1875, ((0, 16),)),
        "w_key": scatter_about(streams_of[9], (D, D), D ** -0.5, 0.1875, ((0, 16),)),
        "w_value": scatter_about(streams_of[10], (D, D), D ** -0.5, 0.1875, ((0, 16),)),
        "w_out": scatter_about(streams_of[11], (D, D), (D // 16) ** -0.5, 0.75, ((0, 16),)),
        "variate_bias": scatter_about(streams_of[12], (2, HEADS), 1.0, 3.0, (), jnp.float32),
        "norm_mlp": jnp.clip(1.0 + 0.1 * jax.random.normal(streams_of[13], (D,), jnp.float32), 0.5, 1.5).astype(jnp.bfloat16),
        "w_gate": scatter_about(streams_of[14], (D, FF), D ** -0.5, 0.1875, ((0, 16),)),
        "w_up": scatter_about(streams_of[15], (D, FF), D ** -0.5, 0.1875, ((0, 16),)),
        "w_down": scatter_about(streams_of[16], (FF, D), (FF // 4) ** -0.5, 0.1875, ((0, 16),)),
    }


epsilon = 1e-06
masked_score = -1e+30

@jax.custom_vjp
def low(v):
    return lax.optimization_barrier(v.astype(jnp.bfloat16)).astype(jnp.float32)

@jax.custom_vjp
def low_back(v):
    return v

def low_keep(v):
    return (low(v), None)

def low_pass(kept, grad):
    return (grad,)

def back_keep(v):
    return (v, None)

def back_low(kept, grad):
    return (low(grad),)
low.defvjp(low_keep, low_pass)
low_back.defvjp(back_keep, back_low)

def product(left, right):
    return jnp.dot(left, right, precision=lax.Precision.HIGHEST)

def rms_scale(values, gain):
    return values * lax.rsqrt(lax.optimization_barrier(jnp.mean(values * values, axis=-1, keepdims=True)) + epsilon) * gain

def angles(position):
    half_dim = HD // 2
    inverse_freq = 1.0 / 10000.0 ** (jnp.arange(half_dim, dtype=jnp.float32) / half_dim)
    theta_angle = position.astype(jnp.float32)[:, None] * inverse_freq[None, :]
    return (jnp.cos(theta_angle), jnp.sin(theta_angle))

def rotate(values, cosine_table, sine_table):
    row_count = values.shape[0]
    half_dim = HD // 2
    halves = values.reshape(row_count, HEADS, 2, half_dim)
    former = halves[:, :, 0]
    latter = halves[:, :, 1]
    cosine_wide = cosine_table[:, None, :]
    sine_wide = sine_table[:, None, :]
    turned = jnp.stack([former * cosine_wide - latter * sine_wide, latter * cosine_wide + former * sine_wide], axis=2)
    return turned.reshape(row_count, HEADS * HD)

def layout(lengths_row):
    slot_ids = jnp.arange(TOK_DEV, dtype=jnp.int32)
    seq_ends = jnp.cumsum(lengths_row).astype(jnp.int32)
    segment = lax.optimization_barrier(jnp.sum((slot_ids[:, None] >= seq_ends[None, :]).astype(jnp.int32), axis=1)).astype(jnp.int32)
    starts = (seq_ends - lengths_row).astype(jnp.int32)
    chosen = segment[:, None] == jnp.arange(SEQS, dtype=jnp.int32)[None, :]
    begins = lax.optimization_barrier(jnp.sum(jnp.where(chosen, starts[None, :], 0), axis=1)).astype(jnp.int32)
    return (segment, (slot_ids - begins).astype(jnp.int32))

def block_attention(variate_bias, pieces):
    queries, key_rows, value_rows, segment, variate, valid_mask = pieces
    scores = jnp.einsum('qhd,khd->hqk', queries, key_rows, precision=lax.Precision.HIGHEST)
    same_variate = variate[:, None] == variate[None, :]
    scores = scores + jnp.where(same_variate[None], variate_bias[0][:, None, None], variate_bias[1][:, None, None])
    scores = low_back(scores)
    itself = jnp.arange(TOK_DEV)[:, None] == jnp.arange(TOK_DEV)[None, :]
    visible = (segment[:, None] == segment[None, :]) & ((valid_mask[None, :] > 0) | itself)
    scores = jnp.where(visible[None], scores, masked_score)
    softmax_rows = jax.nn.softmax(scores, axis=-1)
    return jnp.einsum('hqk,khd->qhd', low(softmax_rows), value_rows, precision=lax.Precision.HIGHEST)

def layer_rows(weights, pieces):
    norm_attn, w_query, w_key, w_value, w_out, variate_bias, norm_mlp, w_gate, w_up, w_down = weights
    stream, segment, position, variate, valid_mask = pieces
    row_count = stream.shape[0]
    blocks = row_count // TOK_DEV
    normed = low(rms_scale(stream, norm_attn))
    cosine_table, sine_table = angles(position)
    queries = low(rotate(low_back(product(normed, w_query)), cosine_table, sine_table) * (1.0 / math.sqrt(HD)))
    key_rows = low(rotate(low_back(product(normed, w_key)), cosine_table, sine_table))
    value_rows = low(low_back(product(normed, w_value)))

    def split_heads(flat_array):
        return flat_array.reshape(blocks, TOK_DEV, HEADS, HD)

    def attend(pieces_block):
        return jax.checkpoint(block_attention)(variate_bias, pieces_block)
    attended = lax.map(attend, (split_heads(queries), split_heads(key_rows), split_heads(value_rows), segment.reshape(blocks, TOK_DEV), variate.reshape(blocks, TOK_DEV), valid_mask.reshape(blocks, TOK_DEV)))
    attended = low(low_back(attended.reshape(row_count, HEADS * HD)))
    attn_out = product(attended, w_out)
    middle = stream + low_back(attn_out)
    normed_mlp = low(rms_scale(middle, norm_mlp))
    gate_proj = low_back(product(normed_mlp, w_gate))
    up_proj = low_back(product(normed_mlp, w_up))
    hidden = low(gate_proj * jax.nn.sigmoid(gate_proj) * up_proj)
    mlp_out = product(hidden, w_down)
    result = middle + low_back(mlp_out)
    weight_rows = (valid_mask > 0).astype(stream.dtype)[:, None]
    square_sums = jnp.stack([jnp.sum(weight_rows * branch_value * branch_value) for branch_value in (stream, attn_out, middle, mlp_out, result)] + [jnp.sum(weight_rows)])
    return (result, square_sums)

def reference(tokens, cotangent, send_slot, recv_slot, lengths, variate, valid_mask, norm_attn, w_query, w_key, w_value, w_out, variate_bias, norm_mlp, w_gate, w_up, w_down):
    token_ids = jnp.arange(TOKENS, dtype=jnp.int32)
    block_ids = (token_ids // TOK_DEV).astype(jnp.int32)
    in_keys = (block_ids * (N_SHARD * CAP) + send_slot).astype(jnp.int32)
    group_ids = (block_ids // N_SHARD).astype(jnp.int32)
    senders = (recv_slot // CAP).astype(jnp.int32)
    out_keys = ((group_ids * N_SHARD + senders) * (N_SHARD * CAP) + block_ids % N_SHARD * CAP + recv_slot % CAP).astype(jnp.int32)
    lookup = jnp.zeros((BLOCKS * N_SHARD * CAP,), jnp.int32).at[in_keys].set(token_ids)
    source = lookup[out_keys].astype(jnp.int32)
    inverse = jnp.zeros((TOKENS,), jnp.int32).at[source].set(token_ids)
    segment, position = jax.vmap(layout)(lengths)
    per_span = 4 if BLOCKS % 4 == 0 else 1
    span_count = BLOCKS // per_span
    span_rows = per_span * TOK_DEV

    def forward(stream_in, gain_attn, query_w, key_w, value_w, out_w, bias_w, gain_mlp, gate_w, up_w, down_w):
        weights = (gain_attn, query_w, key_w, value_w, out_w, bias_w, gain_mlp, gate_w, up_w, down_w)
        stream = stream_in[source]

        def run_span(pieces):
            return jax.checkpoint(layer_rows)(weights, pieces)
        results, square_sums = lax.map(run_span, (stream.reshape(span_count, span_rows, D), segment.reshape(span_count, span_rows), position.reshape(span_count, span_rows), variate.reshape(span_count, span_rows), valid_mask.reshape(span_count, span_rows)))
        return (results.reshape(TOKENS, D)[inverse], lax.optimization_barrier(jnp.sum(square_sums, axis=0)))
    output, pullback, square_sums = jax.vjp(forward, tokens.astype(jnp.float32), norm_attn.astype(jnp.float32), w_query.astype(jnp.float32), w_key.astype(jnp.float32), w_value.astype(jnp.float32), w_out.astype(jnp.float32), variate_bias, norm_mlp.astype(jnp.float32), w_gate.astype(jnp.float32), w_up.astype(jnp.float32), w_down.astype(jnp.float32), has_aux=True)
    gradients = pullback(cotangent.astype(jnp.float32))
    root_means = jnp.sqrt(square_sums[:5] / (square_sums[5] * D))
    return (output.astype(jnp.bfloat16), gradients[0].astype(jnp.bfloat16), gradients[1], gradients[2], gradients[3], gradients[4], gradients[5], gradients[6], gradients[7], gradients[8], gradients[9], gradients[10], root_means)
```

```python
import functools
import math

import jax
import jax.numpy as jnp
from jax import lax
from jax.experimental import pallas as pl
from jax.experimental.pallas import tpu as pltpu
from jax.sharding import PartitionSpec as P

MESH = pl.DeviceIdType.MESH
DMA = pltpu.SemaphoreType.DMA

epsilon = 1e-06
masked_score = -1e30


def rms_parts(stream):
    factor = lax.rsqrt(jnp.mean(stream * stream, axis=-1, keepdims=True) + epsilon)
    return (stream * factor, factor)


def rms_back(grad_normed, normed, factor, gain):
    scaled = grad_normed * gain
    return factor * (scaled - normed * jnp.mean(scaled * normed, axis=-1, keepdims=True))


def angle_tables(position, head_dim):
    half_dim = head_dim // 2
    inverse_freq = 1.0 / 10000.0 ** (jnp.arange(half_dim, dtype=jnp.float32) / half_dim)
    theta_angle = position.astype(jnp.float32)[:, None] * inverse_freq[None, :]
    return (jnp.cos(theta_angle), jnp.sin(theta_angle))


def rotate(values, cosine_table, sine_table, head_count, direction):
    row_count = values.shape[0]
    half_dim = cosine_table.shape[1]
    halves = values.reshape(row_count, head_count, 2, half_dim)
    former = halves[:, :, 0]
    latter = halves[:, :, 1]
    cosine_wide = cosine_table[:, None, :]
    sine_wide = direction * sine_table[:, None, :]
    turned = jnp.stack(
        [former * cosine_wide - latter * sine_wide, latter * cosine_wide + former * sine_wide],
        axis=2,
    )
    return turned.reshape(row_count, head_count * 2 * half_dim)


def layout(lengths_row, tok_rows):
    slot_ids = jnp.arange(tok_rows, dtype=jnp.int32)
    seq_ends = jnp.cumsum(lengths_row)
    segment = jnp.sum((slot_ids[:, None] >= seq_ends[None, :]).astype(jnp.int32), axis=1)
    starts = seq_ends - lengths_row
    chosen = segment[:, None] == jnp.arange(lengths_row.shape[0], dtype=jnp.int32)[None, :]
    begins = jnp.sum(jnp.where(chosen, starts[None, :], 0), axis=1)
    return (segment, slot_ids - begins)


def group_scores(query_part, key_part, same_variate, visible, bias_same, bias_other):
    scores = jnp.einsum("qhd,khd->hqk", query_part, key_part, preferred_element_type=jnp.float32)
    scores = scores + jnp.where(
        same_variate[None], bias_same[:, None, None], bias_other[:, None, None]
    )
    return jnp.where(visible[None], scores, masked_score)


def attention_forward(
    queries, key_rows, value_rows, same_variate, visible, variate_bias, group_size
):
    head_count = variate_bias.shape[1]
    row_count = queries.shape[0]
    head_dim = queries.shape[1] // head_count
    query_heads = queries.reshape(row_count, head_count, head_dim)
    key_heads = key_rows.reshape(row_count, head_count, head_dim)
    value_heads = value_rows.reshape(row_count, head_count, head_dim)
    outputs = []
    log_sums = []
    for head_start in range(0, head_count, group_size):
        picked = slice(head_start, head_start + group_size)
        scores = group_scores(
            query_heads[:, picked],
            key_heads[:, picked],
            same_variate,
            visible,
            variate_bias[0, picked],
            variate_bias[1, picked],
        )
        top_score = jnp.max(scores, axis=-1, keepdims=True)
        exponent_rows = jnp.exp(scores - top_score)
        row_total = jnp.sum(exponent_rows, axis=-1, keepdims=True)
        softmax_rows = (exponent_rows / row_total).astype(jnp.bfloat16)
        outputs.append(
            jnp.einsum(
                "hqk,khd->qhd",
                softmax_rows,
                value_heads[:, picked],
                preferred_element_type=jnp.float32,
            )
        )
        log_sums.append(top_score + jnp.log(row_total))
    return (jnp.concatenate(outputs, axis=1).reshape(row_count, head_count * head_dim), log_sums)


def attention_backward(
    queries,
    key_rows,
    value_rows,
    grad_attended,
    log_sums,
    same_variate,
    visible,
    variate_bias,
    group_size,
):
    head_count = variate_bias.shape[1]
    row_count = queries.shape[0]
    head_dim = queries.shape[1] // head_count
    query_heads = queries.reshape(row_count, head_count, head_dim)
    key_heads = key_rows.reshape(row_count, head_count, head_dim)
    value_heads = value_rows.reshape(row_count, head_count, head_dim)
    grad_heads = grad_attended.reshape(row_count, head_count, head_dim)
    query_grads = []
    key_grads = []
    value_grads = []
    same_grads = []
    other_grads = []
    for group_index, head_start in enumerate(range(0, head_count, group_size)):
        picked = slice(head_start, head_start + group_size)
        query_part = query_heads[:, picked]
        key_part = key_heads[:, picked]
        grad_part = grad_heads[:, picked]
        scores = group_scores(
            query_part,
            key_part,
            same_variate,
            visible,
            variate_bias[0, picked],
            variate_bias[1, picked],
        )
        softmax_rows = jnp.exp(scores - log_sums[group_index])
        grad_soft = jnp.einsum(
            "qhd,khd->hqk", grad_part, value_heads[:, picked], preferred_element_type=jnp.float32
        )
        inner_sum = jnp.sum(softmax_rows * grad_soft, axis=-1, keepdims=True)
        grad_scores = (softmax_rows * (grad_soft - inner_sum)).astype(jnp.bfloat16)
        grad_wide = grad_scores.astype(jnp.float32)
        same_grads.append(jnp.sum(jnp.where(same_variate[None], grad_wide, 0.0), axis=(1, 2)))
        other_grads.append(jnp.sum(jnp.where(same_variate[None], 0.0, grad_wide), axis=(1, 2)))
        query_grads.append(
            jnp.einsum("hqk,khd->qhd", grad_scores, key_part, preferred_element_type=jnp.float32)
        )
        key_grads.append(
            jnp.einsum("hqk,qhd->khd", grad_scores, query_part, preferred_element_type=jnp.float32)
        )
        value_grads.append(
            jnp.einsum(
                "hqk,qhd->khd",
                softmax_rows.astype(jnp.bfloat16),
                grad_part,
                preferred_element_type=jnp.float32,
            )
        )
    width_total = head_count * head_dim
    bias_grad = jnp.stack([jnp.concatenate(same_grads), jnp.concatenate(other_grads)])
    return (
        jnp.concatenate(query_grads, axis=1).reshape(row_count, width_total),
        jnp.concatenate(key_grads, axis=1).reshape(row_count, width_total),
        jnp.concatenate(value_grads, axis=1).reshape(row_count, width_total),
        bias_grad,
    )


def deal_buffer(rows_in, slot_ids, slot_total):
    return jnp.zeros((slot_total, rows_in.shape[1]), rows_in.dtype).at[slot_ids].set(rows_in)


def contract_rows(left, right):
    return lax.dot_general(
        left, right, (((0,), (0,)), ((), ())), preferred_element_type=jnp.float32
    )


def contract_cols(left, right):
    return lax.dot_general(
        left, right, (((1,), (1,)), ((), ())), preferred_element_type=jnp.float32
    )


def ring_place(chip, chips):
    return jnp.where(chip % 2 == 0, chip // 2, chips - 1 - chip // 2)


def ring_chip(place, chips):
    wrapped = lax.rem(place + 2 * chips, chips)
    return jnp.where(wrapped < chips // 2, 2 * wrapped, 2 * (chips - 1 - wrapped) + 1)


class Spot:
    def __init__(self, shards):
        self.shards = shards
        self.chips = shards // 2
        self.hops = self.chips - 1
        self.rep = lax.axis_index("rep")
        self.shard = lax.axis_index("shard")
        self.core = lax.rem(self.shard, 2)
        self.place = ring_place(self.shard // 2, self.chips)
        self.sibling = self.shard + 1 - 2 * self.core

    def block(self, place, core=None):
        return 2 * ring_chip(place, self.chips) + (self.core if core is None else core)

    def along(self, way, distance):
        return self.place - distance if way == 0 else self.place + distance

    def ahead(self, way):
        return (self.rep, self.block(self.along(way, -1)))


def greet(spot, everyone=False):
    barrier = pltpu.get_barrier_semaphore()
    shards = spot.shards

    def peer(k, carry):
        target = lax.rem(spot.shard + k, shards)
        pl.semaphore_signal(barrier, inc=1, device_id=(spot.rep, target), device_id_type=MESH)
        return carry

    lax.fori_loop(1, shards, peer, 0)
    if not everyone:
        pl.semaphore_signal(
            barrier, inc=1, device_id=(1 - spot.rep, spot.shard), device_id_type=MESH
        )
        pl.semaphore_wait(barrier, shards)
        return

    def other(k, carry):
        pl.semaphore_signal(barrier, inc=1, device_id=(1 - spot.rep, k), device_id_type=MESH)
        return carry

    lax.fori_loop(0, shards, other, 0)
    pl.semaphore_wait(barrier, 2 * shards - 1)


def remote(src, dst, sems, at, target):
    return pltpu.make_async_remote_copy(
        src_ref=src,
        dst_ref=dst,
        send_sem=sems[0].at[at],
        recv_sem=sems[1].at[at],
        device_id=target,
        device_id_type=MESH,
    )


class Swap:
    def __init__(self, spot, source, arrived, sems, own_sem):
        self.spot, self.sems = spot, sems
        self.source, self.arrived = source, arrived
        self.capacity = source.shape[0] // spot.shards
        mine = pl.ds(spot.shard * self.capacity, self.capacity)
        self.own = pltpu.make_async_copy(source.at[mine], arrived.at[mine], own_sem)

    def copy(self, k):
        spot = self.spot
        target = lax.rem(spot.shard + k, spot.shards)
        return remote(
            self.source.at[pl.ds(target * self.capacity, self.capacity)],
            self.arrived.at[pl.ds(spot.shard * self.capacity, self.capacity)],
            self.sems,
            (k,),
            (spot.rep, target),
        )

    def start(self):
        def one(k, carry):
            self.copy(k).start()
            return carry

        lax.fori_loop(1, self.spot.shards, one, 0)
        self.own.start()

    def finish(self):
        def one(k, carry):
            self.copy(k).wait()
            return carry

        lax.fori_loop(1, self.spot.shards, one, 0)
        self.own.wait()


class Gather:
    def __init__(self, spot, shard_ref, full_ref, sems):
        self.spot, self.shard_ref, self.full_ref = spot, shard_ref, full_ref
        self.rows = shard_ref.shape[0]
        self.unit = shard_ref.shape[1] // 8
        self.ring_sems, self.near_sems, self.far_sems, self.far_near_sems = (
            sems[0:2],
            sems[2:4],
            sems[4:6],
            sems[6:8],
        )
        self.whole_sems, self.own_sem = sems[8:10], sems[10]

    def cut(self, block, first, count):
        columns = pl.ds(pl.multiple_of(first * self.unit, 128), count * self.unit)
        return self.full_ref.at[pl.ds(block * self.rows, self.rows), columns]

    def ring(self, way, hop, source=None):
        spot = self.spot
        region = self.cut(spot.block(spot.along(way, hop)), 2 * spot.rep + 3 * way, 3)
        return remote(
            region if source is None else source,
            region,
            self.ring_sems,
            (way, hop),
            spot.ahead(way),
        )

    def near(self, way, hop):
        spot = self.spot
        region = self.cut(spot.block(spot.along(way, hop + 1)), 2 * spot.rep + 3 * way, 3)
        return remote(region, region, self.near_sems, (way, hop), (spot.rep, spot.sibling))

    def far(self, hop):
        spot = self.spot
        turn = (1 - 2 * spot.rep) * (hop + 1)
        region = self.cut(spot.block(spot.place - turn), 6 * spot.rep, 2)
        return remote(region, region, self.far_sems, (hop,), (1 - spot.rep, spot.shard))

    def far_near(self, hop):
        spot = self.spot
        turn = (1 - 2 * spot.rep) * (hop + 1)
        region = self.cut(spot.block(spot.place + turn), 6 * (1 - spot.rep), 2)
        return remote(region, region, self.far_near_sems, (hop,), (spot.rep, spot.sibling))

    def own(self):
        spot = self.spot
        mine = self.full_ref.at[pl.ds(spot.shard * self.rows, self.rows)]
        whole = remote(self.shard_ref, mine, self.whole_sems, (0,), (spot.rep, spot.sibling))
        return whole, pltpu.make_async_copy(self.shard_ref, mine, self.own_sem)

    def start(self):
        for way in (0, 1):
            first = 2 * self.spot.rep + 3 * way
            columns = pl.ds(pl.multiple_of(first * self.unit, 128), 3 * self.unit)
            self.ring(way, 0, self.shard_ref.at[:, columns]).start()
        for copy in self.own():
            copy.start()

    def step(self, hop, last=False):
        for way in (0, 1):
            self.ring(way, hop).wait_recv()
            if not last:
                self.ring(way, hop + 1).start()
            self.near(way, hop).start()
        self.far(hop).start()

    def relay(self, hop):
        self.far(hop).wait_recv()
        self.far_near(hop).start()

    def finish(self):
        for copy in self.own():
            copy.wait()

        def one(hop, carry):
            for way in (0, 1):
                self.ring(way, hop).wait_send()
                self.near(way, hop).wait()
            self.far(hop).wait_send()
            self.far_near(hop).wait()
            return carry

        lax.fori_loop(0, self.spot.hops, one, 0)

    @staticmethod
    def scratch(hops):
        pairs = [DMA((2, hops))] * 4 + [DMA((hops,))] * 4 + [DMA((1,))] * 2
        return pairs + [DMA]


def run_gathers(gathers, hops):
    for gather in gathers:
        gather.start()

    def one(hop, carry):
        for gather in gathers:
            gather.step(hop)

            @pl.when(hop > 0)
            def _():
                gather.relay(hop - 1)

        return carry

    lax.fori_loop(0, hops - 1, one, 0)
    for gather in gathers:
        gather.step(hops - 1, last=True)
        gather.relay(hops - 2)
    for gather in gathers:
        gather.relay(hops - 1)
        gather.finish()


def gather_kernel(shards, group_count, swap_count, *refs):
    spot = Spot(shards)
    inputs, rest = refs[: group_count + swap_count], refs[group_count + swap_count :]
    outputs, scratch = rest[: group_count + swap_count], rest[group_count + swap_count :]
    greet(spot)
    gathers = [
        Gather(spot, inputs[g], outputs[g], scratch[11 * g : 11 * g + 11])
        for g in range(group_count)
    ]
    scratch = scratch[11 * group_count :]
    swaps = [
        Swap(
            spot,
            inputs[group_count + i],
            outputs[group_count + i],
            scratch[3 * i : 3 * i + 2],
            scratch[3 * i + 2],
        )
        for i in range(swap_count)
    ]
    for swap in swaps:
        swap.start()
    run_gathers(gathers, spot.hops)
    for swap in swaps:
        swap.finish()


def gather_call(shards, pieces, sent, collective_id):
    hops = shards // 2 - 1
    scratch = Gather.scratch(hops) * len(pieces)
    scratch += [DMA((shards,)), DMA((shards,)), DMA] * len(sent)
    anywhere = pl.BlockSpec(memory_space=pl.ANY)
    results = pl.pallas_call(
        functools.partial(gather_kernel, shards, len(pieces), len(sent)),
        out_shape=[
            jax.ShapeDtypeStruct((shards * piece.shape[0], piece.shape[1]), piece.dtype)
            for piece in pieces
        ]
        + [jax.ShapeDtypeStruct(rows.shape, rows.dtype) for rows in sent],
        in_specs=[anywhere] * (len(pieces) + len(sent)),
        out_specs=[anywhere] * (len(pieces) + len(sent)),
        scratch_shapes=scratch,
        compiler_params=pltpu.CompilerParams(
            collective_id=collective_id, has_side_effects=True
        ),
    )(*pieces, *sent)
    return results[: len(pieces)], results[len(pieces) :]


class Reduce:
    def __init__(self, spot, partial_ref, out_ref, refs):
        self.spot, self.partial, self.out = spot, partial_ref, out_ref
        self.rows, self.columns = out_ref.shape
        self.unit = self.columns // 8
        (
            self.own_ring,
            self.sib_ring,
            self.got_ring,
            self.own_far,
            self.sib_far,
            self.got_far,
            self.got_last,
        ) = refs[:7]
        sems = refs[7:]
        self.load_ring_sem, self.load_far_sem = sems[0], sems[1]
        self.sib_ring_sems, self.sib_far_sems = sems[2:4], sems[4:6]
        self.ring_sems, self.far_sems, self.last_sems = sems[6:8], sems[8:10], sems[10:12]

    @staticmethod
    def scratch(shards, rows, columns):
        chips = shards // 2
        unit = columns // 8
        half = jnp.bfloat16
        buffers = [
            pltpu.VMEM((2, chips, rows, 3 * unit), half),
            pltpu.VMEM((2, chips, rows, 3 * unit), half),
            pltpu.VMEM((2, chips - 1, rows, 3 * unit), half),
            pltpu.VMEM((chips, rows, 2 * unit), half),
            pltpu.VMEM((chips, rows, 2 * unit), half),
            pltpu.VMEM((chips, rows, 2 * unit), half),
            pltpu.VMEM((2, rows, 3 * unit), half),
        ]
        sems = [DMA((2, chips)), DMA((chips,))]
        sems += [DMA((2, chips))] * 2 + [DMA((chips,))] * 2
        sems += [DMA((2, chips))] * 2 + [DMA((chips,))] * 2 + [DMA((2,))] * 2
        return buffers + sems

    def cut(self, block, first, count):
        columns = pl.ds(pl.multiple_of(first * self.unit, 128), count * self.unit)
        return self.partial.at[pl.ds(block * self.rows, self.rows), columns]

    def ring_cut(self, way, step, core):
        spot = self.spot
        return self.cut(
            spot.block(spot.along(way, step + 1), core), 2 * spot.rep + 3 * way, 3
        )

    def far_cut(self, step, core):
        spot = self.spot
        place = spot.place + (1 - 2 * spot.rep) * (step + 1)
        return self.cut(spot.block(place, core), 6 * (1 - spot.rep), 2)

    def load_ring(self, way, step):
        return pltpu.make_async_copy(
            self.ring_cut(way, step, self.spot.core),
            self.own_ring.at[way, step],
            self.load_ring_sem.at[way, step],
        )

    def load_far(self, step):
        return pltpu.make_async_copy(
            self.far_cut(step, self.spot.core), self.own_far.at[step], self.load_far_sem.at[step]
        )

    def give_ring(self, way, step):
        spot = self.spot
        return remote(
            self.ring_cut(way, step, 1 - spot.core),
            self.sib_ring.at[way, step],
            self.sib_ring_sems,
            (way, step),
            (spot.rep, spot.sibling),
        )

    def give_far(self, step):
        spot = self.spot
        return remote(
            self.far_cut(step, 1 - spot.core),
            self.sib_far.at[step],
            self.sib_far_sems,
            (step,),
            (spot.rep, spot.sibling),
        )

    def ring(self, way, step):
        return remote(
            self.own_ring.at[way, step],
            self.got_ring.at[way, step],
            self.ring_sems,
            (way, step),
            self.spot.ahead(way),
        )

    def far(self, step):
        spot = self.spot
        return remote(
            self.own_far.at[step],
            self.got_far.at[step],
            self.far_sems,
            (step,),
            (1 - spot.rep, spot.shard),
        )

    def last(self, way):
        spot = self.spot
        return remote(
            self.own_ring.at[way, spot.hops],
            self.got_last.at[way],
            self.last_sems,
            (way,),
            (1 - spot.rep, spot.shard),
        )

    def start(self):
        def one(step, carry):
            self.load_far(step).start()
            self.give_far(step).start()
            for way in (0, 1):
                self.load_ring(way, step).start()
                self.give_ring(way, step).start()
            return carry

        lax.fori_loop(0, self.spot.chips, one, 0)

    def tiles(self, body):
        def one(tile, carry):
            body(pl.ds(pl.multiple_of(tile * 16, 16), 16))
            return carry

        lax.fori_loop(0, self.rows // 16, one, 0)

    def far_step(self, step):
        self.load_far(step).wait()
        self.give_far(step).wait_recv()

        def add(rows):
            total = self.own_far[step, rows].astype(jnp.float32)
            total += self.sib_far[step, rows].astype(jnp.float32)
            self.own_far[step, rows] = total.astype(jnp.bfloat16)

        self.tiles(add)
        self.far(step).start()

    def ring_step(self, way, step, first=False, last=False):
        unit = self.unit
        self.load_ring(way, step).wait()
        self.give_ring(way, step).wait_recv()
        if not first:
            self.ring(way, step - 1).wait_recv()

        @pl.when(self.spot.rep == way)
        def _():
            self.far(step).wait_recv()

            def add_far(rows):
                part = pl.ds(way * unit, 2 * unit)
                total = self.sib_ring[way, step, rows, part].astype(jnp.float32)
                total += self.got_far[step, rows].astype(jnp.float32)
                self.sib_ring[way, step, rows, part] = total.astype(jnp.bfloat16)

            self.tiles(add_far)

        def add(rows):
            total = self.own_ring[way, step, rows].astype(jnp.float32)
            total += self.sib_ring[way, step, rows].astype(jnp.float32)
            if not first:
                total += self.got_ring[way, step - 1, rows].astype(jnp.float32)
            self.own_ring[way, step, rows] = total.astype(jnp.bfloat16)

        self.tiles(add)
        if last:
            self.last(way).start()
        else:
            self.ring(way, step).start()

    def finish(self):
        spot, unit = self.spot, self.unit
        for way in (0, 1):
            self.last(way).wait()
        mine = [self.own_ring.at[way, spot.hops] for way in (0, 1)]
        theirs = [self.got_last.at[way] for way in (0, 1)]

        def write(lower, upper):
            def body(rows):
                def read(ref, first, count):
                    return ref[rows, pl.ds(first * unit, count * unit)].astype(jnp.float32)

                def put(first, count, value):
                    self.out[rows, pl.ds(first * unit, count * unit)] = value

                put(0, 2, read(lower[0], 0, 2))
                put(2, 1, read(lower[0], 2, 1) + read(upper[0], 0, 1))
                put(3, 2, read(lower[1], 0, 2) + read(upper[0], 1, 2))
                put(5, 1, read(lower[1], 2, 1) + read(upper[1], 0, 1))
                put(6, 2, read(upper[1], 1, 2))

            self.tiles(body)

        @pl.when(spot.rep == 0)
        def _():
            write(mine, theirs)

        @pl.when(spot.rep == 1)
        def _():
            write(theirs, mine)

        def one(step, carry):
            self.give_far(step).wait_send()
            self.far(step).wait_send()
            for way in (0, 1):
                self.give_ring(way, step).wait_send()

            @pl.when(step < spot.hops)
            def _():
                for way in (0, 1):
                    self.ring(way, step).wait_send()

            return carry

        lax.fori_loop(0, spot.chips, one, 0)


def run_reduces(reduces, hops):
    for reduce in reduces:
        reduce.start()
    for reduce in reduces:
        reduce.far_step(0)
    for reduce in reduces:
        for way in (0, 1):
            reduce.ring_step(way, 0, first=True)
        reduce.far_step(1)

    def one(step, carry):
        for reduce in reduces:
            for way in (0, 1):
                reduce.ring_step(way, step)
            reduce.far_step(step + 1)
        return carry

    lax.fori_loop(1, hops, one, 0)
    for reduce in reduces:
        for way in (0, 1):
            reduce.ring_step(way, hops, last=True)
    for reduce in reduces:
        reduce.finish()


class Tally:
    def __init__(self, spot, mine, out, got, sems, own_sem):
        self.spot, self.mine, self.out, self.got = spot, mine, out, got
        self.sems = sems
        self.whole = 2 * spot.shards
        self.rank = spot.rep * spot.shards + spot.shard
        self.own = pltpu.make_async_copy(mine, got.at[self.rank], own_sem)

    def copy(self, k):
        target = lax.rem(self.rank + k, self.whole)
        shards = self.spot.shards
        return remote(
            self.mine,
            self.got.at[self.rank],
            self.sems,
            (k,),
            (target // shards, lax.rem(target, shards)),
        )

    def start(self):
        def one(k, carry):
            self.copy(k).start()
            return carry

        lax.fori_loop(1, self.whole, one, 0)
        self.own.start()

    def finish(self):
        def one(k, carry):
            self.copy(k).wait()
            return carry

        lax.fori_loop(1, self.whole, one, 0)
        self.own.wait()

        def add(k, total):
            return total + self.got[k]

        self.out[...] = lax.fori_loop(0, self.whole, add, jnp.zeros_like(self.out))


def reduce_kernel(shards, group_count, swap_count, tally_count, *refs):
    spot = Spot(shards)
    total = group_count + swap_count + tally_count
    inputs, outputs, scratch = refs[:total], refs[total : 2 * total], refs[2 * total :]
    greet(spot, everyone=tally_count > 0)
    reduces = [
        Reduce(spot, inputs[g], outputs[g], scratch[19 * g : 19 * g + 19])
        for g in range(group_count)
    ]
    scratch = scratch[19 * group_count :]
    swaps = [
        Swap(
            spot,
            inputs[group_count + i],
            outputs[group_count + i],
            scratch[3 * i : 3 * i + 2],
            scratch[3 * i + 2],
        )
        for i in range(swap_count)
    ]
    scratch = scratch[3 * swap_count :]
    tallies = [
        Tally(spot, inputs[-1], outputs[-1], scratch[0], scratch[1:3], scratch[3])
        for _ in range(tally_count)
    ]
    for each in tallies + swaps:
        each.start()
    run_reduces(reduces, spot.hops)
    for each in tallies + swaps:
        each.finish()


def reduce_call(shards, partials, sent, tallied, collective_id):
    scratch = []
    out_shape, out_specs = [], []
    anywhere = pl.BlockSpec(memory_space=pl.ANY)
    inside = pl.BlockSpec(memory_space=pltpu.VMEM)
    for part in partials:
        rows, columns = part.shape[0] // shards, part.shape[1]
        scratch += Reduce.scratch(shards, rows, columns)
        out_shape.append(jax.ShapeDtypeStruct((rows, columns), jnp.float32))
        out_specs.append(inside)
    for rows in sent:
        scratch += [DMA((shards,)), DMA((shards,)), DMA]
        out_shape.append(jax.ShapeDtypeStruct(rows.shape, rows.dtype))
        out_specs.append(anywhere)
    for each in tallied:
        scratch += [pltpu.VMEM((2 * shards, *each.shape), each.dtype)]
        scratch += [DMA((2 * shards,)), DMA((2 * shards,)), DMA]
        out_shape.append(jax.ShapeDtypeStruct(each.shape, each.dtype))
        out_specs.append(inside)
    in_specs = [anywhere] * (len(partials) + len(sent)) + [inside] * len(tallied)
    results = pl.pallas_call(
        functools.partial(reduce_kernel, shards, len(partials), len(sent), len(tallied)),
        out_shape=out_shape,
        in_specs=in_specs,
        out_specs=out_specs,
        scratch_shapes=scratch,
        compiler_params=pltpu.CompilerParams(
            collective_id=collective_id, has_side_effects=True, vmem_limit_bytes=56 << 20
        ),
    )(*partials, *sent, *tallied)
    first, second = len(partials), len(partials) + len(sent)
    return results[:first], results[first:second], results[second:]


def on_device(
    tokens,
    cotangent,
    send_slot,
    recv_slot,
    lengths,
    variate,
    valid_mask,
    norm_attn,
    w_query,
    w_key,
    w_value,
    w_out,
    variate_bias,
    norm_mlp,
    w_gate,
    w_up,
    w_down,
):
    shards = lax.axis_size("shard")
    tok_rows, model_width = tokens.shape
    capacity = 2 * tok_rows // shards
    slot_total = shards * capacity
    head_count = variate_bias.shape[1]
    head_dim = model_width // head_count
    hidden_width = w_gate.shape[1]
    group_size = 4
    score_scale = 1.0 / math.sqrt(head_dim)
    outgoing = (
        deal_buffer(tokens, send_slot, slot_total),
        deal_buffer(cotangent, send_slot, slot_total),
    )
    (full_in, full_out), (arrived_tokens,) = gather_call(
        shards, [jnp.concatenate([w_query, w_key, w_value], axis=1), w_out], [outgoing[0]], 1
    )
    full_query, full_key, full_value = (
        full_in[:, i * model_width : (i + 1) * model_width] for i in range(3)
    )
    (full_gate, full_up, full_down), (arrived_grads,) = gather_call(
        shards, [w_gate, w_up, w_down], [outgoing[1]], 2
    )
    stream_rows = jnp.take(arrived_tokens, recv_slot, axis=0)
    grad_out_rows = jnp.take(arrived_grads, recv_slot, axis=0)
    segment, position = layout(lengths[0], tok_rows)
    same_variate = variate[:, None] == variate[None, :]
    itself = jnp.arange(tok_rows)[:, None] == jnp.arange(tok_rows)[None, :]
    visible = (segment[:, None] == segment[None, :]) & ((valid_mask[None, :] > 0) | itself)
    cosine_table, sine_table = angle_tables(position, head_dim)
    gain_bf_attn, gain_bf_mlp = (
        lax.all_gather(norm_attn, "shard", axis=0, tiled=True),
        lax.all_gather(norm_mlp, "shard", axis=0, tiled=True),
    )
    gain_attn = gain_bf_attn.astype(jnp.float32)
    gain_mlp = gain_bf_mlp.astype(jnp.float32)
    stream = stream_rows.astype(jnp.float32)
    normed_attn, factor_attn = rms_parts(stream)
    input_attn = (normed_attn * gain_attn).astype(jnp.bfloat16)
    query_proj = jnp.dot(input_attn, full_query, preferred_element_type=jnp.float32)
    key_proj = jnp.dot(input_attn, full_key, preferred_element_type=jnp.float32)
    value_proj = jnp.dot(input_attn, full_value, preferred_element_type=jnp.float32)
    queries = (rotate(query_proj, cosine_table, sine_table, head_count, 1.0) * score_scale).astype(
        jnp.bfloat16
    )
    key_rows = rotate(key_proj, cosine_table, sine_table, head_count, 1.0).astype(jnp.bfloat16)
    value_rows = value_proj.astype(jnp.bfloat16)
    attended, log_sums = attention_forward(
        queries, key_rows, value_rows, same_variate, visible, variate_bias, group_size
    )
    attended_bf = attended.astype(jnp.bfloat16)
    attn_out = jnp.dot(attended_bf, full_out, preferred_element_type=jnp.float32)
    middle = stream + attn_out
    normed_mlp, factor_mlp = rms_parts(middle)
    input_mlp = (normed_mlp * gain_mlp).astype(jnp.bfloat16)
    pieces = (full_gate, full_up)
    columns = input_mlp
    gate_proj = jnp.dot(columns, pieces[0], preferred_element_type=jnp.float32)
    up_proj = jnp.dot(columns, pieces[1], preferred_element_type=jnp.float32)
    sigmoid_gate = jax.nn.sigmoid(gate_proj)
    hidden = (gate_proj * sigmoid_gate * up_proj).astype(jnp.bfloat16)
    columns = hidden
    mlp_out = jnp.dot(
        columns,
        full_down,
        preferred_element_type=jnp.float32,
    )
    result = middle + mlp_out
    result_bf = result.astype(jnp.bfloat16)
    grad_result = grad_out_rows.astype(jnp.float32)
    grad_hidden = contract_cols(grad_out_rows, full_down)
    grad_gate = (
        grad_hidden * up_proj * sigmoid_gate * (1.0 + gate_proj * (1.0 - sigmoid_gate))
    ).astype(jnp.bfloat16)
    grad_up = (grad_hidden * gate_proj * sigmoid_gate).astype(jnp.bfloat16)
    pieces = (full_gate, full_up)
    block_cols = contract_cols(grad_gate, pieces[0]) + contract_cols(grad_up, pieces[1])
    grad_gain_mlp = jnp.sum(block_cols * normed_mlp, axis=0)
    grad_middle = grad_result + rms_back(block_cols, normed_mlp, factor_mlp, gain_mlp)
    grad_branch = grad_middle.astype(jnp.bfloat16)
    grad_attended = contract_cols(grad_branch, full_out).astype(jnp.bfloat16)
    grad_queries, grad_keys, grad_values, grad_bias_local = attention_backward(
        queries,
        key_rows,
        value_rows,
        grad_attended,
        log_sums,
        same_variate,
        visible,
        variate_bias,
        group_size,
    )
    grad_query_proj = (
        rotate(grad_queries, cosine_table, sine_table, head_count, -1.0) * score_scale
    ).astype(jnp.bfloat16)
    grad_key_proj = rotate(grad_keys, cosine_table, sine_table, head_count, -1.0).astype(
        jnp.bfloat16
    )
    grad_value_proj = grad_values.astype(jnp.bfloat16)
    grad_input_attn = (
        contract_cols(grad_query_proj, full_query)
        + contract_cols(grad_key_proj, full_key)
        + contract_cols(grad_value_proj, full_value)
    )
    grad_gain_attn = jnp.sum(grad_input_attn * normed_attn, axis=0)
    grad_stream = grad_middle + rms_back(grad_input_attn, normed_attn, factor_attn, gain_attn)
    grad_stream_bf = grad_stream.astype(jnp.bfloat16)
    projection_grads = jnp.concatenate([grad_query_proj, grad_key_proj, grad_value_proj], axis=1)
    homeward = (
        deal_buffer(result_bf, recv_slot, slot_total),
        deal_buffer(grad_stream_bf, recv_slot, slot_total),
    )
    (grad_gate_w, grad_up_w, hidden_share), (home_out,), _ = reduce_call(
        shards,
        [
            contract_rows(input_mlp, grad_gate).astype(jnp.bfloat16),
            contract_rows(input_mlp, grad_up).astype(jnp.bfloat16),
            contract_rows(hidden, grad_out_rows).astype(jnp.bfloat16),
        ],
        [homeward[0]],
        [],
        3,
    )
    weight_rows = (valid_mask > 0).astype(jnp.float32)[:, None]
    square_sums = jnp.stack(
        [
            jnp.sum(weight_rows * stream * stream),
            jnp.sum(weight_rows * attn_out * attn_out),
            jnp.sum(weight_rows * middle * middle),
            jnp.sum(weight_rows * mlp_out * mlp_out),
            jnp.sum(weight_rows * result * result),
            jnp.sum(weight_rows),
        ]
    )
    gain_grads = jnp.stack([grad_gain_attn, grad_gain_mlp])
    small = [gain_grads.reshape(-1), grad_bias_local.reshape(-1), square_sums]
    small_size = sum(each.shape[0] for each in small)
    padded = -(-small_size // 1024) * 1024
    small = jnp.concatenate([*small, jnp.zeros((padded - small_size,), jnp.float32)])
    (grad_in, grad_out), (home_grad,), (small,) = reduce_call(
        shards,
        [
            contract_rows(input_attn, projection_grads).astype(jnp.bfloat16),
            contract_rows(attended_bf, grad_branch).astype(jnp.bfloat16),
        ],
        [homeward[1]],
        [small.reshape(-1, 128)],
        4,
    )
    small = small.reshape(-1)
    gain_totals = small[: 2 * model_width].reshape(2, model_width)
    bias_grads = small[2 * model_width : 2 * model_width + 2 * head_count].reshape(2, head_count)
    total_sums = small[2 * model_width + 2 * head_count :][:6]
    root_means = jnp.sqrt(total_sums[:5] / (total_sums[5] * model_width))
    share_rows = model_width // shards
    share_start = lax.axis_index("shard") * share_rows
    grad_norm_attn = lax.dynamic_slice_in_dim(gain_totals[0], share_start, share_rows)
    grad_norm_mlp = lax.dynamic_slice_in_dim(gain_totals[1], share_start, share_rows)
    output = jnp.take(home_out, send_slot, axis=0)
    input_grad = jnp.take(home_grad, send_slot, axis=0)
    grad_query, grad_key, grad_value = (
        grad_in[:, i * model_width : (i + 1) * model_width] for i in range(3)
    )
    return (
        output,
        input_grad,
        grad_norm_attn,
        grad_query,
        grad_key,
        grad_value,
        grad_out,
        bias_grads,
        grad_norm_mlp,
        grad_gate_w,
        grad_up_w,
        hidden_share,
        root_means,
    )


def solution(mesh):
    in_specs = (
        P(("rep", "shard"), None),
        P(("rep", "shard"), None),
        P(("rep", "shard")),
        P(("rep", "shard")),
        P(("rep", "shard"), None),
        P(("rep", "shard")),
        P(("rep", "shard")),
        P("shard"),
        P("shard", None),
        P("shard", None),
        P("shard", None),
        P("shard", None),
        P(),
        P("shard"),
        P("shard", None),
        P("shard", None),
        P("shard", None),
    )
    out_specs = (
        P(("rep", "shard"), None),
        P(("rep", "shard"), None),
        P("shard"),
        P("shard", None),
        P("shard", None),
        P("shard", None),
        P("shard", None),
        P(),
        P("shard"),
        P("shard", None),
        P("shard", None),
        P("shard", None),
        P(),
    )
    return jax.shard_map(
        on_device, mesh=mesh, in_specs=in_specs, out_specs=out_specs, check_vma=False
    )
```

```python
import functools
import math

import jax
import jax.numpy as jnp
from jax import lax
from jax.experimental import pallas as pl
from jax.experimental.pallas import tpu as pltpu
from jax.sharding import PartitionSpec as P

MESH = pl.DeviceIdType.MESH
DMA = pltpu.SemaphoreType.DMA
epsilon = 1e-06
masked_score = -1e30


def angle_tables(position, head_dim):
    half_dim = head_dim // 2
    inverse_freq = 1.0 / 10000.0 ** (jnp.arange(half_dim, dtype=jnp.float32) / half_dim)
    theta_angle = position.astype(jnp.float32)[:, None] * inverse_freq[None, :]
    return (jnp.cos(theta_angle), jnp.sin(theta_angle))


def layout(lengths_row, tok_rows):
    slot_ids = jnp.arange(tok_rows, dtype=jnp.int32)
    seq_ends = jnp.cumsum(lengths_row)
    segment = jnp.sum((slot_ids[:, None] >= seq_ends[None, :]).astype(jnp.int32), axis=1)
    starts = seq_ends - lengths_row
    chosen = segment[:, None] == jnp.arange(lengths_row.shape[0], dtype=jnp.int32)[None, :]
    begins = jnp.sum(jnp.where(chosen, starts[None, :], 0), axis=1)
    return (segment, slot_ids - begins)


def ring_place(chip, chips):
    return jnp.where(chip % 2 == 0, chip // 2, chips - 1 - chip // 2)


def ring_chip(place, chips):
    wrapped = lax.rem(place + 2 * chips, chips)
    return jnp.where(wrapped < chips // 2, 2 * wrapped, 2 * (chips - 1 - wrapped) + 1)


class Spot:
    def __init__(self, shards):
        self.shards = shards
        self.chips = shards // 2
        self.hops = self.chips - 1
        self.rep = lax.axis_index("rep")
        self.shard = lax.axis_index("shard")
        self.core = lax.rem(self.shard, 2)
        self.place = ring_place(self.shard // 2, self.chips)
        self.sibling = self.shard + 1 - 2 * self.core

    def block(self, place, core=None):
        return 2 * ring_chip(place, self.chips) + (self.core if core is None else core)

    def along(self, way, distance):
        return self.place - distance if way == 0 else self.place + distance

    def ahead(self, way):
        return (self.rep, self.block(self.along(way, -1)))


def greet(spot, everyone=False):
    barrier = pltpu.get_barrier_semaphore()
    shards = spot.shards

    def peer(k, carry):
        target = lax.rem(spot.shard + k, shards)
        pl.semaphore_signal(barrier, inc=1, device_id=(spot.rep, target), device_id_type=MESH)
        return carry

    lax.fori_loop(1, shards, peer, 0)
    if not everyone:
        pl.semaphore_signal(
            barrier, inc=1, device_id=(1 - spot.rep, spot.shard), device_id_type=MESH
        )
        pl.semaphore_wait(barrier, shards)
        return

    def other(k, carry):
        pl.semaphore_signal(barrier, inc=1, device_id=(1 - spot.rep, k), device_id_type=MESH)
        return carry

    lax.fori_loop(0, shards, other, 0)
    pl.semaphore_wait(barrier, 2 * shards - 1)


def remote(src, dst, sems, at, target):
    return pltpu.make_async_remote_copy(
        src_ref=src,
        dst_ref=dst,
        send_sem=sems[0].at[at],
        recv_sem=sems[1].at[at],
        device_id=target,
        device_id_type=MESH,
    )


class Swap:
    def __init__(self, spot, source, arrived, sems, own_sem):
        self.spot, self.sems = spot, sems
        self.source, self.arrived = source, arrived
        self.capacity = arrived.shape[0] // spot.shards
        self.own = pltpu.make_async_copy(
            self.part(spot.shard), arrived.at[self.rows(spot.shard)], own_sem
        )

    def rows(self, shard):
        return pl.ds(pl.multiple_of(shard * self.capacity, 8), self.capacity)

    def part(self, shard):
        if self.source.shape[0] == self.capacity:
            return self.source
        return self.source.at[self.rows(shard)]

    def copy(self, k):
        spot = self.spot
        target = lax.rem(spot.shard + k, spot.shards)
        return remote(
            self.part(target),
            self.arrived.at[self.rows(spot.shard)],
            self.sems,
            (k,),
            (spot.rep, target),
        )

    def start(self, slot, slots):
        size = -(-self.spot.shards // slots)

        def one(k, carry):
            @pl.when(k == 0)
            def _():
                self.own.start()

            @pl.when(k > 0)
            def _():
                self.copy(k).start()

            return carry

        first = jnp.minimum(slot * size, self.spot.shards)
        lax.fori_loop(first, jnp.minimum(first + size, self.spot.shards), one, 0)

    def finish(self):
        def one(k, carry):
            self.copy(k).wait()
            return carry

        lax.fori_loop(1, self.spot.shards, one, 0)
        self.own.wait()


class Gather:
    def __init__(self, spot, lent, shard_ref, full_ref, sems):
        self.spot, self.lent, self.shard_ref, self.full_ref = spot, lent, shard_ref, full_ref
        self.rows = shard_ref.shape[0]
        self.unit = shard_ref.shape[1] // 8
        self.count = (8 - lent) // 2
        self.ring_sems, self.near_sems, self.far_sems, self.far_near_sems = (
            sems[0:2],
            sems[2:4],
            sems[4:6],
            sems[6:8],
        )
        self.whole_sems, self.own_sem = sems[8:10], sems[10]
        self.far_ways = (0, 1) if lent == 4 else (0,)

    def first(self, way):
        return self.lent * self.spot.rep + self.count * way

    def cut(self, block, first, count):
        columns = pl.ds(pl.multiple_of(first * self.unit, 128), count * self.unit)
        return self.full_ref.at[pl.ds(block * self.rows, self.rows), columns]

    def ring(self, way, hop, source=None):
        spot = self.spot
        region = self.cut(spot.block(spot.along(way, hop)), self.first(way), self.count)
        return remote(
            region if source is None else source,
            region,
            self.ring_sems,
            (way, hop),
            spot.ahead(way),
        )

    def near(self, way, hop):
        spot = self.spot
        region = self.cut(spot.block(spot.along(way, hop + 1)), self.first(way), self.count)
        return remote(region, region, self.near_sems, (way, hop), (spot.rep, spot.sibling))

    def far_region(self, way, hop, owner):
        spot = self.spot
        if self.lent == 4:
            block = spot.block(spot.along(way, hop + 1))
            return self.cut(block, 4 * owner + 2 * way, 2)
        turn = (1 - 2 * owner) * (hop + 1)
        return self.cut(spot.block(spot.place - turn), 6 * owner, 2)

    def far(self, way, hop):
        spot = self.spot
        region = self.far_region(way, hop, spot.rep)
        return remote(region, region, self.far_sems, (way, hop), (1 - spot.rep, spot.shard))

    def far_near(self, way, hop):
        spot = self.spot
        region = self.far_region(way, hop, 1 - spot.rep)
        return remote(region, region, self.far_near_sems, (way, hop), (spot.rep, spot.sibling))

    def own(self):
        spot = self.spot
        mine = self.full_ref.at[pl.ds(spot.shard * self.rows, self.rows)]
        whole = remote(self.shard_ref, mine, self.whole_sems, (0,), (spot.rep, spot.sibling))
        return whole, pltpu.make_async_copy(self.shard_ref, mine, self.own_sem)

    def start(self):
        for way in (0, 1):
            columns = pl.ds(
                pl.multiple_of(self.first(way) * self.unit, 128), self.count * self.unit
            )
            self.ring(way, 0, self.shard_ref.at[:, columns]).start()
        for copy in self.own():
            copy.start()

    def step(self, hop):
        for way in (0, 1):
            self.ring(way, hop).wait_recv()

            @pl.when(hop < self.spot.hops - 1)
            def _():
                self.ring(way, hop + 1).start()

        for way in self.far_ways:
            self.far(way, hop).start()
        for way in (0, 1):
            self.near(way, hop).start()

        @pl.when(hop > 0)
        def _():
            self.relay(hop - 1)

    def relay(self, hop):
        for way in self.far_ways:
            self.far(way, hop).wait_recv()
            self.far_near(way, hop).start()

    def finish(self):
        for copy in self.own():
            copy.wait()

        def one(hop, carry):
            for way in (0, 1):
                self.ring(way, hop).wait_send()
                self.near(way, hop).wait()
            for way in self.far_ways:
                self.far(way, hop).wait_send()
                self.far_near(way, hop).wait()
            return carry

        lax.fori_loop(0, self.spot.hops, one, 0)

    @staticmethod
    def scratch(hops):
        return [DMA((2, hops))] * 8 + [DMA((1,))] * 2 + [DMA]


class GatherAll:
    def __init__(self, spot, lents, swap_count, inputs, outputs, scratch):
        count = len(lents)
        self.spot = spot
        self.gathers = [
            Gather(spot, lents[g], inputs[g], outputs[g], scratch[11 * g : 11 * g + 11])
            for g in range(count)
        ]
        scratch = scratch[11 * count :]
        self.swaps = [
            Swap(
                spot,
                inputs[count + i],
                outputs[count + i],
                scratch[3 * i : 3 * i + 2],
                scratch[3 * i + 2],
            )
            for i in range(swap_count)
        ]

    def start(self):
        greet(self.spot)
        for gather in self.gathers:
            gather.start()

    def step(self, hop):
        for swap in self.swaps:
            swap.start(hop, self.spot.hops)
        for gather in self.gathers:
            gather.step(hop)

    def steps(self, slot, slots):
        size = -(-self.spot.hops // slots)

        def one(hop, carry):
            self.step(hop)
            return carry

        first = jnp.minimum(slot * size, self.spot.hops)
        lax.fori_loop(first, jnp.minimum(first + size, self.spot.hops), one, 0)

    def finish(self):
        for gather in self.gathers:
            gather.relay(self.spot.hops - 1)
        for each in self.gathers + self.swaps:
            each.finish()

    @staticmethod
    def scratch(shards, count, swap_count):
        return Gather.scratch(shards // 2 - 1) * count + [
            DMA((shards,)),
            DMA((shards,)),
            DMA,
        ] * swap_count


def gather_kernel(shards, lents, swap_count, *refs):
    spot = Spot(shards)
    total = len(lents) + swap_count
    work = GatherAll(
        spot, lents, swap_count, refs[:total], refs[total : 2 * total], refs[2 * total :]
    )
    work.start()
    work.steps(0, 1)
    work.finish()


def gather_shapes(shards, pieces, sent, shared):
    return (
        [
            jax.ShapeDtypeStruct((shards * piece.shape[0], piece.shape[1]), piece.dtype)
            for piece in pieces
        ]
        + [jax.ShapeDtypeStruct(rows.shape, rows.dtype) for rows in sent]
        + [
            jax.ShapeDtypeStruct((shards * each.shape[0], each.shape[1]), each.dtype)
            for each in shared
        ]
    )


def gather_call(shards, pieces, lents, sent, shared, collective_id):
    swaps = [*sent, *shared]
    anywhere = pl.BlockSpec(memory_space=pl.ANY)
    results = pl.pallas_call(
        functools.partial(gather_kernel, shards, lents, len(swaps)),
        out_shape=gather_shapes(shards, pieces, sent, shared),
        in_specs=[anywhere] * (len(pieces) + len(swaps)),
        out_specs=[anywhere] * (len(pieces) + len(swaps)),
        scratch_shapes=GatherAll.scratch(shards, len(pieces), len(swaps)),
        compiler_params=pltpu.CompilerParams(
            collective_id=collective_id, has_side_effects=True
        ),
    )(*pieces, *swaps)
    first, second = len(pieces), len(pieces) + len(sent)
    return results[:first], results[first:second], results[second:]


class Reduce:
    def __init__(self, spot, partial_ref, out_ref, refs):
        self.spot, self.partial, self.out = spot, partial_ref, out_ref
        self.rows, self.columns = out_ref.shape
        self.unit = self.columns // 8
        (
            self.own_ring,
            self.sib_ring,
            self.got_ring,
            self.own_far,
            self.sib_far,
            self.got_far,
            self.got_last,
        ) = refs[:7]
        sems = refs[7:]
        self.load_ring_sem, self.load_far_sem = sems[0], sems[1]
        self.sib_ring_sems, self.sib_far_sems = sems[2:4], sems[4:6]
        self.ring_sems, self.far_sems, self.last_sems = sems[6:8], sems[8:10], sems[10:12]

    @staticmethod
    def scratch(shards, rows, columns):
        chips = shards // 2
        unit = columns // 8
        half = jnp.bfloat16
        buffers = [
            pltpu.VMEM((2, chips, rows, 3 * unit), half),
            pltpu.VMEM((2, chips, rows, 3 * unit), half),
            pltpu.VMEM((2, chips - 1, rows, 3 * unit), half),
            pltpu.VMEM((chips, rows, 2 * unit), half),
            pltpu.VMEM((chips, rows, 2 * unit), half),
            pltpu.VMEM((chips, rows, 2 * unit), half),
            pltpu.VMEM((2, rows, 3 * unit), half),
        ]
        sems = [DMA((2, chips)), DMA((chips,))]
        sems += [DMA((2, chips))] * 2 + [DMA((chips,))] * 2
        sems += [DMA((2, chips))] * 2 + [DMA((chips,))] * 2 + [DMA((2,))] * 2
        return buffers + sems

    def cut(self, block, first, count):
        columns = pl.ds(pl.multiple_of(first * self.unit, 128), count * self.unit)
        return self.partial.at[pl.ds(block * self.rows, self.rows), columns]

    def ring_cut(self, way, step, core):
        spot = self.spot
        return self.cut(
            spot.block(spot.along(way, step + 1), core), 2 * spot.rep + 3 * way, 3
        )

    def far_cut(self, step, core):
        spot = self.spot
        place = spot.place + (1 - 2 * spot.rep) * (step + 1)
        return self.cut(spot.block(place, core), 6 * (1 - spot.rep), 2)

    def load_ring(self, way, step):
        return pltpu.make_async_copy(
            self.ring_cut(way, step, self.spot.core),
            self.own_ring.at[way, step],
            self.load_ring_sem.at[way, step],
        )

    def load_far(self, step):
        return pltpu.make_async_copy(
            self.far_cut(step, self.spot.core), self.own_far.at[step], self.load_far_sem.at[step]
        )

    def give_ring(self, way, step):
        spot = self.spot
        return remote(
            self.ring_cut(way, step, 1 - spot.core),
            self.sib_ring.at[way, step],
            self.sib_ring_sems,
            (way, step),
            (spot.rep, spot.sibling),
        )

    def give_far(self, step):
        spot = self.spot
        return remote(
            self.far_cut(step, 1 - spot.core),
            self.sib_far.at[step],
            self.sib_far_sems,
            (step,),
            (spot.rep, spot.sibling),
        )

    def ring(self, way, step):
        return remote(
            self.own_ring.at[way, step],
            self.got_ring.at[way, step],
            self.ring_sems,
            (way, step),
            self.spot.ahead(way),
        )

    def far(self, step):
        spot = self.spot
        return remote(
            self.own_far.at[step],
            self.got_far.at[step],
            self.far_sems,
            (step,),
            (1 - spot.rep, spot.shard),
        )

    def last(self, way):
        spot = self.spot
        return remote(
            self.own_ring.at[way, spot.hops],
            self.got_last.at[way],
            self.last_sems,
            (way,),
            (1 - spot.rep, spot.shard),
        )

    def start(self, step):
        self.load_far(step).start()
        self.give_far(step).start()
        for way in (0, 1):
            self.load_ring(way, step).start()
            self.give_ring(way, step).start()

    def tiles(self, body):
        def one(tile, carry):
            body(pl.ds(pl.multiple_of(tile * 16, 16), 16))
            return carry

        lax.fori_loop(0, self.rows // 16, one, 0)

    def far_step(self, step):
        self.load_far(step).wait()
        self.give_far(step).wait_recv()

        def add(rows):
            total = self.own_far[step, rows].astype(jnp.float32)
            total += self.sib_far[step, rows].astype(jnp.float32)
            self.own_far[step, rows] = total.astype(jnp.bfloat16)

        self.tiles(add)
        self.far(step).start()

    def ring_step(self, way, step):
        unit = self.unit
        self.load_ring(way, step).wait()
        self.give_ring(way, step).wait_recv()

        @pl.when(self.spot.rep == way)
        def _():
            self.far(step).wait_recv()

            def add_far(rows):
                part = pl.ds(way * unit, 2 * unit)
                total = self.sib_ring[way, step, rows, part].astype(jnp.float32)
                total += self.got_far[step, rows].astype(jnp.float32)
                self.sib_ring[way, step, rows, part] = total.astype(jnp.bfloat16)

            self.tiles(add_far)

        @pl.when(step == 0)
        def _():
            def add(rows):
                total = self.own_ring[way, step, rows].astype(jnp.float32)
                total += self.sib_ring[way, step, rows].astype(jnp.float32)
                self.own_ring[way, step, rows] = total.astype(jnp.bfloat16)

            self.tiles(add)

        @pl.when(step > 0)
        def _():
            self.ring(way, step - 1).wait_recv()

            def add(rows):
                total = self.own_ring[way, step, rows].astype(jnp.float32)
                total += self.sib_ring[way, step, rows].astype(jnp.float32)
                total += self.got_ring[way, step - 1, rows].astype(jnp.float32)
                self.own_ring[way, step, rows] = total.astype(jnp.bfloat16)

            self.tiles(add)

        @pl.when(step < self.spot.hops)
        def _():
            self.ring(way, step).start()

        @pl.when(step == self.spot.hops)
        def _():
            self.last(way).start()

    def finish(self):
        spot, unit = self.spot, self.unit
        for way in (0, 1):
            self.last(way).wait()
        mine = [self.own_ring.at[way, spot.hops] for way in (0, 1)]
        theirs = [self.got_last.at[way] for way in (0, 1)]

        def write(lower, upper):
            def body(rows):
                def read(ref, first, count):
                    return ref[rows, pl.ds(first * unit, count * unit)].astype(jnp.float32)

                def put(first, count, value):
                    self.out[rows, pl.ds(first * unit, count * unit)] = value

                put(0, 2, read(lower[0], 0, 2))
                put(2, 1, read(lower[0], 2, 1) + read(upper[0], 0, 1))
                put(3, 2, read(lower[1], 0, 2) + read(upper[0], 1, 2))
                put(5, 1, read(lower[1], 2, 1) + read(upper[1], 0, 1))
                put(6, 2, read(upper[1], 1, 2))

            self.tiles(body)

        @pl.when(spot.rep == 0)
        def _():
            write(mine, theirs)

        @pl.when(spot.rep == 1)
        def _():
            write(theirs, mine)

        def one(step, carry):
            self.give_far(step).wait_send()
            self.far(step).wait_send()
            for way in (0, 1):
                self.give_ring(way, step).wait_send()

            @pl.when(step < spot.hops)
            def _():
                for way in (0, 1):
                    self.ring(way, step).wait_send()

            return carry

        lax.fori_loop(0, spot.chips, one, 0)


class Tally:
    def __init__(self, spot, mine, out, got, sems, own_sem):
        self.spot, self.mine, self.out, self.got = spot, mine, out, got
        self.sems = sems
        self.whole = 2 * spot.shards
        self.rank = spot.rep * spot.shards + spot.shard
        self.own = pltpu.make_async_copy(mine, got.at[self.rank], own_sem)

    def copy(self, k):
        target = lax.rem(self.rank + k, self.whole)
        shards = self.spot.shards
        return remote(
            self.mine,
            self.got.at[self.rank],
            self.sems,
            (k,),
            (target // shards, lax.rem(target, shards)),
        )

    def start(self):
        def one(k, carry):
            self.copy(k).start()
            return carry

        lax.fori_loop(1, self.whole, one, 0)
        self.own.start()

    def finish(self):
        def one(k, carry):
            self.copy(k).wait()
            return carry

        lax.fori_loop(1, self.whole, one, 0)
        self.own.wait()

        def add(k, total):
            return total + self.got[k]

        self.out[...] = lax.fori_loop(0, self.whole, add, jnp.zeros_like(self.out))


class ReduceAll:
    def __init__(self, spot, count, swap_count, tally_count, inputs, outputs, scratch):
        self.spot = spot
        self.reduces = [
            Reduce(spot, inputs[g], outputs[g], scratch[19 * g : 19 * g + 19])
            for g in range(count)
        ]
        scratch = scratch[19 * count :]
        self.swaps = [
            Swap(
                spot,
                inputs[count + i],
                outputs[count + i],
                scratch[3 * i : 3 * i + 2],
                scratch[3 * i + 2],
            )
            for i in range(swap_count)
        ]
        scratch = scratch[3 * swap_count :]
        self.tallies = [
            Tally(spot, inputs[-1], outputs[-1], scratch[0], scratch[1:3], scratch[3])
            for _ in range(tally_count)
        ]

    def start(self):
        greet(self.spot, everyone=len(self.tallies) > 0)

        def one(step, carry):
            for reduce in self.reduces:
                reduce.start(step)
            return carry

        lax.fori_loop(0, self.spot.chips, one, 0)
        for tally in self.tallies:
            tally.start()
        for reduce in self.reduces:
            reduce.far_step(0)

    def step(self, step):
        chips = self.spot.chips
        for swap in self.swaps:
            swap.start(step, chips)
        for reduce in self.reduces:
            for way in (0, 1):
                reduce.ring_step(way, step)

            @pl.when(step < chips - 1)
            def _():
                reduce.far_step(step + 1)

    def steps(self, slot, slots):
        size = -(-self.spot.chips // slots)

        def one(step, carry):
            self.step(step)
            return carry

        first = jnp.minimum(slot * size, self.spot.chips)
        lax.fori_loop(first, jnp.minimum(first + size, self.spot.chips), one, 0)

    def finish(self):
        for each in self.reduces + self.swaps + self.tallies:
            each.finish()


def reduce_kernel(shards, group_count, swap_count, tally_count, *refs):
    total = group_count + swap_count + tally_count
    work = ReduceAll(
        Spot(shards),
        group_count,
        swap_count,
        tally_count,
        refs[:total],
        refs[total : 2 * total],
        refs[2 * total :],
    )
    work.start()
    work.steps(0, 1)
    work.finish()


def reduce_call(shards, partials, sent, tallied, collective_id):
    scratch = []
    out_shape, out_specs = [], []
    anywhere = pl.BlockSpec(memory_space=pl.ANY)
    inside = pl.BlockSpec(memory_space=pltpu.VMEM)
    for part in partials:
        rows, columns = part.shape[0] // shards, part.shape[1]
        scratch += Reduce.scratch(shards, rows, columns)
        out_shape.append(jax.ShapeDtypeStruct((rows, columns), jnp.float32))
        out_specs.append(inside)
    for rows in sent:
        scratch += [DMA((shards,)), DMA((shards,)), DMA]
        out_shape.append(jax.ShapeDtypeStruct(rows.shape, rows.dtype))
        out_specs.append(anywhere)
    for each in tallied:
        scratch += [pltpu.VMEM((2 * shards, *each.shape), each.dtype)]
        scratch += [DMA((2 * shards,)), DMA((2 * shards,)), DMA]
        out_shape.append(jax.ShapeDtypeStruct(each.shape, each.dtype))
        out_specs.append(inside)
    in_specs = [anywhere] * (len(partials) + len(sent)) + [inside] * len(tallied)
    results = pl.pallas_call(
        functools.partial(reduce_kernel, shards, len(partials), len(sent), len(tallied)),
        out_shape=out_shape,
        in_specs=in_specs,
        out_specs=out_specs,
        scratch_shapes=scratch,
        compiler_params=pltpu.CompilerParams(
            collective_id=collective_id, has_side_effects=True, vmem_limit_bytes=56 << 20
        ),
    )(*partials, *sent, *tallied)
    first, second = len(partials), len(partials) + len(sent)
    return results[:first], results[first:second], results[second:]


def matmul(left, right, left_dim=1, right_dim=0):
    return lax.dot_general(
        left, right, (((left_dim,), (right_dim,)), ((), ())), preferred_element_type=jnp.float32
    )


def pick_rows(slot_column, slot_total):
    shape = (slot_column.shape[0], slot_total)
    return (slot_column == lax.broadcasted_iota(jnp.int32, shape, 1)).astype(jnp.bfloat16)


def place_rows(slot_row, slot_total):
    shape = (slot_total, slot_row.shape[1])
    return (slot_row == lax.broadcasted_iota(jnp.int32, shape, 0)).astype(jnp.bfloat16)


def pack_kernel(rows_ref, tokens_ref, cotangent_ref, tokens_out, cotangent_out):
    chosen = place_rows(rows_ref[0:1, :], tokens_out.shape[0])
    tokens_out[...] = matmul(chosen, tokens_ref[...]).astype(jnp.bfloat16)
    cotangent_out[...] = matmul(chosen, cotangent_ref[...]).astype(jnp.bfloat16)


def unpack_kernel(columns_ref, output_ref, grad_ref, output_out, grad_out):
    chosen = pick_rows(columns_ref[:, 0:1], output_ref.shape[0])
    output_out[...] = matmul(chosen, output_ref[...]).astype(jnp.bfloat16)
    grad_out[...] = matmul(chosen, grad_ref[...]).astype(jnp.bfloat16)


def local_call(kernel, out_shape, inputs, spaces=None, scratch=()):
    inside = pl.BlockSpec(memory_space=pltpu.VMEM)
    return pl.pallas_call(
        kernel,
        out_shape=out_shape,
        in_specs=spaces or [inside] * len(inputs),
        out_specs=[inside] * len(out_shape),
        scratch_shapes=list(scratch),
        compiler_params=pltpu.CompilerParams(vmem_limit_bytes=56 << 20),
    )(*inputs)


def segment_of(index, lengths_ref):
    first = lengths_ref[0, 0]
    second = first + lengths_ref[0, 1]
    third = second + lengths_ref[0, 2]
    return (
        (index >= first).astype(jnp.int32)
        + (index >= second).astype(jnp.int32)
        + (index >= third).astype(jnp.int32)
    )


def pair_masks(columns_ref, rows_ref, lengths_ref, same_ref, hidden_ref):
    size = columns_ref.shape[0]
    shape = (size, size)
    key_id = lax.broadcasted_iota(jnp.int32, shape, 0)
    query_id = lax.broadcasted_iota(jnp.int32, shape, 1)
    key_column = lax.broadcasted_iota(jnp.int32, (size, 1), 0)
    query_row = lax.broadcasted_iota(jnp.int32, (1, size), 1)
    together = segment_of(key_column, lengths_ref) == segment_of(query_row, lengths_ref)
    seen = together & ((columns_ref[:, 3:4] > 0) | (key_id == query_id))
    same_ref[...] = (columns_ref[:, 2:3] == rows_ref[2:3, :]).astype(jnp.float32)
    hidden_ref[...] = jnp.where(seen, 0.0, masked_score)


def turn(values, cosine, sine):
    width = values.shape[1]
    lane = lax.broadcasted_iota(jnp.int32, values.shape, 1)
    other = jnp.where(
        lane % 64 < 32, pltpu.roll(values, width - 32, 1), pltpu.roll(values, 32, 1)
    )
    return values * cosine + other * sine


def head_lanes(values, head):
    lane = lax.broadcasted_iota(jnp.int32, values.shape, 1)
    return jnp.where((lane < 64) == (head == 0), values, jnp.zeros_like(values))


def project(input_ref, weight_ref, cosine_ref, sine_ref, out_ref, scale):
    width = weight_ref.shape[0]
    cosine = jnp.concatenate([cosine_ref[...]] * 2, axis=1)
    sine = jnp.concatenate([sine_ref[...]] * 2, axis=1)

    def one(i, carry):
        def columns(part):
            return pl.ds(pl.multiple_of(part * width + i * 256, 256), 256)

        query = matmul(input_ref[...], weight_ref[:, columns(0)])
        out_ref[:, columns(0)] = (turn(query, cosine, sine) * scale).astype(jnp.bfloat16)
        key = matmul(input_ref[...], weight_ref[:, columns(1)])
        out_ref[:, columns(1)] = turn(key, cosine, sine).astype(jnp.bfloat16)
        out_ref[:, columns(2)] = matmul(input_ref[...], weight_ref[:, columns(2)]).astype(
            jnp.bfloat16
        )
        return carry

    lax.fori_loop(0, width // 256, one, 0)


def attend_pair(pair, width, heads_ref, bias_ref, same_ref, hidden_ref, out_ref, log_ref):
    def columns(part):
        return pl.ds(pl.multiple_of(part * width + pair * 128, 128), 128)

    query, key, value = (heads_ref[:, columns(part)] for part in range(3))
    total = None
    for which in (0, 1):
        head = 2 * pair + which
        gap = bias_ref[0, head] - bias_ref[1, head]
        scores = matmul(head_lanes(key, which), query, 1, 1)
        scores = scores + same_ref[...] * gap + hidden_ref[...]
        top = jnp.max(scores, axis=0, keepdims=True)
        weights = jnp.exp(scores - top)
        weight_sum = jnp.sum(weights, axis=0, keepdims=True)
        log_ref[pl.ds(head, 1), :] = top + jnp.log(weight_sum)
        soft = (weights * (1.0 / weight_sum)).astype(jnp.bfloat16)
        part = matmul(head_lanes(value, which), soft, 0, 0)
        total = part if total is None else total + part
    out_ref[:, pl.ds(pl.multiple_of(pair * 128, 128), 128)] = total.T.astype(jnp.bfloat16)


def normed(values):
    factor = lax.rsqrt(jnp.mean(values * values, axis=-1, keepdims=True) + epsilon)
    return values * factor, factor


def forward_body(refs, between=None):
    (
        arrived_ref, columns_ref, rows_ref, lengths_ref, bias_ref, gain_ref, weight_ref,
        cosine_ref, sine_ref,
        stream_ref, input_ref, heads_ref, out_ref, log_ref,
        same_ref, hidden_ref,
    ) = refs
    width = gain_ref.shape[1]
    scale = 1.0 / math.sqrt(64)
    chosen = pick_rows(columns_ref[:, 1:2], arrived_ref.shape[0])
    stream = matmul(chosen, arrived_ref[...])
    stream_ref[...] = stream.astype(jnp.bfloat16)
    input_ref[...] = (normed(stream)[0] * gain_ref[...]).astype(jnp.bfloat16)
    pair_masks(columns_ref, rows_ref, lengths_ref, same_ref, hidden_ref)
    project(input_ref, weight_ref, cosine_ref, sine_ref, heads_ref, scale)

    def one(pair, carry):
        if between is not None:
            between(pair)
        attend_pair(pair, width, heads_ref, bias_ref, same_ref, hidden_ref, out_ref, log_ref)
        return carry

    lax.fori_loop(0, width // 128, one, 0)


def forward_kernel(*refs):
    forward_body(refs)


def mlp_kernel(
    head_count, columns_ref, rows_ref, gain_ref, stream_ref, attended_ref, arrived_ref, out_w_ref,
    gate_ref, up_ref, down_ref,
    grad_gate_ref, grad_up_ref, grad_down_ref, packed_ref, dh_ref, grad_out_ref, do_ref, stats_ref,
    attn_ref, middle_ref, input_ref, input_t_ref, dy_ref, mlp_ref, back_ref,
):
    step = pl.program_id(0)
    final = pl.num_programs(0) - 1
    half = jnp.bfloat16

    @pl.when(step == 0)
    def _():
        attn_out = matmul(attended_ref[...], out_w_ref[...])
        attn_ref[...] = attn_out
        middle = stream_ref[...].astype(jnp.float32) + attn_out
        middle_ref[...] = middle
        entry = normed(middle)[0] * gain_ref[...]
        input_ref[...] = entry.astype(half)
        input_t_ref[...] = entry.T.astype(half)
        chosen = pick_rows(columns_ref[:, 1:2], arrived_ref.shape[0])
        dy_ref[...] = matmul(chosen, arrived_ref[...]).astype(half)
        mlp_ref[...] = jnp.zeros_like(mlp_ref)
        back_ref[...] = jnp.zeros_like(back_ref)

    gate = matmul(input_ref[...], gate_ref[...])
    up = matmul(input_ref[...], up_ref[...])
    grad_hidden = matmul(dy_ref[...], down_ref[...], 1, 1)
    sigmoid = jax.nn.sigmoid(gate)
    silu = gate * sigmoid
    hidden = (silu * up).astype(half)
    grad_gate = (grad_hidden * up * sigmoid * (1.0 + gate * (1.0 - sigmoid))).astype(half)
    grad_up = (grad_hidden * silu).astype(half)
    mlp_ref[...] += matmul(hidden, down_ref[...])
    back_ref[...] += matmul(grad_gate, gate_ref[...], 1, 1) + matmul(grad_up, up_ref[...], 1, 1)
    grad_gate_ref[...] = matmul(input_t_ref[...], grad_gate).astype(half)
    grad_up_ref[...] = matmul(input_t_ref[...], grad_up).astype(half)
    grad_down_ref[...] = matmul(hidden, dy_ref[...], 0, 0).astype(half)

    @pl.when(step == final)
    def _():
        valid = (columns_ref[:, 3:4] > 0).astype(jnp.float32)
        width = gain_ref.shape[1]

        def square(values, at):
            across = jnp.sum(values * values * valid, axis=0, keepdims=True)
            folded = across[:, 0:128]
            for i in range(1, width // 128):
                folded += across[:, i * 128 : (i + 1) * 128]
            stats_ref[at : at + 1, :] = folded

        stats_ref[...] = jnp.zeros_like(stats_ref)
        middle, mlp_out = middle_ref[...], mlp_ref[...]
        result = middle + mlp_out
        square(stream_ref[...].astype(jnp.float32), 8)
        square(attn_ref[...], 9)
        square(middle, 10)
        square(mlp_out, 11)
        square(result, 12)
        lane = lax.broadcasted_iota(jnp.int32, (valid.shape[0], 128), 1)
        stats_ref[13:14, :] = jnp.sum(jnp.where(lane == 0, valid, 0.0), axis=0, keepdims=True)
        placed = place_rows(rows_ref[1:2, :], packed_ref.shape[0])
        packed_ref[...] = matmul(placed, result.astype(half)).astype(half)
        entry, factor = normed(middle)
        back = back_ref[...]
        gain_grad = jnp.sum(back * entry, axis=0, keepdims=True)
        for i in range(width // 128):
            stats_ref[i : i + 1, :] = gain_grad[:, i * 128 : (i + 1) * 128]
        scaled = back * gain_ref[...]
        inner = jnp.mean(scaled * entry, axis=-1, keepdims=True)
        dh = dy_ref[...].astype(jnp.float32) + factor * (scaled - entry * inner)
        dh_ref[...] = dh
        branch = dh.astype(half)
        do_ref[...] = matmul(branch, out_w_ref[...], 1, 1).astype(half)
        grad_out_ref[...] = matmul(attended_ref[...], branch, 0, 0).astype(half)


def mlp_call(head_count, slot_total, inputs, weights):
    columns, rows, gain, stream, attended, arrived, out_w = inputs
    gate, up, down = weights
    tokens, width = stream.shape
    hidden = gate.shape[1]
    tile = 512

    def whole(array):
        return pl.BlockSpec(array.shape, lambda i: (0,) * len(array.shape))

    half, full = jnp.bfloat16, jnp.float32
    across = pl.BlockSpec((width, tile), lambda i: (0, i))
    down_spec = pl.BlockSpec((tile, width), lambda i: (i, 0))
    out_shape = [
        jax.ShapeDtypeStruct((width, hidden), half),
        jax.ShapeDtypeStruct((width, hidden), half),
        jax.ShapeDtypeStruct((hidden, width), half),
        jax.ShapeDtypeStruct((slot_total, width), half),
        jax.ShapeDtypeStruct((tokens, width), full),
        jax.ShapeDtypeStruct((width, width), half),
        jax.ShapeDtypeStruct((tokens, width), half),
        jax.ShapeDtypeStruct((16, 128), full),
    ]
    rest = [pl.BlockSpec(each.shape, lambda i: (0, 0)) for each in out_shape[3:]]
    flops = 2 * tokens * width * hidden * 9
    return pl.pallas_call(
        functools.partial(mlp_kernel, head_count),
        out_shape=out_shape,
        grid=(hidden // tile,),
        in_specs=[whole(each) for each in inputs] + [across, across, down_spec],
        out_specs=[across, across, down_spec, *rest],
        scratch_shapes=[
            pltpu.VMEM((tokens, width), full),
            pltpu.VMEM((tokens, width), full),
            pltpu.VMEM((tokens, width), half),
            pltpu.VMEM((width, tokens), half),
            pltpu.VMEM((tokens, width), half),
            pltpu.VMEM((tokens, width), full),
            pltpu.VMEM((tokens, width), full),
        ],
        compiler_params=pltpu.CompilerParams(vmem_limit_bytes=60 << 20),
        cost_estimate=pl.CostEstimate(
            flops=flops, bytes_accessed=6 * 2 * width * hidden, transcendentals=tokens * hidden
        ),
    )(*inputs, *weights)


def attend_back_pair(
    pair, width, scale, heads_ref, do_ref, bias_ref, log_ref, same_ref, hidden_ref, cosine_ref,
    sine_ref, grads_ref, bias_same_ref, bias_all_ref,
):
    half = jnp.bfloat16

    def columns(part):
        return pl.ds(pl.multiple_of(part * width + pair * 128, 128), 128)

    query, key, value = (heads_ref[:, columns(part)] for part in range(3))
    grad_out = do_ref[:, columns(0)]
    query_t = key_grad = value_grad = None
    for which in (0, 1):
        head = 2 * pair + which
        gap = bias_ref[0, head] - bias_ref[1, head]
        key_part = head_lanes(key, which)
        scores = matmul(key_part, query, 1, 1)
        scores = scores + same_ref[...] * gap + hidden_ref[...]
        soft = jnp.exp(scores - log_ref[pl.ds(head, 1), :])
        grad_soft = matmul(head_lanes(value, which), grad_out, 1, 1)
        inner = jnp.sum(soft * grad_soft, axis=0, keepdims=True)
        grad_scores = (soft * (grad_soft - inner)).astype(half)
        wide = grad_scores.astype(jnp.float32)
        bias_all_ref[pl.ds(head, 1), :] = jnp.sum(wide, axis=0, keepdims=True)
        bias_same_ref[pl.ds(head, 1), :] = jnp.sum(wide * same_ref[...], axis=0, keepdims=True)
        parts = (
            matmul(key_part, grad_scores, 0, 0),
            matmul(grad_scores, head_lanes(query, which)),
            matmul(soft.astype(half), head_lanes(grad_out, which)),
        )
        if which == 0:
            query_t, key_grad, value_grad = parts
        else:
            query_t, key_grad, value_grad = (
                query_t + parts[0],
                key_grad + parts[1],
                value_grad + parts[2],
            )
    cosine, sine = cosine_ref[...], -sine_ref[...]
    grads_ref[:, columns(0)] = (turn(query_t.T, cosine, sine) * scale).astype(half)
    grads_ref[:, columns(1)] = turn(key_grad, cosine, sine).astype(half)
    grads_ref[:, columns(2)] = value_grad.astype(half)


def backward_body(refs, between=None):
    (
        columns_ref, rows_ref, lengths_ref, bias_ref, gain_ref, weight_ref, cosine_ref, sine_ref,
        stream_ref, input_ref, heads_ref, log_ref, do_ref, dh_ref,
        grad_weight_ref, packed_ref, stats_ref,
        same_ref, hidden_ref, grads_ref, bias_same_ref, bias_all_ref, back_ref,
    ) = refs
    width = gain_ref.shape[1]
    half = jnp.bfloat16
    scale = 1.0 / math.sqrt(64)
    pair_masks(columns_ref, rows_ref, lengths_ref, same_ref, hidden_ref)

    def one(pair, carry):
        if between is not None:
            between(pair)
        attend_back_pair(
            pair, width, scale, heads_ref, do_ref, bias_ref, log_ref, same_ref, hidden_ref,
            cosine_ref, sine_ref, grads_ref, bias_same_ref, bias_all_ref,
        )
        return carry

    lax.fori_loop(0, width // 128, one, 0)
    back_ref[...] = jnp.zeros_like(back_ref)

    def combine(i, carry):
        at = pl.ds(pl.multiple_of(i * 512, 512), 512)
        part = grads_ref[:, at]
        back_ref[...] += matmul(part, weight_ref[:, at], 1, 1)
        grad_weight_ref[:, at] = matmul(input_ref[...], part, 0, 0).astype(half)
        return carry

    lax.fori_loop(0, 3 * width // 512, combine, 0)
    back = back_ref[...]
    entry, factor = normed(stream_ref[...].astype(jnp.float32))
    gain_grad = jnp.sum(back * entry, axis=0, keepdims=True)
    stats_ref[...] = jnp.zeros_like(stats_ref)
    for i in range(width // 128):
        stats_ref[i : i + 1, :] = gain_grad[:, i * 128 : (i + 1) * 128]
    heads = bias_all_ref.shape[0]
    lane = lax.broadcasted_iota(jnp.int32, (heads, 128), 1)
    row = lax.broadcasted_iota(jnp.int32, (heads, 128), 0)
    same = jnp.sum(bias_same_ref[...], axis=1, keepdims=True)
    other = jnp.sum(bias_all_ref[...], axis=1, keepdims=True) - same
    stats_ref[8:9, :] = jnp.sum(
        jnp.where(lane == row, same, 0.0) + jnp.where(lane == row + heads, other, 0.0),
        axis=0,
        keepdims=True,
    )
    scaled = back * gain_ref[...]
    inner = jnp.mean(scaled * entry, axis=-1, keepdims=True)
    grad_stream = dh_ref[...] + factor * (scaled - entry * inner)
    placed = place_rows(rows_ref[1:2, :], packed_ref.shape[0])
    packed_ref[...] = matmul(placed, grad_stream.astype(half)).astype(half)


def backward_kernel(*refs):
    backward_body(refs)


def forward_gather_kernel(shards, lents, swap_count, compute_counts, *refs):
    ins, outs = compute_counts
    total = len(lents) + swap_count
    in_refs, refs = refs[: ins + total], refs[ins + total :]
    out_refs, refs = refs[: outs + total], refs[outs + total :]
    masks, scratch = refs[:2], refs[2:]
    work = GatherAll(
        Spot(shards), lents, swap_count, in_refs[ins:], out_refs[outs:], scratch
    )
    work.start()
    pairs = in_refs[5].shape[1] // 128
    forward_body(
        (*in_refs[:ins], *out_refs[:outs], *masks), lambda pair: work.steps(pair, pairs)
    )
    work.finish()


def forward_gather_call(shards, inputs, spaces, out_shape, pieces, lents, sent, collective_id):
    anywhere = pl.BlockSpec(memory_space=pl.ANY)
    inside = pl.BlockSpec(memory_space=pltpu.VMEM)
    tokens = out_shape[0].shape[0]
    counts = (len(inputs), len(out_shape))
    comm = len(pieces) + len(sent)
    results = pl.pallas_call(
        functools.partial(forward_gather_kernel, shards, lents, len(sent), counts),
        out_shape=[*out_shape, *gather_shapes(shards, pieces, sent, [])],
        in_specs=spaces + [anywhere] * comm,
        out_specs=[inside] * len(out_shape) + [anywhere] * comm,
        scratch_shapes=[pltpu.VMEM((tokens, tokens), jnp.float32)] * 2
        + GatherAll.scratch(shards, len(pieces), len(sent)),
        compiler_params=pltpu.CompilerParams(
            collective_id=collective_id, has_side_effects=True, vmem_limit_bytes=56 << 20
        ),
    )(*inputs, *pieces, *sent)
    first = len(out_shape)
    second = first + len(pieces)
    return results[:first], results[first:second], results[second:]


def on_device(
    tokens,
    cotangent,
    send_slot,
    recv_slot,
    lengths,
    variate,
    valid_mask,
    norm_attn,
    w_query,
    w_key,
    w_value,
    w_out,
    variate_bias,
    norm_mlp,
    w_gate,
    w_up,
    w_down,
):
    shards = lax.axis_size("shard")
    tok_rows, width = tokens.shape
    slot_total = 2 * tok_rows
    heads = variate_bias.shape[1]
    half, full = jnp.bfloat16, jnp.float32
    share = width // shards
    indices = jnp.stack([send_slot, recv_slot, variate, valid_mask])
    rows = jnp.concatenate([indices, jnp.zeros_like(indices)])
    columns = rows.T
    _, position = layout(lengths[0], tok_rows)
    cosine, sine = angle_tables(position, width // heads)
    cosine = jnp.concatenate([cosine] * 4, axis=1)
    sine = jnp.concatenate([-sine, sine] * 2, axis=1)
    gains = jnp.stack([norm_attn, norm_mlp]).astype(full)
    gains = jnp.pad(gains, ((0, 6), (0, 128 - share)))
    shape = jax.ShapeDtypeStruct
    packed_shape = shape((slot_total, width), half)
    token_shape = shape((tok_rows, width), half)
    out_tokens, out_cotangent = local_call(
        pack_kernel, [packed_shape] * 2, [rows, tokens, cotangent]
    )
    (full_in,), (arrived_tokens,), (gains,) = gather_call(
        shards,
        [jnp.concatenate([w_query, w_key, w_value], axis=1)],
        (4,),
        [out_tokens],
        [gains],
        1,
    )
    gains = gains.reshape(shards, 8, 128)
    gain_attn = gains[:, 0, :share].reshape(1, width)
    gain_mlp = gains[:, 1, :share].reshape(1, width)
    inside = pl.BlockSpec(memory_space=pltpu.VMEM)
    scalar = pl.BlockSpec(memory_space=pltpu.SMEM)
    (
        (stream, input_attn, head_rows, attended, logs),
        (full_out, full_gate, full_up, full_down),
        (arrived_grads,),
    ) = forward_gather_call(
        shards,
        [
            arrived_tokens, columns, rows, lengths, variate_bias, gain_attn, full_in, cosine, sine,
        ],
        [inside] * 3 + [scalar] * 2 + [inside] * 4,
        [
            token_shape,
            token_shape,
            shape((tok_rows, 3 * width), half),
            token_shape,
            shape((heads, tok_rows), full),
        ],
        [w_out, w_gate, w_up, w_down],
        (2, 4, 4, 2),
        [out_cotangent],
        2,
    )
    part_gate, part_up, part_down, home_out, grad_middle, part_out, grad_attended, stats_mlp = (
        mlp_call(
            heads,
            slot_total,
            [columns, rows, gain_mlp, stream, attended, arrived_grads, full_out],
            [full_gate, full_up, full_down],
        )
    )
    part_in, home_grad, stats_attn = local_call(
        backward_kernel,
        [shape((width, 3 * width), half), packed_shape, shape((16, 128), full)],
        [
            columns, rows, lengths, variate_bias, gain_attn, full_in, cosine, sine,
            stream, input_attn, head_rows, logs, grad_attended, grad_middle,
        ],
        [inside] * 2 + [scalar] * 2 + [inside] * 10,
        [
            pltpu.VMEM((tok_rows, tok_rows), full),
            pltpu.VMEM((tok_rows, tok_rows), full),
            pltpu.VMEM((tok_rows, 3 * width), half),
            pltpu.VMEM((heads, tok_rows), full),
            pltpu.VMEM((heads, tok_rows), full),
            pltpu.VMEM((tok_rows, width), full),
        ],
    )
    (grad_gate, grad_up, grad_down, grad_out), (home_out,), _ = reduce_call(
        shards, [part_gate, part_up, part_down, part_out], [home_out], [], 3
    )
    (grad_in,), (home_grad,), (sums,) = reduce_call(
        shards, [part_in], [home_grad], [jnp.concatenate([stats_mlp, stats_attn])], 4
    )
    output, input_grad = local_call(
        unpack_kernel, [token_shape] * 2, [columns, home_out, home_grad]
    )
    squares = jnp.sum(sums[8:14], axis=1)
    root_means = jnp.sqrt(squares[:5] / (squares[5] * width))
    share_start = lax.axis_index("shard") * share
    grad_norm_mlp = lax.dynamic_slice_in_dim(sums[0:8].reshape(-1), share_start, share)
    grad_norm_attn = lax.dynamic_slice_in_dim(sums[16:24].reshape(-1), share_start, share)
    bias_grads = sums[24, : 2 * heads].reshape(2, heads)
    grad_query, grad_key, grad_value = (grad_in[:, i * width : (i + 1) * width] for i in range(3))
    return (
        output,
        input_grad,
        grad_norm_attn,
        grad_query,
        grad_key,
        grad_value,
        grad_out,
        bias_grads,
        grad_norm_mlp,
        grad_gate,
        grad_up,
        grad_down,
        root_means,
    )


def solution(mesh):
    in_specs = (
        P(("rep", "shard"), None),
        P(("rep", "shard"), None),
        P(("rep", "shard")),
        P(("rep", "shard")),
        P(("rep", "shard"), None),
        P(("rep", "shard")),
        P(("rep", "shard")),
        P("shard"),
        P("shard", None),
        P("shard", None),
        P("shard", None),
        P("shard", None),
        P(),
        P("shard"),
        P("shard", None),
        P("shard", None),
        P("shard", None),
    )
    out_specs = (
        P(("rep", "shard"), None),
        P(("rep", "shard"), None),
        P("shard"),
        P("shard", None),
        P("shard", None),
        P("shard", None),
        P("shard", None),
        P(),
        P("shard"),
        P("shard", None),
        P("shard", None),
        P("shard", None),
        P(),
    )
    return jax.shard_map(
        on_device, mesh=mesh, in_specs=in_specs, out_specs=out_specs, check_vma=False
    )
```

```python
import functools
import math

import jax
import jax.numpy as jnp
from jax import lax
from jax.experimental import pallas as pl
from jax.experimental.pallas import tpu as pltpu
from jax.sharding import PartitionSpec as P

MESH = pl.DeviceIdType.MESH
DMA = pltpu.SemaphoreType.DMA
epsilon = 1e-06
masked_score = -1e30
VMEM_LIMIT = 62 << 20


def angle_tables(position, head_dim):
    half_dim = head_dim // 2
    inverse_freq = 1.0 / 10000.0 ** (jnp.arange(half_dim, dtype=jnp.float32) / half_dim)
    theta_angle = position.astype(jnp.float32)[:, None] * inverse_freq[None, :]
    return (jnp.cos(theta_angle), jnp.sin(theta_angle))


def layout(lengths_row, tok_rows):
    slot_ids = jnp.arange(tok_rows, dtype=jnp.int32)
    seq_ends = jnp.cumsum(lengths_row)
    segment = jnp.sum((slot_ids[:, None] >= seq_ends[None, :]).astype(jnp.int32), axis=1)
    starts = seq_ends - lengths_row
    chosen = segment[:, None] == jnp.arange(lengths_row.shape[0], dtype=jnp.int32)[None, :]
    begins = jnp.sum(jnp.where(chosen, starts[None, :], 0), axis=1)
    return (segment, slot_ids - begins)


def ring_place(chip, chips):
    return jnp.where(chip % 2 == 0, chip // 2, chips - 1 - chip // 2)


def ring_chip(place, chips):
    wrapped = lax.rem(place + 2 * chips, chips)
    return jnp.where(wrapped < chips // 2, 2 * wrapped, 2 * (chips - 1 - wrapped) + 1)


class Spot:
    def __init__(self, shards):
        self.shards = shards
        self.chips = shards // 2
        self.half = self.chips // 2
        self.rep = lax.axis_index("rep")
        self.shard = lax.axis_index("shard")
        self.core = lax.rem(self.shard, 2)
        self.place = ring_place(self.shard // 2, self.chips)
        self.sibling = self.shard + 1 - 2 * self.core

    def block(self, place, core=None):
        return 2 * ring_chip(place, self.chips) + (self.core if core is None else core)

    def along(self, way, distance):
        return self.place - distance if way == 0 else self.place + distance

    def ahead(self, way):
        return (self.rep, self.block(self.along(way, -1)))


def greet(spot):
    barrier = pltpu.get_barrier_semaphore()

    def peer(k, carry):
        target = lax.rem(spot.shard + k, spot.shards)
        pl.semaphore_signal(barrier, inc=1, device_id=(spot.rep, target), device_id_type=MESH)
        return carry

    lax.fori_loop(1, spot.shards, peer, 0)
    pl.semaphore_signal(
        barrier, inc=1, device_id=(1 - spot.rep, spot.shard), device_id_type=MESH
    )
    pl.semaphore_wait(barrier, spot.shards)


def remote(src, dst, sems, at, target):
    return pltpu.make_async_remote_copy(
        src_ref=src,
        dst_ref=dst,
        send_sem=sems[0].at[at],
        recv_sem=sems[1].at[at],
        device_id=target,
        device_id_type=MESH,
    )


class Swap:
    def __init__(self, spot, source, arrived, sems, own_sem):
        self.spot, self.sems = spot, sems
        self.source, self.arrived = source, arrived
        self.capacity = arrived.shape[0] // spot.shards
        self.own = pltpu.make_async_copy(
            self.part(spot.shard), arrived.at[self.rows(spot.shard)], own_sem
        )

    def rows(self, shard):
        return pl.ds(pl.multiple_of(shard * self.capacity, 8), self.capacity)

    def part(self, shard):
        if self.source.shape[0] == self.capacity:
            return self.source
        return self.source.at[self.rows(shard)]

    def copy(self, k):
        spot = self.spot
        target = lax.rem(spot.shard + k, spot.shards)
        return remote(
            self.part(target),
            self.arrived.at[self.rows(spot.shard)],
            self.sems,
            (k,),
            (spot.rep, target),
        )

    def start(self, slot, slots):
        size = -(-self.spot.shards // slots)

        def one(k, carry):
            @pl.when(k == 0)
            def _():
                self.own.start()

            @pl.when(k > 0)
            def _():
                self.copy(k).start()

            return carry

        first = jnp.minimum(slot * size, self.spot.shards)
        lax.fori_loop(first, jnp.minimum(first + size, self.spot.shards), one, 0)

    def finish(self):
        def one(k, carry):
            self.copy(k).wait()
            return carry

        lax.fori_loop(1, self.spot.shards, one, 0)
        self.own.wait()


class Gather:
    def __init__(self, spot, lent, shard_ref, full_ref, sems):
        self.spot, self.lent, self.shard_ref, self.full_ref = spot, lent, shard_ref, full_ref
        self.rows = shard_ref.shape[0]
        self.unit = shard_ref.shape[1] // 8
        self.kept = 8 - lent
        self.ring_sems, self.near_sems, self.far_sems, self.far_near_sems = (
            sems[0:2],
            sems[2:4],
            sems[4:6],
            sems[6:8],
        )
        self.whole_sems, self.own_sem = sems[8:10], sems[10]

    def span(self, way, short):
        first, count = self.lent * self.spot.rep, self.kept
        if short:
            first, count = first + way * (count // 2), count // 2
        return pl.ds(pl.multiple_of(first * self.unit, 128), count * self.unit)

    def region(self, way, hop, short):
        block = self.spot.block(self.spot.along(way, hop))
        return self.full_ref.at[pl.ds(block * self.rows, self.rows), self.span(way, short)]

    def ring(self, way, hop, short, source=None):
        region = self.region(way, hop, short)
        return remote(
            region if source is None else source,
            region,
            self.ring_sems,
            (way, hop),
            self.spot.ahead(way),
        )

    def near(self, way, hop, short):
        region = self.region(way, hop + 1, short)
        target = (self.spot.rep, self.spot.sibling)
        return remote(region, region, self.near_sems, (way, hop), target)

    def lent_region(self, way, hop, owner):
        block = self.spot.block(self.spot.along(way, hop + 1))
        columns = pl.ds(
            pl.multiple_of(self.kept * owner * self.unit, 128), self.lent * self.unit
        )
        return self.full_ref.at[pl.ds(block * self.rows, self.rows), columns]

    def far(self, way, hop):
        region = self.lent_region(way, hop, self.spot.rep)
        target = (1 - self.spot.rep, self.spot.shard)
        return remote(region, region, self.far_sems, (way, hop), target)

    def far_near(self, way, hop):
        region = self.lent_region(way, hop, 1 - self.spot.rep)
        target = (self.spot.rep, self.spot.sibling)
        return remote(region, region, self.far_near_sems, (way, hop), target)

    def own(self):
        spot = self.spot
        mine = self.full_ref.at[pl.ds(spot.shard * self.rows, self.rows)]
        whole = remote(self.shard_ref, mine, self.whole_sems, (0,), (spot.rep, spot.sibling))
        return whole, pltpu.make_async_copy(self.shard_ref, mine, self.own_sem)

    def start(self):
        for way in (0, 1):
            self.ring(way, 0, False, self.shard_ref.at[:, self.span(way, False)]).start()
        for copy in self.own():
            copy.start()

    def step(self, hop):
        final = self.spot.half - 1

        @pl.when(hop < final)
        def _():
            for way in (0, 1):
                self.ring(way, hop, False).wait_recv()

                @pl.when(hop < final - 1)
                def _():
                    self.ring(way, hop + 1, False).start()

                @pl.when(hop == final - 1)
                def _():
                    self.ring(way, hop + 1, True).start()

            for way in (0, 1):
                self.far(way, hop).start()
                self.near(way, hop, False).start()

        @pl.when(hop == final)
        def _():
            for way in (0, 1):
                self.ring(way, hop, True).wait_recv()
            self.far(0, hop).start()
            for way in (0, 1):
                self.near(way, hop, True).start()

        @pl.when(hop > 0)
        def _():
            for way in (0, 1):
                self.relay(way, hop - 1)

    def relay(self, way, hop):
        self.far(way, hop).wait_recv()
        self.far_near(way, hop).start()

    def finish(self):
        final = self.spot.half - 1
        for copy in self.own():
            copy.wait()

        def one(hop, carry):
            for way in (0, 1):
                self.ring(way, hop, False).wait_send()
                self.near(way, hop, False).wait()
                self.far(way, hop).wait_send()
                self.far_near(way, hop).wait()
            return carry

        lax.fori_loop(0, final, one, 0)
        for way in (0, 1):
            self.ring(way, final, True).wait_send()
            self.near(way, final, True).wait()
        self.far(0, final).wait_send()
        self.far_near(0, final).wait()

    @staticmethod
    def scratch(half):
        return [DMA((2, half))] * 8 + [DMA((1,))] * 2 + [DMA]


class GatherAll:
    def __init__(self, spot, lents, swap_count, inputs, outputs, scratch):
        count = len(lents)
        self.spot = spot
        self.gathers = [
            Gather(spot, lents[g], inputs[g], outputs[g], scratch[11 * g : 11 * g + 11])
            for g in range(count)
        ]
        scratch = scratch[11 * count :]
        self.swaps = [
            Swap(
                spot,
                inputs[count + i],
                outputs[count + i],
                scratch[3 * i : 3 * i + 2],
                scratch[3 * i + 2],
            )
            for i in range(swap_count)
        ]

    def start(self):
        greet(self.spot)
        for gather in self.gathers:
            gather.start()

    def step(self, hop):
        for swap in self.swaps:
            swap.start(hop, self.spot.half)
        for gather in self.gathers:
            gather.step(hop)

    def steps(self, slot, slots):
        size = -(-self.spot.half // slots)

        def one(hop, carry):
            self.step(hop)
            return carry

        first = jnp.minimum(slot * size, self.spot.half)
        lax.fori_loop(first, jnp.minimum(first + size, self.spot.half), one, 0)

    def finish(self):
        for gather in self.gathers:
            gather.relay(0, self.spot.half - 1)
        for each in self.gathers + self.swaps:
            each.finish()

    @staticmethod
    def scratch(shards, count, swap_count):
        return Gather.scratch(shards // 4) * count + [
            DMA((shards,)),
            DMA((shards,)),
            DMA,
        ] * swap_count


def gather_kernel(shards, lents, swap_count, *refs):
    spot = Spot(shards)
    total = len(lents) + swap_count
    work = GatherAll(
        spot, lents, swap_count, refs[:total], refs[total : 2 * total], refs[2 * total :]
    )
    work.start()
    work.steps(0, 1)
    work.finish()


def gather_shapes(shards, pieces, sent, shared):
    return (
        [
            jax.ShapeDtypeStruct((shards * piece.shape[0], piece.shape[1]), piece.dtype)
            for piece in pieces
        ]
        + [jax.ShapeDtypeStruct(rows.shape, rows.dtype) for rows in sent]
        + [
            jax.ShapeDtypeStruct((shards * each.shape[0], each.shape[1]), each.dtype)
            for each in shared
        ]
    )


def gather_call(shards, pieces, lents, sent, shared, collective_id):
    swaps = [*sent, *shared]
    anywhere = pl.BlockSpec(memory_space=pl.ANY)
    results = pl.pallas_call(
        functools.partial(gather_kernel, shards, lents, len(swaps)),
        out_shape=gather_shapes(shards, pieces, sent, shared),
        in_specs=[anywhere] * (len(pieces) + len(swaps)),
        out_specs=[anywhere] * (len(pieces) + len(swaps)),
        scratch_shapes=GatherAll.scratch(shards, len(pieces), len(swaps)),
        compiler_params=pltpu.CompilerParams(
            collective_id=collective_id, has_side_effects=True
        ),
    )(*pieces, *swaps)
    first, second = len(pieces), len(pieces) + len(sent)
    return results[:first], results[first:second], results[second:]


class Reduce:
    def __init__(self, spot, lent, partial_ref, out_ref, refs):
        self.spot, self.lent, self.partial, self.out = spot, lent, partial_ref, out_ref
        self.rows, self.columns = out_ref.shape
        self.unit = self.columns // 8
        self.kept = 8 - lent
        self.width = self.kept * self.unit
        (
            self.own,
            self.sib,
            self.got,
            self.own_far,
            self.sib_far,
            self.got_far,
            self.got_last,
        ) = refs[:7]
        sems = refs[7:]
        self.load_sem, self.load_far_sem = sems[0], sems[1]
        self.sib_sems, self.sib_far_sems = sems[2:4], sems[4:6]
        self.ring_sems, self.far_sems, self.last_sems = sems[6:8], sems[8:10], sems[10:12]

    @staticmethod
    def scratch(shards, lent, rows, columns):
        chips = shards // 2
        unit = columns // 8
        kept, lend = (8 - lent) * unit, lent * unit
        half = jnp.bfloat16
        buffers = [
            pltpu.VMEM((chips, rows, kept), half),
            pltpu.VMEM((chips, rows, kept), half),
            pltpu.VMEM((2, chips // 2, rows, kept), half),
            pltpu.VMEM((chips, rows, lend), half),
            pltpu.VMEM((chips, rows, lend), half),
            pltpu.VMEM((chips, rows, lend), half),
            pltpu.VMEM((rows, kept), half),
        ]
        sems = [DMA((chips,))] * 6 + [DMA((2, chips // 2))] * 2
        sems += [DMA((chips,))] * 2 + [DMA((1,))] * 2
        return buffers + sems

    def owner(self, item, core):
        half = self.spot.half
        pair = (item + 1) // 2
        ahead = lax.rem(item, 2) == 1
        distance = half - pair
        place = jnp.where(ahead, self.spot.place + distance, self.spot.place - distance)
        return self.spot.block(place, core)

    def cut(self, item, core, first, count):
        columns = pl.ds(pl.multiple_of(first * self.unit, 128), count * self.unit)
        block = self.owner(item, core)
        return self.partial.at[pl.ds(block * self.rows, self.rows), columns]

    def kept_cut(self, item, core):
        return self.cut(item, core, self.lent * self.spot.rep, self.kept)

    def lent_cut(self, item, core):
        return self.cut(item, core, self.kept * (1 - self.spot.rep), self.lent)

    def load(self, item):
        source = self.kept_cut(item, self.spot.core)
        return pltpu.make_async_copy(source, self.own.at[item], self.load_sem.at[item])

    def load_far(self, item):
        source = self.lent_cut(item, self.spot.core)
        return pltpu.make_async_copy(source, self.own_far.at[item], self.load_far_sem.at[item])

    def give(self, item):
        source = self.kept_cut(item, 1 - self.spot.core)
        target = (self.spot.rep, self.spot.sibling)
        return remote(source, self.sib.at[item], self.sib_sems, (item,), target)

    def give_far(self, item):
        source = self.lent_cut(item, 1 - self.spot.core)
        target = (self.spot.rep, self.spot.sibling)
        return remote(source, self.sib_far.at[item], self.sib_far_sems, (item,), target)

    def ring(self, way, step, short=False):
        item = 0 if short else 2 * step - 1 + way
        columns = pl.ds(way * self.width // 2, self.width // 2) if short else slice(None)
        return remote(
            self.own.at[item, :, columns],
            self.got.at[way, step, :, columns],
            self.ring_sems,
            (way, step),
            self.spot.ahead(way),
        )

    def far(self, item):
        target = (1 - self.spot.rep, self.spot.shard)
        return remote(
            self.own_far.at[item], self.got_far.at[item], self.far_sems, (item,), target
        )

    def last(self):
        target = (1 - self.spot.rep, self.spot.shard)
        source = self.own.at[self.spot.chips - 1]
        return remote(source, self.got_last, self.last_sems, (0,), target)

    def start(self, item):
        self.load_far(item).start()
        self.give_far(item).start()
        self.load(item).start()
        self.give(item).start()

    def tiles(self, width, body):
        chunk = width if width <= 768 else 512

        def one(tile, carry):
            for first in range(0, width, chunk):
                body(pl.ds(pl.multiple_of(tile * 16, 16), 16), first, chunk)
            return carry

        lax.fori_loop(0, self.rows // 16, one, 0)

    def far_step(self, item):
        self.load_far(item).wait()
        self.give_far(item).wait_recv()

        def add(rows, first, count):
            at = pl.ds(first, count)
            total = self.own_far[item, rows, at].astype(jnp.float32)
            total += self.sib_far[item, rows, at].astype(jnp.float32)
            self.own_far[item, rows, at] = total.astype(jnp.bfloat16)

        self.tiles(self.lent * self.unit, add)
        self.far(item).start()

    def fold(self, item, extra=(), start=0, width=None):
        def add(rows, first, count):
            at = pl.ds(start + first, count)
            total = self.own[item, rows, at].astype(jnp.float32)
            total += self.sib[item, rows, at].astype(jnp.float32)
            for way, step in extra:
                total += self.got[way, step, rows, at].astype(jnp.float32)
            self.own[item, rows, at] = total.astype(jnp.bfloat16)

        self.tiles(self.width if width is None else width, add)

    def ready(self, item):
        self.load(item).wait()
        self.give(item).wait_recv()
        self.far(item).wait_recv()
        offset = self.spot.rep * (self.kept - self.lent) * self.unit

        def add(rows, first, count):
            at = pl.ds(pl.multiple_of(offset + first, 128), count)
            total = self.sib[item, rows, at].astype(jnp.float32)
            total += self.got_far[item, rows, pl.ds(first, count)].astype(jnp.float32)
            self.sib[item, rows, at] = total.astype(jnp.bfloat16)

        self.tiles(self.lent * self.unit, add)

    def step(self, step):
        half, chips = self.spot.half, self.spot.chips

        @pl.when(step == 0)
        def _():
            self.ready(0)
            self.fold(0)
            for way in (0, 1):
                self.ring(way, 0, True).start()

        @pl.when((step > 0) & (step < half))
        def _():
            for way in (0, 1):
                item = 2 * step - 1 + way
                self.ready(item)

                @pl.when(step == 1)
                def _():
                    self.ring(way, 0, True).wait_recv()
                    middle = self.width // 2
                    self.fold(item, [(way, 0)], way * middle, middle)
                    self.fold(item, [], (1 - way) * middle, middle)

                @pl.when(step > 1)
                def _():
                    self.ring(way, step - 1).wait_recv()
                    self.fold(item, [(way, step - 1)])

                self.ring(way, step).start()

        @pl.when(step == half)
        def _():
            self.ready(chips - 1)
            for way in (0, 1):
                self.ring(way, half - 1).wait_recv()
            self.fold(chips - 1, [(0, half - 1), (1, half - 1)])
            self.last().start()

        @pl.when(step < half)
        def _():
            self.far_step(2 * step + 1)

            @pl.when(step < half - 1)
            def _():
                self.far_step(2 * step + 2)

    def finish(self):
        spot, unit, lent = self.spot, self.unit, self.lent
        self.last().wait()
        mine = self.own.at[spot.chips - 1]
        theirs = self.got_last

        def write(lower, upper):
            def one(tile, carry):
                rows = pl.ds(pl.multiple_of(tile * 16, 16), 16)

                def read(ref, first, count):
                    return ref[rows, pl.ds(first * unit, count * unit)].astype(jnp.float32)

                kept, both = self.kept, self.kept - lent
                self.out[rows, pl.ds(0, lent * unit)] = read(lower, 0, lent)
                for i in range(both):
                    self.out[rows, pl.ds((lent + i) * unit, unit)] = read(
                        lower, lent + i, 1
                    ) + read(upper, i, 1)
                self.out[rows, pl.ds(kept * unit, lent * unit)] = read(upper, both, lent)
                return carry

            lax.fori_loop(0, self.rows // 16, one, 0)

        @pl.when(spot.rep == 0)
        def _():
            write(mine, theirs)

        @pl.when(spot.rep == 1)
        def _():
            write(theirs, mine)

        def one(item, carry):
            self.give_far(item).wait_send()
            self.far(item).wait_send()
            self.give(item).wait_send()
            return carry

        lax.fori_loop(0, spot.chips, one, 0)
        for way in (0, 1):
            self.ring(way, 0, True).wait_send()

        def two(step, carry):
            for way in (0, 1):
                self.ring(way, step).wait_send()
            return carry

        lax.fori_loop(1, spot.half, two, 0)


class Tally:
    def __init__(self, spot, mine, out, refs):
        self.spot, self.mine, self.out = spot, mine, out
        self.got, self.half, self.other = refs[0:3]
        self.sems, self.own_sem, self.far_sems = refs[3:5], refs[5], refs[6:8]
        self.own = pltpu.make_async_copy(mine, self.got.at[spot.shard], self.own_sem)

    def copy(self, k):
        spot = self.spot
        target = lax.rem(spot.shard + k, spot.shards)
        return remote(self.mine, self.got.at[spot.shard], self.sems, (k,), (spot.rep, target))

    def far(self):
        target = (1 - self.spot.rep, self.spot.shard)
        return remote(self.half, self.other, self.far_sems, (0,), target)

    def start(self):
        def one(k, carry):
            self.copy(k).start()
            return carry

        lax.fori_loop(1, self.spot.shards, one, 0)
        self.own.start()

    def middle(self):
        def one(k, carry):
            self.copy(k).wait()
            return carry

        lax.fori_loop(1, self.spot.shards, one, 0)
        self.own.wait()

        def add(k, total):
            return total + self.got[k]

        self.half[...] = lax.fori_loop(0, self.spot.shards, add, jnp.zeros_like(self.half))
        self.far().start()

    def finish(self):
        self.far().wait()
        self.out[...] = self.half[...] + self.other[...]

    @staticmethod
    def scratch(shards, shape):
        full = jnp.float32
        return [
            pltpu.VMEM((shards, *shape), full),
            pltpu.VMEM(shape, full),
            pltpu.VMEM(shape, full),
            DMA((shards,)),
            DMA((shards,)),
            DMA,
            DMA((1,)),
            DMA((1,)),
        ]


class ReduceAll:
    def __init__(self, spot, lents, swap_count, tally_count, inputs, outputs, scratch):
        count = len(lents)
        self.spot = spot
        self.reduces = [
            Reduce(spot, lents[g], inputs[g], outputs[g], scratch[19 * g : 19 * g + 19])
            for g in range(count)
        ]
        scratch = scratch[19 * count :]
        self.swaps = [
            Swap(
                spot,
                inputs[count + i],
                outputs[count + i],
                scratch[3 * i : 3 * i + 2],
                scratch[3 * i + 2],
            )
            for i in range(swap_count)
        ]
        scratch = scratch[3 * swap_count :]
        self.tallies = [
            Tally(spot, inputs[-1], outputs[-1], scratch[:8]) for _ in range(tally_count)
        ]

    def start(self):
        greet(self.spot)

        def one(item, carry):
            for reduce in self.reduces:
                reduce.start(item)
            return carry

        lax.fori_loop(0, self.spot.chips, one, 0)
        for tally in self.tallies:
            tally.start()
        for reduce in self.reduces:
            reduce.far_step(0)

    def step(self, step):
        for swap in self.swaps:
            swap.start(step, self.spot.half + 1)
        for reduce in self.reduces:
            reduce.step(step)

    def steps(self, slot, slots):
        total = self.spot.half + 1
        size = -(-total // slots)

        def one(step, carry):
            self.step(step)
            return carry

        first = jnp.minimum(slot * size, total)
        lax.fori_loop(first, jnp.minimum(first + size, total), one, 0)

    def finish(self):
        for tally in self.tallies:
            tally.middle()
        for each in self.reduces + self.swaps + self.tallies:
            each.finish()

    @staticmethod
    def scratch(shards, lents, partials, swap_count, tallied):
        scratch = []
        for lent, part in zip(lents, partials, strict=True):
            scratch += Reduce.scratch(shards, lent, part.shape[0] // shards, part.shape[1])
        scratch += [DMA((shards,)), DMA((shards,)), DMA] * swap_count
        for each in tallied:
            scratch += Tally.scratch(shards, each.shape)
        return scratch


def reduce_kernel(shards, lents, swap_count, tally_count, *refs):
    total = len(lents) + swap_count + tally_count
    work = ReduceAll(
        Spot(shards),
        lents,
        swap_count,
        tally_count,
        refs[:total],
        refs[total : 2 * total],
        refs[2 * total :],
    )
    work.start()
    work.steps(0, 1)
    work.finish()


def reduce_specs(shards, partials, sent, tallied):
    anywhere = pl.BlockSpec(memory_space=pl.ANY)
    inside = pl.BlockSpec(memory_space=pltpu.VMEM)
    out_shape = [
        jax.ShapeDtypeStruct((part.shape[0] // shards, part.shape[1]), jnp.float32)
        for part in partials
    ]
    out_shape += [jax.ShapeDtypeStruct(each.shape, each.dtype) for each in [*sent, *tallied]]
    out_specs = [inside] * len(partials) + [anywhere] * len(sent) + [inside] * len(tallied)
    in_specs = [anywhere] * (len(partials) + len(sent)) + [inside] * len(tallied)
    return in_specs, out_specs, out_shape


def reduce_call(shards, partials, lents, sent, tallied, collective_id):
    in_specs, out_specs, out_shape = reduce_specs(shards, partials, sent, tallied)
    results = pl.pallas_call(
        functools.partial(reduce_kernel, shards, lents, len(sent), len(tallied)),
        out_shape=out_shape,
        in_specs=in_specs,
        out_specs=out_specs,
        scratch_shapes=ReduceAll.scratch(shards, lents, partials, len(sent), tallied),
        compiler_params=pltpu.CompilerParams(
            collective_id=collective_id, has_side_effects=True, vmem_limit_bytes=56 << 20
        ),
    )(*partials, *sent, *tallied)
    first, second = len(partials), len(partials) + len(sent)
    return results[:first], results[first:second], results[second:]


def matmul(left, right, left_dim=1, right_dim=0):
    return lax.dot_general(
        left, right, (((left_dim,), (right_dim,)), ((), ())), preferred_element_type=jnp.float32
    )


def pick_rows(slot_column, slot_total):
    shape = (slot_column.shape[0], slot_total)
    return (slot_column == lax.broadcasted_iota(jnp.int32, shape, 1)).astype(jnp.bfloat16)


def place_rows(slot_row, slot_total):
    shape = (slot_total, slot_row.shape[1])
    return (slot_row == lax.broadcasted_iota(jnp.int32, shape, 0)).astype(jnp.bfloat16)


def pack_kernel(rows_ref, tokens_ref, cotangent_ref, tokens_out, cotangent_out):
    chosen = place_rows(rows_ref[0:1, :], tokens_out.shape[0])
    tokens_out[...] = matmul(chosen, tokens_ref[...]).astype(jnp.bfloat16)
    cotangent_out[...] = matmul(chosen, cotangent_ref[...]).astype(jnp.bfloat16)


def unpack_kernel(columns_ref, output_ref, grad_ref, output_out, grad_out):
    chosen = pick_rows(columns_ref[:, 0:1], output_ref.shape[0])
    output_out[...] = matmul(chosen, output_ref[...]).astype(jnp.bfloat16)
    grad_out[...] = matmul(chosen, grad_ref[...]).astype(jnp.bfloat16)


def local_call(kernel, out_shape, inputs, spaces=None, scratch=()):
    inside = pl.BlockSpec(memory_space=pltpu.VMEM)
    return pl.pallas_call(
        kernel,
        out_shape=out_shape,
        in_specs=spaces or [inside] * len(inputs),
        out_specs=[inside] * len(out_shape),
        scratch_shapes=list(scratch),
        compiler_params=pltpu.CompilerParams(vmem_limit_bytes=56 << 20),
    )(*inputs)


def segment_of(index, lengths_ref):
    first = lengths_ref[0, 0]
    second = first + lengths_ref[0, 1]
    third = second + lengths_ref[0, 2]
    return (
        (index >= first).astype(jnp.int32)
        + (index >= second).astype(jnp.int32)
        + (index >= third).astype(jnp.int32)
    )


def pair_masks(columns_ref, rows_ref, lengths_ref, same_ref, hidden_ref):
    size = columns_ref.shape[0]
    shape = (size, size)
    key_id = lax.broadcasted_iota(jnp.int32, shape, 0)
    query_id = lax.broadcasted_iota(jnp.int32, shape, 1)
    key_column = lax.broadcasted_iota(jnp.int32, (size, 1), 0)
    query_row = lax.broadcasted_iota(jnp.int32, (1, size), 1)
    together = segment_of(key_column, lengths_ref) == segment_of(query_row, lengths_ref)
    seen = together & ((columns_ref[:, 3:4] > 0) | (key_id == query_id))
    same_ref[...] = (columns_ref[:, 2:3] == rows_ref[2:3, :]).astype(jnp.float32)
    hidden_ref[...] = jnp.where(seen, 0.0, masked_score)


def turn(values, cosine, sine):
    width = values.shape[1]
    lane = lax.broadcasted_iota(jnp.int32, values.shape, 1)
    other = jnp.where(
        lane % 64 < 32, pltpu.roll(values, width - 32, 1), pltpu.roll(values, 32, 1)
    )
    return values * cosine + other * sine


def head_lanes(values, head):
    lane = lax.broadcasted_iota(jnp.int32, values.shape, 1)
    return jnp.where((lane < 64) == (head == 0), values, jnp.zeros_like(values))


def project(input_ref, weight_refs, cosine_ref, sine_ref, out_ref, scale):
    width = weight_refs[0].shape[0]
    cosine = jnp.concatenate([cosine_ref[...]] * 2, axis=1)
    sine = jnp.concatenate([sine_ref[...]] * 2, axis=1)

    def one(i, carry):
        def columns(part):
            return pl.ds(pl.multiple_of(part * width + i * 256, 256), 256)

        at = pl.ds(pl.multiple_of(i * 256, 256), 256)
        query = matmul(input_ref[...], weight_refs[0][:, at])
        out_ref[:, columns(0)] = (turn(query, cosine, sine) * scale).astype(jnp.bfloat16)
        key = matmul(input_ref[...], weight_refs[1][:, at])
        out_ref[:, columns(1)] = turn(key, cosine, sine).astype(jnp.bfloat16)
        out_ref[:, columns(2)] = matmul(input_ref[...], weight_refs[2][:, at]).astype(
            jnp.bfloat16
        )
        return carry

    lax.fori_loop(0, width // 256, one, 0)


def attend_pair(pair, width, heads_ref, bias_ref, same_ref, hidden_ref, out_ref, log_ref):
    def columns(part):
        return pl.ds(pl.multiple_of(part * width + pair * 128, 128), 128)

    query, key, value = (heads_ref[:, columns(part)] for part in range(3))
    total = None
    for which in (0, 1):
        head = 2 * pair + which
        gap = bias_ref[0, head] - bias_ref[1, head]
        scores = matmul(head_lanes(key, which), query, 1, 1)
        scores = scores + same_ref[...] * gap + hidden_ref[...]
        top = jnp.max(scores, axis=0, keepdims=True)
        weights = jnp.exp(scores - top)
        weight_sum = jnp.sum(weights, axis=0, keepdims=True)
        log_ref[pl.ds(head, 1), :] = top + jnp.log(weight_sum)
        soft = (weights * (1.0 / weight_sum)).astype(jnp.bfloat16)
        part = matmul(head_lanes(value, which), soft, 0, 0)
        total = part if total is None else total + part
    out_ref[:, pl.ds(pl.multiple_of(pair * 128, 128), 128)] = total.T.astype(jnp.bfloat16)


def normed(values):
    factor = lax.rsqrt(jnp.mean(values * values, axis=-1, keepdims=True) + epsilon)
    return values * factor, factor


def forward_body(refs, between=None):
    (
        arrived_ref, columns_ref, rows_ref, lengths_ref, bias_ref, gain_ref,
        query_w_ref, key_w_ref, value_w_ref, cosine_ref, sine_ref,
        stream_ref, input_ref, heads_ref, out_ref, log_ref,
        same_ref, hidden_ref,
    ) = refs
    width = gain_ref.shape[1]
    scale = 1.0 / math.sqrt(64)
    chosen = pick_rows(columns_ref[:, 1:2], arrived_ref.shape[0])
    stream = matmul(chosen, arrived_ref[...])
    stream_ref[...] = stream.astype(jnp.bfloat16)
    input_ref[...] = (normed(stream)[0] * gain_ref[...]).astype(jnp.bfloat16)
    pair_masks(columns_ref, rows_ref, lengths_ref, same_ref, hidden_ref)
    weight_refs = (query_w_ref, key_w_ref, value_w_ref)
    project(input_ref, weight_refs, cosine_ref, sine_ref, heads_ref, scale)

    def one(pair, carry):
        if between is not None:
            between(pair)
        attend_pair(pair, width, heads_ref, bias_ref, same_ref, hidden_ref, out_ref, log_ref)
        return carry

    lax.fori_loop(0, width // 128, one, 0)


def forward_kernel(*refs):
    forward_body(refs)


def fold_lanes(row):
    folded = row[:, 0:128]
    for i in range(1, row.shape[1] // 128):
        folded += row[:, i * 128 : (i + 1) * 128]
    return folded


def mlp_kernel(
    shards, columns_ref, rows_ref, gain_ref, stream_ref, attended_ref, arrived_ref, out_w_ref,
    gate_ref, up_ref, down_ref,
    grad_gate_ref, grad_up_ref, grad_down_ref, dh_ref, grad_out_ref, do_ref, stats_ref, home_ref,
    middle_ref, input_ref, input_t_ref, dy_ref, mlp_ref, back_ref, packed_ref, gates_ref, ups_ref,
    send_sems, recv_sems, own_sem,
):
    step = pl.program_id(0)
    final = pl.num_programs(0) - 1
    tiles = pl.num_programs(0) // 2
    half = jnp.bfloat16
    spot = Spot(shards)
    swap = Swap(spot, packed_ref, home_ref, (send_sems, recv_sems), own_sem)

    def square(values, at):
        valid = (columns_ref[:, 3:4] > 0).astype(jnp.float32)
        across = jnp.sum(values * values * valid, axis=0, keepdims=True)
        stats_ref[at : at + 1, :] = fold_lanes(across)

    @pl.when(step == 0)
    def _():
        greet(spot)
        stats_ref[...] = jnp.zeros_like(stats_ref)
        stream = stream_ref[...].astype(jnp.float32)
        square(stream, 8)
        attn_out = matmul(attended_ref[...], out_w_ref[...])
        square(attn_out, 9)
        middle = stream + attn_out
        square(middle, 10)
        middle_ref[...] = middle
        entry = normed(middle)[0] * gain_ref[...]
        input_ref[...] = entry.astype(half)
        input_t_ref[...] = entry.T.astype(half)
        chosen = pick_rows(columns_ref[:, 1:2], arrived_ref.shape[0])
        dy_ref[...] = matmul(chosen, arrived_ref[...]).astype(half)
        mlp_ref[...] = jnp.zeros_like(mlp_ref)
        back_ref[...] = jnp.zeros_like(back_ref)

    @pl.when(step < tiles)
    def _():
        gate = matmul(input_ref[...], gate_ref[...])
        up = matmul(input_ref[...], up_ref[...])
        gates_ref[step] = gate
        ups_ref[step] = up
        hidden = (gate * jax.nn.sigmoid(gate) * up).astype(half)
        mlp_ref[...] += matmul(hidden, down_ref[...])

    @pl.when(step == tiles - 1)
    def _():
        valid = (columns_ref[:, 3:4] > 0).astype(jnp.float32)
        mlp_out = mlp_ref[...]
        result = middle_ref[...] + mlp_out
        placed = place_rows(rows_ref[1:2, :], packed_ref.shape[0])
        packed_ref[...] = matmul(placed, result.astype(half)).astype(half)
        swap.start(0, 1)
        square(mlp_out, 11)
        square(result, 12)
        lane = lax.broadcasted_iota(jnp.int32, (valid.shape[0], 128), 1)
        stats_ref[13:14, :] = jnp.sum(jnp.where(lane == 0, valid, 0.0), axis=0, keepdims=True)

    @pl.when(step >= tiles)
    def _():
        gate, up = gates_ref[step - tiles], ups_ref[step - tiles]
        grad_hidden = matmul(dy_ref[...], down_ref[...], 1, 1)
        sigmoid = jax.nn.sigmoid(gate)
        silu = gate * sigmoid
        hidden = (silu * up).astype(half)
        grad_gate = (grad_hidden * up * sigmoid * (1.0 + gate * (1.0 - sigmoid))).astype(half)
        grad_up = (grad_hidden * silu).astype(half)
        back_ref[...] += matmul(grad_gate, gate_ref[...], 1, 1) + matmul(
            grad_up, up_ref[...], 1, 1
        )
        grad_gate_ref[...] = matmul(input_t_ref[...], grad_gate).astype(half)
        grad_up_ref[...] = matmul(input_t_ref[...], grad_up).astype(half)
        grad_down_ref[...] = matmul(hidden, dy_ref[...], 0, 0).astype(half)

    @pl.when(step == final)
    def _():
        width = gain_ref.shape[1]
        entry, factor = normed(middle_ref[...])
        back = back_ref[...]
        gain_grad = jnp.sum(back * entry, axis=0, keepdims=True)
        for i in range(width // 128):
            stats_ref[i : i + 1, :] = gain_grad[:, i * 128 : (i + 1) * 128]
        scaled = back * gain_ref[...]
        inner = jnp.mean(scaled * entry, axis=-1, keepdims=True)
        dh = dy_ref[...].astype(jnp.float32) + factor * (scaled - entry * inner)
        dh_ref[...] = dh
        branch = dh.astype(half)
        do_ref[...] = matmul(branch, out_w_ref[...], 1, 1).astype(half)
        grad_out_ref[...] = matmul(attended_ref[...], branch, 0, 0).astype(half)
        swap.finish()


def mlp_call(shards, slot_total, inputs, weights, collective_id):
    columns, rows, gain, stream, attended, arrived, out_w = inputs
    gate, up, down = weights
    tokens, width = stream.shape
    hidden = gate.shape[1]
    tile = 512
    tiles = hidden // tile

    def whole(array):
        return pl.BlockSpec(
            array.shape, lambda i: (0,) * len(array.shape), pipeline_mode=pl.Buffered(1)
        )

    half, full = jnp.bfloat16, jnp.float32
    across = pl.BlockSpec((width, tile), lambda i: (0, lax.rem(i, tiles)))
    down_spec = pl.BlockSpec((tile, width), lambda i: (lax.rem(i, tiles), 0))
    across_out = pl.BlockSpec((width, tile), lambda i: (0, jnp.maximum(i - tiles, 0)))
    down_out = pl.BlockSpec((tile, width), lambda i: (jnp.maximum(i - tiles, 0), 0))
    out_shape = [
        jax.ShapeDtypeStruct((width, hidden), half),
        jax.ShapeDtypeStruct((width, hidden), half),
        jax.ShapeDtypeStruct((hidden, width), half),
        jax.ShapeDtypeStruct((tokens, width), full),
        jax.ShapeDtypeStruct((width, width), half),
        jax.ShapeDtypeStruct((tokens, width), half),
        jax.ShapeDtypeStruct((16, 128), full),
        jax.ShapeDtypeStruct((slot_total, width), half),
    ]
    rest = [pl.BlockSpec(each.shape, lambda i: (0, 0)) for each in out_shape[3:7]]
    return pl.pallas_call(
        functools.partial(mlp_kernel, shards),
        out_shape=out_shape,
        grid=(2 * tiles,),
        in_specs=[whole(each) for each in inputs] + [across, across, down_spec],
        out_specs=[across_out, across_out, down_out, *rest, pl.BlockSpec(memory_space=pl.ANY)],
        scratch_shapes=[
            pltpu.VMEM((tokens, width), full),
            pltpu.VMEM((tokens, width), half),
            pltpu.VMEM((width, tokens), half),
            pltpu.VMEM((tokens, width), half),
            pltpu.VMEM((tokens, width), full),
            pltpu.VMEM((tokens, width), full),
            pltpu.VMEM((slot_total, width), half),
            pltpu.VMEM((tiles, tokens, tile), full),
            pltpu.VMEM((tiles, tokens, tile), full),
            DMA((shards,)),
            DMA((shards,)),
            DMA,
        ],
        compiler_params=pltpu.CompilerParams(
            collective_id=collective_id, has_side_effects=True, vmem_limit_bytes=VMEM_LIMIT
        ),
    )(*inputs, *weights)


def attend_back_pair(
    pair, width, scale, heads_ref, do_ref, bias_ref, log_ref, same_ref, hidden_ref, cosine_ref,
    sine_ref, grads_ref, bias_same_ref, bias_all_ref,
):
    half = jnp.bfloat16

    def columns(part):
        return pl.ds(pl.multiple_of(part * width + pair * 128, 128), 128)

    query, key, value = (heads_ref[:, columns(part)] for part in range(3))
    grad_out = do_ref[:, columns(0)]
    query_t = key_grad = value_grad = None
    for which in (0, 1):
        head = 2 * pair + which
        gap = bias_ref[0, head] - bias_ref[1, head]
        key_part = head_lanes(key, which)
        scores = matmul(key_part, query, 1, 1)
        scores = scores + same_ref[...] * gap + hidden_ref[...]
        soft = jnp.exp(scores - log_ref[pl.ds(head, 1), :])
        grad_soft = matmul(head_lanes(value, which), grad_out, 1, 1)
        inner = jnp.sum(soft * grad_soft, axis=0, keepdims=True)
        grad_scores = (soft * (grad_soft - inner)).astype(half)
        wide = grad_scores.astype(jnp.float32)
        bias_all_ref[pl.ds(head, 1), :] = jnp.sum(wide, axis=0, keepdims=True)
        bias_same_ref[pl.ds(head, 1), :] = jnp.sum(wide * same_ref[...], axis=0, keepdims=True)
        parts = (
            matmul(key_part, grad_scores, 0, 0),
            matmul(grad_scores, head_lanes(query, which)),
            matmul(soft.astype(half), head_lanes(grad_out, which)),
        )
        if which == 0:
            query_t, key_grad, value_grad = parts
        else:
            query_t, key_grad, value_grad = (
                query_t + parts[0],
                key_grad + parts[1],
                value_grad + parts[2],
            )
    cosine, sine = cosine_ref[...], -sine_ref[...]
    grads_ref[:, columns(0)] = (turn(query_t.T, cosine, sine) * scale).astype(half)
    grads_ref[:, columns(1)] = turn(key_grad, cosine, sine).astype(half)
    grads_ref[:, columns(2)] = value_grad.astype(half)


def backward_reduce_kernel(shards, lents, *refs):
    (
        columns_ref, rows_ref, lengths_ref, bias_ref, cosine_ref, sine_ref, heads_ref, log_ref,
        do_ref,
    ) = refs[:9]
    count = len(lents)
    partials, refs = refs[9 : 9 + count], refs[9 + count :]
    (grads_ref, bias_out_ref), refs = refs[:2], refs[2:]
    outputs, refs = refs[:count], refs[count:]
    same_ref, hidden_ref, bias_same_ref, bias_all_ref = refs[:4]
    work = ReduceAll(Spot(shards), lents, 0, 0, partials, outputs, refs[4:])
    work.start()
    width = do_ref.shape[1]
    scale = 1.0 / math.sqrt(64)
    pair_masks(columns_ref, rows_ref, lengths_ref, same_ref, hidden_ref)
    pairs = width // 128

    def one(pair, carry):
        work.steps(pair, pairs)
        attend_back_pair(
            pair, width, scale, heads_ref, do_ref, bias_ref, log_ref, same_ref, hidden_ref,
            cosine_ref, sine_ref, grads_ref, bias_same_ref, bias_all_ref,
        )
        return carry

    lax.fori_loop(0, pairs, one, 0)
    heads = bias_all_ref.shape[0]
    lane = lax.broadcasted_iota(jnp.int32, (heads, 128), 1)
    row = lax.broadcasted_iota(jnp.int32, (heads, 128), 0)
    same = jnp.sum(bias_same_ref[...], axis=1, keepdims=True)
    other = jnp.sum(bias_all_ref[...], axis=1, keepdims=True) - same
    bias_out_ref[...] = jnp.broadcast_to(
        jnp.sum(
            jnp.where(lane == row, same, 0.0) + jnp.where(lane == row + heads, other, 0.0),
            axis=0,
            keepdims=True,
        ),
        bias_out_ref.shape,
    )
    work.finish()


def backward_reduce_call(shards, inputs, spaces, partials, lents, heads, collective_id):
    in_specs, out_specs, out_shape = reduce_specs(shards, partials, [], [])
    inside = pl.BlockSpec(memory_space=pltpu.VMEM)
    tokens, width = inputs[-1].shape
    full = jnp.float32
    results = pl.pallas_call(
        functools.partial(backward_reduce_kernel, shards, lents),
        out_shape=[
            jax.ShapeDtypeStruct((tokens, 3 * width), jnp.bfloat16),
            jax.ShapeDtypeStruct((8, 128), full),
            *out_shape,
        ],
        in_specs=[*spaces, *in_specs],
        out_specs=[inside, inside, *out_specs],
        scratch_shapes=[
            pltpu.VMEM((tokens, tokens), full),
            pltpu.VMEM((tokens, tokens), full),
            pltpu.VMEM((heads, tokens), full),
            pltpu.VMEM((heads, tokens), full),
            *ReduceAll.scratch(shards, lents, partials, 0, []),
        ],
        compiler_params=pltpu.CompilerParams(
            collective_id=collective_id, has_side_effects=True, vmem_limit_bytes=VMEM_LIMIT
        ),
    )(*inputs, *partials)
    return results[0], results[1], results[2:]


def entry_kernel(shards, lents, *refs):
    (
        rows_ref, gain_ref, query_w_ref, key_w_ref, value_w_ref, stream_ref, input_ref, grads_ref,
        dh_ref, stats_mlp_ref, bias_ref,
    ) = refs[:11]
    outputs, home_ref, sums_ref = refs[11:14], refs[14], refs[15]
    partials, back_ref, packed_ref, stats_ref = refs[16:19], refs[19], refs[20], refs[21]
    spot = Spot(shards)
    work = ReduceAll(
        spot, lents, 1, 1, [*partials, packed_ref, stats_ref], [*outputs, home_ref, sums_ref],
        refs[22:],
    )
    half = jnp.bfloat16
    width = gain_ref.shape[1]
    greet(spot)
    columns = [pl.ds(which * width, width) for which in range(3)]
    for which in range(3):
        reduce = work.reduces[which]

        def one(i, carry, which=which):
            at = pl.ds(pl.multiple_of(i * 256, 256), 256)
            part = grads_ref[:, pl.ds(pl.multiple_of(which * width + i * 256, 256), 256)]
            partials[which][:, at] = matmul(input_ref[...], part, 0, 0).astype(half)
            return carry

        lax.fori_loop(0, width // 256, one, 0)

        def begin(item, carry, reduce=reduce):
            reduce.start(item)
            return carry

        lax.fori_loop(0, spot.chips, begin, 0)
        reduce.far_step(0)
    back_ref[...] = matmul(grads_ref[:, columns[0]], query_w_ref[...], 1, 1)
    for reduce in work.reduces:
        reduce.step(0)
    back_ref[...] += matmul(grads_ref[:, columns[1]], key_w_ref[...], 1, 1)
    back_ref[...] += matmul(grads_ref[:, columns[2]], value_w_ref[...], 1, 1)
    back = back_ref[...]
    entry, factor = normed(stream_ref[...].astype(jnp.float32))
    gain_grad = jnp.sum(back * entry, axis=0, keepdims=True)
    scaled = back * gain_ref[...]
    inner = jnp.mean(scaled * entry, axis=-1, keepdims=True)
    grad_stream = dh_ref[...] + factor * (scaled - entry * inner)
    placed = place_rows(rows_ref[1:2, :], packed_ref.shape[0])
    packed_ref[...] = matmul(placed, grad_stream.astype(half)).astype(half)
    stats_ref[0:16, :] = stats_mlp_ref[...]
    for i in range(width // 128):
        stats_ref[16 + i : 17 + i, :] = gain_grad[:, i * 128 : (i + 1) * 128]
    stats_ref[24:32, :] = bias_ref[...]
    for swap in work.swaps:
        swap.start(0, 1)
    for tally in work.tallies:
        tally.start()

    def rest(step, carry):
        for reduce in work.reduces:
            reduce.step(step)
        return carry

    lax.fori_loop(1, spot.half + 1, rest, 0)
    work.finish()


def entry_call(shards, slot_total, inputs, lents, collective_id):
    anywhere = pl.BlockSpec(memory_space=pl.ANY)
    inside = pl.BlockSpec(memory_space=pltpu.VMEM)
    weights, stream = inputs[2:5], inputs[5]
    tokens, width = stream.shape
    half, full = jnp.bfloat16, jnp.float32
    tallied = jax.ShapeDtypeStruct((32, 128), full)
    results = pl.pallas_call(
        functools.partial(entry_kernel, shards, lents),
        out_shape=[
            *[jax.ShapeDtypeStruct((width // shards, width), full)] * 3,
            jax.ShapeDtypeStruct((slot_total, width), half),
            tallied,
        ],
        in_specs=[inside] * len(inputs),
        out_specs=[inside] * 3 + [anywhere, inside],
        scratch_shapes=[
            *[pltpu.VMEM((width, width), half)] * 3,
            pltpu.VMEM((tokens, width), full),
            pltpu.VMEM((slot_total, width), half),
            pltpu.VMEM((32, 128), full),
            *ReduceAll.scratch(shards, lents, weights, 1, [tallied]),
        ],
        compiler_params=pltpu.CompilerParams(
            collective_id=collective_id, has_side_effects=True, vmem_limit_bytes=VMEM_LIMIT
        ),
    )(*inputs)
    return results[:3], results[3], results[4]


def forward_gather_kernel(shards, lents, swap_count, compute_counts, *refs):
    ins, outs = compute_counts
    total = len(lents) + swap_count
    in_refs, refs = refs[: ins + total], refs[ins + total :]
    out_refs, refs = refs[: outs + total], refs[outs + total :]
    masks, scratch = refs[:2], refs[2:]
    work = GatherAll(
        Spot(shards), lents, swap_count, in_refs[ins:], out_refs[outs:], scratch
    )
    work.start()
    pairs = in_refs[5].shape[1] // 128
    forward_body(
        (*in_refs[:ins], *out_refs[:outs], *masks), lambda pair: work.steps(pair, pairs)
    )
    work.finish()


def forward_gather_call(shards, inputs, spaces, out_shape, pieces, lents, sent, collective_id):
    anywhere = pl.BlockSpec(memory_space=pl.ANY)
    inside = pl.BlockSpec(memory_space=pltpu.VMEM)
    tokens = out_shape[0].shape[0]
    counts = (len(inputs), len(out_shape))
    comm = len(pieces) + len(sent)
    results = pl.pallas_call(
        functools.partial(forward_gather_kernel, shards, lents, len(sent), counts),
        out_shape=[*out_shape, *gather_shapes(shards, pieces, sent, [])],
        in_specs=spaces + [anywhere] * comm,
        out_specs=[inside] * len(out_shape) + [anywhere] * comm,
        scratch_shapes=[pltpu.VMEM((tokens, tokens), jnp.float32)] * 2
        + GatherAll.scratch(shards, len(pieces), len(sent)),
        compiler_params=pltpu.CompilerParams(
            collective_id=collective_id, has_side_effects=True, vmem_limit_bytes=56 << 20
        ),
    )(*inputs, *pieces, *sent)
    first = len(out_shape)
    second = first + len(pieces)
    return results[:first], results[first:second], results[second:]


def on_device(
    tokens,
    cotangent,
    send_slot,
    recv_slot,
    lengths,
    variate,
    valid_mask,
    norm_attn,
    w_query,
    w_key,
    w_value,
    w_out,
    variate_bias,
    norm_mlp,
    w_gate,
    w_up,
    w_down,
):
    shards = lax.axis_size("shard")
    tok_rows, width = tokens.shape
    slot_total = 2 * tok_rows
    heads = variate_bias.shape[1]
    half, full = jnp.bfloat16, jnp.float32
    share = width // shards
    indices = jnp.stack([send_slot, recv_slot, variate, valid_mask])
    rows = jnp.concatenate([indices, jnp.zeros_like(indices)])
    columns = rows.T
    _, position = layout(lengths[0], tok_rows)
    cosine, sine = angle_tables(position, width // heads)
    cosine = jnp.concatenate([cosine] * 4, axis=1)
    sine = jnp.concatenate([-sine, sine] * 2, axis=1)
    gains = jnp.stack([norm_attn, norm_mlp]).astype(full)
    gains = jnp.pad(gains, ((0, 6), (0, 128 - share)))
    shape = jax.ShapeDtypeStruct
    packed_shape = shape((slot_total, width), half)
    token_shape = shape((tok_rows, width), half)
    out_tokens, out_cotangent = local_call(
        pack_kernel, [packed_shape] * 2, [rows, tokens, cotangent]
    )
    full_in, (arrived_tokens,), (gains,) = gather_call(
        shards,
        [w_query, w_key, w_value],
        (4, 4, 4),
        [out_tokens],
        [gains],
        1,
    )
    gains = gains.reshape(shards, 8, 128)
    gain_attn = gains[:, 0, :share].reshape(1, width)
    gain_mlp = gains[:, 1, :share].reshape(1, width)
    inside = pl.BlockSpec(memory_space=pltpu.VMEM)
    scalar = pl.BlockSpec(memory_space=pltpu.SMEM)
    (
        (stream, input_attn, head_rows, attended, logs),
        (full_out, full_gate, full_up, full_down),
        (arrived_grads,),
    ) = forward_gather_call(
        shards,
        [
            arrived_tokens, columns, rows, lengths, variate_bias, gain_attn, *full_in,
            cosine, sine,
        ],
        [inside] * 3 + [scalar] * 2 + [inside] * 6,
        [
            token_shape,
            token_shape,
            shape((tok_rows, 3 * width), half),
            token_shape,
            shape((heads, tok_rows), full),
        ],
        [w_out, w_gate, w_up, w_down],
        (2, 4, 4, 2),
        [out_cotangent],
        2,
    )
    part_gate, part_up, part_down, grad_middle, part_out, grad_attended, stats_mlp, home_out = (
        mlp_call(
            shards,
            slot_total,
            [columns, rows, gain_mlp, stream, attended, arrived_grads, full_out],
            [full_gate, full_up, full_down],
            3,
        )
    )
    head_grads, bias_sums, (grad_gate, grad_up, grad_down, grad_out) = backward_reduce_call(
        shards,
        [columns, rows, lengths, variate_bias, cosine, sine, head_rows, logs, grad_attended],
        [inside] * 2 + [scalar] * 2 + [inside] * 5,
        [part_gate, part_up, part_down, part_out],
        (2, 2, 2, 2),
        heads,
        4,
    )
    (grad_query, grad_key, grad_value), home_grad, sums = entry_call(
        shards,
        slot_total,
        [
            rows, gain_attn, *full_in, stream, input_attn, head_grads, grad_middle, stats_mlp,
            bias_sums,
        ],
        (2, 2, 2),
        5,
    )
    output, input_grad = local_call(
        unpack_kernel, [token_shape] * 2, [columns, home_out, home_grad]
    )
    squares = jnp.sum(sums[8:14], axis=1)
    root_means = jnp.sqrt(squares[:5] / (squares[5] * width))
    share_start = lax.axis_index("shard") * share
    grad_norm_mlp = lax.dynamic_slice_in_dim(sums[0:8].reshape(-1), share_start, share)
    grad_norm_attn = lax.dynamic_slice_in_dim(sums[16:24].reshape(-1), share_start, share)
    bias_grads = sums[24, : 2 * heads].reshape(2, heads)
    return (
        output,
        input_grad,
        grad_norm_attn,
        grad_query,
        grad_key,
        grad_value,
        grad_out,
        bias_grads,
        grad_norm_mlp,
        grad_gate,
        grad_up,
        grad_down,
        root_means,
    )


def solution(mesh):
    in_specs = (
        P(("rep", "shard"), None),
        P(("rep", "shard"), None),
        P(("rep", "shard")),
        P(("rep", "shard")),
        P(("rep", "shard"), None),
        P(("rep", "shard")),
        P(("rep", "shard")),
        P("shard"),
        P("shard", None),
        P("shard", None),
        P("shard", None),
        P("shard", None),
        P(),
        P("shard"),
        P("shard", None),
        P("shard", None),
        P("shard", None),
    )
    out_specs = (
        P(("rep", "shard"), None),
        P(("rep", "shard"), None),
        P("shard"),
        P("shard", None),
        P("shard", None),
        P("shard", None),
        P("shard", None),
        P(),
        P("shard"),
        P("shard", None),
        P("shard", None),
        P("shard", None),
        P(),
    )
    return jax.shard_map(
        on_device, mesh=mesh, in_specs=in_specs, out_specs=out_specs, check_vma=False
    )
```

```python
import functools
import math

import jax
import jax.numpy as jnp
from jax import lax
from jax.experimental import pallas as pl
from jax.experimental.pallas import tpu as pltpu
from jax.sharding import PartitionSpec as P

MESH = pl.DeviceIdType.MESH
DMA = pltpu.SemaphoreType.DMA
epsilon = 1e-06
masked_score = -1e30
VMEM_LIMIT = 62 << 20


def angle_tables(position, head_dim):
    half_dim = head_dim // 2
    inverse_freq = 1.0 / 10000.0 ** (jnp.arange(half_dim, dtype=jnp.float32) / half_dim)
    theta_angle = position.astype(jnp.float32)[:, None] * inverse_freq[None, :]
    return (jnp.cos(theta_angle), jnp.sin(theta_angle))


def layout(lengths_row, tok_rows):
    slot_ids = jnp.arange(tok_rows, dtype=jnp.int32)
    seq_ends = jnp.cumsum(lengths_row)
    segment = jnp.sum((slot_ids[:, None] >= seq_ends[None, :]).astype(jnp.int32), axis=1)
    starts = seq_ends - lengths_row
    chosen = segment[:, None] == jnp.arange(lengths_row.shape[0], dtype=jnp.int32)[None, :]
    begins = jnp.sum(jnp.where(chosen, starts[None, :], 0), axis=1)
    return (segment, slot_ids - begins)


def ring_place(chip, chips):
    return jnp.where(chip % 2 == 0, chip // 2, chips - 1 - chip // 2)


def ring_chip(place, chips):
    wrapped = lax.rem(place + 2 * chips, chips)
    return jnp.where(wrapped < chips // 2, 2 * wrapped, 2 * (chips - 1 - wrapped) + 1)


class Spot:
    def __init__(self, shards):
        self.shards = shards
        self.chips = shards // 2
        self.half = self.chips // 2
        self.rep = lax.axis_index("rep")
        self.shard = lax.axis_index("shard")
        self.core = lax.rem(self.shard, 2)
        self.place = ring_place(self.shard // 2, self.chips)
        self.sibling = self.shard + 1 - 2 * self.core

    def block(self, place, core=None):
        return 2 * ring_chip(place, self.chips) + (self.core if core is None else core)

    def along(self, way, distance):
        return self.place - distance if way == 0 else self.place + distance

    def ahead(self, way):
        return (self.rep, self.block(self.along(way, -1)))


def greet(spot):
    barrier = pltpu.get_barrier_semaphore()

    def peer(k, carry):
        target = lax.rem(spot.shard + k, spot.shards)
        pl.semaphore_signal(barrier, inc=1, device_id=(spot.rep, target), device_id_type=MESH)
        return carry

    lax.fori_loop(1, spot.shards, peer, 0)
    pl.semaphore_signal(
        barrier, inc=1, device_id=(1 - spot.rep, spot.shard), device_id_type=MESH
    )
    pl.semaphore_wait(barrier, spot.shards)


def remote(src, dst, sems, at, target):
    return pltpu.make_async_remote_copy(
        src_ref=src,
        dst_ref=dst,
        send_sem=sems[0].at[at],
        recv_sem=sems[1].at[at],
        device_id=target,
        device_id_type=MESH,
    )


class Swap:
    def __init__(self, spot, source, arrived, sems, own_sem):
        self.spot, self.sems = spot, sems
        self.source, self.arrived = source, arrived
        self.capacity = arrived.shape[0] // spot.shards
        self.own = pltpu.make_async_copy(
            self.part(spot.shard), arrived.at[self.rows(spot.shard)], own_sem
        )

    def rows(self, shard):
        return pl.ds(pl.multiple_of(shard * self.capacity, 8), self.capacity)

    def part(self, shard):
        if self.source.shape[0] == self.capacity:
            return self.source
        return self.source.at[self.rows(shard)]

    def copy(self, k):
        spot = self.spot
        target = lax.rem(spot.shard + 7 * k, spot.shards)
        return remote(
            self.part(target),
            self.arrived.at[self.rows(spot.shard)],
            self.sems,
            (k,),
            (spot.rep, target),
        )

    def start(self, slot, slots):
        size = -(-self.spot.shards // slots)

        def one(k, carry):
            @pl.when(k == 0)
            def _():
                self.own.start()

            @pl.when(k > 0)
            def _():
                self.copy(k).start()

            return carry

        first = jnp.minimum(slot * size, self.spot.shards)
        lax.fori_loop(first, jnp.minimum(first + size, self.spot.shards), one, 0)

    def finish(self):
        def one(k, carry):
            self.copy(k).wait()
            return carry

        lax.fori_loop(1, self.spot.shards, one, 0)
        self.own.wait()


class Gather:
    def __init__(self, spot, lent, shard_ref, full_ref, sems):
        self.spot, self.lent, self.shard_ref, self.full_ref = spot, lent, shard_ref, full_ref
        self.rows = shard_ref.shape[0]
        self.unit = shard_ref.shape[1] // 8
        self.kept = 8 - lent
        self.ring_sems, self.near_sems, self.far_sems, self.far_near_sems = (
            sems[0:2],
            sems[2:4],
            sems[4:6],
            sems[6:8],
        )
        self.whole_sems, self.own_sem = sems[8:10], sems[10]

    def span(self, way, short):
        first, count = self.lent * self.spot.rep, self.kept
        if short:
            first, count = first + way * (count // 2), count // 2
        return pl.ds(pl.multiple_of(first * self.unit, 128), count * self.unit)

    def region(self, way, hop, short):
        block = self.spot.block(self.spot.along(way, hop))
        return self.full_ref.at[pl.ds(block * self.rows, self.rows), self.span(way, short)]

    def ring(self, way, hop, short, source=None):
        region = self.region(way, hop, short)
        return remote(
            region if source is None else source,
            region,
            self.ring_sems,
            (way, hop),
            self.spot.ahead(way),
        )

    def near(self, way, hop, short):
        region = self.region(way, hop + 1, short)
        target = (self.spot.rep, self.spot.sibling)
        return remote(region, region, self.near_sems, (way, hop), target)

    def lent_region(self, way, hop, owner):
        block = self.spot.block(self.spot.along(way, hop + 1))
        columns = pl.ds(
            pl.multiple_of(self.kept * owner * self.unit, 128), self.lent * self.unit
        )
        return self.full_ref.at[pl.ds(block * self.rows, self.rows), columns]

    def far(self, way, hop):
        region = self.lent_region(way, hop, self.spot.rep)
        target = (1 - self.spot.rep, self.spot.shard)
        return remote(region, region, self.far_sems, (way, hop), target)

    def far_near(self, way, hop):
        region = self.lent_region(way, hop, 1 - self.spot.rep)
        target = (self.spot.rep, self.spot.sibling)
        return remote(region, region, self.far_near_sems, (way, hop), target)

    def own(self):
        spot = self.spot
        mine = self.full_ref.at[pl.ds(spot.shard * self.rows, self.rows)]
        whole = remote(self.shard_ref, mine, self.whole_sems, (0,), (spot.rep, spot.sibling))
        return whole, pltpu.make_async_copy(self.shard_ref, mine, self.own_sem)

    def start(self):
        for way in (0, 1):
            self.ring(way, 0, False, self.shard_ref.at[:, self.span(way, False)]).start()
        for copy in self.own():
            copy.start()

    def step(self, hop):
        final = self.spot.half - 1

        @pl.when(hop < final)
        def _():
            for way in (0, 1):
                self.ring(way, hop, False).wait_recv()

                @pl.when(hop < final - 1)
                def _():
                    self.ring(way, hop + 1, False).start()

                @pl.when(hop == final - 1)
                def _():
                    self.ring(way, hop + 1, True).start()

            for way in (0, 1):
                self.far(way, hop).start()
                self.near(way, hop, False).start()

        @pl.when(hop == final)
        def _():
            for way in (0, 1):
                self.ring(way, hop, True).wait_recv()
            self.far(0, hop).start()
            for way in (0, 1):
                self.near(way, hop, True).start()

        @pl.when(hop > 0)
        def _():
            for way in (0, 1):
                self.relay(way, hop - 1)

    def relay(self, way, hop):
        self.far(way, hop).wait_recv()
        self.far_near(way, hop).start()

    def finish(self):
        final = self.spot.half - 1
        for copy in self.own():
            copy.wait()

        def one(hop, carry):
            for way in (0, 1):
                self.ring(way, hop, False).wait_send()
                self.near(way, hop, False).wait()
                self.far(way, hop).wait_send()
                self.far_near(way, hop).wait()
            return carry

        lax.fori_loop(0, final, one, 0)
        for way in (0, 1):
            self.ring(way, final, True).wait_send()
            self.near(way, final, True).wait()
        self.far(0, final).wait_send()
        self.far_near(0, final).wait()

    @staticmethod
    def scratch(half):
        return [DMA((2, half))] * 8 + [DMA((1,))] * 2 + [DMA]


class GatherAll:
    def __init__(self, spot, lents, swap_count, inputs, outputs, scratch, late=False):
        count = len(lents)
        self.spot, self.late = spot, late
        self.gathers = [
            Gather(spot, lents[g], inputs[g], outputs[g], scratch[11 * g : 11 * g + 11])
            for g in range(count)
        ]
        scratch = scratch[11 * count :]
        self.swaps = [
            Swap(
                spot,
                inputs[count + i],
                outputs[count + i],
                scratch[3 * i : 3 * i + 2],
                scratch[3 * i + 2],
            )
            for i in range(swap_count)
        ]

    def start(self):
        greet(self.spot)
        for gather in self.gathers:
            gather.start()

    def step(self, hop):
        if not self.late:
            for swap in self.swaps:
                swap.start(hop, self.spot.half)
        for gather in self.gathers:
            gather.step(hop)

    def steps(self, slot, slots):
        size = -(-self.spot.half // slots)

        def one(hop, carry):
            self.step(hop)
            return carry

        first = jnp.minimum(slot * size, self.spot.half)
        lax.fori_loop(first, jnp.minimum(first + size, self.spot.half), one, 0)

    def finish_gathers(self):
        for gather in self.gathers:
            gather.relay(0, self.spot.half - 1)
        if self.late:
            for swap in self.swaps:
                swap.start(0, 1)
        for gather in self.gathers:
            gather.finish()

    def finish(self):
        self.finish_gathers()
        for swap in self.swaps:
            swap.finish()

    @staticmethod
    def scratch(shards, count, swap_count):
        return Gather.scratch(shards // 4) * count + [
            DMA((shards,)),
            DMA((shards,)),
            DMA,
        ] * swap_count


def gather_kernel(shards, lents, swap_count, *refs):
    spot = Spot(shards)
    total = len(lents) + swap_count
    work = GatherAll(
        spot, lents, swap_count, refs[:total], refs[total : 2 * total], refs[2 * total :]
    )
    work.start()
    work.steps(0, 1)
    work.finish()


def gather_shapes(shards, pieces, sent, shared):
    return (
        [
            jax.ShapeDtypeStruct((shards * piece.shape[0], piece.shape[1]), piece.dtype)
            for piece in pieces
        ]
        + [jax.ShapeDtypeStruct(rows.shape, rows.dtype) for rows in sent]
        + [
            jax.ShapeDtypeStruct((shards * each.shape[0], each.shape[1]), each.dtype)
            for each in shared
        ]
    )


def gather_call(shards, pieces, lents, sent, shared, collective_id):
    swaps = [*sent, *shared]
    anywhere = pl.BlockSpec(memory_space=pl.ANY)
    results = pl.pallas_call(
        functools.partial(gather_kernel, shards, lents, len(swaps)),
        out_shape=gather_shapes(shards, pieces, sent, shared),
        in_specs=[anywhere] * (len(pieces) + len(swaps)),
        out_specs=[anywhere] * (len(pieces) + len(swaps)),
        scratch_shapes=GatherAll.scratch(shards, len(pieces), len(swaps)),
        compiler_params=pltpu.CompilerParams(
            collective_id=collective_id, has_side_effects=True
        ),
    )(*pieces, *swaps)
    first, second = len(pieces), len(pieces) + len(sent)
    return results[:first], results[first:second], results[second:]


class Reduce:
    def __init__(self, spot, lent, partial_ref, out_ref, refs):
        self.spot, self.lent, self.partial, self.out = spot, lent, partial_ref, out_ref
        self.rows, self.columns = out_ref.shape
        self.unit = self.columns // 8
        self.kept = 8 - lent
        self.width = self.kept * self.unit
        (
            self.own,
            self.sib,
            self.got,
            self.own_far,
            self.sib_far,
            self.got_far,
            self.got_last,
        ) = refs[:7]
        sems = refs[7:]
        self.load_sem, self.load_far_sem = sems[0], sems[1]
        self.sib_sems, self.sib_far_sems = sems[2:4], sems[4:6]
        self.ring_sems, self.far_sems, self.last_sems = sems[6:8], sems[8:10], sems[10:12]

    @staticmethod
    def scratch(shards, lent, rows, columns):
        chips = shards // 2
        unit = columns // 8
        kept, lend = (8 - lent) * unit, lent * unit
        half = jnp.bfloat16
        buffers = [
            pltpu.VMEM((chips, rows, kept), half),
            pltpu.VMEM((chips, rows, kept), half),
            pltpu.VMEM((2, chips // 2, rows, kept), half),
            pltpu.VMEM((chips, rows, lend), half),
            pltpu.VMEM((chips, rows, lend), half),
            pltpu.VMEM((chips, rows, lend), half),
            pltpu.VMEM((rows, kept), half),
        ]
        sems = [DMA((chips,))] * 6 + [DMA((2, chips // 2))] * 2
        sems += [DMA((chips,))] * 2 + [DMA((1,))] * 2
        return buffers + sems

    def owner(self, item, core):
        half = self.spot.half
        pair = (item + 1) // 2
        ahead = lax.rem(item, 2) == 1
        distance = half - pair
        place = jnp.where(ahead, self.spot.place + distance, self.spot.place - distance)
        return self.spot.block(place, core)

    def cut(self, item, core, first, count):
        columns = pl.ds(pl.multiple_of(first * self.unit, 128), count * self.unit)
        block = self.owner(item, core)
        return self.partial.at[pl.ds(block * self.rows, self.rows), columns]

    def kept_cut(self, item, core):
        return self.cut(item, core, self.lent * self.spot.rep, self.kept)

    def lent_cut(self, item, core):
        return self.cut(item, core, self.kept * (1 - self.spot.rep), self.lent)

    def load(self, item):
        source = self.kept_cut(item, self.spot.core)
        return pltpu.make_async_copy(source, self.own.at[item], self.load_sem.at[item])

    def load_far(self, item):
        source = self.lent_cut(item, self.spot.core)
        return pltpu.make_async_copy(source, self.own_far.at[item], self.load_far_sem.at[item])

    def give(self, item):
        source = self.kept_cut(item, 1 - self.spot.core)
        target = (self.spot.rep, self.spot.sibling)
        return remote(source, self.sib.at[item], self.sib_sems, (item,), target)

    def give_far(self, item):
        source = self.lent_cut(item, 1 - self.spot.core)
        target = (self.spot.rep, self.spot.sibling)
        return remote(source, self.sib_far.at[item], self.sib_far_sems, (item,), target)

    def ring(self, way, step, short=False):
        item = 0 if short else 2 * step - 1 + way
        columns = pl.ds(way * self.width // 2, self.width // 2) if short else slice(None)
        return remote(
            self.own.at[item, :, columns],
            self.got.at[way, step, :, columns],
            self.ring_sems,
            (way, step),
            self.spot.ahead(way),
        )

    def far(self, item):
        target = (1 - self.spot.rep, self.spot.shard)
        return remote(
            self.own_far.at[item], self.got_far.at[item], self.far_sems, (item,), target
        )

    def last(self):
        target = (1 - self.spot.rep, self.spot.shard)
        source = self.own.at[self.spot.chips - 1]
        return remote(source, self.got_last, self.last_sems, (0,), target)

    def start(self, item):
        self.load_far(item).start()
        self.give_far(item).start()
        self.load(item).start()
        self.give(item).start()

    def tiles(self, width, body):
        chunk = width if width <= 768 else 512

        def one(tile, carry):
            for first in range(0, width, chunk):
                body(pl.ds(pl.multiple_of(tile * 16, 16), 16), first, chunk)
            return carry

        lax.fori_loop(0, self.rows // 16, one, 0)

    def far_step(self, item):
        self.load_far(item).wait()
        self.give_far(item).wait_recv()

        def add(rows, first, count):
            at = pl.ds(first, count)
            total = self.own_far[item, rows, at].astype(jnp.float32)
            total += self.sib_far[item, rows, at].astype(jnp.float32)
            self.own_far[item, rows, at] = total.astype(jnp.bfloat16)

        self.tiles(self.lent * self.unit, add)
        self.far(item).start()

    def fold(self, item, extra=(), start=0, width=None):
        def add(rows, first, count):
            at = pl.ds(start + first, count)
            total = self.own[item, rows, at].astype(jnp.float32)
            total += self.sib[item, rows, at].astype(jnp.float32)
            for way, step in extra:
                total += self.got[way, step, rows, at].astype(jnp.float32)
            self.own[item, rows, at] = total.astype(jnp.bfloat16)

        self.tiles(self.width if width is None else width, add)

    def ready(self, item):
        self.load(item).wait()
        self.give(item).wait_recv()
        self.far(item).wait_recv()
        offset = self.spot.rep * (self.kept - self.lent) * self.unit

        def add(rows, first, count):
            at = pl.ds(pl.multiple_of(offset + first, 128), count)
            total = self.sib[item, rows, at].astype(jnp.float32)
            total += self.got_far[item, rows, pl.ds(first, count)].astype(jnp.float32)
            self.sib[item, rows, at] = total.astype(jnp.bfloat16)

        self.tiles(self.lent * self.unit, add)

    def step(self, step):
        half, chips = self.spot.half, self.spot.chips

        @pl.when(step == 0)
        def _():
            self.ready(0)
            self.fold(0)
            for way in (0, 1):
                self.ring(way, 0, True).start()

        @pl.when((step > 0) & (step < half))
        def _():
            for way in (0, 1):
                item = 2 * step - 1 + way
                self.ready(item)

                @pl.when(step == 1)
                def _():
                    self.ring(way, 0, True).wait_recv()
                    middle = self.width // 2
                    self.fold(item, [(way, 0)], way * middle, middle)
                    self.fold(item, [], (1 - way) * middle, middle)

                @pl.when(step > 1)
                def _():
                    self.ring(way, step - 1).wait_recv()
                    self.fold(item, [(way, step - 1)])

                self.ring(way, step).start()

        @pl.when(step == half)
        def _():
            self.ready(chips - 1)
            for way in (0, 1):
                self.ring(way, half - 1).wait_recv()
            self.fold(chips - 1, [(0, half - 1), (1, half - 1)])
            self.last().start()

        @pl.when(step < half)
        def _():
            self.far_step(2 * step + 1)

            @pl.when(step < half - 1)
            def _():
                self.far_step(2 * step + 2)

    def finish(self):
        spot, unit, lent = self.spot, self.unit, self.lent
        self.last().wait()
        mine = self.own.at[spot.chips - 1]
        theirs = self.got_last

        def write(lower, upper):
            def one(tile, carry):
                rows = pl.ds(pl.multiple_of(tile * 16, 16), 16)

                def read(ref, first, count):
                    return ref[rows, pl.ds(first * unit, count * unit)].astype(jnp.float32)

                kept, both = self.kept, self.kept - lent
                self.out[rows, pl.ds(0, lent * unit)] = read(lower, 0, lent)
                for i in range(both):
                    self.out[rows, pl.ds((lent + i) * unit, unit)] = read(
                        lower, lent + i, 1
                    ) + read(upper, i, 1)
                self.out[rows, pl.ds(kept * unit, lent * unit)] = read(upper, both, lent)
                return carry

            lax.fori_loop(0, self.rows // 16, one, 0)

        @pl.when(spot.rep == 0)
        def _():
            write(mine, theirs)

        @pl.when(spot.rep == 1)
        def _():
            write(theirs, mine)

        def one(item, carry):
            self.give_far(item).wait_send()
            self.far(item).wait_send()
            self.give(item).wait_send()
            return carry

        lax.fori_loop(0, spot.chips, one, 0)
        for way in (0, 1):
            self.ring(way, 0, True).wait_send()

        def two(step, carry):
            for way in (0, 1):
                self.ring(way, step).wait_send()
            return carry

        lax.fori_loop(1, spot.half, two, 0)


class Tally:
    def __init__(self, spot, mine, out, refs):
        self.spot, self.mine, self.out = spot, mine, out
        self.got, self.half, self.other = refs[0:3]
        self.sems, self.own_sem, self.far_sems = refs[3:5], refs[5], refs[6:8]
        self.own = pltpu.make_async_copy(mine, self.got.at[spot.shard], self.own_sem)

    def copy(self, k):
        spot = self.spot
        target = lax.rem(spot.shard + k, spot.shards)
        return remote(self.mine, self.got.at[spot.shard], self.sems, (k,), (spot.rep, target))

    def far(self):
        target = (1 - self.spot.rep, self.spot.shard)
        return remote(self.half, self.other, self.far_sems, (0,), target)

    def start(self):
        def one(k, carry):
            self.copy(k).start()
            return carry

        lax.fori_loop(1, self.spot.shards, one, 0)
        self.own.start()

    def middle(self):
        def one(k, carry):
            self.copy(k).wait()
            return carry

        lax.fori_loop(1, self.spot.shards, one, 0)
        self.own.wait()

        def add(k, total):
            return total + self.got[k]

        self.half[...] = lax.fori_loop(0, self.spot.shards, add, jnp.zeros_like(self.half))
        self.far().start()

    def finish(self):
        self.far().wait()
        self.out[...] = self.half[...] + self.other[...]

    @staticmethod
    def scratch(shards, shape):
        full = jnp.float32
        return [
            pltpu.VMEM((shards, *shape), full),
            pltpu.VMEM(shape, full),
            pltpu.VMEM(shape, full),
            DMA((shards,)),
            DMA((shards,)),
            DMA,
            DMA((1,)),
            DMA((1,)),
        ]


def matmul(left, right, left_dim=1, right_dim=0):
    return lax.dot_general(
        left, right, (((left_dim,), (right_dim,)), ((), ())), preferred_element_type=jnp.float32
    )


def pick_rows(slot_column, slot_total):
    shape = (slot_column.shape[0], slot_total)
    return (slot_column == lax.broadcasted_iota(jnp.int32, shape, 1)).astype(jnp.bfloat16)


def place_rows(slot_row, slot_total):
    shape = (slot_total, slot_row.shape[1])
    return (slot_row == lax.broadcasted_iota(jnp.int32, shape, 0)).astype(jnp.bfloat16)


def pack_kernel(rows_ref, tokens_ref, cotangent_ref, tokens_out, cotangent_out):
    chosen = place_rows(rows_ref[0:1, :], tokens_out.shape[0])
    tokens_out[...] = matmul(chosen, tokens_ref[...]).astype(jnp.bfloat16)
    cotangent_out[...] = matmul(chosen, cotangent_ref[...]).astype(jnp.bfloat16)


def local_call(kernel, out_shape, inputs, spaces=None, scratch=()):
    inside = pl.BlockSpec(memory_space=pltpu.VMEM)
    return pl.pallas_call(
        kernel,
        out_shape=out_shape,
        in_specs=spaces or [inside] * len(inputs),
        out_specs=[inside] * len(out_shape),
        scratch_shapes=list(scratch),
        compiler_params=pltpu.CompilerParams(vmem_limit_bytes=VMEM_LIMIT),
    )(*inputs)


def segment_of(index, lengths_ref):
    first = lengths_ref[0, 0]
    second = first + lengths_ref[0, 1]
    third = second + lengths_ref[0, 2]
    return (
        (index >= first).astype(jnp.int32)
        + (index >= second).astype(jnp.int32)
        + (index >= third).astype(jnp.int32)
    )


def pair_masks(columns_ref, rows_ref, lengths_ref, same_ref, hidden_ref):
    size = columns_ref.shape[0]
    shape = (size, size)
    key_id = lax.broadcasted_iota(jnp.int32, shape, 0)
    query_id = lax.broadcasted_iota(jnp.int32, shape, 1)
    key_column = lax.broadcasted_iota(jnp.int32, (size, 1), 0)
    query_row = lax.broadcasted_iota(jnp.int32, (1, size), 1)
    together = segment_of(key_column, lengths_ref) == segment_of(query_row, lengths_ref)
    seen = together & ((columns_ref[:, 3:4] > 0) | (key_id == query_id))
    same_ref[...] = (columns_ref[:, 2:3] == rows_ref[2:3, :]).astype(jnp.float32)
    hidden_ref[...] = jnp.where(seen, 0.0, masked_score)


def turn(values, cosine, sine):
    width = values.shape[1]
    lane = lax.broadcasted_iota(jnp.int32, values.shape, 1)
    other = jnp.where(
        lane % 64 < 32, pltpu.roll(values, width - 32, 1), pltpu.roll(values, 32, 1)
    )
    return values * cosine + other * sine


def head_lanes(values, head):
    lane = lax.broadcasted_iota(jnp.int32, values.shape, 1)
    return jnp.where((lane < 64) == (head == 0), values, jnp.zeros_like(values))


def project(input_ref, weight_refs, cosine_ref, sine_ref, out_ref, scale):
    width = weight_refs[0].shape[0]
    cosine = jnp.concatenate([cosine_ref[...]] * 2, axis=1)
    sine = jnp.concatenate([sine_ref[...]] * 2, axis=1)

    def one(i, carry):
        def columns(part):
            return pl.ds(pl.multiple_of(part * width + i * 256, 256), 256)

        at = pl.ds(pl.multiple_of(i * 256, 256), 256)
        query = matmul(input_ref[...], weight_refs[0][:, at])
        out_ref[:, columns(0)] = (turn(query, cosine, sine) * scale).astype(jnp.bfloat16)
        key = matmul(input_ref[...], weight_refs[1][:, at])
        out_ref[:, columns(1)] = turn(key, cosine, sine).astype(jnp.bfloat16)
        out_ref[:, columns(2)] = matmul(input_ref[...], weight_refs[2][:, at]).astype(
            jnp.bfloat16
        )
        return carry

    lax.fori_loop(0, width // 256, one, 0)


def attend_pair(pair, width, heads_ref, bias_ref, same_ref, hidden_ref, out_ref, log_ref):
    def columns(part):
        return pl.ds(pl.multiple_of(part * width + pair * 128, 128), 128)

    query, key, value = (heads_ref[:, columns(part)] for part in range(3))
    total = None
    for which in (0, 1):
        head = 2 * pair + which
        gap = bias_ref[0, head] - bias_ref[1, head]
        scores = matmul(head_lanes(key, which), query, 1, 1)
        scores = scores + same_ref[...] * gap + hidden_ref[...]
        top = jnp.max(scores, axis=0, keepdims=True)
        weights = jnp.exp(scores - top)
        weight_sum = jnp.sum(weights, axis=0, keepdims=True)
        log_ref[pl.ds(head, 1), :] = top + jnp.log(weight_sum)
        soft = (weights * (1.0 / weight_sum)).astype(jnp.bfloat16)
        part = matmul(head_lanes(value, which), soft, 0, 0)
        total = part if total is None else total + part
    out_ref[:, pl.ds(pl.multiple_of(pair * 128, 128), 128)] = total.T.astype(jnp.bfloat16)


def normed(values):
    factor = lax.rsqrt(jnp.mean(values * values, axis=-1, keepdims=True) + epsilon)
    return values * factor, factor


def forward_body(refs, between=None):
    (
        arrived_ref, columns_ref, rows_ref, lengths_ref, bias_ref, gain_ref,
        query_w_ref, key_w_ref, value_w_ref, cosine_ref, sine_ref,
        stream_ref, input_ref, heads_ref, out_ref, log_ref,
        same_ref, hidden_ref,
    ) = refs
    width = gain_ref.shape[1]
    scale = 1.0 / math.sqrt(64)
    chosen = pick_rows(columns_ref[:, 1:2], arrived_ref.shape[0])
    stream = matmul(chosen, arrived_ref[...])
    stream_ref[...] = stream.astype(jnp.bfloat16)
    input_ref[...] = (normed(stream)[0] * gain_ref[...]).astype(jnp.bfloat16)
    pair_masks(columns_ref, rows_ref, lengths_ref, same_ref, hidden_ref)
    weight_refs = (query_w_ref, key_w_ref, value_w_ref)
    project(input_ref, weight_refs, cosine_ref, sine_ref, heads_ref, scale)

    def one(pair, carry):
        if between is not None:
            between(pair)
        attend_pair(pair, width, heads_ref, bias_ref, same_ref, hidden_ref, out_ref, log_ref)
        return carry

    lax.fori_loop(0, width // 128, one, 0)


def fold_lanes(row):
    folded = row[:, 0:128]
    for i in range(1, row.shape[1] // 128):
        folded += row[:, i * 128 : (i + 1) * 128]
    return folded


def square_into(stats_ref, at, values, columns_ref):
    valid = (columns_ref[:, 3:4] > 0).astype(jnp.float32)
    across = jnp.sum(values * values * valid, axis=0, keepdims=True)
    stats_ref[at : at + 1, :] = fold_lanes(across)


def attend_back_pair(
    pair, width, scale, heads_ref, do_ref, bias_ref, log_ref, same_ref, hidden_ref, cosine_ref,
    sine_ref, grads_ref, bias_same_ref, bias_all_ref,
):
    half = jnp.bfloat16

    def columns(part):
        return pl.ds(pl.multiple_of(part * width + pair * 128, 128), 128)

    query, key, value = (heads_ref[:, columns(part)] for part in range(3))
    grad_out = do_ref[:, columns(0)]
    query_t = key_grad = value_grad = None
    for which in (0, 1):
        head = 2 * pair + which
        gap = bias_ref[0, head] - bias_ref[1, head]
        key_part = head_lanes(key, which)
        scores = matmul(key_part, query, 1, 1)
        scores = scores + same_ref[...] * gap + hidden_ref[...]
        soft = jnp.exp(scores - log_ref[pl.ds(head, 1), :])
        grad_soft = matmul(head_lanes(value, which), grad_out, 1, 1)
        inner = jnp.sum(soft * grad_soft, axis=0, keepdims=True)
        grad_scores = (soft * (grad_soft - inner)).astype(half)
        wide = grad_scores.astype(jnp.float32)
        bias_all_ref[pl.ds(head, 1), :] = jnp.sum(wide, axis=0, keepdims=True)
        bias_same_ref[pl.ds(head, 1), :] = jnp.sum(wide * same_ref[...], axis=0, keepdims=True)
        parts = (
            matmul(key_part, grad_scores, 0, 0),
            matmul(grad_scores, head_lanes(query, which)),
            matmul(soft.astype(half), head_lanes(grad_out, which)),
        )
        if which == 0:
            query_t, key_grad, value_grad = parts
        else:
            query_t, key_grad, value_grad = (
                query_t + parts[0],
                key_grad + parts[1],
                value_grad + parts[2],
            )
    cosine, sine = cosine_ref[...], -sine_ref[...]
    grads_ref[:, columns(0)] = (turn(query_t.T, cosine, sine) * scale).astype(half)
    grads_ref[:, columns(1)] = turn(key_grad, cosine, sine).astype(half)
    grads_ref[:, columns(2)] = value_grad.astype(half)


def feed_forward(refs, weights, gates_out, ups_out, hidden_out, scratch):
    columns_ref, rows_ref, gain_ref, stream_ref, attended_ref, out_w_ref = refs[:6]
    packed_ref, middle_ref, input_ref, stats_ref = refs[6:]
    (
        gate_buf, up_buf, down_buf, gates_buf, ups_buf, hidden_buf, mlp_ref,
        load_sems, store_sems,
    ) = scratch
    tile = gate_buf.shape[2]
    tiles = gates_out.shape[1] // tile
    half = jnp.bfloat16

    def at(i):
        return pl.ds(pl.multiple_of(i * tile, tile), tile)

    def loads(i):
        slot = lax.rem(i, 2)
        return [
            pltpu.make_async_copy(weights[0].at[:, at(i)], gate_buf.at[slot], load_sems.at[slot, 0]),
            pltpu.make_async_copy(weights[1].at[:, at(i)], up_buf.at[slot], load_sems.at[slot, 1]),
            pltpu.make_async_copy(weights[2].at[at(i)], down_buf.at[slot], load_sems.at[slot, 2]),
        ]

    def stores(i):
        slot = lax.rem(i, 2)
        return [
            pltpu.make_async_copy(gates_buf.at[slot], gates_out.at[:, at(i)], store_sems.at[slot, 0]),
            pltpu.make_async_copy(ups_buf.at[slot], ups_out.at[:, at(i)], store_sems.at[slot, 1]),
            pltpu.make_async_copy(
                hidden_buf.at[slot], hidden_out.at[:, at(i)], store_sems.at[slot, 2]
            ),
        ]

    for copy in loads(0):
        copy.start()
    stats_ref[...] = jnp.zeros_like(stats_ref)
    stream = stream_ref[...].astype(jnp.float32)
    square_into(stats_ref, 0, stream, columns_ref)
    attn_out = matmul(attended_ref[...], out_w_ref[...])
    square_into(stats_ref, 1, attn_out, columns_ref)
    middle = stream + attn_out
    square_into(stats_ref, 2, middle, columns_ref)
    middle_ref[...] = middle
    input_ref[...] = (normed(middle)[0] * gain_ref[...]).astype(half)
    mlp_ref[...] = jnp.zeros_like(mlp_ref)

    def one(i, carry):
        slot = lax.rem(i, 2)
        for copy in loads(i):
            copy.wait()

        @pl.when(i + 1 < tiles)
        def _():
            for copy in loads(i + 1):
                copy.start()

        @pl.when(i >= 2)
        def _():
            for copy in stores(i - 2):
                copy.wait()

        gate = matmul(input_ref[...], gate_buf[slot])
        up = matmul(input_ref[...], up_buf[slot])
        gates_buf[slot] = gate
        ups_buf[slot] = up
        hidden = (gate * jax.nn.sigmoid(gate) * up).astype(half)
        hidden_buf[slot] = hidden
        for copy in stores(i):
            copy.start()
        mlp_ref[...] += matmul(hidden, down_buf[slot])
        return carry

    lax.fori_loop(0, tiles, one, 0)
    valid = (columns_ref[:, 3:4] > 0).astype(jnp.float32)
    mlp_out = mlp_ref[...]
    result = middle_ref[...] + mlp_out
    placed = place_rows(rows_ref[1:2, :], packed_ref.shape[0])
    packed_ref[...] = matmul(placed, result.astype(half)).astype(half)
    square_into(stats_ref, 3, mlp_out, columns_ref)
    square_into(stats_ref, 4, result, columns_ref)
    lane = lax.broadcasted_iota(jnp.int32, (valid.shape[0], 128), 1)
    stats_ref[5:6, :] = jnp.sum(jnp.where(lane == 0, valid, 0.0), axis=0, keepdims=True)
    for i in (tiles - 2, tiles - 1):
        for copy in stores(i):
            copy.wait()


def forward_gather_kernel(shards, lents, swap_count, late, compute_counts, *refs):
    ins, outs = compute_counts
    total = len(lents) + swap_count
    in_refs, refs = refs[: ins + total], refs[ins + total :]
    out_refs, refs = refs[: outs + total], refs[outs + total :]
    masks, out_w_buf, out_w_sem, feed_scratch, scratch = (
        refs[:2], refs[2], refs[3], refs[4:13], refs[13:],
    )
    work = GatherAll(
        Spot(shards), lents, swap_count, in_refs[ins:], out_refs[outs:], scratch, late
    )
    work.start()
    *attend_ins, gain_mlp_ref = in_refs[:ins]
    pairs = attend_ins[5].shape[1] // 128
    attend_outs, feed_outs = out_refs[:5], out_refs[5:outs]
    forward_body((*attend_ins, *attend_outs, *masks), lambda pair: work.steps(pair, pairs))
    work.finish_gathers()
    full_refs = out_refs[outs:]
    copy = pltpu.make_async_copy(full_refs[0], out_w_buf, out_w_sem)
    copy.start()
    copy.wait()
    gates_out, ups_out, hidden_out, *feed_outs = feed_outs
    feed_forward(
        (
            attend_ins[1], attend_ins[2], gain_mlp_ref, attend_outs[0], attend_outs[3], out_w_buf,
            *feed_outs,
        ),
        full_refs[1:4], gates_out, ups_out, hidden_out, feed_scratch,
    )
    for swap in work.swaps:
        swap.finish()


def forward_gather_call(
    shards, inputs, spaces, out_shape, out_specs, pieces, lents, sent, late, collective_id
):
    anywhere = pl.BlockSpec(memory_space=pl.ANY)
    tokens, width = out_shape[0].shape
    tile = 512
    half, full = jnp.bfloat16, jnp.float32
    counts = (len(inputs), len(out_shape))
    comm = len(pieces) + len(sent)
    results = pl.pallas_call(
        functools.partial(forward_gather_kernel, shards, lents, len(sent), late, counts),
        out_shape=[*out_shape, *gather_shapes(shards, pieces, sent, [])],
        in_specs=spaces + [anywhere] * comm,
        out_specs=out_specs + [anywhere] * comm,
        scratch_shapes=[
            pltpu.VMEM((tokens, tokens), full),
            pltpu.VMEM((tokens, tokens), full),
            pltpu.VMEM((width, width), half),
            DMA,
            pltpu.VMEM((2, width, tile), half),
            pltpu.VMEM((2, width, tile), half),
            pltpu.VMEM((2, tile, width), half),
            pltpu.VMEM((2, tokens, tile), full),
            pltpu.VMEM((2, tokens, tile), full),
            pltpu.VMEM((2, tokens, tile), half),
            pltpu.VMEM((tokens, width), full),
            DMA((2, 3)),
            DMA((2, 3)),
            *GatherAll.scratch(shards, len(pieces), len(sent)),
        ],
        compiler_params=pltpu.CompilerParams(
            collective_id=collective_id, has_side_effects=True, vmem_limit_bytes=VMEM_LIMIT
        ),
    )(*inputs, *pieces, *sent)
    first = len(out_shape)
    second = first + len(pieces)
    return results[:first], results[first:second], results[second:]


def input_grad_kernel(shards, lent, *refs):
    (
        columns_ref, rows_ref, lengths_ref, bias_ref, gain_mlp_ref, gain_attn_ref, middle_ref,
        out_w_ref, arrived_ref, heads_ref, log_ref, cosine_ref, sine_ref, stream_ref,
        query_w_ref, key_w_ref, value_w_ref, packed_out_ref, gates_ref, ups_ref, rows_mlp_ref,
        gate_w_ref, up_w_ref, down_w_ref,
        dy_ref, grads_ref, packed_ref, stats_ref, grad_down_ref,
        grad_gate_ref, grad_up_ref, home_ref, partial_ref,
        gates_buf, ups_buf, gate_buf, up_buf, down_buf, grad_gate_buf, grad_up_buf,
        back_ref, dh_ref, do_ref, same_ref, hidden_ref, bias_same_ref, bias_all_ref,
        load_sems, store_sems, weight_sems, send_sems, recv_sems, own_sem,
    ) = refs[:53]
    spot = Spot(shards)
    swap = Swap(spot, packed_out_ref, home_ref, (send_sems, recv_sems), own_sem)
    reduce = Reduce(spot, lent, partial_ref, grad_down_ref, refs[53:])
    tile = gate_buf.shape[2]
    tiles = gates_ref.shape[1] // tile
    width = gain_attn_ref.shape[1]
    half = jnp.bfloat16

    def at(i):
        return pl.ds(pl.multiple_of(i * tile, tile), tile)

    def loads(i):
        slot = lax.rem(i, 2)
        pairs = [
            (gates_ref.at[:, at(i)], gates_buf),
            (ups_ref.at[:, at(i)], ups_buf),
            (gate_w_ref.at[:, at(i)], gate_buf),
            (up_w_ref.at[:, at(i)], up_buf),
            (down_w_ref.at[at(i)], down_buf),
        ]
        return [
            pltpu.make_async_copy(source, buffer.at[slot], load_sems.at[slot, j])
            for j, (source, buffer) in enumerate(pairs)
        ]

    def stores(i):
        slot = lax.rem(i, 2)
        pairs = [(grad_gate_buf, grad_gate_ref), (grad_up_buf, grad_up_ref)]
        return [
            pltpu.make_async_copy(buffer.at[slot], target.at[:, at(i)], store_sems.at[slot, j])
            for j, (buffer, target) in enumerate(pairs)
        ]

    def row_loads(i):
        slot = lax.rem(i, 2)
        return [
            pltpu.make_async_copy(
                rows_mlp_ref.at[:, at(i)], grad_gate_buf.at[slot], load_sems.at[slot, 0]
            )
        ]

    def row_stores(i):
        slot = lax.rem(i, 2)
        return [
            pltpu.make_async_copy(
                down_buf.at[slot], partial_ref.at[at(i)], store_sems.at[slot, 0]
            )
        ]

    pairs = width // 128
    slots = tiles + pairs
    steps = spot.half + 1

    def reduce_steps(slot):
        def one(step, carry):
            reduce.step(step)
            return carry

        lax.fori_loop(slot * steps // slots, (slot + 1) * steps // slots, one, 0)

    greet(spot)
    swap.start(0, tiles // 2)
    for copy in row_loads(0):
        copy.start()
    chosen = pick_rows(columns_ref[:, 1:2], arrived_ref.shape[0])
    dy_ref[...] = matmul(chosen, arrived_ref[...]).astype(half)

    def rows_step(i, carry):
        slot = lax.rem(i, 2)
        for copy in row_loads(i):
            copy.wait()

        @pl.when(i + 1 < tiles)
        def _():
            for copy in row_loads(i + 1):
                copy.start()

        @pl.when(i >= 2)
        def _():
            for copy in row_stores(i - 2):
                copy.wait()

        down_buf[slot] = matmul(grad_gate_buf[slot], dy_ref[...], 0, 0).astype(half)
        for copy in row_stores(i):
            copy.start()
        return carry

    lax.fori_loop(0, tiles, rows_step, 0)
    for i in (tiles - 2, tiles - 1):
        for copy in row_stores(i):
            copy.wait()
    for copy in loads(0):
        copy.start()

    def begin(item, carry):
        reduce.start(item)
        return carry

    lax.fori_loop(0, spot.chips, begin, 0)
    back_ref[...] = jnp.zeros_like(back_ref)
    pair_masks(columns_ref, rows_ref, lengths_ref, same_ref, hidden_ref)
    reduce.far_step(0)

    def one(i, carry):
        slot = lax.rem(i, 2)

        @pl.when(i < tiles // 2 - 1)
        def _():
            swap.start(i + 1, tiles // 2)

        reduce_steps(i)
        for copy in loads(i):
            copy.wait()

        @pl.when(i + 1 < tiles)
        def _():
            for copy in loads(i + 1):
                copy.start()

        @pl.when(i >= 2)
        def _():
            for copy in stores(i - 2):
                copy.wait()

        gate, up = gates_buf[slot], ups_buf[slot]
        grad_hidden = matmul(dy_ref[...], down_buf[slot], 1, 1)
        sigmoid = jax.nn.sigmoid(gate)
        grad_gate = (grad_hidden * up * sigmoid * (1.0 + gate * (1.0 - sigmoid))).astype(half)
        grad_up = (grad_hidden * gate * sigmoid).astype(half)
        grad_gate_buf[slot] = grad_gate
        grad_up_buf[slot] = grad_up
        for copy in stores(i):
            copy.start()
        back_ref[...] += matmul(grad_gate, gate_buf[slot], 1, 1) + matmul(
            grad_up, up_buf[slot], 1, 1
        )
        return carry

    lax.fori_loop(0, tiles, one, 0)
    stats_ref[...] = jnp.zeros_like(stats_ref)

    def through_norm(values, grad, gain_ref, first):
        entry, factor = normed(values)
        gain_grad = jnp.sum(grad * entry, axis=0, keepdims=True)
        for i in range(width // 128):
            stats_ref[first + i : first + i + 1, :] = gain_grad[:, i * 128 : (i + 1) * 128]
        scaled = grad * gain_ref[...]
        inner = jnp.mean(scaled * entry, axis=-1, keepdims=True)
        return factor * (scaled - entry * inner)

    dh = dy_ref[...].astype(jnp.float32) + through_norm(
        middle_ref[...], back_ref[...], gain_mlp_ref, 0
    )
    dh_ref[...] = dh
    branch = dh.astype(half)
    grads_ref[:, pl.ds(3 * width, width)] = branch
    do_ref[...] = matmul(branch, out_w_ref[...], 1, 1).astype(half)
    scale = 1.0 / math.sqrt(64)
    for i in (tiles - 2, tiles - 1):
        for copy in stores(i):
            copy.wait()
    halves = [pl.ds(0, tile), pl.ds(tile, tile)]

    def weight_loads(source, buffer, which):
        return [
            pltpu.make_async_copy(source.at[:, columns], buffer.at[j], weight_sems.at[which, j])
            for j, columns in enumerate(halves)
        ]

    for copy in weight_loads(query_w_ref, gate_buf, 0) + weight_loads(key_w_ref, up_buf, 1):
        copy.start()

    def two(pair, carry):
        reduce_steps(tiles + pair)
        attend_back_pair(
            pair, width, scale, heads_ref, do_ref, bias_ref, log_ref, same_ref, hidden_ref,
            cosine_ref, sine_ref, grads_ref, bias_same_ref, bias_all_ref,
        )
        return carry

    lax.fori_loop(0, width // 128, two, 0)
    heads = bias_all_ref.shape[0]
    lane = lax.broadcasted_iota(jnp.int32, (heads, 128), 1)
    row = lax.broadcasted_iota(jnp.int32, (heads, 128), 0)
    same = jnp.sum(bias_same_ref[...], axis=1, keepdims=True)
    other = jnp.sum(bias_all_ref[...], axis=1, keepdims=True) - same
    stats_ref[16:17, :] = jnp.sum(
        jnp.where(lane == row, same, 0.0) + jnp.where(lane == row + heads, other, 0.0),
        axis=0,
        keepdims=True,
    )
    def through(buffer, first):
        return sum(
            matmul(grads_ref[:, pl.ds(first + j * tile, tile)], buffer[j], 1, 1) for j in (0, 1)
        )

    for copy in weight_loads(query_w_ref, gate_buf, 0):
        copy.wait()
    back_ref[...] = through(gate_buf, 0)
    for copy in weight_loads(value_w_ref, gate_buf, 0):
        copy.start()
    for copy in weight_loads(key_w_ref, up_buf, 1):
        copy.wait()
    back_ref[...] += through(up_buf, width)
    for copy in weight_loads(value_w_ref, gate_buf, 0):
        copy.wait()
    back_ref[...] += through(gate_buf, 2 * width)
    grad_stream = dh_ref[...] + through_norm(
        stream_ref[...].astype(jnp.float32), back_ref[...], gain_attn_ref, 8
    )
    placed = place_rows(rows_ref[1:2, :], packed_ref.shape[0])
    packed_ref[...] = matmul(placed, grad_stream.astype(half)).astype(half)
    swap.finish()
    reduce.finish()


def input_grad_call(shards, inputs, spaces, far_inputs, lent, collective_id):
    anywhere = pl.BlockSpec(memory_space=pl.ANY)
    inside = pl.BlockSpec(memory_space=pltpu.VMEM)
    packed, gates = far_inputs[3], far_inputs[4]
    tokens, hidden = gates.shape
    width = packed.shape[1]
    heads = inputs[10].shape[0]
    tile = 512
    assert 2 * tile == width
    half, full = jnp.bfloat16, jnp.float32
    vmem, shape = pltpu.VMEM, jax.ShapeDtypeStruct
    return pl.pallas_call(
        functools.partial(input_grad_kernel, shards, lent),
        out_shape=[
            shape((tokens, width), half),
            shape((tokens, 4 * width), half),
            shape(packed.shape, half),
            shape((24, 128), full),
            shape((hidden // shards, width), full),
            shape((tokens, hidden), half),
            shape((tokens, hidden), half),
            shape(packed.shape, half),
            shape((hidden, width), half),
        ],
        in_specs=[*spaces, *[anywhere] * len(far_inputs)],
        out_specs=[inside] * 5 + [anywhere] * 4,
        scratch_shapes=[
            vmem((2, tokens, tile), full),
            vmem((2, tokens, tile), full),
            vmem((2, width, tile), half),
            vmem((2, width, tile), half),
            vmem((2, tile, width), half),
            vmem((2, tokens, tile), half),
            vmem((2, tokens, tile), half),
            vmem((tokens, width), full),
            vmem((tokens, width), full),
            vmem((tokens, width), half),
            vmem((tokens, tokens), full),
            vmem((tokens, tokens), full),
            vmem((heads, tokens), full),
            vmem((heads, tokens), full),
            DMA((2, 5)),
            DMA((2, 2)),
            DMA((2, 2)),
            DMA((shards,)),
            DMA((shards,)),
            DMA,
            *Reduce.scratch(shards, lent, hidden // shards, width),
        ],
        compiler_params=pltpu.CompilerParams(
            collective_id=collective_id, has_side_effects=True, vmem_limit_bytes=VMEM_LIMIT
        ),
    )(*inputs, *far_inputs)


def weight_grad_kernel(shards, lents, *refs):
    (
        columns_ref, input_attn_ref, attended_ref, input_mlp_ref, stats_forward_ref,
        stats_back_ref, home_out_ref, packed_ref, gate_ref, up_ref, entry_ref,
        grad_gate_ref, grad_up_ref, grad_in_ref, output_ref, input_grad_ref, sums_ref,
    ) = refs[:17]
    partials = refs[17:20]
    (
        attn_t_ref, attended_t_ref, mlp_t_ref, home_ref, stats_ref, tile_buf, part_buf,
        load_sems, store_sems, send_sems, recv_sems, own_sem,
    ) = refs[20:32]
    tally_refs, refs = refs[32:40], refs[40:]
    half, full = jnp.bfloat16, jnp.float32
    spot = Spot(shards)
    swap = Swap(spot, packed_ref, home_ref, (send_sems, recv_sems), own_sem)
    tally = Tally(spot, stats_ref, sums_ref, tally_refs)
    outputs = (grad_gate_ref, grad_up_ref, grad_in_ref)
    reduces = [
        Reduce(spot, lents[g], partials[g], outputs[g], refs[19 * g : 19 * g + 19])
        for g in range(3)
    ]
    steps = spot.half + 1
    parts = 5
    tile = tile_buf.shape[2]
    tiles = gate_ref.shape[1] // tile

    def at(i):
        return pl.ds(pl.multiple_of(i * tile, tile), tile)

    def product(source, lefts, partial, reduce):
        def load(i):
            slot = lax.rem(i, 2)
            return pltpu.make_async_copy(
                source.at[:, at(i)], tile_buf.at[slot], load_sems.at[slot]
            )

        def store(i):
            slot = lax.rem(i, 2)
            return pltpu.make_async_copy(
                part_buf.at[slot], partial.at[:, at(i)], store_sems.at[slot]
            )

        load(0).start()
        first = 0
        for left, count in lefts:

            def one(i, carry, left=left):
                slot = lax.rem(i, 2)
                load(i).wait()

                @pl.when(i + 1 < tiles)
                def _():
                    load(i + 1).start()

                @pl.when(i >= 2)
                def _():
                    store(i - 2).wait()

                part_buf[slot] = matmul(left[...], tile_buf[slot]).astype(half)
                store(i).start()
                return carry

            lax.fori_loop(first, first + count, one, 0)
            first += count
        for i in (tiles - 2, tiles - 1):
            store(i).wait()

        def begin(item, carry):
            reduce.start(item)
            return carry

        lax.fori_loop(0, spot.chips, begin, 0)
        reduce.far_step(0)

    greet(spot)
    swap.start(0, parts)
    stats_ref[0:8, :] = stats_forward_ref[...]
    stats_ref[8:32, :] = stats_back_ref[...]
    tally.start()
    mlp_t_ref[...] = input_mlp_ref[...].astype(full).T.astype(half)
    product(gate_ref, [(mlp_t_ref, tiles)], partials[0], reduces[0])
    swap.start(1, parts)
    product(up_ref, [(mlp_t_ref, tiles)], partials[1], reduces[1])
    swap.start(2, parts)
    chosen = pick_rows(columns_ref[:, 0:1], home_ref.shape[0])

    def ticks(tick, carry):
        @pl.when(tick < steps)
        def _():
            reduces[0].step(tick)

        @pl.when(tick < 2)
        def _():
            swap.start(3 + tick, parts)

        @pl.when(tick == 0)
        def _():
            attn_t_ref[...] = input_attn_ref[...].astype(full).T.astype(half)
            attended_t_ref[...] = attended_ref[...].astype(full).T.astype(half)
            product(
                entry_ref,
                [(attn_t_ref, tiles - tiles // 4), (attended_t_ref, tiles // 4)],
                partials[2],
                reduces[2],
            )

        @pl.when((tick > 0) & (tick < steps + 1))
        def _():
            reduces[1].step(tick - 1)

        @pl.when(tick == 1)
        def _():
            output_ref[...] = matmul(chosen, home_out_ref[...]).astype(half)
            tally.middle()

        @pl.when(tick > 1)
        def _():
            reduces[2].step(tick - 2)

        return carry

    lax.fori_loop(0, steps + 2, ticks, 0)
    swap.finish()
    input_grad_ref[...] = matmul(chosen, home_ref[...]).astype(half)
    tally.finish()
    for reduce in reduces:
        reduce.finish()


def weight_grad_call(shards, inputs, far_inputs, lents, collective_id):
    tile = 512
    packed, hidden = far_inputs[0], far_inputs[1].shape[1]
    tokens, width = inputs[1].shape
    assert hidden == 4 * width
    half, full = jnp.bfloat16, jnp.float32
    shape = jax.ShapeDtypeStruct
    anywhere = pl.BlockSpec(memory_space=pl.ANY)
    inside = pl.BlockSpec(memory_space=pltpu.VMEM)
    scratch = []
    for lent in lents:
        scratch += Reduce.scratch(shards, lent, width // shards, hidden)
    results = pl.pallas_call(
        functools.partial(weight_grad_kernel, shards, lents),
        out_shape=[
            *[shape((width // shards, hidden), full)] * 3,
            shape((tokens, width), half),
            shape((tokens, width), half),
            shape((32, 128), full),
            *[shape((width, hidden), half)] * 3,
        ],
        in_specs=[inside] * len(inputs) + [anywhere] * len(far_inputs),
        out_specs=[inside] * 6 + [anywhere] * 3,
        scratch_shapes=[
            *[pltpu.VMEM((width, tokens), half)] * 3,
            pltpu.VMEM(packed.shape, half),
            pltpu.VMEM((32, 128), full),
            pltpu.VMEM((2, tokens, tile), half),
            pltpu.VMEM((2, width, tile), half),
            DMA((2,)),
            DMA((2,)),
            DMA((shards,)),
            DMA((shards,)),
            DMA,
            *Tally.scratch(shards, (32, 128)),
            *scratch,
        ],
        compiler_params=pltpu.CompilerParams(
            collective_id=collective_id, has_side_effects=True, vmem_limit_bytes=VMEM_LIMIT
        ),
    )(*inputs, *far_inputs)
    return results[:6]


def on_device(
    tokens,
    cotangent,
    send_slot,
    recv_slot,
    lengths,
    variate,
    valid_mask,
    norm_attn,
    w_query,
    w_key,
    w_value,
    w_out,
    variate_bias,
    norm_mlp,
    w_gate,
    w_up,
    w_down,
):
    shards = lax.axis_size("shard")
    tok_rows, width = tokens.shape
    slot_total = 2 * tok_rows
    heads = variate_bias.shape[1]
    half, full = jnp.bfloat16, jnp.float32
    share = width // shards
    indices = jnp.stack([send_slot, recv_slot, variate, valid_mask])
    rows = jnp.concatenate([indices, jnp.zeros_like(indices)])
    columns = rows.T
    _, position = layout(lengths[0], tok_rows)
    cosine, sine = angle_tables(position, width // heads)
    cosine = jnp.concatenate([cosine] * 4, axis=1)
    sine = jnp.concatenate([-sine, sine] * 2, axis=1)
    gains = jnp.stack([norm_attn, norm_mlp]).astype(full)
    gains = jnp.pad(gains, ((0, 6), (0, 128 - share)))
    shape = jax.ShapeDtypeStruct
    packed_shape = shape((slot_total, width), half)
    token_shape = shape((tok_rows, width), half)
    out_tokens, out_cotangent = local_call(
        pack_kernel, [packed_shape] * 2, [rows, tokens, cotangent]
    )
    full_in, (arrived_tokens,), (gains,) = gather_call(
        shards,
        [w_query, w_key, w_value],
        (4, 4, 4),
        [out_tokens],
        [gains],
        1,
    )
    gains = gains.reshape(shards, 8, 128)
    gain_attn = gains[:, 0, :share].reshape(1, width)
    gain_mlp = gains[:, 1, :share].reshape(1, width)
    inside = pl.BlockSpec(memory_space=pltpu.VMEM)
    scalar = pl.BlockSpec(memory_space=pltpu.SMEM)
    anywhere = pl.BlockSpec(memory_space=pl.ANY)
    hidden = w_gate.shape[1]
    (
        (
            stream, input_attn, head_rows, attended, logs,
            gates, ups, hidden_rows, packed, middle, input_mlp, stats_forward,
        ),
        (full_out, full_gate, full_up, full_down),
        (arrived_grads,),
    ) = forward_gather_call(
        shards,
        [
            arrived_tokens, columns, rows, lengths, variate_bias, gain_attn, *full_in,
            cosine, sine, gain_mlp,
        ],
        [inside] * 3 + [scalar] * 2 + [inside] * 7,
        [
            token_shape,
            token_shape,
            shape((tok_rows, 3 * width), half),
            token_shape,
            shape((heads, tok_rows), full),
            shape((tok_rows, hidden), full),
            shape((tok_rows, hidden), full),
            shape((tok_rows, hidden), half),
            packed_shape,
            shape((tok_rows, width), full),
            token_shape,
            shape((8, 128), full),
        ],
        [inside] * 5 + [anywhere] * 3 + [inside] * 4,
        [w_out, w_gate, w_up, w_down],
        (4, 4, 4, 2),
        [out_cotangent],
        False,
        2,
    )
    (
        _, entry_grads, packed_grad, stats_back, grad_down, grad_gates, grad_ups, home_out, _,
    ) = input_grad_call(
        shards,
        [
            columns, rows, lengths, variate_bias, gain_mlp, gain_attn, middle, full_out,
            arrived_grads, head_rows, logs, cosine, sine, stream,
        ],
        [inside] * 2 + [scalar] * 2 + [inside] * 10,
        [*full_in, packed, gates, ups, hidden_rows, full_gate, full_up, full_down],
        2,
        3,
    )
    grad_gate, grad_up, grad_in, output, input_grad, sums = weight_grad_call(
        shards,
        [columns, input_attn, attended, input_mlp, stats_forward, stats_back, home_out],
        [packed_grad, grad_gates, grad_ups, entry_grads],
        (2, 2, 2),
        4,
    )
    grad_query, grad_key, grad_value, grad_out = (
        grad_in[:, i * width : (i + 1) * width] for i in range(4)
    )
    squares = jnp.sum(sums[0:6], axis=1)
    root_means = jnp.sqrt(squares[:5] / (squares[5] * width))
    share_start = lax.axis_index("shard") * share
    grad_norm_mlp = lax.dynamic_slice_in_dim(sums[8:16].reshape(-1), share_start, share)
    grad_norm_attn = lax.dynamic_slice_in_dim(sums[16:24].reshape(-1), share_start, share)
    bias_grads = sums[24, : 2 * heads].reshape(2, heads)
    return (
        output,
        input_grad,
        grad_norm_attn,
        grad_query,
        grad_key,
        grad_value,
        grad_out,
        bias_grads,
        grad_norm_mlp,
        grad_gate,
        grad_up,
        grad_down,
        root_means,
    )


def solution(mesh):
    in_specs = (
        P(("rep", "shard"), None),
        P(("rep", "shard"), None),
        P(("rep", "shard")),
        P(("rep", "shard")),
        P(("rep", "shard"), None),
        P(("rep", "shard")),
        P(("rep", "shard")),
        P("shard"),
        P("shard", None),
        P("shard", None),
        P("shard", None),
        P("shard", None),
        P(),
        P("shard"),
        P("shard", None),
        P("shard", None),
        P("shard", None),
    )
    out_specs = (
        P(("rep", "shard"), None),
        P(("rep", "shard"), None),
        P("shard"),
        P("shard", None),
        P("shard", None),
        P("shard", None),
        P("shard", None),
        P(),
        P("shard"),
        P("shard", None),
        P("shard", None),
        P("shard", None),
        P(),
    )
    return jax.shard_map(
        on_device, mesh=mesh, in_specs=in_specs, out_specs=out_specs, check_vma=False
    )
```

```python
import functools
import math

import jax
import jax.numpy as jnp
from jax import lax
from jax.experimental import pallas as pl
from jax.experimental.pallas import tpu as pltpu
from jax.sharding import PartitionSpec as P

MESH = pl.DeviceIdType.MESH
DMA = pltpu.SemaphoreType.DMA
epsilon = 1e-06
masked_score = -1e30
VMEM_LIMIT = 62 << 20


def angle_tables(position, head_dim):
    half_dim = head_dim // 2
    inverse_freq = 1.0 / 10000.0 ** (jnp.arange(half_dim, dtype=jnp.float32) / half_dim)
    theta_angle = position.astype(jnp.float32)[:, None] * inverse_freq[None, :]
    return (jnp.cos(theta_angle), jnp.sin(theta_angle))


def layout(lengths_row, tok_rows):
    slot_ids = jnp.arange(tok_rows, dtype=jnp.int32)
    seq_ends = jnp.cumsum(lengths_row)
    segment = jnp.sum((slot_ids[:, None] >= seq_ends[None, :]).astype(jnp.int32), axis=1)
    starts = seq_ends - lengths_row
    chosen = segment[:, None] == jnp.arange(lengths_row.shape[0], dtype=jnp.int32)[None, :]
    begins = jnp.sum(jnp.where(chosen, starts[None, :], 0), axis=1)
    return (segment, slot_ids - begins)


def ring_place(chip, chips):
    return jnp.where(chip % 2 == 0, chip // 2, chips - 1 - chip // 2)


def ring_chip(place, chips):
    wrapped = lax.rem(place + 2 * chips, chips)
    return jnp.where(wrapped < chips // 2, 2 * wrapped, 2 * (chips - 1 - wrapped) + 1)


class Spot:
    def __init__(self, shards):
        self.shards = shards
        self.chips = shards // 2
        self.half = self.chips // 2
        self.rep = lax.axis_index("rep")
        self.shard = lax.axis_index("shard")
        self.core = lax.rem(self.shard, 2)
        self.place = ring_place(self.shard // 2, self.chips)
        self.sibling = self.shard + 1 - 2 * self.core

    def block(self, place, core=None):
        return 2 * ring_chip(place, self.chips) + (self.core if core is None else core)

    def along(self, way, distance):
        return self.place - distance if way == 0 else self.place + distance

    def ahead(self, way):
        return (self.rep, self.block(self.along(way, -1)))


def greet(spot):
    barrier = pltpu.get_barrier_semaphore()

    def peer(k, carry):
        target = lax.rem(spot.shard + k, spot.shards)
        pl.semaphore_signal(barrier, inc=1, device_id=(spot.rep, target), device_id_type=MESH)
        return carry

    lax.fori_loop(1, spot.shards, peer, 0)
    pl.semaphore_signal(
        barrier, inc=1, device_id=(1 - spot.rep, spot.shard), device_id_type=MESH
    )
    pl.semaphore_wait(barrier, spot.shards)


def remote(src, dst, sems, at, target):
    return pltpu.make_async_remote_copy(
        src_ref=src,
        dst_ref=dst,
        send_sem=sems[0].at[at],
        recv_sem=sems[1].at[at],
        device_id=target,
        device_id_type=MESH,
    )


class Swap:
    def __init__(self, spot, source, arrived, sems, own_sem):
        self.spot, self.sems = spot, sems
        self.source, self.arrived = source, arrived
        self.capacity = arrived.shape[0] // spot.shards
        self.own = pltpu.make_async_copy(
            self.part(spot.shard), arrived.at[self.rows(spot.shard)], own_sem
        )

    def rows(self, shard):
        return pl.ds(pl.multiple_of(shard * self.capacity, 8), self.capacity)

    def part(self, shard):
        if self.source.shape[0] == self.capacity:
            return self.source
        return self.source.at[self.rows(shard)]

    def copy(self, k):
        spot = self.spot
        target = lax.rem(spot.shard + 7 * k, spot.shards)
        return remote(
            self.part(target),
            self.arrived.at[self.rows(spot.shard)],
            self.sems,
            (k,),
            (spot.rep, target),
        )

    def start(self, slot, slots):
        size = -(-self.spot.shards // slots)

        def one(k, carry):
            @pl.when(k == 0)
            def _():
                self.own.start()

            @pl.when(k > 0)
            def _():
                self.copy(k).start()

            return carry

        first = jnp.minimum(slot * size, self.spot.shards)
        lax.fori_loop(first, jnp.minimum(first + size, self.spot.shards), one, 0)

    def finish(self):
        def one(k, carry):
            self.copy(k).wait()
            return carry

        lax.fori_loop(1, self.spot.shards, one, 0)
        self.own.wait()


class Gather:
    def __init__(self, spot, lent, shard_ref, full_ref, sems):
        self.spot, self.lent, self.shard_ref, self.full_ref = spot, lent, shard_ref, full_ref
        self.rows = shard_ref.shape[0]
        self.unit = shard_ref.shape[1] // 8
        self.kept = 8 - lent
        self.ring_sems, self.near_sems, self.far_sems, self.far_near_sems = (
            sems[0:2],
            sems[2:4],
            sems[4:6],
            sems[6:8],
        )
        self.whole_sems, self.own_sem = sems[8:10], sems[10]

    def span(self, way, short):
        first, count = self.lent * self.spot.rep, self.kept
        if short:
            first, count = first + way * (count // 2), count // 2
        return pl.ds(pl.multiple_of(first * self.unit, 128), count * self.unit)

    def region(self, way, hop, short):
        block = self.spot.block(self.spot.along(way, hop))
        return self.full_ref.at[pl.ds(block * self.rows, self.rows), self.span(way, short)]

    def ring(self, way, hop, short, source=None):
        region = self.region(way, hop, short)
        return remote(
            region if source is None else source,
            region,
            self.ring_sems,
            (way, hop),
            self.spot.ahead(way),
        )

    def near(self, way, hop, short):
        region = self.region(way, hop + 1, short)
        target = (self.spot.rep, self.spot.sibling)
        return remote(region, region, self.near_sems, (way, hop), target)

    def lent_region(self, way, hop, owner):
        block = self.spot.block(self.spot.along(way, hop + 1))
        columns = pl.ds(
            pl.multiple_of(self.kept * owner * self.unit, 128), self.lent * self.unit
        )
        return self.full_ref.at[pl.ds(block * self.rows, self.rows), columns]

    def far(self, way, hop):
        region = self.lent_region(way, hop, self.spot.rep)
        target = (1 - self.spot.rep, self.spot.shard)
        return remote(region, region, self.far_sems, (way, hop), target)

    def far_near(self, way, hop):
        region = self.lent_region(way, hop, 1 - self.spot.rep)
        target = (self.spot.rep, self.spot.sibling)
        return remote(region, region, self.far_near_sems, (way, hop), target)

    def own(self):
        spot = self.spot
        mine = self.full_ref.at[pl.ds(spot.shard * self.rows, self.rows)]
        whole = remote(self.shard_ref, mine, self.whole_sems, (0,), (spot.rep, spot.sibling))
        return whole, pltpu.make_async_copy(self.shard_ref, mine, self.own_sem)

    def start(self):
        for way in (0, 1):
            self.ring(way, 0, False, self.shard_ref.at[:, self.span(way, False)]).start()
        for copy in self.own():
            copy.start()

    def step(self, hop):
        final = self.spot.half - 1

        @pl.when(hop < final)
        def _():
            for way in (0, 1):
                self.ring(way, hop, False).wait_recv()

                @pl.when(hop < final - 1)
                def _():
                    self.ring(way, hop + 1, False).start()

                @pl.when(hop == final - 1)
                def _():
                    self.ring(way, hop + 1, True).start()

            for way in (0, 1):
                self.far(way, hop).start()
                self.near(way, hop, False).start()

        @pl.when(hop == final)
        def _():
            for way in (0, 1):
                self.ring(way, hop, True).wait_recv()
            self.far(0, hop).start()
            for way in (0, 1):
                self.near(way, hop, True).start()

        @pl.when(hop > 0)
        def _():
            for way in (0, 1):
                self.relay(way, hop - 1)

    def relay(self, way, hop):
        self.far(way, hop).wait_recv()
        self.far_near(way, hop).start()

    def finish(self):
        final = self.spot.half - 1
        for copy in self.own():
            copy.wait()

        def one(hop, carry):
            for way in (0, 1):
                self.ring(way, hop, False).wait_send()
                self.near(way, hop, False).wait()
                self.far(way, hop).wait_send()
                self.far_near(way, hop).wait()
            return carry

        lax.fori_loop(0, final, one, 0)
        for way in (0, 1):
            self.ring(way, final, True).wait_send()
            self.near(way, final, True).wait()
        self.far(0, final).wait_send()
        self.far_near(0, final).wait()

    @staticmethod
    def scratch(half):
        return [DMA((2, half))] * 8 + [DMA((1,))] * 2 + [DMA]


class GatherAll:
    def __init__(self, spot, lents, swap_count, inputs, outputs, scratch):
        count = len(lents)
        self.spot = spot
        self.gathers = [
            Gather(spot, lents[g], inputs[g], outputs[g], scratch[11 * g : 11 * g + 11])
            for g in range(count)
        ]
        scratch = scratch[11 * count :]
        self.swaps = [
            Swap(
                spot,
                inputs[count + i],
                outputs[count + i],
                scratch[3 * i : 3 * i + 2],
                scratch[3 * i + 2],
            )
            for i in range(swap_count)
        ]

    def start(self):
        greet(self.spot)
        for gather in self.gathers:
            gather.start()

    def exchange(self, slot, slots):
        for swap in self.swaps:
            swap.start(slot, slots)

    def steps(self, slot, slots):
        def one(hop, carry):
            for gather in self.gathers:
                gather.step(hop)
            return carry

        half = self.spot.half
        lax.fori_loop(slot * half // slots, (slot + 1) * half // slots, one, 0)

    def finish_gathers(self):
        for gather in self.gathers:
            gather.relay(0, self.spot.half - 1)
        for gather in self.gathers:
            gather.finish()

    def finish(self):
        self.finish_gathers()
        for swap in self.swaps:
            swap.finish()

    @staticmethod
    def scratch(shards, count, swap_count):
        return Gather.scratch(shards // 4) * count + [
            DMA((shards,)),
            DMA((shards,)),
            DMA,
        ] * swap_count


def gather_kernel(shards, lents, *refs):
    spot = Spot(shards)
    rows_ref, tokens_ref, cotangent_ref = refs[:3]
    count = len(lents)
    pieces, gains_ref, refs = refs[3 : 3 + count], refs[3 + count], refs[4 + count :]
    outputs, packed_out, refs = refs[: count + 2], refs[count + 2], refs[count + 3 :]
    packed_ref, scratch = refs[0], refs[1:]
    work = GatherAll(spot, lents, 2, [*pieces, packed_ref, gains_ref], outputs, scratch)
    work.start()
    chosen = place_rows(rows_ref[0:1, :], packed_ref.shape[0])
    packed_ref[...] = matmul(chosen, tokens_ref[...]).astype(jnp.bfloat16)

    def one(hop, carry):
        work.exchange(hop, spot.half)

        @pl.when(hop == 0)
        def _():
            packed_out[...] = matmul(chosen, cotangent_ref[...]).astype(jnp.bfloat16)

        work.steps(hop, spot.half)
        return carry

    lax.fori_loop(0, spot.half, one, 0)
    work.finish()


def gather_shapes(shards, pieces, sent, shared):
    return (
        [
            jax.ShapeDtypeStruct((shards * piece.shape[0], piece.shape[1]), piece.dtype)
            for piece in pieces
        ]
        + [jax.ShapeDtypeStruct(rows.shape, rows.dtype) for rows in sent]
        + [
            jax.ShapeDtypeStruct((shards * each.shape[0], each.shape[1]), each.dtype)
            for each in shared
        ]
    )


def gather_call(shards, rows, tokens, cotangent, pieces, lents, gains, collective_id):
    anywhere = pl.BlockSpec(memory_space=pl.ANY)
    inside = pl.BlockSpec(memory_space=pltpu.VMEM)
    count = len(pieces)
    packed = jax.ShapeDtypeStruct((2 * tokens.shape[0], tokens.shape[1]), tokens.dtype)
    results = pl.pallas_call(
        functools.partial(gather_kernel, shards, lents),
        out_shape=[*gather_shapes(shards, pieces, [packed], [gains]), packed],
        in_specs=[inside] * 3 + [anywhere] * (count + 1),
        out_specs=[anywhere] * (count + 2) + [inside],
        scratch_shapes=[
            pltpu.VMEM(packed.shape, packed.dtype),
            *GatherAll.scratch(shards, count, 2),
        ],
        compiler_params=pltpu.CompilerParams(
            collective_id=collective_id, has_side_effects=True, vmem_limit_bytes=VMEM_LIMIT
        ),
    )(rows, tokens, cotangent, *pieces, gains)
    return results[:count], *results[count:]


class Reduce:
    def __init__(self, spot, lent, partial_ref, out_ref, refs, part=0, parts=1):
        self.spot, self.lent, self.partial, self.out = spot, lent, partial_ref, out_ref
        self.block_rows = partial_ref.shape[0] // spot.shards
        self.columns = partial_ref.shape[1]
        self.rows = self.block_rows // parts
        self.offset = part * self.rows
        self.unit = self.columns // 8
        self.kept = 8 - lent
        self.width = self.kept * self.unit
        (
            self.own,
            self.sib,
            self.got,
            self.own_far,
            self.sib_far,
            self.got_far,
            self.got_last,
        ) = refs[:7]
        sems = refs[7:]
        self.load_sem, self.load_far_sem = sems[0], sems[1]
        self.sib_sems, self.sib_far_sems = sems[2:4], sems[4:6]
        self.ring_sems, self.far_sems, self.last_sems = sems[6:8], sems[8:10], sems[10:12]
        self.out_sems = sems[12]

    @staticmethod
    def scratch(shards, lent, rows, columns):
        chips = shards // 2
        unit = columns // 8
        kept, lend = (8 - lent) * unit, lent * unit
        half = jnp.bfloat16
        buffers = [
            pltpu.VMEM((chips, rows, kept), half),
            pltpu.VMEM((chips, rows, kept), half),
            pltpu.VMEM((2, chips // 2, rows, kept), half),
            pltpu.VMEM((chips, rows, lend), half),
            pltpu.VMEM((chips, rows, lend), half),
            pltpu.VMEM((chips, rows, lend), half),
            pltpu.VMEM((rows, kept), half),
        ]
        sems = [DMA((chips,))] * 6 + [DMA((2, chips // 2))] * 2
        sems += [DMA((chips,))] * 2 + [DMA((1,))] * 2 + [DMA((2,))]
        return buffers + sems

    def owner(self, item, core):
        half = self.spot.half
        pair = (item + 1) // 2
        ahead = lax.rem(item, 2) == 1
        distance = half - pair
        place = jnp.where(ahead, self.spot.place + distance, self.spot.place - distance)
        return self.spot.block(place, core)

    def cut(self, item, core, first, count):
        columns = pl.ds(pl.multiple_of(first * self.unit, 128), count * self.unit)
        block = self.owner(item, core)
        first = pl.multiple_of(block * self.block_rows + self.offset, 16)
        return self.partial.at[pl.ds(first, self.rows), columns]

    def kept_cut(self, item, core):
        return self.cut(item, core, self.lent * self.spot.rep, self.kept)

    def lent_cut(self, item, core):
        return self.cut(item, core, self.kept * (1 - self.spot.rep), self.lent)

    def load(self, item):
        source = self.kept_cut(item, self.spot.core)
        return pltpu.make_async_copy(source, self.own.at[item], self.load_sem.at[item])

    def load_far(self, item):
        source = self.lent_cut(item, self.spot.core)
        return pltpu.make_async_copy(source, self.own_far.at[item], self.load_far_sem.at[item])

    def give(self, item):
        source = self.kept_cut(item, 1 - self.spot.core)
        target = (self.spot.rep, self.spot.sibling)
        return remote(source, self.sib.at[item], self.sib_sems, (item,), target)

    def give_far(self, item):
        source = self.lent_cut(item, 1 - self.spot.core)
        target = (self.spot.rep, self.spot.sibling)
        return remote(source, self.sib_far.at[item], self.sib_far_sems, (item,), target)

    def ring(self, way, step, short=False):
        item = 0 if short else 2 * step - 1 + way
        columns = pl.ds(way * self.width // 2, self.width // 2) if short else slice(None)
        return remote(
            self.own.at[item, :, columns],
            self.got.at[way, step, :, columns],
            self.ring_sems,
            (way, step),
            self.spot.ahead(way),
        )

    def far(self, item):
        target = (1 - self.spot.rep, self.spot.shard)
        return remote(
            self.own_far.at[item], self.got_far.at[item], self.far_sems, (item,), target
        )

    @staticmethod
    def out_shape(shards, lent, partial):
        rows, columns = partial.shape[0] // shards, partial.shape[1]
        return jax.ShapeDtypeStruct((2, rows, (8 - lent) * columns // 8), jnp.bfloat16)

    def last(self):
        target = (1 - self.spot.rep, self.spot.shard)
        source = self.own.at[self.spot.chips - 1]
        return remote(source, self.got_last, self.last_sems, (0,), target)

    def start(self, item):
        self.load_far(item).start()
        self.give_far(item).start()
        self.load(item).start()
        self.give(item).start()

    def tiles(self, width, body):
        chunk = width if width <= 768 else 512

        def one(tile, carry):
            for first in range(0, width, chunk):
                body(pl.ds(pl.multiple_of(tile * 16, 16), 16), first, chunk)
            return carry

        lax.fori_loop(0, self.rows // 16, one, 0)

    def far_step(self, item):
        self.load_far(item).wait()
        self.give_far(item).wait_recv()

        def add(rows, first, count):
            at = pl.ds(first, count)
            total = self.own_far[item, rows, at].astype(jnp.float32)
            total += self.sib_far[item, rows, at].astype(jnp.float32)
            self.own_far[item, rows, at] = total.astype(jnp.bfloat16)

        self.tiles(self.lent * self.unit, add)
        self.far(item).start()

    def fold(self, item, extra=(), start=0, width=None):
        def add(rows, first, count):
            at = pl.ds(start + first, count)
            total = self.own[item, rows, at].astype(jnp.float32)
            total += self.sib[item, rows, at].astype(jnp.float32)
            for way, step in extra:
                total += self.got[way, step, rows, at].astype(jnp.float32)
            self.own[item, rows, at] = total.astype(jnp.bfloat16)

        self.tiles(self.width if width is None else width, add)

    def ready(self, item):
        self.load(item).wait()
        self.give(item).wait_recv()
        self.far(item).wait_recv()
        offset = self.spot.rep * (self.kept - self.lent) * self.unit

        def add(rows, first, count):
            at = pl.ds(pl.multiple_of(offset + first, 128), count)
            total = self.sib[item, rows, at].astype(jnp.float32)
            total += self.got_far[item, rows, pl.ds(first, count)].astype(jnp.float32)
            self.sib[item, rows, at] = total.astype(jnp.bfloat16)

        self.tiles(self.lent * self.unit, add)

    def step(self, step):
        half, chips = self.spot.half, self.spot.chips

        @pl.when(step == 0)
        def _():
            self.ready(0)
            self.fold(0)
            for way in (0, 1):
                self.ring(way, 0, True).start()

        @pl.when((step > 0) & (step < half))
        def _():
            for way in (0, 1):
                item = 2 * step - 1 + way
                self.ready(item)

                @pl.when(step == 1)
                def _():
                    self.ring(way, 0, True).wait_recv()
                    middle = self.width // 2
                    self.fold(item, [(way, 0)], way * middle, middle)
                    self.fold(item, [], (1 - way) * middle, middle)

                @pl.when(step > 1)
                def _():
                    self.ring(way, step - 1).wait_recv()
                    self.fold(item, [(way, step - 1)])

                self.ring(way, step).start()

        @pl.when(step == half)
        def _():
            self.ready(chips - 1)
            for way in (0, 1):
                self.ring(way, half - 1).wait_recv()
            self.fold(chips - 1, [(0, half - 1), (1, half - 1)])
            self.last().start()

        @pl.when(step < half)
        def _():
            self.far_step(2 * step + 1)

            @pl.when(step < half - 1)
            def _():
                self.far_step(2 * step + 2)

    def finish(self):
        spot = self.spot
        rows = pl.ds(self.offset, self.rows)
        mine = pltpu.make_async_copy(
            self.own.at[spot.chips - 1], self.out.at[0, rows], self.out_sems.at[0]
        )
        mine.start()
        self.last().wait()
        theirs = pltpu.make_async_copy(
            self.got_last, self.out.at[1, rows], self.out_sems.at[1]
        )
        theirs.start()
        mine.wait()
        theirs.wait()

        def one(item, carry):
            self.give_far(item).wait_send()
            self.far(item).wait_send()
            self.give(item).wait_send()
            return carry

        lax.fori_loop(0, spot.chips, one, 0)
        for way in (0, 1):
            self.ring(way, 0, True).wait_send()

        def two(step, carry):
            for way in (0, 1):
                self.ring(way, step).wait_send()
            return carry

        lax.fori_loop(1, spot.half, two, 0)


class Tally:
    def __init__(self, spot, mine, out, refs):
        self.spot, self.mine, self.out = spot, mine, out
        self.got, self.half, self.other = refs[0:3]
        self.sems, self.own_sem, self.far_sems = refs[3:5], refs[5], refs[6:8]
        self.own = pltpu.make_async_copy(mine, self.got.at[spot.shard], self.own_sem)

    def copy(self, k):
        spot = self.spot
        target = lax.rem(spot.shard + k, spot.shards)
        return remote(self.mine, self.got.at[spot.shard], self.sems, (k,), (spot.rep, target))

    def far(self):
        target = (1 - self.spot.rep, self.spot.shard)
        return remote(self.half, self.other, self.far_sems, (0,), target)

    def start(self):
        def one(k, carry):
            self.copy(k).start()
            return carry

        lax.fori_loop(1, self.spot.shards, one, 0)
        self.own.start()

    def middle(self):
        def one(k, carry):
            self.copy(k).wait()
            return carry

        lax.fori_loop(1, self.spot.shards, one, 0)
        self.own.wait()

        def add(k, total):
            return total + self.got[k]

        self.half[...] = lax.fori_loop(0, self.spot.shards, add, jnp.zeros_like(self.half))
        self.far().start()

    def finish(self):
        self.far().wait()
        self.out[...] = self.half[...] + self.other[...]

    @staticmethod
    def scratch(shards, shape):
        full = jnp.float32
        return [
            pltpu.VMEM((shards, *shape), full),
            pltpu.VMEM(shape, full),
            pltpu.VMEM(shape, full),
            DMA((shards,)),
            DMA((shards,)),
            DMA,
            DMA((1,)),
            DMA((1,)),
        ]


def matmul(left, right, left_dim=1, right_dim=0):
    return lax.dot_general(
        left, right, (((left_dim,), (right_dim,)), ((), ())), preferred_element_type=jnp.float32
    )


def pick_rows(slot_column, slot_total):
    shape = (slot_column.shape[0], slot_total)
    return (slot_column == lax.broadcasted_iota(jnp.int32, shape, 1)).astype(jnp.bfloat16)


def place_rows(slot_row, slot_total):
    shape = (slot_total, slot_row.shape[1])
    return (slot_row == lax.broadcasted_iota(jnp.int32, shape, 0)).astype(jnp.bfloat16)


def assemble_kernel(rep_ref, *refs):
    raws, plain, refs = refs[:4], refs[4:6], refs[6:]
    plain_outs, outs, whole_ref = refs[:2], refs[2:9], refs[9]
    for source, target in zip(plain, plain_outs, strict=True):
        target[...] = source[...]
    for raw_ref, out_ref in zip(raws, [*outs[:3], whole_ref], strict=True):
        kept = raw_ref.shape[2]
        columns = out_ref.shape[1]
        lent = columns - kept

        def write(low, high, raw_ref=raw_ref, out_ref=out_ref, kept=kept, lent=lent):
            def part(which, first, count):
                return raw_ref[which, :, first : first + count].astype(jnp.float32)

            out_ref[:, 0:lent] = part(low, 0, lent)
            if kept > lent:
                out_ref[:, lent:kept] = part(low, lent, kept - lent) + part(high, 0, kept - lent)
            out_ref[:, kept:] = part(high, kept - lent, lent)

        @pl.when(rep_ref[0, 0] == 0)
        def _(write=write):
            write(0, 1)

        @pl.when(rep_ref[0, 0] != 0)
        def _(write=write):
            write(1, 0)

    width = outs[3].shape[1]
    for i in range(4):
        outs[3 + i][...] = whole_ref[:, i * width : (i + 1) * width]


def local_call(kernel, out_shape, inputs, spaces=None, scratch=()):
    inside = pl.BlockSpec(memory_space=pltpu.VMEM)
    return pl.pallas_call(
        kernel,
        out_shape=out_shape,
        in_specs=spaces or [inside] * len(inputs),
        out_specs=[inside] * len(out_shape),
        scratch_shapes=list(scratch),
        compiler_params=pltpu.CompilerParams(vmem_limit_bytes=VMEM_LIMIT),
    )(*inputs)


def segment_of(index, lengths_ref):
    first = lengths_ref[0, 0]
    second = first + lengths_ref[0, 1]
    third = second + lengths_ref[0, 2]
    return (
        (index >= first).astype(jnp.int32)
        + (index >= second).astype(jnp.int32)
        + (index >= third).astype(jnp.int32)
    )


def pair_masks(columns_ref, rows_ref, lengths_ref, same_ref, hidden_ref):
    size = columns_ref.shape[0]
    shape = (size, size)
    key_id = lax.broadcasted_iota(jnp.int32, shape, 0)
    query_id = lax.broadcasted_iota(jnp.int32, shape, 1)
    key_column = lax.broadcasted_iota(jnp.int32, (size, 1), 0)
    query_row = lax.broadcasted_iota(jnp.int32, (1, size), 1)
    together = segment_of(key_column, lengths_ref) == segment_of(query_row, lengths_ref)
    seen = together & ((columns_ref[:, 3:4] > 0) | (key_id == query_id))
    same_ref[...] = (columns_ref[:, 2:3] == rows_ref[2:3, :]).astype(jnp.float32)
    hidden_ref[...] = jnp.where(seen, 0.0, masked_score)


def turn(values, cosine, sine):
    width = values.shape[1]
    lane = lax.broadcasted_iota(jnp.int32, values.shape, 1)
    other = jnp.where(
        lane % 64 < 32, pltpu.roll(values, width - 32, 1), pltpu.roll(values, 32, 1)
    )
    return values * cosine + other * sine


def head_lanes(values, head):
    lane = lax.broadcasted_iota(jnp.int32, values.shape, 1)
    return jnp.where((lane < 64) == (head == 0), values, jnp.zeros_like(values))


def project(input_ref, weight_refs, cosine_ref, sine_ref, out_ref, scale):
    width = weight_refs[0].shape[0]
    cosine = jnp.concatenate([cosine_ref[...]] * 2, axis=1)
    sine = jnp.concatenate([sine_ref[...]] * 2, axis=1)

    def one(i, carry):
        def columns(part):
            return pl.ds(pl.multiple_of(part * width + i * 256, 256), 256)

        at = pl.ds(pl.multiple_of(i * 256, 256), 256)
        query = matmul(input_ref[...], weight_refs[0][:, at])
        out_ref[:, columns(0)] = (turn(query, cosine, sine) * scale).astype(jnp.bfloat16)
        key = matmul(input_ref[...], weight_refs[1][:, at])
        out_ref[:, columns(1)] = turn(key, cosine, sine).astype(jnp.bfloat16)
        out_ref[:, columns(2)] = matmul(input_ref[...], weight_refs[2][:, at]).astype(
            jnp.bfloat16
        )
        return carry

    lax.fori_loop(0, width // 256, one, 0)


def attend_pair(pair, width, heads_ref, bias_ref, same_ref, hidden_ref, out_ref, log_ref):
    def columns(part):
        return pl.ds(pl.multiple_of(part * width + pair * 128, 128), 128)

    query, key, value = (heads_ref[:, columns(part)] for part in range(3))
    total = None
    for which in (0, 1):
        head = 2 * pair + which
        gap = bias_ref[0, head] - bias_ref[1, head]
        scores = matmul(head_lanes(key, which), query, 1, 1)
        scores = scores + same_ref[...] * gap + hidden_ref[...]
        top = jnp.max(scores, axis=0, keepdims=True)
        weights = jnp.exp(scores - top)
        weight_sum = jnp.sum(weights, axis=0, keepdims=True)
        log_ref[pl.ds(head, 1), :] = top + jnp.log(weight_sum)
        soft = (weights * (1.0 / weight_sum)).astype(jnp.bfloat16)
        part = matmul(head_lanes(value, which), soft, 0, 0)
        total = part if total is None else total + part
    out_ref[:, pl.ds(pl.multiple_of(pair * 128, 128), 128)] = total.T.astype(jnp.bfloat16)


def normed(values):
    factor = lax.rsqrt(jnp.mean(values * values, axis=-1, keepdims=True) + epsilon)
    return values * factor, factor


def forward_body(refs, between, loaded):
    (
        arrived_ref, columns_ref, rows_ref, lengths_ref, bias_ref, gain_ref,
        query_w_ref, key_w_ref, value_w_ref, cosine_ref, sine_ref,
        stream_ref, input_ref, heads_ref, out_ref, log_ref,
        same_ref, hidden_ref,
    ) = refs
    width = gain_ref.shape[1]
    scale = 1.0 / math.sqrt(64)
    pair_masks(columns_ref, rows_ref, lengths_ref, same_ref, hidden_ref)
    chosen = pick_rows(columns_ref[:, 1:2], arrived_ref.shape[0])
    loaded(0)
    stream = matmul(chosen, arrived_ref[...])
    stream_ref[...] = stream.astype(jnp.bfloat16)
    input_ref[...] = (normed(stream)[0] * gain_ref[...]).astype(jnp.bfloat16)
    weight_refs = (query_w_ref, key_w_ref, value_w_ref)
    for i in (1, 2, 3):
        loaded(i)
    project(input_ref, weight_refs, cosine_ref, sine_ref, heads_ref, scale)

    def one(pair, carry):
        between(pair)
        attend_pair(pair, width, heads_ref, bias_ref, same_ref, hidden_ref, out_ref, log_ref)
        return carry

    lax.fori_loop(0, width // 128, one, 0)


def fold_lanes(row):
    folded = row[:, 0:128]
    for i in range(1, row.shape[1] // 128):
        folded += row[:, i * 128 : (i + 1) * 128]
    return folded


def square_into(stats_ref, at, values, columns_ref):
    valid = (columns_ref[:, 3:4] > 0).astype(jnp.float32)
    across = jnp.sum(values * values * valid, axis=0, keepdims=True)
    stats_ref[at : at + 1, :] = fold_lanes(across)


def attend_back_pair(
    pair, width, scale, heads_ref, do_ref, bias_ref, log_ref, same_ref, hidden_ref, cosine_ref,
    sine_ref, grads_ref, bias_same_ref, bias_all_ref,
):
    half = jnp.bfloat16

    def columns(part):
        return pl.ds(pl.multiple_of(part * width + pair * 128, 128), 128)

    query, key, value = (heads_ref[:, columns(part)] for part in range(3))
    grad_out = do_ref[:, columns(0)]
    query_t = key_grad = value_grad = None
    for which in (0, 1):
        head = 2 * pair + which
        gap = bias_ref[0, head] - bias_ref[1, head]
        key_part = head_lanes(key, which)
        scores = matmul(key_part, query, 1, 1)
        scores = scores + same_ref[...] * gap + hidden_ref[...]
        soft = jnp.exp(scores - log_ref[pl.ds(head, 1), :])
        grad_soft = matmul(head_lanes(value, which), grad_out, 1, 1)
        inner = jnp.sum(soft * grad_soft, axis=0, keepdims=True)
        grad_scores = (soft * (grad_soft - inner)).astype(half)
        wide = grad_scores.astype(jnp.float32)
        bias_all_ref[pl.ds(head, 1), :] = jnp.sum(wide, axis=0, keepdims=True)
        bias_same_ref[pl.ds(head, 1), :] = jnp.sum(wide * same_ref[...], axis=0, keepdims=True)
        parts = (
            matmul(key_part, grad_scores, 0, 0),
            matmul(grad_scores, head_lanes(query, which)),
            matmul(soft.astype(half), head_lanes(grad_out, which)),
        )
        if which == 0:
            query_t, key_grad, value_grad = parts
        else:
            query_t, key_grad, value_grad = (
                query_t + parts[0],
                key_grad + parts[1],
                value_grad + parts[2],
            )
    cosine, sine = cosine_ref[...], -sine_ref[...]
    grads_ref[:, columns(0)] = (turn(query_t.T, cosine, sine) * scale).astype(half)
    grads_ref[:, columns(1)] = turn(key_grad, cosine, sine).astype(half)
    grads_ref[:, columns(2)] = value_grad.astype(half)


def feed_forward(refs, weights, gates_out, ups_out, hidden_out, scratch, saves):
    columns_ref, rows_ref, gain_ref, stream_ref, attended_ref, out_w_ref = refs[:6]
    packed_ref, middle_ref, input_ref, stats_ref = refs[6:]
    (
        gate_buf, up_buf, down_buf, gates_buf, ups_buf, hidden_buf, mlp_ref,
        load_sems, store_sems,
    ) = scratch
    tile = gate_buf.shape[2]
    tiles = gates_out.shape[1] // tile
    half = jnp.bfloat16

    def at(i):
        return pl.ds(pl.multiple_of(i * tile, tile), tile)

    def loads(i):
        slot = lax.rem(i, 2)
        return [
            pltpu.make_async_copy(weights[0].at[:, at(i)], gate_buf.at[slot], load_sems.at[slot, 0]),
            pltpu.make_async_copy(weights[1].at[:, at(i)], up_buf.at[slot], load_sems.at[slot, 1]),
            pltpu.make_async_copy(weights[2].at[at(i)], down_buf.at[slot], load_sems.at[slot, 2]),
        ]

    def stores(i):
        slot = lax.rem(i, 2)
        return [
            pltpu.make_async_copy(gates_buf.at[slot], gates_out.at[:, at(i)], store_sems.at[slot, 0]),
            pltpu.make_async_copy(ups_buf.at[slot], ups_out.at[:, at(i)], store_sems.at[slot, 1]),
            pltpu.make_async_copy(
                hidden_buf.at[slot], hidden_out.at[:, at(i)], store_sems.at[slot, 2]
            ),
        ]

    for copy in loads(0):
        copy.start()
    stats_ref[...] = jnp.zeros_like(stats_ref)
    stream = stream_ref[...].astype(jnp.float32)
    square_into(stats_ref, 0, stream, columns_ref)
    attn_out = matmul(attended_ref[...], out_w_ref[...])
    square_into(stats_ref, 1, attn_out, columns_ref)
    middle = stream + attn_out
    square_into(stats_ref, 2, middle, columns_ref)
    middle_ref[...] = middle
    input_ref[...] = (normed(middle)[0] * gain_ref[...]).astype(half)
    for copy in saves:
        copy.start()
    mlp_ref[...] = jnp.zeros_like(mlp_ref)

    def one(i, carry):
        slot = lax.rem(i, 2)
        for copy in loads(i):
            copy.wait()

        @pl.when(i + 1 < tiles)
        def _():
            for copy in loads(i + 1):
                copy.start()

        @pl.when(i >= 2)
        def _():
            for copy in stores(i - 2):
                copy.wait()

        gate = matmul(input_ref[...], gate_buf[slot])
        up = matmul(input_ref[...], up_buf[slot])
        gates_buf[slot] = gate
        ups_buf[slot] = up
        hidden = (gate * jax.nn.sigmoid(gate) * up).astype(half)
        hidden_buf[slot] = hidden
        for copy in stores(i):
            copy.start()
        mlp_ref[...] += matmul(hidden, down_buf[slot])
        return carry

    lax.fori_loop(0, tiles, one, 0)
    valid = (columns_ref[:, 3:4] > 0).astype(jnp.float32)
    mlp_out = mlp_ref[...]
    result = middle_ref[...] + mlp_out
    placed = place_rows(rows_ref[1:2, :], packed_ref.shape[0])
    packed_ref[...] = matmul(placed, result.astype(half)).astype(half)
    square_into(stats_ref, 3, mlp_out, columns_ref)
    square_into(stats_ref, 4, result, columns_ref)
    lane = lax.broadcasted_iota(jnp.int32, (valid.shape[0], 128), 1)
    stats_ref[5:6, :] = jnp.sum(jnp.where(lane == 0, valid, 0.0), axis=0, keepdims=True)
    for i in (tiles - 2, tiles - 1):
        for copy in stores(i):
            copy.wait()


def forward_gather_kernel(shards, lents, swap_count, compute_counts, *refs):
    ins, outs = compute_counts
    total = len(lents) + swap_count
    in_refs, refs = refs[: ins + total], refs[ins + total :]
    out_refs, refs = refs[: outs + total], refs[outs + total :]
    masks, out_w_buf, out_w_sem, feed_scratch, staged, sems, scratch = (
        refs[:2], refs[2], refs[3], refs[4:13], refs[13:24], refs[24:26], refs[26:],
    )
    work = GatherAll(
        Spot(shards), lents, swap_count, in_refs[ins:], out_refs[outs:], scratch
    )
    work.start()
    *attend_ins, gain_mlp_ref = in_refs[:ins]
    arriving, leaving = staged[:4], staged[4:]
    loads = [
        pltpu.make_async_copy(attend_ins[at], arriving[i], sems[0].at[i])
        for i, at in enumerate((0, 6, 7, 8))
    ]
    for copy in loads:
        copy.start()
    attend_ins[0], attend_ins[6:9] = arriving[0], arriving[1:4]
    attend_outs, feed_outs = leaving[:5], [*out_refs[5:9], *leaving[5:], out_refs[outs - 1]]
    saves = [
        pltpu.make_async_copy(leaving[i], out_refs[at], sems[1].at[i])
        for i, at in enumerate((0, 1, 2, 3, 4, 9, 10))
    ]
    pairs = attend_ins[5].shape[1] // 128

    def between(pair):
        work.exchange(pair, pairs)
        work.steps(pair, pairs)

    forward_body(
        (*attend_ins, *attend_outs, *masks), between, lambda i: loads[i].wait()
    )
    for copy in saves[:5]:
        copy.start()
    work.finish_gathers()
    full_refs = out_refs[outs:]
    copy = pltpu.make_async_copy(full_refs[0], out_w_buf, out_w_sem)
    copy.start()
    copy.wait()
    gates_out, ups_out, hidden_out, *feed_outs = feed_outs
    feed_forward(
        (
            attend_ins[1], attend_ins[2], gain_mlp_ref, attend_outs[0], attend_outs[3], out_w_buf,
            *feed_outs,
        ),
        full_refs[1:4], gates_out, ups_out, hidden_out, feed_scratch, saves[5:],
    )
    for copy in saves:
        copy.wait()
    for swap in work.swaps:
        swap.finish()


def forward_gather_call(
    shards, inputs, spaces, out_shape, out_specs, pieces, lents, sent, collective_id
):
    anywhere = pl.BlockSpec(memory_space=pl.ANY)
    tokens, width = out_shape[0].shape
    tile = 512
    half, full = jnp.bfloat16, jnp.float32
    counts = (len(inputs), len(out_shape))
    comm = len(pieces) + len(sent)
    results = pl.pallas_call(
        functools.partial(forward_gather_kernel, shards, lents, len(sent), counts),
        out_shape=[*out_shape, *gather_shapes(shards, pieces, sent, [])],
        in_specs=spaces + [anywhere] * comm,
        out_specs=out_specs + [anywhere] * comm,
        scratch_shapes=[
            pltpu.VMEM((tokens, tokens), full),
            pltpu.VMEM((tokens, tokens), full),
            pltpu.VMEM((width, width), half),
            DMA,
            pltpu.VMEM((2, width, tile), half),
            pltpu.VMEM((2, width, tile), half),
            pltpu.VMEM((2, tile, width), half),
            pltpu.VMEM((2, tokens, tile), full),
            pltpu.VMEM((2, tokens, tile), full),
            pltpu.VMEM((2, tokens, tile), half),
            pltpu.VMEM((tokens, width), full),
            DMA((2, 3)),
            DMA((2, 3)),
            *[pltpu.VMEM(inputs[at].shape, half) for at in (0, 6, 7, 8)],
            *[
                pltpu.VMEM(out_shape[at].shape, out_shape[at].dtype)
                for at in (0, 1, 2, 3, 4, 9, 10)
            ],
            DMA((4,)),
            DMA((7,)),
            *GatherAll.scratch(shards, len(pieces), len(sent)),
        ],
        compiler_params=pltpu.CompilerParams(
            collective_id=collective_id, has_side_effects=True, vmem_limit_bytes=VMEM_LIMIT
        ),
    )(*inputs, *pieces, *sent)
    first = len(out_shape)
    second = first + len(pieces)
    return results[:first], results[first:second], results[second:]


def input_grad_kernel(shards, lent, *refs):
    (
        columns_ref, rows_ref, lengths_ref, bias_ref, gain_mlp_ref, gain_attn_ref, middle_ref,
        out_w_ref, arrived_ref, heads_ref, log_ref, cosine_ref, sine_ref, stream_ref,
        query_w_ref, key_w_ref, value_w_ref, packed_out_ref, gates_ref, ups_ref, rows_mlp_ref,
        gate_w_ref, up_w_ref, down_w_ref,
        grads_ref, packed_ref, stats_ref, grad_down_ref,
        grad_gate_ref, grad_up_ref, home_ref, partial_ref,
        gates_buf, ups_buf, gate_buf, up_buf, down_buf, grad_gate_buf, grad_up_buf,
        back_ref, dh_ref, do_ref, same_ref, hidden_ref, bias_same_ref, bias_all_ref,
        load_sems, store_sems, weight_sems, send_sems, recv_sems, own_sem,
    ) = refs[:52]
    staged, in_sems, out_sem, refs = refs[52:59], refs[59], refs[60], refs[61:]
    arriving = [
        pltpu.make_async_copy(source, buffer, in_sems.at[i])
        for i, (source, buffer) in enumerate(
            zip(
                (arrived_ref, out_w_ref, middle_ref, heads_ref, cosine_ref, sine_ref, stream_ref),
                staged,
                strict=True,
            )
        )
    ]
    arrived_ref, out_w_ref, middle_ref, heads_ref, cosine_ref, sine_ref, stream_ref = staged
    saved_ref, grads_ref = grads_ref, refs[0]
    dy_ref, refs = refs[1], refs[2:]
    save = pltpu.make_async_copy(grads_ref, saved_ref, out_sem)
    spot = Spot(shards)
    swap = Swap(spot, packed_out_ref, home_ref, (send_sems, recv_sems), own_sem)
    reduces = [
        Reduce(spot, lent, partial_ref, grad_down_ref, refs[20 * g : 20 * g + 20], g, 2)
        for g in (0, 1)
    ]
    tile = gate_buf.shape[2]
    tiles = gates_ref.shape[1] // tile
    width = gain_attn_ref.shape[1]
    half = jnp.bfloat16

    def at(i):
        return pl.ds(pl.multiple_of(i * tile, tile), tile)

    def loads(i):
        slot = lax.rem(i, 2)
        pairs = [
            (gates_ref.at[:, at(i)], gates_buf),
            (ups_ref.at[:, at(i)], ups_buf),
            (gate_w_ref.at[:, at(i)], gate_buf),
            (up_w_ref.at[:, at(i)], up_buf),
            (down_w_ref.at[at(i)], down_buf),
        ]
        return [
            pltpu.make_async_copy(source, buffer.at[slot], load_sems.at[slot, j])
            for j, (source, buffer) in enumerate(pairs)
        ]

    def stores(i):
        slot = lax.rem(i, 2)
        pairs = [(grad_gate_buf, grad_gate_ref), (grad_up_buf, grad_up_ref)]
        return [
            pltpu.make_async_copy(buffer.at[slot], target.at[:, at(i)], store_sems.at[slot, j])
            for j, (buffer, target) in enumerate(pairs)
        ]

    def row_loads(i):
        slot = lax.rem(i, 2)
        return [
            pltpu.make_async_copy(
                rows_mlp_ref.at[:, at(i)], grad_gate_buf.at[slot], load_sems.at[slot, 0]
            )
        ]

    def row_stores(i):
        slot = lax.rem(i, 2)
        return [
            pltpu.make_async_copy(
                down_buf.at[slot], partial_ref.at[at(i)], store_sems.at[slot, 0]
            )
        ]

    pairs = width // 128
    slots = tiles + pairs
    steps = spot.half + 1

    def reduce_steps(slot):
        def one(step, carry):
            for reduce in reduces:
                reduce.step(step)
            return carry

        lax.fori_loop(slot * steps // slots, (slot + 1) * steps // slots, one, 0)

    greet(spot)
    for copy in [arriving[0], *row_loads(0), *arriving[1:]]:
        copy.start()
    chosen = pick_rows(columns_ref[:, 1:2], arrived_ref.shape[0])
    arriving[0].wait()
    dy_ref[...] = matmul(chosen, arrived_ref[...]).astype(half)

    def rows_step(i, carry):
        slot = lax.rem(i, 2)
        for copy in row_loads(i):
            copy.wait()

        @pl.when(i + 1 < tiles)
        def _():
            for copy in row_loads(i + 1):
                copy.start()

        @pl.when(i >= 2)
        def _():
            for copy in row_stores(i - 2):
                copy.wait()

        down_buf[slot] = matmul(grad_gate_buf[slot], dy_ref[...], 0, 0).astype(half)
        for copy in row_stores(i):
            copy.start()
        return carry

    lax.fori_loop(0, tiles, rows_step, 0)
    for i in (tiles - 2, tiles - 1):
        for copy in row_stores(i):
            copy.wait()
    for copy in loads(0):
        copy.start()

    def begin(item, carry):
        for reduce in reduces:
            reduce.start(item)
        return carry

    lax.fori_loop(0, spot.chips, begin, 0)
    back_ref[...] = jnp.zeros_like(back_ref)
    pair_masks(columns_ref, rows_ref, lengths_ref, same_ref, hidden_ref)
    for reduce in reduces:
        reduce.far_step(0)

    def one(i, carry):
        slot = lax.rem(i, 2)

        swap.start(i, slots)
        reduce_steps(i)
        for copy in loads(i):
            copy.wait()

        @pl.when(i + 1 < tiles)
        def _():
            for copy in loads(i + 1):
                copy.start()

        @pl.when(i >= 2)
        def _():
            for copy in stores(i - 2):
                copy.wait()

        gate, up = gates_buf[slot], ups_buf[slot]
        grad_hidden = matmul(dy_ref[...], down_buf[slot], 1, 1)
        sigmoid = jax.nn.sigmoid(gate)
        grad_gate = (grad_hidden * up * sigmoid * (1.0 + gate * (1.0 - sigmoid))).astype(half)
        grad_up = (grad_hidden * gate * sigmoid).astype(half)
        grad_gate_buf[slot] = grad_gate
        grad_up_buf[slot] = grad_up
        for copy in stores(i):
            copy.start()
        back_ref[...] += matmul(grad_gate, gate_buf[slot], 1, 1) + matmul(
            grad_up, up_buf[slot], 1, 1
        )
        return carry

    lax.fori_loop(0, tiles, one, 0)
    for copy in arriving[1:]:
        copy.wait()
    stats_ref[...] = jnp.zeros_like(stats_ref)

    def through_norm(values, grad, gain_ref, first):
        entry, factor = normed(values)
        gain_grad = jnp.sum(grad * entry, axis=0, keepdims=True)
        for i in range(width // 128):
            stats_ref[first + i : first + i + 1, :] = gain_grad[:, i * 128 : (i + 1) * 128]
        scaled = grad * gain_ref[...]
        inner = jnp.mean(scaled * entry, axis=-1, keepdims=True)
        return factor * (scaled - entry * inner)

    dh = dy_ref[...].astype(jnp.float32) + through_norm(
        middle_ref[...], back_ref[...], gain_mlp_ref, 0
    )
    dh_ref[...] = dh
    branch = dh.astype(half)
    grads_ref[:, pl.ds(3 * width, width)] = branch
    do_ref[...] = matmul(branch, out_w_ref[...], 1, 1).astype(half)
    scale = 1.0 / math.sqrt(64)
    for i in (tiles - 2, tiles - 1):
        for copy in stores(i):
            copy.wait()
    halves = [pl.ds(0, tile), pl.ds(tile, tile)]

    def weight_loads(source, buffer, which):
        return [
            pltpu.make_async_copy(source.at[:, columns], buffer.at[j], weight_sems.at[which, j])
            for j, columns in enumerate(halves)
        ]

    for copy in weight_loads(query_w_ref, gate_buf, 0) + weight_loads(key_w_ref, up_buf, 1):
        copy.start()

    def two(pair, carry):
        swap.start(tiles + pair, slots)
        reduce_steps(tiles + pair)
        attend_back_pair(
            pair, width, scale, heads_ref, do_ref, bias_ref, log_ref, same_ref, hidden_ref,
            cosine_ref, sine_ref, grads_ref, bias_same_ref, bias_all_ref,
        )
        return carry

    lax.fori_loop(0, width // 128, two, 0)
    save.start()
    heads = bias_all_ref.shape[0]
    lane = lax.broadcasted_iota(jnp.int32, (heads, 128), 1)
    row = lax.broadcasted_iota(jnp.int32, (heads, 128), 0)
    same = jnp.sum(bias_same_ref[...], axis=1, keepdims=True)
    other = jnp.sum(bias_all_ref[...], axis=1, keepdims=True) - same
    stats_ref[16:17, :] = jnp.sum(
        jnp.where(lane == row, same, 0.0) + jnp.where(lane == row + heads, other, 0.0),
        axis=0,
        keepdims=True,
    )
    def through(buffer, first):
        return sum(
            matmul(grads_ref[:, pl.ds(first + j * tile, tile)], buffer[j], 1, 1) for j in (0, 1)
        )

    for copy in weight_loads(query_w_ref, gate_buf, 0):
        copy.wait()
    back_ref[...] = through(gate_buf, 0)
    for copy in weight_loads(value_w_ref, gate_buf, 0):
        copy.start()
    for copy in weight_loads(key_w_ref, up_buf, 1):
        copy.wait()
    back_ref[...] += through(up_buf, width)
    for copy in weight_loads(value_w_ref, gate_buf, 0):
        copy.wait()
    back_ref[...] += through(gate_buf, 2 * width)
    grad_stream = dh_ref[...] + through_norm(
        stream_ref[...].astype(jnp.float32), back_ref[...], gain_attn_ref, 8
    )
    placed = place_rows(rows_ref[1:2, :], packed_ref.shape[0])
    packed_ref[...] = matmul(placed, grad_stream.astype(half)).astype(half)
    save.wait()
    swap.finish()
    for reduce in reduces:
        reduce.finish()


def input_grad_call(shards, inputs, spaces, far_inputs, lent, collective_id):
    anywhere = pl.BlockSpec(memory_space=pl.ANY)
    inside = pl.BlockSpec(memory_space=pltpu.VMEM)
    packed, gates = far_inputs[3], far_inputs[4]
    tokens, hidden = gates.shape
    width = packed.shape[1]
    heads = inputs[10].shape[0]
    tile = 512
    assert 2 * tile == width
    half, full = jnp.bfloat16, jnp.float32
    vmem, shape = pltpu.VMEM, jax.ShapeDtypeStruct
    return pl.pallas_call(
        functools.partial(input_grad_kernel, shards, lent),
        out_shape=[
            shape((tokens, 4 * width), half),
            shape(packed.shape, half),
            shape((24, 128), full),
            Reduce.out_shape(shards, lent, shape((hidden, width), half)),
            shape((tokens, hidden), half),
            shape((tokens, hidden), half),
            shape(packed.shape, half),
            shape((hidden, width), half),
        ],
        in_specs=[*spaces, *[anywhere] * len(far_inputs)],
        out_specs=[anywhere] + [inside] * 2 + [anywhere] * 5,
        scratch_shapes=[
            vmem((2, tokens, tile), full),
            vmem((2, tokens, tile), full),
            vmem((2, width, tile), half),
            vmem((2, width, tile), half),
            vmem((2, tile, width), half),
            vmem((2, tokens, tile), half),
            vmem((2, tokens, tile), half),
            vmem((tokens, width), full),
            vmem((tokens, width), full),
            vmem((tokens, width), half),
            vmem((tokens, tokens), full),
            vmem((tokens, tokens), full),
            vmem((heads, tokens), full),
            vmem((heads, tokens), full),
            DMA((2, 5)),
            DMA((2, 2)),
            DMA((2, 2)),
            DMA((shards,)),
            DMA((shards,)),
            DMA,
            *[vmem(inputs[at].shape, inputs[at].dtype) for at in (8, 7, 6, 9, 11, 12, 13)],
            DMA((7,)),
            DMA,
            vmem((tokens, 4 * width), half),
            vmem((tokens, width), half),
            *Reduce.scratch(shards, lent, hidden // shards // 2, width) * 2,
        ],
        compiler_params=pltpu.CompilerParams(
            collective_id=collective_id, has_side_effects=True, vmem_limit_bytes=VMEM_LIMIT
        ),
    )(*inputs, *far_inputs)


def weight_grad_kernel(shards, lents, *refs):
    (
        columns_ref, input_attn_ref, attended_ref, input_mlp_ref, stats_forward_ref,
        stats_back_ref, home_out_ref, packed_ref, gate_ref, up_ref, entry_ref,
        grad_gate_ref, grad_up_ref, grad_in_ref, output_ref, input_grad_ref, sums_ref,
    ) = refs[:17]
    partials = refs[17:20]
    (
        attn_t_ref, attended_t_ref, mlp_t_ref, home_ref, stats_ref, tile_buf, part_buf,
        load_sems, store_sems, send_sems, recv_sems, own_sem,
    ) = refs[20:32]
    tally_refs, refs = refs[32:40], refs[40:]
    half, full = jnp.bfloat16, jnp.float32
    spot = Spot(shards)
    swap = Swap(spot, packed_ref, home_ref, (send_sems, recv_sems), own_sem)
    tally = Tally(spot, stats_ref, sums_ref, tally_refs)
    outputs = (grad_gate_ref, grad_up_ref, grad_in_ref)
    reduces = [
        Reduce(spot, lents[g], partials[g], outputs[g], refs[20 * g : 20 * g + 20])
        for g in range(3)
    ]
    steps = spot.half + 1
    parts = 5
    tile = tile_buf.shape[2]
    tiles = gate_ref.shape[1] // tile

    def at(i):
        return pl.ds(pl.multiple_of(i * tile, tile), tile)

    def product(source, lefts, partial, reduce):
        def load(i):
            slot = lax.rem(i, 2)
            return pltpu.make_async_copy(
                source.at[:, at(i)], tile_buf.at[slot], load_sems.at[slot]
            )

        def store(i):
            slot = lax.rem(i, 2)
            return pltpu.make_async_copy(
                part_buf.at[slot], partial.at[:, at(i)], store_sems.at[slot]
            )

        load(0).start()
        first = 0
        for left, count in lefts:

            def one(i, carry, left=left):
                slot = lax.rem(i, 2)
                load(i).wait()

                @pl.when(i + 1 < tiles)
                def _():
                    load(i + 1).start()

                @pl.when(i >= 2)
                def _():
                    store(i - 2).wait()

                part_buf[slot] = matmul(left[...], tile_buf[slot]).astype(half)
                store(i).start()
                return carry

            lax.fori_loop(first, first + count, one, 0)
            first += count
        for i in (tiles - 2, tiles - 1):
            store(i).wait()

        def begin(item, carry):
            reduce.start(item)
            return carry

        lax.fori_loop(0, spot.chips, begin, 0)
        reduce.far_step(0)

    greet(spot)
    swap.start(0, parts)
    stats_ref[0:8, :] = stats_forward_ref[...]
    stats_ref[8:32, :] = stats_back_ref[...]
    tally.start()
    mlp_t_ref[...] = input_mlp_ref[...].astype(full).T.astype(half)
    product(gate_ref, [(mlp_t_ref, tiles)], partials[0], reduces[0])
    swap.start(1, parts)
    product(up_ref, [(mlp_t_ref, tiles)], partials[1], reduces[1])
    swap.start(2, parts)
    chosen = pick_rows(columns_ref[:, 0:1], home_ref.shape[0])

    def ticks(tick, carry):
        @pl.when(tick < steps)
        def _():
            reduces[0].step(tick)

        @pl.when(tick < 2)
        def _():
            swap.start(3 + tick, parts)

        @pl.when(tick == 0)
        def _():
            attn_t_ref[...] = input_attn_ref[...].astype(full).T.astype(half)
            attended_t_ref[...] = attended_ref[...].astype(full).T.astype(half)
            product(
                entry_ref,
                [(attn_t_ref, tiles - tiles // 4), (attended_t_ref, tiles // 4)],
                partials[2],
                reduces[2],
            )

        @pl.when((tick > 0) & (tick < steps + 1))
        def _():
            reduces[1].step(tick - 1)

        @pl.when(tick == 1)
        def _():
            output_ref[...] = matmul(chosen, home_out_ref[...]).astype(half)
            tally.middle()

        @pl.when(tick > 1)
        def _():
            reduces[2].step(tick - 2)

        return carry

    lax.fori_loop(0, steps + 2, ticks, 0)
    swap.finish()
    input_grad_ref[...] = matmul(chosen, home_ref[...]).astype(half)
    tally.finish()
    for reduce in reduces:
        reduce.finish()


def weight_grad_call(shards, inputs, far_inputs, lents, collective_id):
    tile = 512
    packed, hidden = far_inputs[0], far_inputs[1].shape[1]
    tokens, width = inputs[1].shape
    assert hidden == 4 * width
    half, full = jnp.bfloat16, jnp.float32
    shape = jax.ShapeDtypeStruct
    anywhere = pl.BlockSpec(memory_space=pl.ANY)
    inside = pl.BlockSpec(memory_space=pltpu.VMEM)
    scratch = []
    for lent in lents:
        scratch += Reduce.scratch(shards, lent, width // shards, hidden)
    results = pl.pallas_call(
        functools.partial(weight_grad_kernel, shards, lents),
        out_shape=[
            *[Reduce.out_shape(shards, lent, shape((width, hidden), half)) for lent in lents],
            shape((tokens, width), half),
            shape((tokens, width), half),
            shape((32, 128), full),
            *[shape((width, hidden), half)] * 3,
        ],
        in_specs=[inside] * len(inputs) + [anywhere] * len(far_inputs),
        out_specs=[anywhere] * 3 + [inside] * 3 + [anywhere] * 3,
        scratch_shapes=[
            *[pltpu.VMEM((width, tokens), half)] * 3,
            pltpu.VMEM(packed.shape, half),
            pltpu.VMEM((32, 128), full),
            pltpu.VMEM((2, tokens, tile), half),
            pltpu.VMEM((2, width, tile), half),
            DMA((2,)),
            DMA((2,)),
            DMA((shards,)),
            DMA((shards,)),
            DMA,
            *Tally.scratch(shards, (32, 128)),
            *scratch,
        ],
        compiler_params=pltpu.CompilerParams(
            collective_id=collective_id, has_side_effects=True, vmem_limit_bytes=VMEM_LIMIT
        ),
    )(*inputs, *far_inputs)
    return results[:6]


def on_device(
    tokens,
    cotangent,
    send_slot,
    recv_slot,
    lengths,
    variate,
    valid_mask,
    norm_attn,
    w_query,
    w_key,
    w_value,
    w_out,
    variate_bias,
    norm_mlp,
    w_gate,
    w_up,
    w_down,
):
    shards = lax.axis_size("shard")
    tok_rows, width = tokens.shape
    slot_total = 2 * tok_rows
    heads = variate_bias.shape[1]
    half, full = jnp.bfloat16, jnp.float32
    share = width // shards
    indices = jnp.stack([send_slot, recv_slot, variate, valid_mask])
    rows = jnp.concatenate([indices, jnp.zeros_like(indices)])
    columns = rows.T
    _, position = layout(lengths[0], tok_rows)
    cosine, sine = angle_tables(position, width // heads)
    cosine = jnp.concatenate([cosine] * 4, axis=1)
    sine = jnp.concatenate([-sine, sine] * 2, axis=1)
    gains = jnp.stack([norm_attn, norm_mlp]).astype(full)
    gains = jnp.pad(gains, ((0, 6), (0, 128 - share)))
    shape = jax.ShapeDtypeStruct
    packed_shape = shape((slot_total, width), half)
    token_shape = shape((tok_rows, width), half)
    full_in, arrived_tokens, gains, out_cotangent = gather_call(
        shards, rows, tokens, cotangent, [w_query, w_key, w_value], (4, 4, 4), gains, 1
    )
    gains = gains.reshape(shards, 8, 128)
    gain_attn = gains[:, 0, :share].reshape(1, width)
    gain_mlp = gains[:, 1, :share].reshape(1, width)
    inside = pl.BlockSpec(memory_space=pltpu.VMEM)
    anywhere = pl.BlockSpec(memory_space=pl.ANY)
    scalar = pl.BlockSpec(memory_space=pltpu.SMEM)
    hidden = w_gate.shape[1]
    (
        (
            stream, input_attn, head_rows, attended, logs,
            gates, ups, hidden_rows, packed, middle, input_mlp, stats_forward,
        ),
        (full_out, full_gate, full_up, full_down),
        (arrived_grads,),
    ) = forward_gather_call(
        shards,
        [
            arrived_tokens, columns, rows, lengths, variate_bias, gain_attn, *full_in,
            cosine, sine, gain_mlp,
        ],
        [anywhere] + [inside] * 2 + [scalar] * 2 + [inside] + [anywhere] * 3 + [inside] * 3,
        [
            token_shape,
            token_shape,
            shape((tok_rows, 3 * width), half),
            token_shape,
            shape((heads, tok_rows), full),
            shape((tok_rows, hidden), full),
            shape((tok_rows, hidden), full),
            shape((tok_rows, hidden), half),
            packed_shape,
            shape((tok_rows, width), full),
            token_shape,
            shape((8, 128), full),
        ],
        [anywhere] * 8 + [inside] + [anywhere] * 2 + [inside],
        [w_out, w_gate, w_up, w_down],
        (4, 4, 4, 2),
        [out_cotangent],
        2,
    )
    (
        entry_grads, packed_grad, stats_back, grad_down, grad_gates, grad_ups, home_out, _,
    ) = input_grad_call(
        shards,
        [
            columns, rows, lengths, variate_bias, gain_mlp, gain_attn, middle, full_out,
            arrived_grads, head_rows, logs, cosine, sine, stream,
        ],
        [inside] * 2
        + [scalar] * 2
        + [inside] * 2
        + [anywhere] * 4
        + [inside]
        + [anywhere] * 3,
        [*full_in, packed, gates, ups, hidden_rows, full_gate, full_up, full_down],
        4,
        3,
    )
    grad_gate, grad_up, grad_in, output, input_grad, sums = weight_grad_call(
        shards,
        [columns, input_attn, attended, input_mlp, stats_forward, stats_back, home_out],
        [packed_grad, grad_gates, grad_ups, entry_grads],
        (4, 2, 2),
        4,
    )
    rep = lax.axis_index("rep").astype(jnp.int32).reshape(1, 1)
    (
        output, input_grad, grad_gate, grad_up, grad_down,
        grad_query, grad_key, grad_value, grad_out,
    ) = local_call(
        assemble_kernel,
        [
            token_shape,
            token_shape,
            *[shape((share, hidden), full)] * 2,
            shape((hidden // shards, width), full),
            *[shape((share, width), full)] * 4,
        ],
        [rep, grad_gate, grad_up, grad_down, grad_in, output, input_grad],
        [scalar] + [inside] * 6,
        [pltpu.VMEM((share, hidden), full)],
    )
    squares = jnp.sum(sums[0:6], axis=1)
    root_means = jnp.sqrt(squares[:5] / (squares[5] * width))
    share_start = lax.axis_index("shard") * share
    grad_norm_mlp = lax.dynamic_slice_in_dim(sums[8:16].reshape(-1), share_start, share)
    grad_norm_attn = lax.dynamic_slice_in_dim(sums[16:24].reshape(-1), share_start, share)
    bias_grads = sums[24, : 2 * heads].reshape(2, heads)
    return (
        output,
        input_grad,
        grad_norm_attn,
        grad_query,
        grad_key,
        grad_value,
        grad_out,
        bias_grads,
        grad_norm_mlp,
        grad_gate,
        grad_up,
        grad_down,
        root_means,
    )


def solution(mesh):
    in_specs = (
        P(("rep", "shard"), None),
        P(("rep", "shard"), None),
        P(("rep", "shard")),
        P(("rep", "shard")),
        P(("rep", "shard"), None),
        P(("rep", "shard")),
        P(("rep", "shard")),
        P("shard"),
        P("shard", None),
        P("shard", None),
        P("shard", None),
        P("shard", None),
        P(),
        P("shard"),
        P("shard", None),
        P("shard", None),
        P("shard", None),
    )
    out_specs = (
        P(("rep", "shard"), None),
        P(("rep", "shard"), None),
        P("shard"),
        P("shard", None),
        P("shard", None),
        P("shard", None),
        P("shard", None),
        P(),
        P("shard"),
        P("shard", None),
        P("shard", None),
        P("shard", None),
        P(),
    )
    return jax.shard_map(
        on_device, mesh=mesh, in_specs=in_specs, out_specs=out_specs, check_vma=False
    )
```

```python
import functools
import math

import jax
import jax.numpy as jnp
from jax import lax
from jax.experimental import pallas as pl
from jax.experimental.pallas import tpu as pltpu
from jax.sharding import PartitionSpec as P

MESH = pl.DeviceIdType.MESH
DMA = pltpu.SemaphoreType.DMA
epsilon = 1e-06
masked_score = -1e30
VMEM_LIMIT = 62 << 20


def angle_tables(position, head_dim):
    half_dim = head_dim // 2
    inverse_freq = 1.0 / 10000.0 ** (jnp.arange(half_dim, dtype=jnp.float32) / half_dim)
    theta_angle = position.astype(jnp.float32)[:, None] * inverse_freq[None, :]
    return (jnp.cos(theta_angle), jnp.sin(theta_angle))


def layout(lengths_row, tok_rows):
    slot_ids = jnp.arange(tok_rows, dtype=jnp.int32)
    seq_ends = jnp.cumsum(lengths_row)
    segment = jnp.sum((slot_ids[:, None] >= seq_ends[None, :]).astype(jnp.int32), axis=1)
    starts = seq_ends - lengths_row
    chosen = segment[:, None] == jnp.arange(lengths_row.shape[0], dtype=jnp.int32)[None, :]
    begins = jnp.sum(jnp.where(chosen, starts[None, :], 0), axis=1)
    return (segment, slot_ids - begins)


def ring_place(chip, chips):
    return jnp.where(chip % 2 == 0, chip // 2, chips - 1 - chip // 2)


def ring_chip(place, chips):
    wrapped = lax.rem(place + 2 * chips, chips)
    return jnp.where(wrapped < chips // 2, 2 * wrapped, 2 * (chips - 1 - wrapped) + 1)


class Spot:
    def __init__(self, shards):
        self.shards = shards
        self.chips = shards // 2
        self.half = self.chips // 2
        self.rep = lax.axis_index("rep")
        self.shard = lax.axis_index("shard")
        self.core = lax.rem(self.shard, 2)
        self.place = ring_place(self.shard // 2, self.chips)
        self.sibling = self.shard + 1 - 2 * self.core

    def block(self, place, core=None):
        return 2 * ring_chip(place, self.chips) + (self.core if core is None else core)

    def along(self, way, distance):
        return self.place - distance if way == 0 else self.place + distance

    def ahead(self, way):
        return (self.rep, self.block(self.along(way, -1)))


def greet(spot):
    barrier = pltpu.get_barrier_semaphore()

    def peer(k, carry):
        target = lax.rem(spot.shard + k, spot.shards)
        pl.semaphore_signal(barrier, inc=1, device_id=(spot.rep, target), device_id_type=MESH)
        return carry

    lax.fori_loop(1, spot.shards, peer, 0)
    pl.semaphore_signal(
        barrier, inc=1, device_id=(1 - spot.rep, spot.shard), device_id_type=MESH
    )
    pl.semaphore_wait(barrier, spot.shards)


def remote(src, dst, sems, at, target):
    return pltpu.make_async_remote_copy(
        src_ref=src,
        dst_ref=dst,
        send_sem=sems[0].at[at],
        recv_sem=sems[1].at[at],
        device_id=target,
        device_id_type=MESH,
    )


class Swap:
    def __init__(self, spot, source, arrived, sems, own_sem):
        self.spot, self.sems = spot, sems
        self.source, self.arrived = source, arrived
        self.capacity = arrived.shape[0] // spot.shards
        self.own = pltpu.make_async_copy(
            self.part(spot.shard), arrived.at[self.rows(spot.shard)], own_sem
        )

    def rows(self, shard):
        return pl.ds(pl.multiple_of(shard * self.capacity, 8), self.capacity)

    def part(self, shard):
        if self.source.shape[0] == self.capacity:
            return self.source
        return self.source.at[self.rows(shard)]

    def copy(self, k):
        spot = self.spot
        target = lax.rem(spot.shard + 7 * k, spot.shards)
        return remote(
            self.part(target),
            self.arrived.at[self.rows(spot.shard)],
            self.sems,
            (k,),
            (spot.rep, target),
        )

    def start(self, slot, slots):
        size = -(-self.spot.shards // slots)

        def one(k, carry):
            @pl.when(k == 0)
            def _():
                self.own.start()

            @pl.when(k > 0)
            def _():
                self.copy(k).start()

            return carry

        first = jnp.minimum(slot * size, self.spot.shards)
        lax.fori_loop(first, jnp.minimum(first + size, self.spot.shards), one, 0)

    def finish(self):
        def one(k, carry):
            self.copy(k).wait()
            return carry

        lax.fori_loop(1, self.spot.shards, one, 0)
        self.own.wait()


class Gather:
    def __init__(self, spot, lent, shard_ref, full_ref, sems):
        self.spot, self.lent, self.shard_ref, self.full_ref = spot, lent, shard_ref, full_ref
        self.rows = shard_ref.shape[0]
        self.unit = shard_ref.shape[1] // 8
        self.kept = 8 - lent
        self.ring_sems, self.near_sems, self.far_sems, self.far_near_sems = (
            sems[0:2],
            sems[2:4],
            sems[4:6],
            sems[6:8],
        )
        self.whole_sems, self.own_sem = sems[8:10], sems[10]

    def span(self, way, short):
        first, count = self.lent * self.spot.rep, self.kept
        if short:
            first, count = first + way * (count // 2), count // 2
        return pl.ds(pl.multiple_of(first * self.unit, 128), count * self.unit)

    def region(self, way, hop, short):
        block = self.spot.block(self.spot.along(way, hop))
        return self.full_ref.at[pl.ds(block * self.rows, self.rows), self.span(way, short)]

    def ring(self, way, hop, short, source=None):
        region = self.region(way, hop, short)
        return remote(
            region if source is None else source,
            region,
            self.ring_sems,
            (way, hop),
            self.spot.ahead(way),
        )

    def near(self, way, hop, short):
        region = self.region(way, hop + 1, short)
        target = (self.spot.rep, self.spot.sibling)
        return remote(region, region, self.near_sems, (way, hop), target)

    def lent_region(self, way, hop, owner):
        block = self.spot.block(self.spot.along(way, hop + 1))
        columns = pl.ds(
            pl.multiple_of(self.kept * owner * self.unit, 128), self.lent * self.unit
        )
        return self.full_ref.at[pl.ds(block * self.rows, self.rows), columns]

    def far(self, way, hop):
        region = self.lent_region(way, hop, self.spot.rep)
        target = (1 - self.spot.rep, self.spot.shard)
        return remote(region, region, self.far_sems, (way, hop), target)

    def far_near(self, way, hop):
        region = self.lent_region(way, hop, 1 - self.spot.rep)
        target = (self.spot.rep, self.spot.sibling)
        return remote(region, region, self.far_near_sems, (way, hop), target)

    def own(self):
        spot = self.spot
        mine = self.full_ref.at[pl.ds(spot.shard * self.rows, self.rows)]
        whole = remote(self.shard_ref, mine, self.whole_sems, (0,), (spot.rep, spot.sibling))
        return whole, pltpu.make_async_copy(self.shard_ref, mine, self.own_sem)

    def start(self):
        for way in (0, 1):
            self.ring(way, 0, False, self.shard_ref.at[:, self.span(way, False)]).start()
        for copy in self.own():
            copy.start()

    def step(self, hop):
        final = self.spot.half - 1

        @pl.when(hop < final)
        def _():
            for way in (0, 1):
                self.ring(way, hop, False).wait_recv()

                @pl.when(hop < final - 1)
                def _():
                    self.ring(way, hop + 1, False).start()

                @pl.when(hop == final - 1)
                def _():
                    self.ring(way, hop + 1, True).start()

            for way in (0, 1):
                self.far(way, hop).start()
                self.near(way, hop, False).start()

        @pl.when(hop == final)
        def _():
            for way in (0, 1):
                self.ring(way, hop, True).wait_recv()
            self.far(0, hop).start()
            for way in (0, 1):
                self.near(way, hop, True).start()

        @pl.when(hop > 0)
        def _():
            for way in (0, 1):
                self.relay(way, hop - 1)

    def relay(self, way, hop):
        self.far(way, hop).wait_recv()
        self.far_near(way, hop).start()

    def finish(self):
        final = self.spot.half - 1
        for copy in self.own():
            copy.wait()

        def one(hop, carry):
            for way in (0, 1):
                self.ring(way, hop, False).wait_send()
                self.near(way, hop, False).wait()
                self.far(way, hop).wait_send()
                self.far_near(way, hop).wait()
            return carry

        lax.fori_loop(0, final, one, 0)
        for way in (0, 1):
            self.ring(way, final, True).wait_send()
            self.near(way, final, True).wait()
        self.far(0, final).wait_send()
        self.far_near(0, final).wait()

    @staticmethod
    def scratch(half):
        return [DMA((2, half))] * 8 + [DMA((1,))] * 2 + [DMA]


class GatherAll:
    def __init__(self, spot, lents, swap_count, inputs, outputs, scratch):
        count = len(lents)
        self.spot = spot
        self.gathers = [
            Gather(spot, lents[g], inputs[g], outputs[g], scratch[11 * g : 11 * g + 11])
            for g in range(count)
        ]
        scratch = scratch[11 * count :]
        self.swaps = [
            Swap(
                spot,
                inputs[count + i],
                outputs[count + i],
                scratch[3 * i : 3 * i + 2],
                scratch[3 * i + 2],
            )
            for i in range(swap_count)
        ]

    def start(self):
        greet(self.spot)
        for gather in self.gathers:
            gather.start()

    def exchange(self, slot, slots):
        for swap in self.swaps:
            swap.start(slot, slots)

    def steps(self, slot, slots):
        def one(hop, carry):
            for gather in self.gathers:
                gather.step(hop)
            return carry

        half = self.spot.half
        lax.fori_loop(slot * half // slots, (slot + 1) * half // slots, one, 0)

    def finish_gathers(self):
        for gather in self.gathers:
            gather.relay(0, self.spot.half - 1)
        for gather in self.gathers:
            gather.finish()

    def finish(self):
        self.finish_gathers()
        for swap in self.swaps:
            swap.finish()

    @staticmethod
    def scratch(shards, count, swap_count):
        return Gather.scratch(shards // 4) * count + [
            DMA((shards,)),
            DMA((shards,)),
            DMA,
        ] * swap_count


def gather_kernel(shards, lents, *refs):
    spot = Spot(shards)
    rows_ref, tokens_ref, cotangent_ref = refs[:3]
    count = len(lents)
    pieces, gains_ref, refs = refs[3 : 3 + count], refs[3 + count], refs[4 + count :]
    outputs, packed_out, refs = refs[: count + 2], refs[count + 2], refs[count + 3 :]
    packed_ref, scratch = refs[0], refs[1:]
    work = GatherAll(spot, lents, 2, [*pieces, packed_ref, gains_ref], outputs, scratch)
    work.start()
    chosen = place_rows(rows_ref[0:1, :], packed_ref.shape[0])
    matmul_columns(packed_ref, chosen, tokens_ref)

    def one(hop, carry):
        work.exchange(hop, spot.half)

        @pl.when(hop == 0)
        def _():
            matmul_columns(packed_out, chosen, cotangent_ref)

        work.steps(hop, spot.half)
        return carry

    lax.fori_loop(0, spot.half, one, 0)
    work.finish()


def gather_shapes(shards, pieces, sent, shared):
    return (
        [
            jax.ShapeDtypeStruct((shards * piece.shape[0], piece.shape[1]), piece.dtype)
            for piece in pieces
        ]
        + [jax.ShapeDtypeStruct(rows.shape, rows.dtype) for rows in sent]
        + [
            jax.ShapeDtypeStruct((shards * each.shape[0], each.shape[1]), each.dtype)
            for each in shared
        ]
    )


def gather_call(shards, rows, tokens, cotangent, pieces, lents, gains, collective_id):
    anywhere = pl.BlockSpec(memory_space=pl.ANY)
    inside = pl.BlockSpec(memory_space=pltpu.VMEM)
    count = len(pieces)
    packed = jax.ShapeDtypeStruct((2 * tokens.shape[0], tokens.shape[1]), tokens.dtype)
    results = pl.pallas_call(
        functools.partial(gather_kernel, shards, lents),
        out_shape=[*gather_shapes(shards, pieces, [packed], [gains]), packed],
        in_specs=[inside] * 3 + [anywhere] * (count + 1),
        out_specs=[anywhere] * (count + 2) + [inside],
        scratch_shapes=[
            pltpu.VMEM(packed.shape, packed.dtype),
            *GatherAll.scratch(shards, count, 2),
        ],
        compiler_params=pltpu.CompilerParams(
            collective_id=collective_id, has_side_effects=True, vmem_limit_bytes=VMEM_LIMIT
        ),
    )(rows, tokens, cotangent, *pieces, gains)
    return results[:count], *results[count:]


class Reduce:
    def __init__(self, spot, lent, partial_ref, out_ref, refs, part=0, parts=1):
        self.spot, self.lent, self.partial, self.out = spot, lent, partial_ref, out_ref
        self.block_rows = partial_ref.shape[0] // spot.shards
        self.columns = partial_ref.shape[1]
        self.rows = self.block_rows // parts
        self.offset = part * self.rows
        self.unit = self.columns // 8
        self.kept = 8 - lent
        self.width = self.kept * self.unit
        (
            self.own,
            self.sib,
            self.got,
            self.own_far,
            self.sib_far,
            self.got_far,
            self.got_last,
        ) = refs[:7]
        sems = refs[7:]
        self.load_sem, self.load_far_sem = sems[0], sems[1]
        self.sib_sems, self.sib_far_sems = sems[2:4], sems[4:6]
        self.ring_sems, self.far_sems, self.last_sems = sems[6:8], sems[8:10], sems[10:12]
        self.out_sems = sems[12]

    @staticmethod
    def scratch(shards, lent, rows, columns):
        chips = shards // 2
        unit = columns // 8
        kept, lend = (8 - lent) * unit, lent * unit
        half = jnp.bfloat16
        buffers = [
            pltpu.VMEM((chips, rows, kept), half),
            pltpu.VMEM((chips, rows, kept), half),
            pltpu.VMEM((2, chips // 2, rows, kept), half),
            pltpu.VMEM((chips, rows, lend), half),
            pltpu.VMEM((chips, rows, lend), half),
            pltpu.VMEM((chips, rows, lend), half),
            pltpu.VMEM((rows, kept), half),
        ]
        sems = [DMA((chips,))] * 6 + [DMA((2, chips // 2))] * 2
        sems += [DMA((chips,))] * 2 + [DMA((1,))] * 2 + [DMA((2,))]
        return buffers + sems

    def owner(self, item, core):
        half = self.spot.half
        pair = (item + 1) // 2
        ahead = lax.rem(item, 2) == 1
        distance = half - pair
        place = jnp.where(ahead, self.spot.place + distance, self.spot.place - distance)
        return self.spot.block(place, core)

    def cut(self, item, core, first, count):
        columns = pl.ds(pl.multiple_of(first * self.unit, 128), count * self.unit)
        block = self.owner(item, core)
        first = pl.multiple_of(block * self.block_rows + self.offset, 16)
        return self.partial.at[pl.ds(first, self.rows), columns]

    def kept_cut(self, item, core):
        return self.cut(item, core, self.lent * self.spot.rep, self.kept)

    def lent_cut(self, item, core):
        return self.cut(item, core, self.kept * (1 - self.spot.rep), self.lent)

    def load(self, item):
        source = self.kept_cut(item, self.spot.core)
        return pltpu.make_async_copy(source, self.own.at[item], self.load_sem.at[item])

    def load_far(self, item):
        source = self.lent_cut(item, self.spot.core)
        return pltpu.make_async_copy(source, self.own_far.at[item], self.load_far_sem.at[item])

    def give(self, item):
        source = self.kept_cut(item, 1 - self.spot.core)
        target = (self.spot.rep, self.spot.sibling)
        return remote(source, self.sib.at[item], self.sib_sems, (item,), target)

    def give_far(self, item):
        source = self.lent_cut(item, 1 - self.spot.core)
        target = (self.spot.rep, self.spot.sibling)
        return remote(source, self.sib_far.at[item], self.sib_far_sems, (item,), target)

    def ring(self, way, step, short=False):
        item = 0 if short else 2 * step - 1 + way
        columns = pl.ds(way * self.width // 2, self.width // 2) if short else slice(None)
        return remote(
            self.own.at[item, :, columns],
            self.got.at[way, step, :, columns],
            self.ring_sems,
            (way, step),
            self.spot.ahead(way),
        )

    def far(self, item):
        target = (1 - self.spot.rep, self.spot.shard)
        return remote(
            self.own_far.at[item], self.got_far.at[item], self.far_sems, (item,), target
        )

    @staticmethod
    def out_shape(shards, lent, partial):
        rows, columns = partial.shape[0] // shards, partial.shape[1]
        return jax.ShapeDtypeStruct((2, rows, (8 - lent) * columns // 8), jnp.bfloat16)

    def last(self):
        target = (1 - self.spot.rep, self.spot.shard)
        source = self.own.at[self.spot.chips - 1]
        return remote(source, self.got_last, self.last_sems, (0,), target)

    def start(self, item):
        self.load_far(item).start()
        self.give_far(item).start()
        self.load(item).start()
        self.give(item).start()

    def tiles(self, width, body):
        chunk = width if width <= 768 else 512
        chunks = width // chunk

        def one(i, carry):
            tile, first = i // chunks, lax.rem(i, chunks) * chunk
            body(pl.ds(pl.multiple_of(tile * 16, 16), 16), first, chunk)
            return carry

        lax.fori_loop(0, self.rows // 16 * chunks, one, 0)

    def far_step(self, item):
        self.load_far(item).wait()
        self.give_far(item).wait_recv()

        def add(rows, first, count):
            at = pl.ds(pl.multiple_of(first, 128), count)
            total = self.own_far[item, rows, at].astype(jnp.float32)
            total += self.sib_far[item, rows, at].astype(jnp.float32)
            self.own_far[item, rows, at] = total.astype(jnp.bfloat16)

        self.tiles(self.lent * self.unit, add)
        self.far(item).start()

    def fold(self, item, extra=(), start=0, width=None):
        def add(rows, first, count):
            at = pl.ds(pl.multiple_of(start + first, 128), count)
            total = self.own[item, rows, at].astype(jnp.float32)
            total += self.sib[item, rows, at].astype(jnp.float32)
            for way, step in extra:
                total += self.got[way, step, rows, at].astype(jnp.float32)
            self.own[item, rows, at] = total.astype(jnp.bfloat16)

        self.tiles(self.width if width is None else width, add)

    def ready(self, item):
        self.load(item).wait()
        self.give(item).wait_recv()
        self.far(item).wait_recv()
        offset = self.spot.rep * (self.kept - self.lent) * self.unit

        def add(rows, first, count):
            at = pl.ds(pl.multiple_of(offset + first, 128), count)
            total = self.sib[item, rows, at].astype(jnp.float32)
            lent_at = pl.ds(pl.multiple_of(first, 128), count)
            total += self.got_far[item, rows, lent_at].astype(jnp.float32)
            self.sib[item, rows, at] = total.astype(jnp.bfloat16)

        self.tiles(self.lent * self.unit, add)

    def step(self, step):
        half, chips = self.spot.half, self.spot.chips

        @pl.when(step == 0)
        def _():
            self.ready(0)
            self.fold(0)
            for way in (0, 1):
                self.ring(way, 0, True).start()

        @pl.when((step > 0) & (step < half))
        def _():
            for way in (0, 1):
                item = 2 * step - 1 + way
                self.ready(item)

                @pl.when(step == 1)
                def _():
                    self.ring(way, 0, True).wait_recv()
                    middle = self.width // 2
                    self.fold(item, [(way, 0)], way * middle, middle)
                    self.fold(item, [], (1 - way) * middle, middle)

                @pl.when(step > 1)
                def _():
                    self.ring(way, step - 1).wait_recv()
                    self.fold(item, [(way, step - 1)])

                self.ring(way, step).start()

        @pl.when(step == half)
        def _():
            self.ready(chips - 1)
            for way in (0, 1):
                self.ring(way, half - 1).wait_recv()
            self.fold(chips - 1, [(0, half - 1), (1, half - 1)])
            self.last().start()

        @pl.when(step < half)
        def _():
            self.far_step(2 * step + 1)

            @pl.when(step < half - 1)
            def _():
                self.far_step(2 * step + 2)

    def finish(self):
        spot = self.spot
        rows = pl.ds(self.offset, self.rows)
        mine = pltpu.make_async_copy(
            self.own.at[spot.chips - 1], self.out.at[0, rows], self.out_sems.at[0]
        )
        mine.start()
        self.last().wait()
        theirs = pltpu.make_async_copy(
            self.got_last, self.out.at[1, rows], self.out_sems.at[1]
        )
        theirs.start()
        mine.wait()
        theirs.wait()

        def one(item, carry):
            self.give_far(item).wait_send()
            self.far(item).wait_send()
            self.give(item).wait_send()
            return carry

        lax.fori_loop(0, spot.chips, one, 0)
        for way in (0, 1):
            self.ring(way, 0, True).wait_send()

        def two(step, carry):
            for way in (0, 1):
                self.ring(way, step).wait_send()
            return carry

        lax.fori_loop(1, spot.half, two, 0)


class Tally:
    def __init__(self, spot, mine, out, refs):
        self.spot, self.mine, self.out = spot, mine, out
        self.got, self.half, self.other = refs[0:3]
        self.sems, self.own_sem, self.far_sems = refs[3:5], refs[5], refs[6:8]
        self.own = pltpu.make_async_copy(mine, self.got.at[spot.shard], self.own_sem)

    def copy(self, k):
        spot = self.spot
        target = lax.rem(spot.shard + k, spot.shards)
        return remote(self.mine, self.got.at[spot.shard], self.sems, (k,), (spot.rep, target))

    def far(self):
        target = (1 - self.spot.rep, self.spot.shard)
        return remote(self.half, self.other, self.far_sems, (0,), target)

    def start(self):
        def one(k, carry):
            self.copy(k).start()
            return carry

        lax.fori_loop(1, self.spot.shards, one, 0)
        self.own.start()

    def middle(self):
        def one(k, carry):
            self.copy(k).wait()
            return carry

        lax.fori_loop(1, self.spot.shards, one, 0)
        self.own.wait()

        def add(k, total):
            return total + self.got[k]

        self.half[...] = lax.fori_loop(0, self.spot.shards, add, jnp.zeros_like(self.half))
        self.far().start()

    def finish(self):
        self.far().wait()
        self.out[...] = self.half[...] + self.other[...]

    @staticmethod
    def scratch(shards, shape):
        full = jnp.float32
        return [
            pltpu.VMEM((shards, *shape), full),
            pltpu.VMEM(shape, full),
            pltpu.VMEM(shape, full),
            DMA((shards,)),
            DMA((shards,)),
            DMA,
            DMA((1,)),
            DMA((1,)),
        ]


def matmul(left, right, left_dim=1, right_dim=0):
    return lax.dot_general(
        left, right, (((left_dim,), (right_dim,)), ((), ())), preferred_element_type=jnp.float32
    )


def matmul_columns(out_ref, left, right_ref):
    def one(i, carry):
        at = pl.ds(pl.multiple_of(i * 512, 512), 512)
        part = matmul(left, right_ref[:, at].astype(jnp.bfloat16))
        out_ref[:, at] = part.astype(out_ref.dtype)
        return carry

    lax.fori_loop(0, out_ref.shape[1] // 512, one, 0)


def pick_rows(slot_column, slot_total):
    shape = (slot_column.shape[0], slot_total)
    return (slot_column == lax.broadcasted_iota(jnp.int32, shape, 1)).astype(jnp.bfloat16)


def place_rows(slot_row, slot_total):
    shape = (slot_total, slot_row.shape[1])
    return (slot_row == lax.broadcasted_iota(jnp.int32, shape, 0)).astype(jnp.bfloat16)


def assemble_kernel(rep_ref, *refs):
    raws, plain, refs = refs[:4], refs[4:6], refs[6:]
    plain_outs, outs, whole_ref = refs[:2], refs[2:9], refs[9]
    for source, target in zip(plain, plain_outs, strict=True):
        target[...] = source[...]
    for raw_ref, out_ref in zip(raws, [*outs[:3], whole_ref], strict=True):
        kept = raw_ref.shape[2]
        columns = out_ref.shape[1]
        lent = columns - kept

        def write(low, high, raw_ref=raw_ref, out_ref=out_ref, kept=kept, lent=lent):
            def part(which, first, count):
                return raw_ref[which, :, first : first + count].astype(jnp.float32)

            out_ref[:, 0:lent] = part(low, 0, lent)
            if kept > lent:
                out_ref[:, lent:kept] = part(low, lent, kept - lent) + part(high, 0, kept - lent)
            out_ref[:, kept:] = part(high, kept - lent, lent)

        @pl.when(rep_ref[0, 0] == 0)
        def _(write=write):
            write(0, 1)

        @pl.when(rep_ref[0, 0] != 0)
        def _(write=write):
            write(1, 0)

    width = outs[3].shape[1]
    for i in range(4):
        outs[3 + i][...] = whole_ref[:, i * width : (i + 1) * width]


def local_call(kernel, out_shape, inputs, spaces=None, scratch=()):
    inside = pl.BlockSpec(memory_space=pltpu.VMEM)
    return pl.pallas_call(
        kernel,
        out_shape=out_shape,
        in_specs=spaces or [inside] * len(inputs),
        out_specs=[inside] * len(out_shape),
        scratch_shapes=list(scratch),
        compiler_params=pltpu.CompilerParams(vmem_limit_bytes=VMEM_LIMIT),
    )(*inputs)


def segment_of(index, lengths_ref):
    first = lengths_ref[0, 0]
    second = first + lengths_ref[0, 1]
    third = second + lengths_ref[0, 2]
    return (
        (index >= first).astype(jnp.int32)
        + (index >= second).astype(jnp.int32)
        + (index >= third).astype(jnp.int32)
    )


def pair_masks(columns_ref, rows_ref, lengths_ref, same_ref, hidden_ref):
    size = columns_ref.shape[0]
    shape = (size, size)
    key_id = lax.broadcasted_iota(jnp.int32, shape, 0)
    query_id = lax.broadcasted_iota(jnp.int32, shape, 1)
    key_column = lax.broadcasted_iota(jnp.int32, (size, 1), 0)
    query_row = lax.broadcasted_iota(jnp.int32, (1, size), 1)
    together = segment_of(key_column, lengths_ref) == segment_of(query_row, lengths_ref)
    seen = together & ((columns_ref[:, 3:4] > 0) | (key_id == query_id))
    same_ref[...] = (columns_ref[:, 2:3] == rows_ref[2:3, :]).astype(jnp.float32)
    hidden_ref[...] = jnp.where(seen, 0.0, masked_score)


def turn(values, cosine, sine):
    width = values.shape[1]
    lane = lax.broadcasted_iota(jnp.int32, values.shape, 1)
    other = jnp.where(
        lane % 64 < 32, pltpu.roll(values, width - 32, 1), pltpu.roll(values, 32, 1)
    )
    return values * cosine + other * sine


def head_lanes(values, head):
    lane = lax.broadcasted_iota(jnp.int32, values.shape, 1)
    return jnp.where((lane < 64) == (head == 0), values, jnp.zeros_like(values))


def project(input_ref, weight_refs, cosine_ref, sine_ref, out_ref, scale):
    width = weight_refs[0].shape[0]
    cosine = jnp.concatenate([cosine_ref[...]] * 2, axis=1)
    sine = jnp.concatenate([sine_ref[...]] * 2, axis=1)

    def one(i, carry):
        def columns(part):
            return pl.ds(pl.multiple_of(part * width + i * 256, 256), 256)

        at = pl.ds(pl.multiple_of(i * 256, 256), 256)
        query = matmul(input_ref[...], weight_refs[0][:, at])
        out_ref[:, columns(0)] = (turn(query, cosine, sine) * scale).astype(jnp.bfloat16)
        key = matmul(input_ref[...], weight_refs[1][:, at])
        out_ref[:, columns(1)] = turn(key, cosine, sine).astype(jnp.bfloat16)
        out_ref[:, columns(2)] = matmul(input_ref[...], weight_refs[2][:, at]).astype(
            jnp.bfloat16
        )
        return carry

    lax.fori_loop(0, width // 256, one, 0)


def attend_pair(pair, width, heads_ref, bias_ref, same_ref, hidden_ref, out_ref, log_ref):
    def columns(part):
        return pl.ds(pl.multiple_of(part * width + pair * 128, 128), 128)

    query, key, value = (heads_ref[:, columns(part)] for part in range(3))
    total = None
    for which in (0, 1):
        head = 2 * pair + which
        gap = bias_ref[0, head] - bias_ref[1, head]
        scores = matmul(head_lanes(key, which), query, 1, 1)
        scores = scores + same_ref[...] * gap + hidden_ref[...]
        top = jnp.max(scores, axis=0, keepdims=True)
        weights = jnp.exp(scores - top)
        weight_sum = jnp.sum(weights, axis=0, keepdims=True)
        log_ref[pl.ds(head, 1), :] = top + jnp.log(weight_sum)
        soft = (weights * (1.0 / weight_sum)).astype(jnp.bfloat16)
        part = matmul(head_lanes(value, which), soft, 0, 0)
        total = part if total is None else total + part
    out_ref[:, pl.ds(pl.multiple_of(pair * 128, 128), 128)] = total.T.astype(jnp.bfloat16)


def normed(values):
    factor = lax.rsqrt(jnp.mean(values * values, axis=-1, keepdims=True) + epsilon)
    return values * factor, factor


def forward_body(refs, between, loaded):
    (
        arrived_ref, columns_ref, rows_ref, lengths_ref, bias_ref, gain_ref,
        query_w_ref, key_w_ref, value_w_ref, cosine_ref, sine_ref,
        stream_ref, input_ref, heads_ref, out_ref, log_ref,
        same_ref, hidden_ref,
    ) = refs
    width = gain_ref.shape[1]
    scale = 1.0 / math.sqrt(64)
    pair_masks(columns_ref, rows_ref, lengths_ref, same_ref, hidden_ref)
    chosen = pick_rows(columns_ref[:, 1:2], arrived_ref.shape[0])
    loaded(0)
    matmul_columns(stream_ref, chosen, arrived_ref)
    stream = stream_ref[...].astype(jnp.float32)
    input_ref[...] = (normed(stream)[0] * gain_ref[...]).astype(jnp.bfloat16)
    weight_refs = (query_w_ref, key_w_ref, value_w_ref)
    for i in (1, 2, 3):
        loaded(i)
    project(input_ref, weight_refs, cosine_ref, sine_ref, heads_ref, scale)

    def one(pair, carry):
        between(pair)
        attend_pair(pair, width, heads_ref, bias_ref, same_ref, hidden_ref, out_ref, log_ref)
        return carry

    lax.fori_loop(0, width // 128, one, 0)


def fold_lanes(row):
    folded = row[:, 0:128]
    for i in range(1, row.shape[1] // 128):
        folded += row[:, i * 128 : (i + 1) * 128]
    return folded


def square_into(stats_ref, at, values, columns_ref):
    valid = (columns_ref[:, 3:4] > 0).astype(jnp.float32)
    across = jnp.sum(values * values * valid, axis=0, keepdims=True)
    stats_ref[at : at + 1, :] = fold_lanes(across)


def attend_back_pair(
    pair, width, scale, heads_ref, do_ref, bias_ref, log_ref, same_ref, hidden_ref, cosine_ref,
    sine_ref, grads_ref, bias_same_ref, bias_all_ref,
):
    half = jnp.bfloat16

    def columns(part):
        return pl.ds(pl.multiple_of(part * width + pair * 128, 128), 128)

    query, key, value = (heads_ref[:, columns(part)] for part in range(3))
    grad_out = do_ref[:, columns(0)]
    query_t = key_grad = value_grad = None
    for which in (0, 1):
        head = 2 * pair + which
        gap = bias_ref[0, head] - bias_ref[1, head]
        key_part = head_lanes(key, which)
        scores = matmul(key_part, query, 1, 1)
        scores = scores + same_ref[...] * gap + hidden_ref[...]
        soft = jnp.exp(scores - log_ref[pl.ds(head, 1), :])
        grad_soft = matmul(head_lanes(value, which), grad_out, 1, 1)
        inner = jnp.sum(soft * grad_soft, axis=0, keepdims=True)
        grad_scores = (soft * (grad_soft - inner)).astype(half)
        wide = grad_scores.astype(jnp.float32)
        bias_all_ref[pl.ds(head, 1), :] = jnp.sum(wide, axis=0, keepdims=True)
        bias_same_ref[pl.ds(head, 1), :] = jnp.sum(wide * same_ref[...], axis=0, keepdims=True)
        parts = (
            matmul(key_part, grad_scores, 0, 0),
            matmul(grad_scores, head_lanes(query, which)),
            matmul(soft.astype(half), head_lanes(grad_out, which)),
        )
        if which == 0:
            query_t, key_grad, value_grad = parts
        else:
            query_t, key_grad, value_grad = (
                query_t + parts[0],
                key_grad + parts[1],
                value_grad + parts[2],
            )
    cosine, sine = cosine_ref[...], -sine_ref[...]
    grads_ref[:, columns(0)] = (turn(query_t.T, cosine, sine) * scale).astype(half)
    grads_ref[:, columns(1)] = turn(key_grad, cosine, sine).astype(half)
    grads_ref[:, columns(2)] = value_grad.astype(half)


def feed_forward(refs, weights, gates_out, ups_out, hidden_out, scratch, saves, between):
    columns_ref, rows_ref, gain_ref, stream_ref, attended_ref, out_w_ref = refs[:6]
    packed_ref, middle_ref, input_ref, stats_ref = refs[6:]
    (
        gate_buf, up_buf, down_buf, gates_buf, ups_buf, hidden_buf, mlp_ref,
        load_sems, store_sems,
    ) = scratch
    tile = gate_buf.shape[2]
    tiles = gates_out.shape[1] // tile
    half = jnp.bfloat16

    def at(i):
        return pl.ds(pl.multiple_of(i * tile, tile), tile)

    def loads(i):
        slot = lax.rem(i, 2)
        return [
            pltpu.make_async_copy(weights[0].at[:, at(i)], gate_buf.at[slot], load_sems.at[slot, 0]),
            pltpu.make_async_copy(weights[1].at[:, at(i)], up_buf.at[slot], load_sems.at[slot, 1]),
            pltpu.make_async_copy(weights[2].at[at(i)], down_buf.at[slot], load_sems.at[slot, 2]),
        ]

    def stores(i):
        slot = lax.rem(i, 2)
        return [
            pltpu.make_async_copy(gates_buf.at[slot], gates_out.at[:, at(i)], store_sems.at[slot, 0]),
            pltpu.make_async_copy(ups_buf.at[slot], ups_out.at[:, at(i)], store_sems.at[slot, 1]),
            pltpu.make_async_copy(
                hidden_buf.at[slot], hidden_out.at[:, at(i)], store_sems.at[slot, 2]
            ),
        ]

    for copy in loads(0):
        copy.start()
    stats_ref[...] = jnp.zeros_like(stats_ref)
    stream = stream_ref[...].astype(jnp.float32)
    square_into(stats_ref, 0, stream, columns_ref)
    matmul_columns(mlp_ref, attended_ref[...], out_w_ref)
    attn_out = mlp_ref[...]
    square_into(stats_ref, 1, attn_out, columns_ref)
    middle = stream + attn_out
    square_into(stats_ref, 2, middle, columns_ref)
    middle_ref[...] = middle
    input_ref[...] = (normed(middle)[0] * gain_ref[...]).astype(half)
    for copy in saves:
        copy.start()
    mlp_ref[...] = jnp.zeros_like(mlp_ref)

    def one(i, carry):
        slot = lax.rem(i, 2)
        between(i)
        for copy in loads(i):
            copy.wait()

        @pl.when(i + 1 < tiles)
        def _():
            for copy in loads(i + 1):
                copy.start()

        @pl.when(i >= 2)
        def _():
            for copy in stores(i - 2):
                copy.wait()

        gate = matmul(input_ref[...], gate_buf[slot])
        up = matmul(input_ref[...], up_buf[slot])
        gates_buf[slot] = gate
        ups_buf[slot] = up
        hidden = (gate * jax.nn.sigmoid(gate) * up).astype(half)
        hidden_buf[slot] = hidden
        for copy in stores(i):
            copy.start()
        mlp_ref[...] += matmul(hidden, down_buf[slot])
        return carry

    lax.fori_loop(0, tiles, one, 0)
    valid = (columns_ref[:, 3:4] > 0).astype(jnp.float32)
    mlp_out = mlp_ref[...]
    result = middle_ref[...] + mlp_out
    placed = place_rows(rows_ref[1:2, :], packed_ref.shape[0])
    mlp_ref[...] = result
    matmul_columns(packed_ref, placed, mlp_ref)
    square_into(stats_ref, 3, mlp_out, columns_ref)
    square_into(stats_ref, 4, result, columns_ref)
    lane = lax.broadcasted_iota(jnp.int32, (valid.shape[0], 128), 1)
    stats_ref[5:6, :] = jnp.sum(jnp.where(lane == 0, valid, 0.0), axis=0, keepdims=True)
    for i in (tiles - 2, tiles - 1):
        for copy in stores(i):
            copy.wait()


def forward_gather_kernel(shards, lents, swap_count, compute_counts, *refs):
    ins, outs = compute_counts
    total = len(lents) + swap_count
    in_refs, refs = refs[: ins + total], refs[ins + total :]
    out_refs, refs = refs[: outs + total], refs[outs + total :]
    masks, out_w_buf, out_w_sem, feed_scratch, staged, sems, scratch = (
        refs[:2], refs[2], refs[3], refs[4:13], refs[13:24], refs[24:26], refs[26:],
    )
    work = GatherAll(
        Spot(shards), lents, swap_count, in_refs[ins:], out_refs[outs:], scratch
    )
    work.start()
    *attend_ins, gain_mlp_ref = in_refs[:ins]
    arriving, leaving = staged[:4], staged[4:]
    loads = [
        pltpu.make_async_copy(attend_ins[at], arriving[i], sems[0].at[i])
        for i, at in enumerate((0, 6, 7, 8))
    ]
    for copy in loads:
        copy.start()
    attend_ins[0], attend_ins[6:9] = arriving[0], arriving[1:4]
    attend_outs, feed_outs = leaving[:5], [*out_refs[5:9], *leaving[5:], out_refs[outs - 1]]
    saves = [
        pltpu.make_async_copy(leaving[i], out_refs[at], sems[1].at[i])
        for i, at in enumerate((0, 1, 2, 3, 4, 9, 10))
    ]
    pairs = attend_ins[5].shape[1] // 128

    tiles = out_refs[5].shape[1] // feed_scratch[0].shape[2]

    def between(pair):
        work.exchange(pair, pairs + tiles)
        work.steps(pair, pairs)

    forward_body(
        (*attend_ins, *attend_outs, *masks), between, lambda i: loads[i].wait()
    )
    for copy in saves[:5]:
        copy.start()
    work.finish_gathers()
    full_refs = out_refs[outs:]
    copy = pltpu.make_async_copy(full_refs[0], out_w_buf, out_w_sem)
    copy.start()
    copy.wait()
    gates_out, ups_out, hidden_out, *feed_outs = feed_outs
    feed_forward(
        (
            attend_ins[1], attend_ins[2], gain_mlp_ref, attend_outs[0], attend_outs[3], out_w_buf,
            *feed_outs,
        ),
        full_refs[1:4], gates_out, ups_out, hidden_out, feed_scratch, saves[5:],
        lambda i: work.exchange(pairs + i, pairs + tiles),
    )
    for copy in saves:
        copy.wait()
    for swap in work.swaps:
        swap.finish()


def forward_gather_call(
    shards, inputs, spaces, out_shape, out_specs, pieces, lents, sent, collective_id
):
    anywhere = pl.BlockSpec(memory_space=pl.ANY)
    tokens, width = out_shape[0].shape
    tile = 512
    half, full = jnp.bfloat16, jnp.float32
    counts = (len(inputs), len(out_shape))
    comm = len(pieces) + len(sent)
    results = pl.pallas_call(
        functools.partial(forward_gather_kernel, shards, lents, len(sent), counts),
        out_shape=[*out_shape, *gather_shapes(shards, pieces, sent, [])],
        in_specs=spaces + [anywhere] * comm,
        out_specs=out_specs + [anywhere] * comm,
        scratch_shapes=[
            pltpu.VMEM((tokens, tokens), full),
            pltpu.VMEM((tokens, tokens), full),
            pltpu.VMEM((width, width), half),
            DMA,
            pltpu.VMEM((2, width, tile), half),
            pltpu.VMEM((2, width, tile), half),
            pltpu.VMEM((2, tile, width), half),
            pltpu.VMEM((2, tokens, tile), full),
            pltpu.VMEM((2, tokens, tile), full),
            pltpu.VMEM((2, tokens, tile), half),
            pltpu.VMEM((tokens, width), full),
            DMA((2, 3)),
            DMA((2, 3)),
            *[pltpu.VMEM(inputs[at].shape, half) for at in (0, 6, 7, 8)],
            *[
                pltpu.VMEM(out_shape[at].shape, out_shape[at].dtype)
                for at in (0, 1, 2, 3, 4, 9, 10)
            ],
            DMA((4,)),
            DMA((7,)),
            *GatherAll.scratch(shards, len(pieces), len(sent)),
        ],
        compiler_params=pltpu.CompilerParams(
            collective_id=collective_id, has_side_effects=True, vmem_limit_bytes=VMEM_LIMIT
        ),
    )(*inputs, *pieces, *sent)
    first = len(out_shape)
    second = first + len(pieces)
    return results[:first], results[first:second], results[second:]


def input_grad_kernel(shards, lent, *refs):
    (
        columns_ref, rows_ref, lengths_ref, bias_ref, gain_mlp_ref, gain_attn_ref, middle_ref,
        out_w_ref, arrived_ref, heads_ref, log_ref, cosine_ref, sine_ref, stream_ref,
        query_w_ref, key_w_ref, value_w_ref, packed_out_ref, gates_ref, ups_ref, rows_mlp_ref,
        gate_w_ref, up_w_ref, down_w_ref,
        grads_ref, packed_ref, stats_ref, grad_down_ref,
        grad_gate_ref, grad_up_ref, home_ref, partial_ref,
        gates_buf, ups_buf, gate_buf, up_buf, down_buf, grad_gate_buf, grad_up_buf,
        back_ref, dh_ref, do_ref, same_ref, hidden_ref, bias_same_ref, bias_all_ref,
        load_sems, store_sems, weight_sems, send_sems, recv_sems, own_sem,
    ) = refs[:52]
    staged, in_sems, out_sem, refs = refs[52:59], refs[59], refs[60], refs[61:]
    arriving = [
        pltpu.make_async_copy(source, buffer, in_sems.at[i])
        for i, (source, buffer) in enumerate(
            zip(
                (arrived_ref, out_w_ref, middle_ref, heads_ref, cosine_ref, sine_ref, stream_ref),
                staged,
                strict=True,
            )
        )
    ]
    arrived_ref, out_w_ref, middle_ref, heads_ref, cosine_ref, sine_ref, stream_ref = staged
    saved_ref, grads_ref = grads_ref, refs[0]
    dy_ref, refs = refs[1], refs[2:]
    save = pltpu.make_async_copy(grads_ref, saved_ref, out_sem)
    spot = Spot(shards)
    swap = Swap(spot, packed_out_ref, home_ref, (send_sems, recv_sems), own_sem)
    reduces = [
        Reduce(spot, lent, partial_ref, grad_down_ref, refs[20 * g : 20 * g + 20], g, 2)
        for g in (0, 1)
    ]
    tile = gate_buf.shape[2]
    tiles = gates_ref.shape[1] // tile
    width = gain_attn_ref.shape[1]
    half = jnp.bfloat16

    def at(i):
        return pl.ds(pl.multiple_of(i * tile, tile), tile)

    def loads(i):
        slot = lax.rem(i, 2)
        pairs = [
            (gates_ref.at[:, at(i)], gates_buf),
            (ups_ref.at[:, at(i)], ups_buf),
            (gate_w_ref.at[:, at(i)], gate_buf),
            (up_w_ref.at[:, at(i)], up_buf),
            (down_w_ref.at[at(i)], down_buf),
        ]
        return [
            pltpu.make_async_copy(source, buffer.at[slot], load_sems.at[slot, j])
            for j, (source, buffer) in enumerate(pairs)
        ]

    def stores(i):
        slot = lax.rem(i, 2)
        pairs = [(grad_gate_buf, grad_gate_ref), (grad_up_buf, grad_up_ref)]
        return [
            pltpu.make_async_copy(buffer.at[slot], target.at[:, at(i)], store_sems.at[slot, j])
            for j, (buffer, target) in enumerate(pairs)
        ]

    def row_loads(i):
        slot = lax.rem(i, 2)
        return [
            pltpu.make_async_copy(
                rows_mlp_ref.at[:, at(i)], grad_gate_buf.at[slot], load_sems.at[slot, 0]
            )
        ]

    def row_stores(i):
        slot = lax.rem(i, 2)
        return [
            pltpu.make_async_copy(
                down_buf.at[slot], partial_ref.at[at(i)], store_sems.at[slot, 0]
            )
        ]

    pairs = width // 128
    slots = tiles + pairs
    steps = spot.half + 1

    def reduce_steps(slot):
        def one(step, carry):
            for reduce in reduces:
                reduce.step(step)
            return carry

        lax.fori_loop(slot * steps // slots, (slot + 1) * steps // slots, one, 0)

    greet(spot)
    for copy in [arriving[0], *row_loads(0), *arriving[1:]]:
        copy.start()
    chosen = pick_rows(columns_ref[:, 1:2], arrived_ref.shape[0])
    arriving[0].wait()
    matmul_columns(dy_ref, chosen, arrived_ref)

    def rows_step(i, carry):
        slot = lax.rem(i, 2)
        for copy in row_loads(i):
            copy.wait()

        @pl.when(i + 1 < tiles)
        def _():
            for copy in row_loads(i + 1):
                copy.start()

        @pl.when(i >= 2)
        def _():
            for copy in row_stores(i - 2):
                copy.wait()

        down_buf[slot] = matmul(grad_gate_buf[slot], dy_ref[...], 0, 0).astype(half)
        for copy in row_stores(i):
            copy.start()
        return carry

    lax.fori_loop(0, tiles, rows_step, 0)
    for i in (tiles - 2, tiles - 1):
        for copy in row_stores(i):
            copy.wait()
    for copy in loads(0):
        copy.start()

    def begin(item, carry):
        for reduce in reduces:
            reduce.start(item)
        return carry

    lax.fori_loop(0, spot.chips, begin, 0)
    back_ref[...] = jnp.zeros_like(back_ref)
    pair_masks(columns_ref, rows_ref, lengths_ref, same_ref, hidden_ref)
    for reduce in reduces:
        reduce.far_step(0)

    def one(i, carry):
        slot = lax.rem(i, 2)

        swap.start(i, slots)
        reduce_steps(i)
        for copy in loads(i):
            copy.wait()

        @pl.when(i + 1 < tiles)
        def _():
            for copy in loads(i + 1):
                copy.start()

        @pl.when(i >= 2)
        def _():
            for copy in stores(i - 2):
                copy.wait()

        gate, up = gates_buf[slot], ups_buf[slot]
        grad_hidden = matmul(dy_ref[...], down_buf[slot], 1, 1)
        sigmoid = jax.nn.sigmoid(gate)
        grad_gate = (grad_hidden * up * sigmoid * (1.0 + gate * (1.0 - sigmoid))).astype(half)
        grad_up = (grad_hidden * gate * sigmoid).astype(half)
        grad_gate_buf[slot] = grad_gate
        grad_up_buf[slot] = grad_up
        for copy in stores(i):
            copy.start()
        back_ref[...] += matmul(grad_gate, gate_buf[slot], 1, 1) + matmul(
            grad_up, up_buf[slot], 1, 1
        )
        return carry

    lax.fori_loop(0, tiles, one, 0)
    for copy in arriving[1:]:
        copy.wait()
    stats_ref[...] = jnp.zeros_like(stats_ref)

    def through_norm(values, grad, gain_ref, first):
        entry, factor = normed(values)
        gain_grad = jnp.sum(grad * entry, axis=0, keepdims=True)
        for i in range(width // 128):
            stats_ref[first + i : first + i + 1, :] = gain_grad[:, i * 128 : (i + 1) * 128]
        scaled = grad * gain_ref[...]
        inner = jnp.mean(scaled * entry, axis=-1, keepdims=True)
        return factor * (scaled - entry * inner)

    dh = dy_ref[...].astype(jnp.float32) + through_norm(
        middle_ref[...], back_ref[...], gain_mlp_ref, 0
    )
    dh_ref[...] = dh
    branch = dh.astype(half)
    grads_ref[:, pl.ds(3 * width, width)] = branch

    def back_out(i, carry):
        at = pl.ds(pl.multiple_of(i * 256, 256), 256)
        do_ref[:, at] = matmul(
            grads_ref[:, pl.ds(3 * width, width)], out_w_ref[at, :], 1, 1
        ).astype(half)
        return carry

    lax.fori_loop(0, width // 256, back_out, 0)
    scale = 1.0 / math.sqrt(64)
    for i in (tiles - 2, tiles - 1):
        for copy in stores(i):
            copy.wait()
    halves = [pl.ds(0, tile), pl.ds(tile, tile)]

    def weight_loads(source, buffer, which):
        return [
            pltpu.make_async_copy(source.at[:, columns], buffer.at[j], weight_sems.at[which, j])
            for j, columns in enumerate(halves)
        ]

    for copy in weight_loads(query_w_ref, gate_buf, 0) + weight_loads(key_w_ref, up_buf, 1):
        copy.start()

    def two(pair, carry):
        swap.start(tiles + pair, slots)
        reduce_steps(tiles + pair)
        attend_back_pair(
            pair, width, scale, heads_ref, do_ref, bias_ref, log_ref, same_ref, hidden_ref,
            cosine_ref, sine_ref, grads_ref, bias_same_ref, bias_all_ref,
        )
        return carry

    lax.fori_loop(0, width // 128, two, 0)
    save.start()
    heads = bias_all_ref.shape[0]
    lane = lax.broadcasted_iota(jnp.int32, (heads, 128), 1)
    row = lax.broadcasted_iota(jnp.int32, (heads, 128), 0)
    same = jnp.sum(bias_same_ref[...], axis=1, keepdims=True)
    other = jnp.sum(bias_all_ref[...], axis=1, keepdims=True) - same
    stats_ref[16:17, :] = jnp.sum(
        jnp.where(lane == row, same, 0.0) + jnp.where(lane == row + heads, other, 0.0),
        axis=0,
        keepdims=True,
    )
    def through(buffer, first):
        def one(j, carry):
            at = pl.ds(pl.multiple_of(first + j * tile, tile), tile)
            back_ref[...] += matmul(grads_ref[:, at], buffer[j], 1, 1)
            return carry

        lax.fori_loop(0, 2, one, 0)

    back_ref[...] = jnp.zeros_like(back_ref)

    for copy in weight_loads(query_w_ref, gate_buf, 0):
        copy.wait()
    through(gate_buf, 0)
    for copy in weight_loads(value_w_ref, gate_buf, 0):
        copy.start()
    for copy in weight_loads(key_w_ref, up_buf, 1):
        copy.wait()
    through(up_buf, width)
    for copy in weight_loads(value_w_ref, gate_buf, 0):
        copy.wait()
    through(gate_buf, 2 * width)
    grad_stream = dh_ref[...] + through_norm(
        stream_ref[...].astype(jnp.float32), back_ref[...], gain_attn_ref, 8
    )
    placed = place_rows(rows_ref[1:2, :], packed_ref.shape[0])
    dh_ref[...] = grad_stream
    matmul_columns(packed_ref, placed, dh_ref)
    save.wait()
    swap.finish()
    for reduce in reduces:
        reduce.finish()


def input_grad_call(shards, inputs, spaces, far_inputs, lent, collective_id):
    anywhere = pl.BlockSpec(memory_space=pl.ANY)
    inside = pl.BlockSpec(memory_space=pltpu.VMEM)
    packed, gates = far_inputs[3], far_inputs[4]
    tokens, hidden = gates.shape
    width = packed.shape[1]
    heads = inputs[10].shape[0]
    tile = 512
    assert 2 * tile == width
    half, full = jnp.bfloat16, jnp.float32
    vmem, shape = pltpu.VMEM, jax.ShapeDtypeStruct
    return pl.pallas_call(
        functools.partial(input_grad_kernel, shards, lent),
        out_shape=[
            shape((tokens, 4 * width), half),
            shape(packed.shape, half),
            shape((24, 128), full),
            Reduce.out_shape(shards, lent, shape((hidden, width), half)),
            shape((tokens, hidden), half),
            shape((tokens, hidden), half),
            shape(packed.shape, half),
            shape((hidden, width), half),
        ],
        in_specs=[*spaces, *[anywhere] * len(far_inputs)],
        out_specs=[anywhere] + [inside] * 2 + [anywhere] * 5,
        scratch_shapes=[
            vmem((2, tokens, tile), full),
            vmem((2, tokens, tile), full),
            vmem((2, width, tile), half),
            vmem((2, width, tile), half),
            vmem((2, tile, width), half),
            vmem((2, tokens, tile), half),
            vmem((2, tokens, tile), half),
            vmem((tokens, width), full),
            vmem((tokens, width), full),
            vmem((tokens, width), half),
            vmem((tokens, tokens), full),
            vmem((tokens, tokens), full),
            vmem((heads, tokens), full),
            vmem((heads, tokens), full),
            DMA((2, 5)),
            DMA((2, 2)),
            DMA((2, 2)),
            DMA((shards,)),
            DMA((shards,)),
            DMA,
            *[vmem(inputs[at].shape, inputs[at].dtype) for at in (8, 7, 6, 9, 11, 12, 13)],
            DMA((7,)),
            DMA,
            vmem((tokens, 4 * width), half),
            vmem((tokens, width), half),
            *Reduce.scratch(shards, lent, hidden // shards // 2, width) * 2,
        ],
        compiler_params=pltpu.CompilerParams(
            collective_id=collective_id, has_side_effects=True, vmem_limit_bytes=VMEM_LIMIT
        ),
    )(*inputs, *far_inputs)


def weight_grad_kernel(shards, lents, *refs):
    (
        columns_ref, input_attn_ref, attended_ref, input_mlp_ref, stats_forward_ref,
        stats_back_ref, home_out_ref, packed_ref, gate_ref, up_ref, entry_ref,
        grad_gate_ref, grad_up_ref, grad_in_ref, output_ref, input_grad_ref, sums_ref,
    ) = refs[:17]
    partials = refs[17:20]
    (
        attn_t_ref, attended_t_ref, mlp_t_ref, home_ref, stats_ref, tile_buf, part_buf,
        load_sems, store_sems, send_sems, recv_sems, own_sem,
    ) = refs[20:32]
    tally_refs, refs = refs[32:40], refs[40:]
    half, full = jnp.bfloat16, jnp.float32
    spot = Spot(shards)
    swap = Swap(spot, packed_ref, home_ref, (send_sems, recv_sems), own_sem)
    tally = Tally(spot, stats_ref, sums_ref, tally_refs)
    outputs = (grad_gate_ref, grad_up_ref, grad_in_ref)
    reduces = [
        Reduce(spot, lents[g], partials[g], outputs[g], refs[20 * g : 20 * g + 20])
        for g in range(3)
    ]
    steps = spot.half + 1
    parts = 5
    tile = tile_buf.shape[2]
    tiles = gate_ref.shape[1] // tile

    def at(i):
        return pl.ds(pl.multiple_of(i * tile, tile), tile)

    def product(source, lefts, partial, reduce):
        def load(i):
            slot = lax.rem(i, 2)
            return pltpu.make_async_copy(
                source.at[:, at(i)], tile_buf.at[slot], load_sems.at[slot]
            )

        def store(i):
            slot = lax.rem(i, 2)
            return pltpu.make_async_copy(
                part_buf.at[slot], partial.at[:, at(i)], store_sems.at[slot]
            )

        load(0).start()
        first = 0
        for left, count in lefts:

            def one(i, carry, left=left):
                slot = lax.rem(i, 2)
                load(i).wait()

                @pl.when(i + 1 < tiles)
                def _():
                    load(i + 1).start()

                @pl.when(i >= 2)
                def _():
                    store(i - 2).wait()

                part_buf[slot] = matmul(left[...], tile_buf[slot]).astype(half)
                store(i).start()
                return carry

            lax.fori_loop(first, first + count, one, 0)
            first += count
        for i in (tiles - 2, tiles - 1):
            store(i).wait()

        def begin(item, carry):
            reduce.start(item)
            return carry

        lax.fori_loop(0, spot.chips, begin, 0)
        reduce.far_step(0)

    greet(spot)
    swap.start(0, parts)
    stats_ref[0:8, :] = stats_forward_ref[...]
    stats_ref[8:32, :] = stats_back_ref[...]
    tally.start()
    mlp_t_ref[...] = input_mlp_ref[...].astype(full).T.astype(half)
    product(gate_ref, [(mlp_t_ref, tiles)], partials[0], reduces[0])
    swap.start(1, parts)
    product(up_ref, [(mlp_t_ref, tiles)], partials[1], reduces[1])
    swap.start(2, parts)
    chosen = pick_rows(columns_ref[:, 0:1], home_ref.shape[0])

    def ticks(tick, carry):
        @pl.when(tick < steps)
        def _():
            reduces[0].step(tick)

        @pl.when(tick < 2)
        def _():
            swap.start(3 + tick, parts)

        @pl.when(tick == 0)
        def _():
            attn_t_ref[...] = input_attn_ref[...].astype(full).T.astype(half)
            attended_t_ref[...] = attended_ref[...].astype(full).T.astype(half)
            product(
                entry_ref,
                [(attn_t_ref, tiles - tiles // 4), (attended_t_ref, tiles // 4)],
                partials[2],
                reduces[2],
            )

        @pl.when((tick > 0) & (tick < steps + 1))
        def _():
            reduces[1].step(tick - 1)

        @pl.when(tick == 1)
        def _():
            matmul_columns(output_ref, chosen, home_out_ref)
            tally.middle()

        @pl.when(tick > 1)
        def _():
            reduces[2].step(tick - 2)

        return carry

    lax.fori_loop(0, steps + 2, ticks, 0)
    swap.finish()
    matmul_columns(input_grad_ref, chosen, home_ref)
    tally.finish()
    for reduce in reduces:
        reduce.finish()


def weight_grad_call(shards, inputs, far_inputs, lents, collective_id):
    tile = 512
    packed, hidden = far_inputs[0], far_inputs[1].shape[1]
    tokens, width = inputs[1].shape
    assert hidden == 4 * width
    half, full = jnp.bfloat16, jnp.float32
    shape = jax.ShapeDtypeStruct
    anywhere = pl.BlockSpec(memory_space=pl.ANY)
    inside = pl.BlockSpec(memory_space=pltpu.VMEM)
    scratch = []
    for lent in lents:
        scratch += Reduce.scratch(shards, lent, width // shards, hidden)
    results = pl.pallas_call(
        functools.partial(weight_grad_kernel, shards, lents),
        out_shape=[
            *[Reduce.out_shape(shards, lent, shape((width, hidden), half)) for lent in lents],
            shape((tokens, width), half),
            shape((tokens, width), half),
            shape((32, 128), full),
            *[shape((width, hidden), half)] * 3,
        ],
        in_specs=[inside] * len(inputs) + [anywhere] * len(far_inputs),
        out_specs=[anywhere] * 3 + [inside] * 3 + [anywhere] * 3,
        scratch_shapes=[
            *[pltpu.VMEM((width, tokens), half)] * 3,
            pltpu.VMEM(packed.shape, half),
            pltpu.VMEM((32, 128), full),
            pltpu.VMEM((2, tokens, tile), half),
            pltpu.VMEM((2, width, tile), half),
            DMA((2,)),
            DMA((2,)),
            DMA((shards,)),
            DMA((shards,)),
            DMA,
            *Tally.scratch(shards, (32, 128)),
            *scratch,
        ],
        compiler_params=pltpu.CompilerParams(
            collective_id=collective_id, has_side_effects=True, vmem_limit_bytes=VMEM_LIMIT
        ),
    )(*inputs, *far_inputs)
    return results[:6]


def on_device(
    tokens,
    cotangent,
    send_slot,
    recv_slot,
    lengths,
    variate,
    valid_mask,
    norm_attn,
    w_query,
    w_key,
    w_value,
    w_out,
    variate_bias,
    norm_mlp,
    w_gate,
    w_up,
    w_down,
):
    shards = lax.axis_size("shard")
    tok_rows, width = tokens.shape
    slot_total = 2 * tok_rows
    heads = variate_bias.shape[1]
    half, full = jnp.bfloat16, jnp.float32
    share = width // shards
    indices = jnp.stack([send_slot, recv_slot, variate, valid_mask])
    rows = jnp.concatenate([indices, jnp.zeros_like(indices)])
    columns = rows.T
    _, position = layout(lengths[0], tok_rows)
    cosine, sine = angle_tables(position, width // heads)
    cosine = jnp.concatenate([cosine] * 4, axis=1)
    sine = jnp.concatenate([-sine, sine] * 2, axis=1)
    gains = jnp.stack([norm_attn, norm_mlp]).astype(full)
    gains = jnp.pad(gains, ((0, 6), (0, 128 - share)))
    shape = jax.ShapeDtypeStruct
    packed_shape = shape((slot_total, width), half)
    token_shape = shape((tok_rows, width), half)
    full_in, arrived_tokens, gains, out_cotangent = gather_call(
        shards, rows, tokens, cotangent, [w_query, w_key, w_value], (4, 4, 4), gains, 1
    )
    gains = gains.reshape(shards, 8, 128)
    gain_attn = gains[:, 0, :share].reshape(1, width)
    gain_mlp = gains[:, 1, :share].reshape(1, width)
    inside = pl.BlockSpec(memory_space=pltpu.VMEM)
    anywhere = pl.BlockSpec(memory_space=pl.ANY)
    scalar = pl.BlockSpec(memory_space=pltpu.SMEM)
    hidden = w_gate.shape[1]
    (
        (
            stream, input_attn, head_rows, attended, logs,
            gates, ups, hidden_rows, packed, middle, input_mlp, stats_forward,
        ),
        (full_out, full_gate, full_up, full_down),
        (arrived_grads,),
    ) = forward_gather_call(
        shards,
        [
            arrived_tokens, columns, rows, lengths, variate_bias, gain_attn, *full_in,
            cosine, sine, gain_mlp,
        ],
        [anywhere] + [inside] * 2 + [scalar] * 2 + [inside] + [anywhere] * 3 + [inside] * 3,
        [
            token_shape,
            token_shape,
            shape((tok_rows, 3 * width), half),
            token_shape,
            shape((heads, tok_rows), full),
            shape((tok_rows, hidden), full),
            shape((tok_rows, hidden), full),
            shape((tok_rows, hidden), half),
            packed_shape,
            shape((tok_rows, width), full),
            token_shape,
            shape((8, 128), full),
        ],
        [anywhere] * 8 + [inside] + [anywhere] * 2 + [inside],
        [w_out, w_gate, w_up, w_down],
        (2, 4, 2, 2),
        [out_cotangent],
        2,
    )
    (
        entry_grads, packed_grad, stats_back, grad_down, grad_gates, grad_ups, home_out, _,
    ) = input_grad_call(
        shards,
        [
            columns, rows, lengths, variate_bias, gain_mlp, gain_attn, middle, full_out,
            arrived_grads, head_rows, logs, cosine, sine, stream,
        ],
        [inside] * 2
        + [scalar] * 2
        + [inside] * 2
        + [anywhere] * 4
        + [inside]
        + [anywhere] * 3,
        [*full_in, packed, gates, ups, hidden_rows, full_gate, full_up, full_down],
        4,
        3,
    )
    grad_gate, grad_up, grad_in, output, input_grad, sums = weight_grad_call(
        shards,
        [columns, input_attn, attended, input_mlp, stats_forward, stats_back, home_out],
        [packed_grad, grad_gates, grad_ups, entry_grads],
        (4, 2, 2),
        4,
    )
    rep = lax.axis_index("rep").astype(jnp.int32).reshape(1, 1)
    (
        output, input_grad, grad_gate, grad_up, grad_down,
        grad_query, grad_key, grad_value, grad_out,
    ) = local_call(
        assemble_kernel,
        [
            token_shape,
            token_shape,
            *[shape((share, hidden), full)] * 2,
            shape((hidden // shards, width), full),
            *[shape((share, width), full)] * 4,
        ],
        [rep, grad_gate, grad_up, grad_down, grad_in, output, input_grad],
        [scalar] + [inside] * 6,
        [pltpu.VMEM((share, hidden), full)],
    )
    squares = jnp.sum(sums[0:6], axis=1)
    root_means = jnp.sqrt(squares[:5] / (squares[5] * width))
    share_start = lax.axis_index("shard") * share
    grad_norm_mlp = lax.dynamic_slice_in_dim(sums[8:16].reshape(-1), share_start, share)
    grad_norm_attn = lax.dynamic_slice_in_dim(sums[16:24].reshape(-1), share_start, share)
    bias_grads = sums[24, : 2 * heads].reshape(2, heads)
    return (
        output,
        input_grad,
        grad_norm_attn,
        grad_query,
        grad_key,
        grad_value,
        grad_out,
        bias_grads,
        grad_norm_mlp,
        grad_gate,
        grad_up,
        grad_down,
        root_means,
    )


def solution(mesh):
    in_specs = (
        P(("rep", "shard"), None),
        P(("rep", "shard"), None),
        P(("rep", "shard")),
        P(("rep", "shard")),
        P(("rep", "shard"), None),
        P(("rep", "shard")),
        P(("rep", "shard")),
        P("shard"),
        P("shard", None),
        P("shard", None),
        P("shard", None),
        P("shard", None),
        P(),
        P("shard"),
        P("shard", None),
        P("shard", None),
        P("shard", None),
    )
    out_specs = (
        P(("rep", "shard"), None),
        P(("rep", "shard"), None),
        P("shard"),
        P("shard", None),
        P("shard", None),
        P("shard", None),
        P("shard", None),
        P(),
        P("shard"),
        P("shard", None),
        P("shard", None),
        P("shard", None),
        P(),
    )
    return jax.shard_map(
        on_device, mesh=mesh, in_specs=in_specs, out_specs=out_specs, check_vma=False
    )
```

```python
import functools
import math

import jax
import jax.numpy as jnp
import numpy as np
from jax import lax
from jax.experimental import pallas as pl
from jax.experimental.pallas import tpu as pltpu
from jax.sharding import PartitionSpec as P

MESH = pl.DeviceIdType.MESH
DMA = pltpu.SemaphoreType.DMA
epsilon = 1e-06
masked_score = -1e30
VMEM_LIMIT = 62 << 20


def ring_place(chip, chips):
    return jnp.where(chip % 2 == 0, chip // 2, chips - 1 - chip // 2)


def ring_chip(place, chips):
    wrapped = lax.rem(place + 2 * chips, chips)
    return jnp.where(wrapped < chips // 2, 2 * wrapped, 2 * (chips - 1 - wrapped) + 1)


class Spot:
    def __init__(self, shards):
        self.shards = shards
        self.chips = shards // 2
        self.half = self.chips // 2
        self.rep = lax.axis_index("rep")
        self.shard = lax.axis_index("shard")
        self.core = lax.rem(self.shard, 2)
        self.place = ring_place(self.shard // 2, self.chips)
        self.sibling = self.shard + 1 - 2 * self.core

    def block(self, place, core=None):
        return 2 * ring_chip(place, self.chips) + (self.core if core is None else core)

    def along(self, way, distance):
        return self.place - distance if way == 0 else self.place + distance

    def ahead(self, way):
        return (self.rep, self.block(self.along(way, -1)))


def greet(spot):
    barrier = pltpu.get_barrier_semaphore()

    def peer(k, carry):
        target = lax.rem(spot.shard + k, spot.shards)
        pl.semaphore_signal(barrier, inc=1, device_id=(spot.rep, target), device_id_type=MESH)
        return carry

    lax.fori_loop(1, spot.shards, peer, 0)
    pl.semaphore_signal(
        barrier, inc=1, device_id=(1 - spot.rep, spot.shard), device_id_type=MESH
    )
    pl.semaphore_wait(barrier, spot.shards)


def remote(src, dst, sems, at, target):
    return pltpu.make_async_remote_copy(
        src_ref=src,
        dst_ref=dst,
        send_sem=sems[0].at[at],
        recv_sem=sems[1].at[at],
        device_id=target,
        device_id_type=MESH,
    )


class Swap:
    def __init__(self, spot, source, arrived, sems, own_sem):
        self.spot, self.sems = spot, sems
        self.source, self.arrived = source, arrived
        self.capacity = arrived.shape[0] // spot.shards
        self.own = pltpu.make_async_copy(
            self.part(spot.shard), arrived.at[self.rows(spot.shard)], own_sem
        )

    def rows(self, shard):
        return pl.ds(pl.multiple_of(shard * self.capacity, 8), self.capacity)

    def part(self, shard):
        if self.source.shape[0] == self.capacity:
            return self.source
        return self.source.at[self.rows(shard)]

    def copy(self, k):
        spot = self.spot
        target = lax.rem(spot.shard + 7 * k, spot.shards)
        return remote(
            self.part(target),
            self.arrived.at[self.rows(spot.shard)],
            self.sems,
            (k,),
            (spot.rep, target),
        )

    def start(self, slot, slots):
        size = -(-self.spot.shards // slots)

        def one(k, carry):
            @pl.when(k == 0)
            def _():
                self.own.start()

            @pl.when(k > 0)
            def _():
                self.copy(k).start()

            return carry

        first = jnp.minimum(slot * size, self.spot.shards)
        lax.fori_loop(first, jnp.minimum(first + size, self.spot.shards), one, 0)

    def finish(self):
        def one(k, carry):
            self.copy(k).wait()
            return carry

        lax.fori_loop(1, self.spot.shards, one, 0)
        self.own.wait()


class Gather:
    def __init__(self, spot, lent, shard_ref, full_ref, sems):
        self.spot, self.lent, self.shard_ref, self.full_ref = spot, lent, shard_ref, full_ref
        self.rows = shard_ref.shape[0]
        self.unit = shard_ref.shape[1] // 8
        self.kept = 8 - lent
        self.ring_sems, self.near_sems, self.far_sems, self.far_near_sems = (
            sems[0:2],
            sems[2:4],
            sems[4:6],
            sems[6:8],
        )
        self.whole_sems, self.own_sem = sems[8:10], sems[10]

    def span(self, way, short):
        first, count = self.lent * self.spot.rep, self.kept
        if short:
            first, count = first + way * (count // 2), count // 2
        return pl.ds(pl.multiple_of(first * self.unit, 128), count * self.unit)

    def region(self, way, hop, short):
        block = self.spot.block(self.spot.along(way, hop))
        return self.full_ref.at[pl.ds(block * self.rows, self.rows), self.span(way, short)]

    def ring(self, way, hop, short, source=None):
        region = self.region(way, hop, short)
        return remote(
            region if source is None else source,
            region,
            self.ring_sems,
            (way, hop),
            self.spot.ahead(way),
        )

    def near(self, way, hop, short):
        region = self.region(way, hop + 1, short)
        target = (self.spot.rep, self.spot.sibling)
        return remote(region, region, self.near_sems, (way, hop), target)

    def lent_region(self, way, hop, owner):
        block = self.spot.block(self.spot.along(way, hop + 1))
        columns = pl.ds(
            pl.multiple_of(self.kept * owner * self.unit, 128), self.lent * self.unit
        )
        return self.full_ref.at[pl.ds(block * self.rows, self.rows), columns]

    def far(self, way, hop):
        region = self.lent_region(way, hop, self.spot.rep)
        target = (1 - self.spot.rep, self.spot.shard)
        return remote(region, region, self.far_sems, (way, hop), target)

    def far_near(self, way, hop):
        region = self.lent_region(way, hop, 1 - self.spot.rep)
        target = (self.spot.rep, self.spot.sibling)
        return remote(region, region, self.far_near_sems, (way, hop), target)

    def own(self):
        spot = self.spot
        mine = self.full_ref.at[pl.ds(spot.shard * self.rows, self.rows)]
        whole = remote(self.shard_ref, mine, self.whole_sems, (0,), (spot.rep, spot.sibling))
        return whole, pltpu.make_async_copy(self.shard_ref, mine, self.own_sem)

    def start(self):
        for way in (0, 1):
            self.ring(way, 0, False, self.shard_ref.at[:, self.span(way, False)]).start()
        for copy in self.own():
            copy.start()

    def step(self, hop):
        final = self.spot.half - 1

        @pl.when(hop < final)
        def _():
            for way in (0, 1):
                self.ring(way, hop, False).wait_recv()

                @pl.when(hop < final - 1)
                def _():
                    self.ring(way, hop + 1, False).start()

                @pl.when(hop == final - 1)
                def _():
                    self.ring(way, hop + 1, True).start()

            for way in (0, 1):
                self.far(way, hop).start()
                self.near(way, hop, False).start()

        @pl.when(hop == final)
        def _():
            for way in (0, 1):
                self.ring(way, hop, True).wait_recv()
            self.far(0, hop).start()
            for way in (0, 1):
                self.near(way, hop, True).start()

        @pl.when(hop > 0)
        def _():
            for way in (0, 1):
                self.relay(way, hop - 1)

    def relay(self, way, hop):
        self.far(way, hop).wait_recv()
        self.far_near(way, hop).start()

    def finish(self):
        final = self.spot.half - 1
        for copy in self.own():
            copy.wait()

        def one(hop, carry):
            for way in (0, 1):
                self.ring(way, hop, False).wait_send()
                self.near(way, hop, False).wait()
                self.far(way, hop).wait_send()
                self.far_near(way, hop).wait()
            return carry

        lax.fori_loop(0, final, one, 0)
        for way in (0, 1):
            self.ring(way, final, True).wait_send()
            self.near(way, final, True).wait()
        self.far(0, final).wait_send()
        self.far_near(0, final).wait()

    @staticmethod
    def scratch(half):
        return [DMA((2, half))] * 8 + [DMA((1,))] * 2 + [DMA]


class GatherAll:
    def __init__(self, spot, lents, swap_count, inputs, outputs, scratch):
        count = len(lents)
        self.spot = spot
        self.gathers = [
            Gather(spot, lents[g], inputs[g], outputs[g], scratch[11 * g : 11 * g + 11])
            for g in range(count)
        ]
        scratch = scratch[11 * count :]
        self.swaps = [
            Swap(
                spot,
                inputs[count + i],
                outputs[count + i],
                scratch[3 * i : 3 * i + 2],
                scratch[3 * i + 2],
            )
            for i in range(swap_count)
        ]

    def start(self):
        greet(self.spot)
        for gather in self.gathers:
            gather.start()

    def exchange(self, slot, slots):
        for swap in self.swaps:
            swap.start(slot, slots)

    def steps(self, slot, slots):
        def one(hop, carry):
            for gather in self.gathers:
                gather.step(hop)
            return carry

        half = self.spot.half
        lax.fori_loop(slot * half // slots, (slot + 1) * half // slots, one, 0)

    def finish_gathers(self):
        for gather in self.gathers:
            gather.relay(0, self.spot.half - 1)
        for gather in self.gathers:
            gather.finish()

    def finish(self):
        self.finish_gathers()
        for swap in self.swaps:
            swap.finish()

    @staticmethod
    def scratch(shards, count, swap_count):
        return Gather.scratch(shards // 4) * count + [
            DMA((shards,)),
            DMA((shards,)),
            DMA,
        ] * swap_count


def gather_kernel(shards, lents, *refs):
    spot = Spot(shards)
    rows_ref, tokens_ref, cotangent_ref, lengths_ref, frequency_ref = refs[:5]
    count = len(lents)
    pieces, gains_ref, refs = refs[5 : 5 + count], refs[5 + count], refs[6 + count :]
    outputs, packed_out, refs = refs[: count + 1], refs[count + 1], refs[count + 2 :]
    cosine_ref, sine_ref, columns_ref, *gain_refs = refs[:5]
    packed_ref, all_gains_ref, scratch = refs[5], refs[6], refs[7:]
    work = GatherAll(
        spot, lents, 2, [*pieces, packed_ref, gains_ref], [*outputs, all_gains_ref], scratch
    )
    work.start()
    chosen = place_rows(rows_ref[0:1, :], packed_ref.shape[0])
    matmul_columns(packed_ref, chosen, tokens_ref)

    def one(hop, carry):
        work.exchange(hop, spot.half)

        @pl.when(hop == 0)
        def _():
            matmul_columns(packed_out, chosen, cotangent_ref)
            angle_tables(lengths_ref, frequency_ref, cosine_ref, sine_ref)
            columns_ref[...] = rows_ref[...].T

        work.steps(hop, spot.half)
        return carry

    lax.fori_loop(0, spot.half, one, 0)
    work.finish()
    share = tokens_ref.shape[1] // shards
    for gain_ref, row in zip(gain_refs, gain_rows(all_gains_ref, share), strict=True):
        gain_ref[...] = row


def gather_shapes(shards, pieces, sent, shared):
    return (
        [
            jax.ShapeDtypeStruct((shards * piece.shape[0], piece.shape[1]), piece.dtype)
            for piece in pieces
        ]
        + [jax.ShapeDtypeStruct(rows.shape, rows.dtype) for rows in sent]
        + [
            jax.ShapeDtypeStruct((shards * each.shape[0], each.shape[1]), each.dtype)
            for each in shared
        ]
    )


def gather_call(
    shards, rows, tokens, cotangent, lengths, frequency, pieces, lents, gains, collective_id
):
    anywhere = pl.BlockSpec(memory_space=pl.ANY)
    inside = pl.BlockSpec(memory_space=pltpu.VMEM)
    count = len(pieces)
    packed = jax.ShapeDtypeStruct((2 * tokens.shape[0], tokens.shape[1]), tokens.dtype)
    results = pl.pallas_call(
        functools.partial(gather_kernel, shards, lents),
        out_shape=[
            *gather_shapes(shards, pieces, [packed], []),
            packed,
            *[jax.ShapeDtypeStruct((tokens.shape[0], 128), jnp.float32)] * 2,
            jax.ShapeDtypeStruct(rows.shape[::-1], rows.dtype),
            *[jax.ShapeDtypeStruct((1, tokens.shape[1]), jnp.float32)] * 2,
        ],
        in_specs=[
            *[inside] * 3,
            pl.BlockSpec(memory_space=pltpu.SMEM),
            inside,
            *[anywhere] * (count + 1),
        ],
        out_specs=[anywhere] * (count + 1) + [inside] * 6,
        scratch_shapes=[
            pltpu.VMEM(packed.shape, packed.dtype),
            pltpu.VMEM((8 * shards, 128), jnp.float32),
            *GatherAll.scratch(shards, count, 2),
        ],
        compiler_params=pltpu.CompilerParams(
            collective_id=collective_id, has_side_effects=True, vmem_limit_bytes=VMEM_LIMIT
        ),
    )(rows, tokens, cotangent, lengths, frequency, *pieces, gains)
    return results


class Reduce:
    def __init__(self, spot, lent, partial_ref, out_ref, refs, part=0, parts=1):
        self.spot, self.lent, self.partial, self.out = spot, lent, partial_ref, out_ref
        self.block_rows = partial_ref.shape[0] // spot.shards
        self.columns = partial_ref.shape[1]
        self.rows = self.block_rows // parts
        self.offset = part * self.rows
        self.unit = self.columns // 8
        self.kept = 8 - lent
        self.width = self.kept * self.unit
        (
            self.own,
            self.sib,
            self.got,
            self.own_far,
            self.sib_far,
            self.got_far,
            self.got_last,
        ) = refs[:7]
        sems = refs[7:]
        self.load_sem, self.load_far_sem = sems[0], sems[1]
        self.sib_sems, self.sib_far_sems = sems[2:4], sems[4:6]
        self.ring_sems, self.far_sems, self.last_sems = sems[6:8], sems[8:10], sems[10:12]
        self.out_sems = sems[12]

    @staticmethod
    def scratch(shards, lent, rows, columns):
        chips = shards // 2
        unit = columns // 8
        kept, lend = (8 - lent) * unit, lent * unit
        half = jnp.bfloat16
        buffers = [
            pltpu.VMEM((chips, rows, kept), half),
            pltpu.VMEM((chips, rows, kept), half),
            pltpu.VMEM((2, chips // 2, rows, kept), half),
            pltpu.VMEM((chips, rows, lend), half),
            pltpu.VMEM((chips, rows, lend), half),
            pltpu.VMEM((chips, rows, lend), half),
            pltpu.VMEM((rows, kept), half),
        ]
        sems = [DMA((chips,))] * 6 + [DMA((2, chips // 2))] * 2
        sems += [DMA((chips,))] * 2 + [DMA((1,))] * 2 + [DMA((2,))]
        return buffers + sems

    def owner(self, item, core):
        half = self.spot.half
        pair = (item + 1) // 2
        ahead = lax.rem(item, 2) == 1
        distance = half - pair
        place = jnp.where(ahead, self.spot.place + distance, self.spot.place - distance)
        return self.spot.block(place, core)

    def cut(self, item, core, first, count):
        columns = pl.ds(pl.multiple_of(first * self.unit, 128), count * self.unit)
        block = self.owner(item, core)
        first = pl.multiple_of(block * self.block_rows + self.offset, 16)
        return self.partial.at[pl.ds(first, self.rows), columns]

    def kept_cut(self, item, core):
        return self.cut(item, core, self.lent * self.spot.rep, self.kept)

    def lent_cut(self, item, core):
        return self.cut(item, core, self.kept * (1 - self.spot.rep), self.lent)

    def load(self, item):
        source = self.kept_cut(item, self.spot.core)
        return pltpu.make_async_copy(source, self.own.at[item], self.load_sem.at[item])

    def load_far(self, item):
        source = self.lent_cut(item, self.spot.core)
        return pltpu.make_async_copy(source, self.own_far.at[item], self.load_far_sem.at[item])

    def give(self, item):
        source = self.kept_cut(item, 1 - self.spot.core)
        target = (self.spot.rep, self.spot.sibling)
        return remote(source, self.sib.at[item], self.sib_sems, (item,), target)

    def give_far(self, item):
        source = self.lent_cut(item, 1 - self.spot.core)
        target = (self.spot.rep, self.spot.sibling)
        return remote(source, self.sib_far.at[item], self.sib_far_sems, (item,), target)

    def ring(self, way, step, short=False):
        item = 0 if short else 2 * step - 1 + way
        columns = pl.ds(way * self.width // 2, self.width // 2) if short else slice(None)
        return remote(
            self.own.at[item, :, columns],
            self.got.at[way, step, :, columns],
            self.ring_sems,
            (way, step),
            self.spot.ahead(way),
        )

    def far(self, item):
        target = (1 - self.spot.rep, self.spot.shard)
        return remote(
            self.own_far.at[item], self.got_far.at[item], self.far_sems, (item,), target
        )

    @staticmethod
    def out_shape(shards, lent, partial):
        rows, columns = partial.shape[0] // shards, partial.shape[1]
        return jax.ShapeDtypeStruct((2, rows, (8 - lent) * columns // 8), jnp.bfloat16)

    def last(self):
        target = (1 - self.spot.rep, self.spot.shard)
        source = self.own.at[self.spot.chips - 1]
        return remote(source, self.got_last, self.last_sems, (0,), target)

    def start(self, item):
        self.load_far(item).start()
        self.give_far(item).start()
        self.load(item).start()
        self.give(item).start()

    def tiles(self, width, body):
        chunk = width if width <= 768 else 512
        chunks = width // chunk

        def one(i, carry):
            tile, first = i // chunks, lax.rem(i, chunks) * chunk
            body(pl.ds(pl.multiple_of(tile * 16, 16), 16), first, chunk)
            return carry

        lax.fori_loop(0, self.rows // 16 * chunks, one, 0)

    def far_step(self, item):
        self.load_far(item).wait()
        self.give_far(item).wait_recv()

        def add(rows, first, count):
            at = pl.ds(pl.multiple_of(first, 128), count)
            total = self.own_far[item, rows, at].astype(jnp.float32)
            total += self.sib_far[item, rows, at].astype(jnp.float32)
            self.own_far[item, rows, at] = total.astype(jnp.bfloat16)

        self.tiles(self.lent * self.unit, add)
        self.far(item).start()

    def fold(self, item, extra=(), start=0, width=None):
        def add(rows, first, count):
            at = pl.ds(pl.multiple_of(start + first, 128), count)
            total = self.own[item, rows, at].astype(jnp.float32)
            total += self.sib[item, rows, at].astype(jnp.float32)
            for way, step in extra:
                total += self.got[way, step, rows, at].astype(jnp.float32)
            self.own[item, rows, at] = total.astype(jnp.bfloat16)

        self.tiles(self.width if width is None else width, add)

    def ready(self, item):
        self.load(item).wait()
        self.give(item).wait_recv()
        self.far(item).wait_recv()
        offset = self.spot.rep * (self.kept - self.lent) * self.unit

        def add(rows, first, count):
            at = pl.ds(pl.multiple_of(offset + first, 128), count)
            total = self.sib[item, rows, at].astype(jnp.float32)
            lent_at = pl.ds(pl.multiple_of(first, 128), count)
            total += self.got_far[item, rows, lent_at].astype(jnp.float32)
            self.sib[item, rows, at] = total.astype(jnp.bfloat16)

        self.tiles(self.lent * self.unit, add)

    def step(self, step):
        half, chips = self.spot.half, self.spot.chips

        @pl.when(step == 0)
        def _():
            self.ready(0)
            self.fold(0)
            for way in (0, 1):
                self.ring(way, 0, True).start()

        @pl.when((step > 0) & (step < half))
        def _():
            for way in (0, 1):
                item = 2 * step - 1 + way
                self.ready(item)

                @pl.when(step == 1)
                def _():
                    self.ring(way, 0, True).wait_recv()
                    middle = self.width // 2
                    self.fold(item, [(way, 0)], way * middle, middle)
                    self.fold(item, [], (1 - way) * middle, middle)

                @pl.when(step > 1)
                def _():
                    self.ring(way, step - 1).wait_recv()
                    self.fold(item, [(way, step - 1)])

                self.ring(way, step).start()

        @pl.when(step == half)
        def _():
            self.ready(chips - 1)
            for way in (0, 1):
                self.ring(way, half - 1).wait_recv()
            self.fold(chips - 1, [(0, half - 1), (1, half - 1)])
            self.last().start()

        @pl.when(step < half)
        def _():
            self.far_step(2 * step + 1)

            @pl.when(step < half - 1)
            def _():
                self.far_step(2 * step + 2)

    def finish(self):
        spot = self.spot
        rows = pl.ds(self.offset, self.rows)
        mine = pltpu.make_async_copy(
            self.own.at[spot.chips - 1], self.out.at[0, rows], self.out_sems.at[0]
        )
        mine.start()
        self.last().wait()
        theirs = pltpu.make_async_copy(
            self.got_last, self.out.at[1, rows], self.out_sems.at[1]
        )
        theirs.start()
        mine.wait()
        theirs.wait()

        def one(item, carry):
            self.give_far(item).wait_send()
            self.far(item).wait_send()
            self.give(item).wait_send()
            return carry

        lax.fori_loop(0, spot.chips, one, 0)
        for way in (0, 1):
            self.ring(way, 0, True).wait_send()

        def two(step, carry):
            for way in (0, 1):
                self.ring(way, step).wait_send()
            return carry

        lax.fori_loop(1, spot.half, two, 0)


class Tally:
    def __init__(self, spot, mine, out, refs):
        self.spot, self.mine, self.out = spot, mine, out
        self.got, self.half, self.other = refs[0:3]
        self.sems, self.own_sem, self.far_sems = refs[3:5], refs[5], refs[6:8]
        self.own = pltpu.make_async_copy(mine, self.got.at[spot.shard], self.own_sem)

    def copy(self, k):
        spot = self.spot
        target = lax.rem(spot.shard + k, spot.shards)
        return remote(self.mine, self.got.at[spot.shard], self.sems, (k,), (spot.rep, target))

    def far(self):
        target = (1 - self.spot.rep, self.spot.shard)
        return remote(self.half, self.other, self.far_sems, (0,), target)

    def start(self):
        def one(k, carry):
            self.copy(k).start()
            return carry

        lax.fori_loop(1, self.spot.shards, one, 0)
        self.own.start()

    def middle(self):
        def one(k, carry):
            self.copy(k).wait()
            return carry

        lax.fori_loop(1, self.spot.shards, one, 0)
        self.own.wait()

        def add(k, total):
            return total + self.got[k]

        self.half[...] = lax.fori_loop(0, self.spot.shards, add, jnp.zeros_like(self.half))
        self.far().start()

    def finish(self):
        self.far().wait()
        self.out[...] = self.half[...] + self.other[...]

    @staticmethod
    def scratch(shards, shape):
        full = jnp.float32
        return [
            pltpu.VMEM((shards, *shape), full),
            pltpu.VMEM(shape, full),
            pltpu.VMEM(shape, full),
            DMA((shards,)),
            DMA((shards,)),
            DMA,
            DMA((1,)),
            DMA((1,)),
        ]


def matmul(left, right, left_dim=1, right_dim=0):
    return lax.dot_general(
        left, right, (((left_dim,), (right_dim,)), ((), ())), preferred_element_type=jnp.float32
    )


def matmul_columns(out_ref, left, right_ref):
    def one(i, carry):
        at = pl.ds(pl.multiple_of(i * 512, 512), 512)
        part = matmul(left, right_ref[:, at].astype(jnp.bfloat16))
        out_ref[:, at] = part.astype(out_ref.dtype)
        return carry

    lax.fori_loop(0, out_ref.shape[1] // 512, one, 0)


def pick_rows(slot_column, slot_total):
    shape = (slot_column.shape[0], slot_total)
    return (slot_column == lax.broadcasted_iota(jnp.int32, shape, 1)).astype(jnp.bfloat16)


def place_rows(slot_row, slot_total):
    shape = (slot_total, slot_row.shape[1])
    return (slot_row == lax.broadcasted_iota(jnp.int32, shape, 0)).astype(jnp.bfloat16)


def assemble_kernel(rep_ref, *refs):
    raws, plain, refs = refs[:4], refs[4:6], refs[6:]
    plain_outs, outs, whole_ref = refs[:2], refs[2:9], refs[9]
    for source, target in zip(plain, plain_outs, strict=True):
        target[...] = source[...]
    for raw_ref, out_ref in zip(raws, [*outs[:3], whole_ref], strict=True):
        kept = raw_ref.shape[2]
        columns = out_ref.shape[1]
        lent = columns - kept

        def write(low, high, raw_ref=raw_ref, out_ref=out_ref, kept=kept, lent=lent):
            def part(which, first, count):
                return raw_ref[which, :, first : first + count].astype(jnp.float32)

            out_ref[:, 0:lent] = part(low, 0, lent)
            if kept > lent:
                out_ref[:, lent:kept] = part(low, lent, kept - lent) + part(high, 0, kept - lent)
            out_ref[:, kept:] = part(high, kept - lent, lent)

        @pl.when(rep_ref[0, 0] == 0)
        def _(write=write):
            write(0, 1)

        @pl.when(rep_ref[0, 0] != 0)
        def _(write=write):
            write(1, 0)

    width = outs[3].shape[1]
    for i in range(4):
        outs[3 + i][...] = whole_ref[:, i * width : (i + 1) * width]


def local_call(kernel, out_shape, inputs, spaces=None, scratch=()):
    inside = pl.BlockSpec(memory_space=pltpu.VMEM)
    return pl.pallas_call(
        kernel,
        out_shape=out_shape,
        in_specs=spaces or [inside] * len(inputs),
        out_specs=[inside] * len(out_shape),
        scratch_shapes=list(scratch),
        compiler_params=pltpu.CompilerParams(vmem_limit_bytes=VMEM_LIMIT),
    )(*inputs)


def segment_of(index, lengths_ref):
    first = lengths_ref[0, 0]
    second = first + lengths_ref[0, 1]
    third = second + lengths_ref[0, 2]
    return (
        (index >= first).astype(jnp.int32)
        + (index >= second).astype(jnp.int32)
        + (index >= third).astype(jnp.int32)
    )


def angle_tables(lengths_ref, frequency_ref, cosine_ref, sine_ref):
    index = lax.broadcasted_iota(jnp.int32, (cosine_ref.shape[0], 1), 0)
    segment = segment_of(index, lengths_ref)
    begin = jnp.zeros_like(index)
    end = 0
    for i in range(3):
        end = end + lengths_ref[0, i]
        begin = jnp.where(segment == i + 1, end, begin)
    angle = (index - begin).astype(jnp.float32) * frequency_ref[...]
    lane = lax.broadcasted_iota(jnp.int32, angle.shape, 1)
    sine = jnp.sin(angle)
    cosine_ref[...] = jnp.cos(angle)
    sine_ref[...] = jnp.where(lane % 64 < 32, -sine, sine)


def gain_rows(gains_ref, share):
    shards = gains_ref.shape[0] // 8
    rows = []
    for which in (0, 1):
        parts = []
        for first in range(0, shards * share, 128):
            total = jnp.zeros((1, 128), jnp.float32)
            for lane in range(0, 128, share):
                at = (first + lane) // share * 8 + which
                part = gains_ref[at : at + 1, :]
                total += part if lane == 0 else pltpu.roll(part, lane, 1)
            parts.append(total)
        rows.append(jnp.concatenate(parts, axis=1))
    return rows


def pair_masks(columns_ref, rows_ref, lengths_ref, same_ref, hidden_ref):
    size = columns_ref.shape[0]
    shape = (size, size)
    key_id = lax.broadcasted_iota(jnp.int32, shape, 0)
    query_id = lax.broadcasted_iota(jnp.int32, shape, 1)
    key_column = lax.broadcasted_iota(jnp.int32, (size, 1), 0)
    query_row = lax.broadcasted_iota(jnp.int32, (1, size), 1)
    together = segment_of(key_column, lengths_ref) == segment_of(query_row, lengths_ref)
    seen = together & ((columns_ref[:, 3:4] > 0) | (key_id == query_id))
    same_ref[...] = (columns_ref[:, 2:3] == rows_ref[2:3, :]).astype(jnp.float32)
    hidden_ref[...] = jnp.where(seen, 0.0, masked_score)


def turn(values, cosine, sine):
    width = values.shape[1]
    lane = lax.broadcasted_iota(jnp.int32, values.shape, 1)
    other = jnp.where(
        lane % 64 < 32, pltpu.roll(values, width - 32, 1), pltpu.roll(values, 32, 1)
    )
    return values * cosine + other * sine


def head_lanes(values, head):
    lane = lax.broadcasted_iota(jnp.int32, values.shape, 1)
    return jnp.where((lane < 64) == (head == 0), values, jnp.zeros_like(values))


def project(input_ref, weight_refs, cosine_ref, sine_ref, out_ref, scale):
    width = weight_refs[0].shape[0]
    cosine = jnp.concatenate([cosine_ref[...]] * 2, axis=1)
    sine = jnp.concatenate([sine_ref[...]] * 2, axis=1)

    def one(i, carry):
        def columns(part):
            return pl.ds(pl.multiple_of(part * width + i * 256, 256), 256)

        at = pl.ds(pl.multiple_of(i * 256, 256), 256)
        query = matmul(input_ref[...], weight_refs[0][:, at])
        out_ref[:, columns(0)] = (turn(query, cosine, sine) * scale).astype(jnp.bfloat16)
        key = matmul(input_ref[...], weight_refs[1][:, at])
        out_ref[:, columns(1)] = turn(key, cosine, sine).astype(jnp.bfloat16)
        out_ref[:, columns(2)] = matmul(input_ref[...], weight_refs[2][:, at]).astype(
            jnp.bfloat16
        )
        return carry

    lax.fori_loop(0, width // 256, one, 0)


def attend_pair(pair, width, heads_ref, bias_ref, same_ref, hidden_ref, out_ref, log_ref):
    def columns(part):
        return pl.ds(pl.multiple_of(part * width + pair * 128, 128), 128)

    query, key, value = (heads_ref[:, columns(part)] for part in range(3))
    total = None
    for which in (0, 1):
        head = 2 * pair + which
        gap = bias_ref[0, head] - bias_ref[1, head]
        scores = matmul(head_lanes(key, which), query, 1, 1)
        scores = scores + same_ref[...] * gap + hidden_ref[...]
        top = jnp.max(scores, axis=0, keepdims=True)
        weights = jnp.exp(scores - top)
        weight_sum = jnp.sum(weights, axis=0, keepdims=True)
        log_ref[pl.ds(head, 1), :] = top + jnp.log(weight_sum)
        soft = (weights * (1.0 / weight_sum)).astype(jnp.bfloat16)
        part = matmul(head_lanes(value, which), soft, 0, 0)
        total = part if total is None else total + part
    out_ref[:, pl.ds(pl.multiple_of(pair * 128, 128), 128)] = total.T.astype(jnp.bfloat16)


def normed(values):
    factor = lax.rsqrt(jnp.mean(values * values, axis=-1, keepdims=True) + epsilon)
    return values * factor, factor


def forward_body(refs, between, loaded):
    (
        arrived_ref, columns_ref, rows_ref, lengths_ref, bias_ref, gain_ref,
        query_w_ref, key_w_ref, value_w_ref, cosine_ref, sine_ref,
        stream_ref, input_ref, heads_ref, out_ref, log_ref,
        same_ref, hidden_ref,
    ) = refs
    width = gain_ref.shape[1]
    scale = 1.0 / math.sqrt(64)
    pair_masks(columns_ref, rows_ref, lengths_ref, same_ref, hidden_ref)
    chosen = pick_rows(columns_ref[:, 1:2], arrived_ref.shape[0])
    loaded(0)
    matmul_columns(stream_ref, chosen, arrived_ref)
    stream = stream_ref[...].astype(jnp.float32)
    input_ref[...] = (normed(stream)[0] * gain_ref[...]).astype(jnp.bfloat16)
    weight_refs = (query_w_ref, key_w_ref, value_w_ref)
    for i in (1, 2, 3):
        loaded(i)
    project(input_ref, weight_refs, cosine_ref, sine_ref, heads_ref, scale)

    def one(pair, carry):
        between(pair)
        attend_pair(pair, width, heads_ref, bias_ref, same_ref, hidden_ref, out_ref, log_ref)
        return carry

    lax.fori_loop(0, width // 128, one, 0)


def fold_lanes(row):
    folded = row[:, 0:128]
    for i in range(1, row.shape[1] // 128):
        folded += row[:, i * 128 : (i + 1) * 128]
    return folded


def square_into(stats_ref, at, values, columns_ref):
    valid = (columns_ref[:, 3:4] > 0).astype(jnp.float32)
    across = jnp.sum(values * values * valid, axis=0, keepdims=True)
    stats_ref[at : at + 1, :] = fold_lanes(across)


def attend_back_pair(
    pair, width, scale, heads_ref, do_ref, bias_ref, log_ref, same_ref, hidden_ref, cosine_ref,
    sine_ref, grads_ref, bias_same_ref, bias_all_ref,
):
    half = jnp.bfloat16

    def columns(part):
        return pl.ds(pl.multiple_of(part * width + pair * 128, 128), 128)

    query, key, value = (heads_ref[:, columns(part)] for part in range(3))
    grad_out = do_ref[:, columns(0)]
    query_t = key_grad = value_grad = None
    for which in (0, 1):
        head = 2 * pair + which
        gap = bias_ref[0, head] - bias_ref[1, head]
        key_part = head_lanes(key, which)
        scores = matmul(key_part, query, 1, 1)
        scores = scores + same_ref[...] * gap + hidden_ref[...]
        soft = jnp.exp(scores - log_ref[pl.ds(head, 1), :])
        grad_soft = matmul(head_lanes(value, which), grad_out, 1, 1)
        inner = jnp.sum(soft * grad_soft, axis=0, keepdims=True)
        grad_scores = (soft * (grad_soft - inner)).astype(half)
        wide = grad_scores.astype(jnp.float32)
        bias_all_ref[pl.ds(head, 1), :] = jnp.sum(wide, axis=0, keepdims=True)
        bias_same_ref[pl.ds(head, 1), :] = jnp.sum(wide * same_ref[...], axis=0, keepdims=True)
        parts = (
            matmul(key_part, grad_scores, 0, 0),
            matmul(grad_scores, head_lanes(query, which)),
            matmul(soft.astype(half), head_lanes(grad_out, which)),
        )
        if which == 0:
            query_t, key_grad, value_grad = parts
        else:
            query_t, key_grad, value_grad = (
                query_t + parts[0],
                key_grad + parts[1],
                value_grad + parts[2],
            )
    cosine, sine = cosine_ref[...], -sine_ref[...]
    grads_ref[:, columns(0)] = (turn(query_t.T, cosine, sine) * scale).astype(half)
    grads_ref[:, columns(1)] = turn(key_grad, cosine, sine).astype(half)
    grads_ref[:, columns(2)] = value_grad.astype(half)


def feed_forward(refs, weights, gates_out, ups_out, hidden_out, scratch, saves, between):
    columns_ref, rows_ref, gain_ref, stream_ref, attended_ref, out_w_ref = refs[:6]
    packed_ref, middle_ref, input_ref, stats_ref = refs[6:]
    (
        gate_buf, up_buf, down_buf, gates_buf, ups_buf, hidden_buf, mlp_ref,
        load_sems, store_sems,
    ) = scratch
    tile = gate_buf.shape[2]
    tiles = gates_out.shape[1] // tile
    half = jnp.bfloat16

    def at(i):
        return pl.ds(pl.multiple_of(i * tile, tile), tile)

    def loads(i):
        slot = lax.rem(i, 2)
        return [
            pltpu.make_async_copy(weights[0].at[:, at(i)], gate_buf.at[slot], load_sems.at[slot, 0]),
            pltpu.make_async_copy(weights[1].at[:, at(i)], up_buf.at[slot], load_sems.at[slot, 1]),
            pltpu.make_async_copy(weights[2].at[at(i)], down_buf.at[slot], load_sems.at[slot, 2]),
        ]

    def stores(i):
        slot = lax.rem(i, 2)
        return [
            pltpu.make_async_copy(gates_buf.at[slot], gates_out.at[:, at(i)], store_sems.at[slot, 0]),
            pltpu.make_async_copy(ups_buf.at[slot], ups_out.at[:, at(i)], store_sems.at[slot, 1]),
            pltpu.make_async_copy(
                hidden_buf.at[slot], hidden_out.at[:, at(i)], store_sems.at[slot, 2]
            ),
        ]

    for copy in loads(0):
        copy.start()
    stats_ref[...] = jnp.zeros_like(stats_ref)
    stream = stream_ref[...].astype(jnp.float32)
    square_into(stats_ref, 0, stream, columns_ref)
    matmul_columns(mlp_ref, attended_ref[...], out_w_ref)
    attn_out = mlp_ref[...]
    square_into(stats_ref, 1, attn_out, columns_ref)
    middle = stream + attn_out
    square_into(stats_ref, 2, middle, columns_ref)
    middle_ref[...] = middle
    input_ref[...] = (normed(middle)[0] * gain_ref[...]).astype(half)
    for copy in saves:
        copy.start()
    mlp_ref[...] = jnp.zeros_like(mlp_ref)

    def one(i, carry):
        slot = lax.rem(i, 2)
        between(i)
        for copy in loads(i):
            copy.wait()

        @pl.when(i + 1 < tiles)
        def _():
            for copy in loads(i + 1):
                copy.start()

        @pl.when(i >= 2)
        def _():
            for copy in stores(i - 2):
                copy.wait()

        gate = matmul(input_ref[...], gate_buf[slot])
        up = matmul(input_ref[...], up_buf[slot])
        gates_buf[slot] = gate
        ups_buf[slot] = up
        hidden = (gate * jax.nn.sigmoid(gate) * up).astype(half)
        hidden_buf[slot] = hidden
        for copy in stores(i):
            copy.start()
        mlp_ref[...] += matmul(hidden, down_buf[slot])
        return carry

    lax.fori_loop(0, tiles, one, 0)
    valid = (columns_ref[:, 3:4] > 0).astype(jnp.float32)
    mlp_out = mlp_ref[...]
    result = middle_ref[...] + mlp_out
    placed = place_rows(rows_ref[1:2, :], packed_ref.shape[0])
    mlp_ref[...] = result
    matmul_columns(packed_ref, placed, mlp_ref)
    square_into(stats_ref, 3, mlp_out, columns_ref)
    square_into(stats_ref, 4, result, columns_ref)
    lane = lax.broadcasted_iota(jnp.int32, (valid.shape[0], 128), 1)
    stats_ref[5:6, :] = jnp.sum(jnp.where(lane == 0, valid, 0.0), axis=0, keepdims=True)
    for i in (tiles - 2, tiles - 1):
        for copy in stores(i):
            copy.wait()


def forward_gather_kernel(shards, lents, swap_count, compute_counts, *refs):
    ins, outs = compute_counts
    total = len(lents) + swap_count
    in_refs, refs = refs[: ins + total], refs[ins + total :]
    out_refs, refs = refs[: outs + total], refs[outs + total :]
    masks, out_w_buf, out_w_sem, feed_scratch, staged, sems, scratch = (
        refs[:2], refs[2], refs[3], refs[4:13], refs[13:24], refs[24:26], refs[26:],
    )
    work = GatherAll(
        Spot(shards), lents, swap_count, in_refs[ins:], out_refs[outs:], scratch
    )
    work.start()
    *attend_ins, gain_mlp_ref = in_refs[:ins]
    arriving, leaving = staged[:4], staged[4:]
    loads = [
        pltpu.make_async_copy(attend_ins[at], arriving[i], sems[0].at[i])
        for i, at in enumerate((0, 6, 7, 8))
    ]
    for copy in loads:
        copy.start()
    attend_ins[0], attend_ins[6:9] = arriving[0], arriving[1:4]
    attend_outs, feed_outs = leaving[:5], [*out_refs[5:9], *leaving[5:], out_refs[outs - 1]]
    saves = [
        pltpu.make_async_copy(leaving[i], out_refs[at], sems[1].at[i])
        for i, at in enumerate((0, 1, 2, 3, 4, 9, 10))
    ]
    pairs = attend_ins[5].shape[1] // 128

    tiles = out_refs[5].shape[1] // feed_scratch[0].shape[2]

    def between(pair):
        work.exchange(pair, pairs + tiles)
        work.steps(pair, pairs)

    forward_body(
        (*attend_ins, *attend_outs, *masks), between, lambda i: loads[i].wait()
    )
    for copy in saves[:5]:
        copy.start()
    work.finish_gathers()
    full_refs = out_refs[outs:]
    copy = pltpu.make_async_copy(full_refs[0], out_w_buf, out_w_sem)
    copy.start()
    copy.wait()
    gates_out, ups_out, hidden_out, *feed_outs = feed_outs
    feed_forward(
        (
            attend_ins[1], attend_ins[2], gain_mlp_ref, attend_outs[0], attend_outs[3], out_w_buf,
            *feed_outs,
        ),
        full_refs[1:4], gates_out, ups_out, hidden_out, feed_scratch, saves[5:],
        lambda i: work.exchange(pairs + i, pairs + tiles),
    )
    for copy in saves:
        copy.wait()
    for swap in work.swaps:
        swap.finish()


def forward_gather_call(
    shards, inputs, spaces, out_shape, out_specs, pieces, lents, sent, collective_id
):
    anywhere = pl.BlockSpec(memory_space=pl.ANY)
    tokens, width = out_shape[0].shape
    tile = 512
    half, full = jnp.bfloat16, jnp.float32
    counts = (len(inputs), len(out_shape))
    comm = len(pieces) + len(sent)
    results = pl.pallas_call(
        functools.partial(forward_gather_kernel, shards, lents, len(sent), counts),
        out_shape=[*out_shape, *gather_shapes(shards, pieces, sent, [])],
        in_specs=spaces + [anywhere] * comm,
        out_specs=out_specs + [anywhere] * comm,
        scratch_shapes=[
            pltpu.VMEM((tokens, tokens), full),
            pltpu.VMEM((tokens, tokens), full),
            pltpu.VMEM((width, width), half),
            DMA,
            pltpu.VMEM((2, width, tile), half),
            pltpu.VMEM((2, width, tile), half),
            pltpu.VMEM((2, tile, width), half),
            pltpu.VMEM((2, tokens, tile), full),
            pltpu.VMEM((2, tokens, tile), full),
            pltpu.VMEM((2, tokens, tile), half),
            pltpu.VMEM((tokens, width), full),
            DMA((2, 3)),
            DMA((2, 3)),
            *[pltpu.VMEM(inputs[at].shape, half) for at in (0, 6, 7, 8)],
            *[
                pltpu.VMEM(out_shape[at].shape, out_shape[at].dtype)
                for at in (0, 1, 2, 3, 4, 9, 10)
            ],
            DMA((4,)),
            DMA((7,)),
            *GatherAll.scratch(shards, len(pieces), len(sent)),
        ],
        compiler_params=pltpu.CompilerParams(
            collective_id=collective_id, has_side_effects=True, vmem_limit_bytes=VMEM_LIMIT
        ),
    )(*inputs, *pieces, *sent)
    first = len(out_shape)
    second = first + len(pieces)
    return results[:first], results[first:second], results[second:]


def input_grad_kernel(shards, lent, *refs):
    (
        columns_ref, rows_ref, lengths_ref, bias_ref, gain_mlp_ref, gain_attn_ref, middle_ref,
        out_w_ref, arrived_ref, heads_ref, log_ref, cosine_ref, sine_ref, stream_ref,
        query_w_ref, key_w_ref, value_w_ref, packed_out_ref, gates_ref, ups_ref, rows_mlp_ref,
        gate_w_ref, up_w_ref, down_w_ref,
        grads_ref, packed_ref, stats_ref, grad_down_ref,
        grad_gate_ref, grad_up_ref, home_ref, partial_ref,
        gates_buf, ups_buf, gate_buf, up_buf, down_buf, grad_gate_buf, grad_up_buf,
        back_ref, dh_ref, do_ref, same_ref, hidden_ref, bias_same_ref, bias_all_ref,
        load_sems, store_sems, weight_sems, send_sems, recv_sems, own_sem,
    ) = refs[:52]
    staged, in_sems, out_sem, refs = refs[52:59], refs[59], refs[60], refs[61:]
    arriving = [
        pltpu.make_async_copy(source, buffer, in_sems.at[i])
        for i, (source, buffer) in enumerate(
            zip(
                (arrived_ref, out_w_ref, middle_ref, heads_ref, cosine_ref, sine_ref, stream_ref),
                staged,
                strict=True,
            )
        )
    ]
    arrived_ref, out_w_ref, middle_ref, heads_ref, cosine_ref, sine_ref, stream_ref = staged
    saved_ref, grads_ref = grads_ref, refs[0]
    dy_ref, refs = refs[1], refs[2:]
    save = pltpu.make_async_copy(grads_ref, saved_ref, out_sem)
    spot = Spot(shards)
    swap = Swap(spot, packed_out_ref, home_ref, (send_sems, recv_sems), own_sem)
    reduces = [
        Reduce(spot, lent, partial_ref, grad_down_ref, refs[20 * g : 20 * g + 20], g, 2)
        for g in (0, 1)
    ]
    tile = gate_buf.shape[2]
    tiles = gates_ref.shape[1] // tile
    width = gain_attn_ref.shape[1]
    half = jnp.bfloat16

    def at(i):
        return pl.ds(pl.multiple_of(i * tile, tile), tile)

    def loads(i):
        slot = lax.rem(i, 2)
        pairs = [
            (gates_ref.at[:, at(i)], gates_buf),
            (ups_ref.at[:, at(i)], ups_buf),
            (gate_w_ref.at[:, at(i)], gate_buf),
            (up_w_ref.at[:, at(i)], up_buf),
            (down_w_ref.at[at(i)], down_buf),
        ]
        return [
            pltpu.make_async_copy(source, buffer.at[slot], load_sems.at[slot, j])
            for j, (source, buffer) in enumerate(pairs)
        ]

    def stores(i):
        slot = lax.rem(i, 2)
        pairs = [(grad_gate_buf, grad_gate_ref), (grad_up_buf, grad_up_ref)]
        return [
            pltpu.make_async_copy(buffer.at[slot], target.at[:, at(i)], store_sems.at[slot, j])
            for j, (buffer, target) in enumerate(pairs)
        ]

    def row_loads(i):
        slot = lax.rem(i, 2)
        return [
            pltpu.make_async_copy(
                rows_mlp_ref.at[:, at(i)], grad_gate_buf.at[slot], load_sems.at[slot, 0]
            )
        ]

    def row_stores(i):
        slot = lax.rem(i, 2)
        return [
            pltpu.make_async_copy(
                down_buf.at[slot], partial_ref.at[at(i)], store_sems.at[slot, 0]
            )
        ]

    pairs = width // 128
    slots = tiles + pairs
    steps = spot.half + 1

    def reduce_steps(slot):
        def one(step, carry):
            for reduce in reduces:
                reduce.step(step)
            return carry

        lax.fori_loop(slot * steps // slots, (slot + 1) * steps // slots, one, 0)

    greet(spot)
    for copy in [arriving[0], *row_loads(0), *arriving[1:]]:
        copy.start()
    chosen = pick_rows(columns_ref[:, 1:2], arrived_ref.shape[0])
    arriving[0].wait()
    matmul_columns(dy_ref, chosen, arrived_ref)

    def rows_step(i, carry):
        slot = lax.rem(i, 2)
        for copy in row_loads(i):
            copy.wait()

        @pl.when(i + 1 < tiles)
        def _():
            for copy in row_loads(i + 1):
                copy.start()

        @pl.when(i >= 2)
        def _():
            for copy in row_stores(i - 2):
                copy.wait()

        down_buf[slot] = matmul(grad_gate_buf[slot], dy_ref[...], 0, 0).astype(half)
        for copy in row_stores(i):
            copy.start()
        return carry

    lax.fori_loop(0, tiles, rows_step, 0)
    for i in (tiles - 2, tiles - 1):
        for copy in row_stores(i):
            copy.wait()
    for copy in loads(0):
        copy.start()

    def begin(item, carry):
        for reduce in reduces:
            reduce.start(item)
        return carry

    lax.fori_loop(0, spot.chips, begin, 0)
    back_ref[...] = jnp.zeros_like(back_ref)
    pair_masks(columns_ref, rows_ref, lengths_ref, same_ref, hidden_ref)
    for reduce in reduces:
        reduce.far_step(0)

    def one(i, carry):
        slot = lax.rem(i, 2)

        swap.start(i, slots)
        reduce_steps(i)
        for copy in loads(i):
            copy.wait()

        @pl.when(i + 1 < tiles)
        def _():
            for copy in loads(i + 1):
                copy.start()

        @pl.when(i >= 2)
        def _():
            for copy in stores(i - 2):
                copy.wait()

        gate, up = gates_buf[slot], ups_buf[slot]
        grad_hidden = matmul(dy_ref[...], down_buf[slot], 1, 1)
        sigmoid = jax.nn.sigmoid(gate)
        grad_gate = (grad_hidden * up * sigmoid * (1.0 + gate * (1.0 - sigmoid))).astype(half)
        grad_up = (grad_hidden * gate * sigmoid).astype(half)
        grad_gate_buf[slot] = grad_gate
        grad_up_buf[slot] = grad_up
        for copy in stores(i):
            copy.start()
        back_ref[...] += matmul(grad_gate, gate_buf[slot], 1, 1) + matmul(
            grad_up, up_buf[slot], 1, 1
        )
        return carry

    lax.fori_loop(0, tiles, one, 0)
    for copy in arriving[1:]:
        copy.wait()
    stats_ref[...] = jnp.zeros_like(stats_ref)

    def through_norm(values, grad, gain_ref, first):
        entry, factor = normed(values)
        gain_grad = jnp.sum(grad * entry, axis=0, keepdims=True)
        for i in range(width // 128):
            stats_ref[first + i : first + i + 1, :] = gain_grad[:, i * 128 : (i + 1) * 128]
        scaled = grad * gain_ref[...]
        inner = jnp.mean(scaled * entry, axis=-1, keepdims=True)
        return factor * (scaled - entry * inner)

    dh = dy_ref[...].astype(jnp.float32) + through_norm(
        middle_ref[...], back_ref[...], gain_mlp_ref, 0
    )
    dh_ref[...] = dh
    branch = dh.astype(half)
    grads_ref[:, pl.ds(3 * width, width)] = branch

    def back_out(i, carry):
        at = pl.ds(pl.multiple_of(i * 256, 256), 256)
        do_ref[:, at] = matmul(
            grads_ref[:, pl.ds(3 * width, width)], out_w_ref[at, :], 1, 1
        ).astype(half)
        return carry

    lax.fori_loop(0, width // 256, back_out, 0)
    scale = 1.0 / math.sqrt(64)
    for i in (tiles - 2, tiles - 1):
        for copy in stores(i):
            copy.wait()
    halves = [pl.ds(0, tile), pl.ds(tile, tile)]

    def weight_loads(source, buffer, which):
        return [
            pltpu.make_async_copy(source.at[:, columns], buffer.at[j], weight_sems.at[which, j])
            for j, columns in enumerate(halves)
        ]

    for copy in weight_loads(query_w_ref, gate_buf, 0) + weight_loads(key_w_ref, up_buf, 1):
        copy.start()

    def two(pair, carry):
        swap.start(tiles + pair, slots)
        reduce_steps(tiles + pair)
        attend_back_pair(
            pair, width, scale, heads_ref, do_ref, bias_ref, log_ref, same_ref, hidden_ref,
            cosine_ref, sine_ref, grads_ref, bias_same_ref, bias_all_ref,
        )
        return carry

    lax.fori_loop(0, width // 128, two, 0)
    save.start()
    heads = bias_all_ref.shape[0]
    lane = lax.broadcasted_iota(jnp.int32, (heads, 128), 1)
    row = lax.broadcasted_iota(jnp.int32, (heads, 128), 0)
    same = jnp.sum(bias_same_ref[...], axis=1, keepdims=True)
    other = jnp.sum(bias_all_ref[...], axis=1, keepdims=True) - same
    stats_ref[16:17, :] = jnp.sum(
        jnp.where(lane == row, same, 0.0) + jnp.where(lane == row + heads, other, 0.0),
        axis=0,
        keepdims=True,
    )
    def through(buffer, first):
        def one(j, carry):
            at = pl.ds(pl.multiple_of(first + j * tile, tile), tile)
            back_ref[...] += matmul(grads_ref[:, at], buffer[j], 1, 1)
            return carry

        lax.fori_loop(0, 2, one, 0)

    back_ref[...] = jnp.zeros_like(back_ref)

    for copy in weight_loads(query_w_ref, gate_buf, 0):
        copy.wait()
    through(gate_buf, 0)
    for copy in weight_loads(value_w_ref, gate_buf, 0):
        copy.start()
    for copy in weight_loads(key_w_ref, up_buf, 1):
        copy.wait()
    through(up_buf, width)
    for copy in weight_loads(value_w_ref, gate_buf, 0):
        copy.wait()
    through(gate_buf, 2 * width)
    grad_stream = dh_ref[...] + through_norm(
        stream_ref[...].astype(jnp.float32), back_ref[...], gain_attn_ref, 8
    )
    placed = place_rows(rows_ref[1:2, :], packed_ref.shape[0])
    dh_ref[...] = grad_stream
    matmul_columns(packed_ref, placed, dh_ref)
    save.wait()
    swap.finish()
    for reduce in reduces:
        reduce.finish()


def input_grad_call(shards, inputs, spaces, far_inputs, lent, collective_id):
    anywhere = pl.BlockSpec(memory_space=pl.ANY)
    inside = pl.BlockSpec(memory_space=pltpu.VMEM)
    packed, gates = far_inputs[3], far_inputs[4]
    tokens, hidden = gates.shape
    width = packed.shape[1]
    heads = inputs[10].shape[0]
    tile = 512
    assert 2 * tile == width
    half, full = jnp.bfloat16, jnp.float32
    vmem, shape = pltpu.VMEM, jax.ShapeDtypeStruct
    return pl.pallas_call(
        functools.partial(input_grad_kernel, shards, lent),
        out_shape=[
            shape((tokens, 4 * width), half),
            shape(packed.shape, half),
            shape((24, 128), full),
            Reduce.out_shape(shards, lent, shape((hidden, width), half)),
            shape((tokens, hidden), half),
            shape((tokens, hidden), half),
            shape(packed.shape, half),
            shape((hidden, width), half),
        ],
        in_specs=[*spaces, *[anywhere] * len(far_inputs)],
        out_specs=[anywhere] + [inside] * 2 + [anywhere] * 5,
        scratch_shapes=[
            vmem((2, tokens, tile), full),
            vmem((2, tokens, tile), full),
            vmem((2, width, tile), half),
            vmem((2, width, tile), half),
            vmem((2, tile, width), half),
            vmem((2, tokens, tile), half),
            vmem((2, tokens, tile), half),
            vmem((tokens, width), full),
            vmem((tokens, width), full),
            vmem((tokens, width), half),
            vmem((tokens, tokens), full),
            vmem((tokens, tokens), full),
            vmem((heads, tokens), full),
            vmem((heads, tokens), full),
            DMA((2, 5)),
            DMA((2, 2)),
            DMA((2, 2)),
            DMA((shards,)),
            DMA((shards,)),
            DMA,
            *[vmem(inputs[at].shape, inputs[at].dtype) for at in (8, 7, 6, 9, 11, 12, 13)],
            DMA((7,)),
            DMA,
            vmem((tokens, 4 * width), half),
            vmem((tokens, width), half),
            *Reduce.scratch(shards, lent, hidden // shards // 2, width) * 2,
        ],
        compiler_params=pltpu.CompilerParams(
            collective_id=collective_id, has_side_effects=True, vmem_limit_bytes=VMEM_LIMIT
        ),
    )(*inputs, *far_inputs)


def weight_grad_kernel(shards, lents, *refs):
    (
        columns_ref, input_attn_ref, attended_ref, input_mlp_ref, stats_forward_ref,
        stats_back_ref, home_out_ref, packed_ref, gate_ref, up_ref, entry_ref,
        grad_gate_ref, grad_up_ref, grad_in_ref, output_ref, input_grad_ref, sums_ref,
    ) = refs[:17]
    partials = refs[17:20]
    (
        attn_t_ref, attended_t_ref, mlp_t_ref, home_ref, stats_ref, tile_buf, part_buf,
        load_sems, store_sems, send_sems, recv_sems, own_sem,
    ) = refs[20:32]
    tally_refs, refs = refs[32:40], refs[40:]
    half, full = jnp.bfloat16, jnp.float32
    spot = Spot(shards)
    swap = Swap(spot, packed_ref, home_ref, (send_sems, recv_sems), own_sem)
    tally = Tally(spot, stats_ref, sums_ref, tally_refs)
    outputs = (grad_gate_ref, grad_up_ref, grad_in_ref)
    reduces = [
        Reduce(spot, lents[g], partials[g], outputs[g], refs[20 * g : 20 * g + 20])
        for g in range(3)
    ]
    steps = spot.half + 1
    parts = 5
    tile = tile_buf.shape[2]
    tiles = gate_ref.shape[1] // tile

    def at(i):
        return pl.ds(pl.multiple_of(i * tile, tile), tile)

    def product(source, lefts, partial, reduce):
        def load(i):
            slot = lax.rem(i, 2)
            return pltpu.make_async_copy(
                source.at[:, at(i)], tile_buf.at[slot], load_sems.at[slot]
            )

        def store(i):
            slot = lax.rem(i, 2)
            return pltpu.make_async_copy(
                part_buf.at[slot], partial.at[:, at(i)], store_sems.at[slot]
            )

        load(0).start()
        first = 0
        for left, count in lefts:

            def one(i, carry, left=left):
                slot = lax.rem(i, 2)
                load(i).wait()

                @pl.when(i + 1 < tiles)
                def _():
                    load(i + 1).start()

                @pl.when(i >= 2)
                def _():
                    store(i - 2).wait()

                part_buf[slot] = matmul(left[...], tile_buf[slot]).astype(half)
                store(i).start()
                return carry

            lax.fori_loop(first, first + count, one, 0)
            first += count
        for i in (tiles - 2, tiles - 1):
            store(i).wait()

        def begin(item, carry):
            reduce.start(item)
            return carry

        lax.fori_loop(0, spot.chips, begin, 0)
        reduce.far_step(0)

    greet(spot)
    swap.start(0, parts)
    stats_ref[0:8, :] = stats_forward_ref[...]
    stats_ref[8:32, :] = stats_back_ref[...]
    tally.start()
    mlp_t_ref[...] = input_mlp_ref[...].astype(full).T.astype(half)
    product(gate_ref, [(mlp_t_ref, tiles)], partials[0], reduces[0])
    swap.start(1, parts)
    product(up_ref, [(mlp_t_ref, tiles)], partials[1], reduces[1])
    swap.start(2, parts)
    chosen = pick_rows(columns_ref[:, 0:1], home_ref.shape[0])

    def ticks(tick, carry):
        reduces[0].step(tick)
        reduces[1].step(tick)

        @pl.when(tick < 2)
        def _():
            swap.start(3 + tick, parts)

        @pl.when(tick == 0)
        def _():
            attn_t_ref[...] = input_attn_ref[...].astype(full).T.astype(half)
            attended_t_ref[...] = attended_ref[...].astype(full).T.astype(half)
            product(
                entry_ref,
                [(attn_t_ref, tiles - tiles // 4), (attended_t_ref, tiles // 4)],
                partials[2],
                reduces[2],
            )

        @pl.when(tick == 1)
        def _():
            matmul_columns(output_ref, chosen, home_out_ref)
            tally.middle()

        reduces[2].step(tick)

        return carry

    lax.fori_loop(0, steps, ticks, 0)
    swap.finish()
    matmul_columns(input_grad_ref, chosen, home_ref)
    tally.finish()
    for reduce in reduces:
        reduce.finish()


def weight_grad_call(shards, inputs, far_inputs, lents, collective_id):
    tile = 512
    packed, hidden = far_inputs[0], far_inputs[1].shape[1]
    tokens, width = inputs[1].shape
    assert hidden == 4 * width
    half, full = jnp.bfloat16, jnp.float32
    shape = jax.ShapeDtypeStruct
    anywhere = pl.BlockSpec(memory_space=pl.ANY)
    inside = pl.BlockSpec(memory_space=pltpu.VMEM)
    scratch = []
    for lent in lents:
        scratch += Reduce.scratch(shards, lent, width // shards, hidden)
    results = pl.pallas_call(
        functools.partial(weight_grad_kernel, shards, lents),
        out_shape=[
            *[Reduce.out_shape(shards, lent, shape((width, hidden), half)) for lent in lents],
            shape((tokens, width), half),
            shape((tokens, width), half),
            shape((32, 128), full),
            *[shape((width, hidden), half)] * 3,
        ],
        in_specs=[inside] * len(inputs) + [anywhere] * len(far_inputs),
        out_specs=[anywhere] * 3 + [inside] * 3 + [anywhere] * 3,
        scratch_shapes=[
            *[pltpu.VMEM((width, tokens), half)] * 3,
            pltpu.VMEM(packed.shape, half),
            pltpu.VMEM((32, 128), full),
            pltpu.VMEM((2, tokens, tile), half),
            pltpu.VMEM((2, width, tile), half),
            DMA((2,)),
            DMA((2,)),
            DMA((shards,)),
            DMA((shards,)),
            DMA,
            *Tally.scratch(shards, (32, 128)),
            *scratch,
        ],
        compiler_params=pltpu.CompilerParams(
            collective_id=collective_id, has_side_effects=True, vmem_limit_bytes=VMEM_LIMIT
        ),
    )(*inputs, *far_inputs)
    return results[:6]


def on_device(
    tokens,
    cotangent,
    send_slot,
    recv_slot,
    lengths,
    variate,
    valid_mask,
    norm_attn,
    w_query,
    w_key,
    w_value,
    w_out,
    variate_bias,
    norm_mlp,
    w_gate,
    w_up,
    w_down,
):
    shards = lax.axis_size("shard")
    tok_rows, width = tokens.shape
    slot_total = 2 * tok_rows
    heads = variate_bias.shape[1]
    half, full = jnp.bfloat16, jnp.float32
    share = width // shards
    indices = jnp.stack([send_slot, recv_slot, variate, valid_mask])
    rows = jnp.concatenate([indices, jnp.zeros_like(indices)])
    pair_count = width // heads // 2
    frequency = 1.0 / 10000.0 ** (np.arange(pair_count, dtype=np.float32) / pair_count)
    frequency = jnp.asarray(np.tile(frequency, 128 // pair_count)[None], full)
    gains = jnp.stack([norm_attn, norm_mlp]).astype(full)
    gains = jnp.pad(gains, ((0, 6), (0, 128 - share)))
    shape = jax.ShapeDtypeStruct
    packed_shape = shape((slot_total, width), half)
    token_shape = shape((tok_rows, width), half)
    *full_in, arrived_tokens, out_cotangent, cosine, sine, columns, gain_attn, gain_mlp = (
        gather_call(
            shards, rows, tokens, cotangent, lengths, frequency, [w_query, w_key, w_value],
            (4, 4, 4), gains, 1,
        )
    )
    inside = pl.BlockSpec(memory_space=pltpu.VMEM)
    anywhere = pl.BlockSpec(memory_space=pl.ANY)
    scalar = pl.BlockSpec(memory_space=pltpu.SMEM)
    hidden = w_gate.shape[1]
    (
        (
            stream, input_attn, head_rows, attended, logs,
            gates, ups, hidden_rows, packed, middle, input_mlp, stats_forward,
        ),
        (full_out, full_gate, full_up, full_down),
        (arrived_grads,),
    ) = forward_gather_call(
        shards,
        [
            arrived_tokens, columns, rows, lengths, variate_bias, gain_attn, *full_in,
            cosine, sine, gain_mlp,
        ],
        [anywhere] + [inside] * 2 + [scalar] * 2 + [inside] + [anywhere] * 3 + [inside] * 3,
        [
            token_shape,
            token_shape,
            shape((tok_rows, 3 * width), half),
            token_shape,
            shape((heads, tok_rows), full),
            shape((tok_rows, hidden), full),
            shape((tok_rows, hidden), full),
            shape((tok_rows, hidden), half),
            packed_shape,
            shape((tok_rows, width), full),
            token_shape,
            shape((8, 128), full),
        ],
        [anywhere] * 8 + [inside] + [anywhere] * 2 + [inside],
        [w_out, w_gate, w_up, w_down],
        (2, 4, 2, 2),
        [out_cotangent],
        2,
    )
    (
        entry_grads, packed_grad, stats_back, grad_down, grad_gates, grad_ups, home_out, _,
    ) = input_grad_call(
        shards,
        [
            columns, rows, lengths, variate_bias, gain_mlp, gain_attn, middle, full_out,
            arrived_grads, head_rows, logs, cosine, sine, stream,
        ],
        [inside] * 2
        + [scalar] * 2
        + [inside] * 2
        + [anywhere] * 4
        + [inside]
        + [anywhere] * 3,
        [*full_in, packed, gates, ups, hidden_rows, full_gate, full_up, full_down],
        4,
        3,
    )
    grad_gate, grad_up, grad_in, output, input_grad, sums = weight_grad_call(
        shards,
        [columns, input_attn, attended, input_mlp, stats_forward, stats_back, home_out],
        [packed_grad, grad_gates, grad_ups, entry_grads],
        (4, 2, 2),
        4,
    )
    rep = lax.axis_index("rep").astype(jnp.int32).reshape(1, 1)
    (
        output, input_grad, grad_gate, grad_up, grad_down,
        grad_query, grad_key, grad_value, grad_out,
    ) = local_call(
        assemble_kernel,
        [
            token_shape,
            token_shape,
            *[shape((share, hidden), full)] * 2,
            shape((hidden // shards, width), full),
            *[shape((share, width), full)] * 4,
        ],
        [rep, grad_gate, grad_up, grad_down, grad_in, output, input_grad],
        [scalar] + [inside] * 6,
        [pltpu.VMEM((share, hidden), full)],
    )
    squares = jnp.sum(sums[0:6], axis=1)
    root_means = jnp.sqrt(squares[:5] / (squares[5] * width))
    share_start = lax.axis_index("shard") * share
    grad_norm_mlp = lax.dynamic_slice_in_dim(sums[8:16].reshape(-1), share_start, share)
    grad_norm_attn = lax.dynamic_slice_in_dim(sums[16:24].reshape(-1), share_start, share)
    bias_grads = sums[24, : 2 * heads].reshape(2, heads)
    return (
        output,
        input_grad,
        grad_norm_attn,
        grad_query,
        grad_key,
        grad_value,
        grad_out,
        bias_grads,
        grad_norm_mlp,
        grad_gate,
        grad_up,
        grad_down,
        root_means,
    )


def solution(mesh):
    in_specs = (
        P(("rep", "shard"), None),
        P(("rep", "shard"), None),
        P(("rep", "shard")),
        P(("rep", "shard")),
        P(("rep", "shard"), None),
        P(("rep", "shard")),
        P(("rep", "shard")),
        P("shard"),
        P("shard", None),
        P("shard", None),
        P("shard", None),
        P("shard", None),
        P(),
        P("shard"),
        P("shard", None),
        P("shard", None),
        P("shard", None),
    )
    out_specs = (
        P(("rep", "shard"), None),
        P(("rep", "shard"), None),
        P("shard"),
        P("shard", None),
        P("shard", None),
        P("shard", None),
        P("shard", None),
        P(),
        P("shard"),
        P("shard", None),
        P("shard", None),
        P("shard", None),
        P(),
    )
    return jax.shard_map(
        on_device, mesh=mesh, in_specs=in_specs, out_specs=out_specs, check_vma=False
    )
```

```python
import functools
import math

import jax
import jax.numpy as jnp
import numpy as np
from jax import lax
from jax.experimental import pallas as pl
from jax.experimental.pallas import tpu as pltpu
from jax.sharding import PartitionSpec as P

MESH = pl.DeviceIdType.MESH
DMA = pltpu.SemaphoreType.DMA
epsilon = 1e-06
masked_score = -1e30
VMEM_LIMIT = 62 << 20


def ring_place(chip, chips):
    return jnp.where(chip % 2 == 0, chip // 2, chips - 1 - chip // 2)


def ring_chip(place, chips):
    wrapped = lax.rem(place + 2 * chips, chips)
    return jnp.where(wrapped < chips // 2, 2 * wrapped, 2 * (chips - 1 - wrapped) + 1)


class Spot:
    def __init__(self, shards):
        self.shards = shards
        self.chips = shards // 2
        self.half = self.chips // 2
        self.rep = lax.axis_index("rep")
        self.shard = lax.axis_index("shard")
        self.core = lax.rem(self.shard, 2)
        self.place = ring_place(self.shard // 2, self.chips)
        self.sibling = self.shard + 1 - 2 * self.core

    def block(self, place, core=None):
        return 2 * ring_chip(place, self.chips) + (self.core if core is None else core)

    def along(self, way, distance):
        return self.place - distance if way == 0 else self.place + distance

    def ahead(self, way):
        return (self.rep, self.block(self.along(way, -1)))


def greet(spot):
    barrier = pltpu.get_barrier_semaphore()

    def peer(k, carry):
        target = lax.rem(spot.shard + k, spot.shards)
        pl.semaphore_signal(barrier, inc=1, device_id=(spot.rep, target), device_id_type=MESH)
        return carry

    lax.fori_loop(1, spot.shards, peer, 0)
    pl.semaphore_signal(
        barrier, inc=1, device_id=(1 - spot.rep, spot.shard), device_id_type=MESH
    )
    pl.semaphore_wait(barrier, spot.shards)


def remote(src, dst, sems, at, target):
    return pltpu.make_async_remote_copy(
        src_ref=src,
        dst_ref=dst,
        send_sem=sems[0].at[at],
        recv_sem=sems[1].at[at],
        device_id=target,
        device_id_type=MESH,
    )


class Swap:
    def __init__(self, spot, source, arrived, sems, own_sem):
        self.spot, self.sems = spot, sems
        self.source, self.arrived = source, arrived
        self.capacity = arrived.shape[0] // spot.shards
        self.own = pltpu.make_async_copy(
            self.part(spot.shard), arrived.at[self.rows(spot.shard)], own_sem
        )

    def rows(self, shard):
        return pl.ds(pl.multiple_of(shard * self.capacity, 8), self.capacity)

    def part(self, shard):
        if self.source.shape[0] == self.capacity:
            return self.source
        return self.source.at[self.rows(shard)]

    def copy(self, k):
        spot = self.spot
        target = lax.rem(spot.shard + 7 * k, spot.shards)
        return remote(
            self.part(target),
            self.arrived.at[self.rows(spot.shard)],
            self.sems,
            (k,),
            (spot.rep, target),
        )

    def start(self, slot, slots):
        size = -(-self.spot.shards // slots)

        def one(k, carry):
            @pl.when(k == 0)
            def _():
                self.own.start()

            @pl.when(k > 0)
            def _():
                self.copy(k).start()

            return carry

        first = jnp.minimum(slot * size, self.spot.shards)
        lax.fori_loop(first, jnp.minimum(first + size, self.spot.shards), one, 0)

    def finish(self):
        def one(k, carry):
            self.copy(k).wait()
            return carry

        lax.fori_loop(1, self.spot.shards, one, 0)
        self.own.wait()


class Gather:
    def __init__(self, spot, lent, shard_ref, full_ref, sems):
        self.spot, self.lent, self.shard_ref, self.full_ref = spot, lent, shard_ref, full_ref
        self.rows = shard_ref.shape[0]
        self.unit = shard_ref.shape[1] // 8
        self.kept = 8 - lent
        self.ring_sems, self.near_sems, self.far_sems, self.far_near_sems = (
            sems[0:2],
            sems[2:4],
            sems[4:6],
            sems[6:8],
        )
        self.whole_sems, self.own_sem = sems[8:10], sems[10]

    def span(self, way, short):
        first, count = self.lent * self.spot.rep, self.kept
        if short:
            first, count = first + way * (count // 2), count // 2
        return pl.ds(pl.multiple_of(first * self.unit, 128), count * self.unit)

    def region(self, way, hop, short):
        block = self.spot.block(self.spot.along(way, hop))
        return self.full_ref.at[pl.ds(block * self.rows, self.rows), self.span(way, short)]

    def ring(self, way, hop, short, source=None):
        region = self.region(way, hop, short)
        return remote(
            region if source is None else source,
            region,
            self.ring_sems,
            (way, hop),
            self.spot.ahead(way),
        )

    def near(self, way, hop, short):
        region = self.region(way, hop + 1, short)
        target = (self.spot.rep, self.spot.sibling)
        return remote(region, region, self.near_sems, (way, hop), target)

    def lent_region(self, way, hop, owner):
        block = self.spot.block(self.spot.along(way, hop + 1))
        columns = pl.ds(
            pl.multiple_of(self.kept * owner * self.unit, 128), self.lent * self.unit
        )
        return self.full_ref.at[pl.ds(block * self.rows, self.rows), columns]

    def far(self, way, hop):
        region = self.lent_region(way, hop, self.spot.rep)
        target = (1 - self.spot.rep, self.spot.shard)
        return remote(region, region, self.far_sems, (way, hop), target)

    def far_near(self, way, hop):
        region = self.lent_region(way, hop, 1 - self.spot.rep)
        target = (self.spot.rep, self.spot.sibling)
        return remote(region, region, self.far_near_sems, (way, hop), target)

    def own(self):
        spot = self.spot
        mine = self.full_ref.at[pl.ds(spot.shard * self.rows, self.rows)]
        whole = remote(self.shard_ref, mine, self.whole_sems, (0,), (spot.rep, spot.sibling))
        return whole, pltpu.make_async_copy(self.shard_ref, mine, self.own_sem)

    def start(self):
        for way in (0, 1):
            self.ring(way, 0, False, self.shard_ref.at[:, self.span(way, False)]).start()
        for copy in self.own():
            copy.start()

    def step(self, hop):
        final = self.spot.half - 1

        @pl.when(hop < final)
        def _():
            for way in (0, 1):
                self.ring(way, hop, False).wait_recv()

                @pl.when(hop < final - 1)
                def _():
                    self.ring(way, hop + 1, False).start()

                @pl.when(hop == final - 1)
                def _():
                    self.ring(way, hop + 1, True).start()

            for way in (0, 1):
                self.far(way, hop).start()
                self.near(way, hop, False).start()

        @pl.when(hop == final)
        def _():
            for way in (0, 1):
                self.ring(way, hop, True).wait_recv()
            self.far(0, hop).start()
            for way in (0, 1):
                self.near(way, hop, True).start()

        @pl.when(hop > 0)
        def _():
            for way in (0, 1):
                self.relay(way, hop - 1)

    def relay(self, way, hop):
        self.far(way, hop).wait_recv()
        self.far_near(way, hop).start()

    def finish(self):
        final = self.spot.half - 1
        for copy in self.own():
            copy.wait()

        def one(hop, carry):
            for way in (0, 1):
                self.ring(way, hop, False).wait_send()
                self.near(way, hop, False).wait()
                self.far(way, hop).wait_send()
                self.far_near(way, hop).wait()
            return carry

        lax.fori_loop(0, final, one, 0)
        for way in (0, 1):
            self.ring(way, final, True).wait_send()
            self.near(way, final, True).wait()
        self.far(0, final).wait_send()
        self.far_near(0, final).wait()

    @staticmethod
    def scratch(half):
        return [DMA((2, half))] * 8 + [DMA((1,))] * 2 + [DMA]


class GatherAll:
    def __init__(self, spot, lents, swap_count, inputs, outputs, scratch):
        count = len(lents)
        self.spot = spot
        self.gathers = [
            Gather(spot, lents[g], inputs[g], outputs[g], scratch[11 * g : 11 * g + 11])
            for g in range(count)
        ]
        scratch = scratch[11 * count :]
        self.swaps = [
            Swap(
                spot,
                inputs[count + i],
                outputs[count + i],
                scratch[3 * i : 3 * i + 2],
                scratch[3 * i + 2],
            )
            for i in range(swap_count)
        ]

    def start(self):
        greet(self.spot)
        for gather in self.gathers:
            gather.start()

    def exchange(self, slot, slots):
        for swap in self.swaps:
            swap.start(slot, slots)

    def steps(self, slot, slots):
        def one(hop, carry):
            for gather in self.gathers:
                gather.step(hop)
            return carry

        half = self.spot.half
        lax.fori_loop(slot * half // slots, (slot + 1) * half // slots, one, 0)

    def finish_gathers(self):
        for gather in self.gathers:
            gather.relay(0, self.spot.half - 1)
        for gather in self.gathers:
            gather.finish()

    def finish(self):
        self.finish_gathers()
        for swap in self.swaps:
            swap.finish()

    @staticmethod
    def scratch(shards, count, swap_count):
        return Gather.scratch(shards // 4) * count + [
            DMA((shards,)),
            DMA((shards,)),
            DMA,
        ] * swap_count


def gather_kernel(shards, lents, *refs):
    spot = Spot(shards)
    rows_ref, tokens_ref, cotangent_ref, lengths_ref, frequency_ref = refs[:5]
    count = len(lents)
    pieces, gains_ref, refs = refs[5 : 5 + count], refs[5 + count], refs[6 + count :]
    outputs, packed_out, refs = refs[: count + 1], refs[count + 1], refs[count + 2 :]
    cosine_ref, sine_ref, columns_ref, *gain_refs = refs[:5]
    packed_ref, all_gains_ref, scratch = refs[5], refs[6], refs[7:]
    work = GatherAll(
        spot, lents, 2, [*pieces, packed_ref, gains_ref], [*outputs, all_gains_ref], scratch
    )
    work.start()
    chosen = place_rows(rows_ref[0:1, :], packed_ref.shape[0])
    matmul_columns(packed_ref, chosen, tokens_ref)

    def one(hop, carry):
        work.exchange(hop, spot.half)

        @pl.when(hop == 0)
        def _():
            matmul_columns(packed_out, chosen, cotangent_ref)
            angle_tables(lengths_ref, frequency_ref, cosine_ref, sine_ref)
            columns_ref[...] = rows_ref[...].T

        work.steps(hop, spot.half)
        return carry

    lax.fori_loop(0, spot.half, one, 0)
    work.finish()
    share = tokens_ref.shape[1] // shards
    for gain_ref, row in zip(gain_refs, gain_rows(all_gains_ref, share), strict=True):
        gain_ref[...] = row


def gather_shapes(shards, pieces, sent, shared):
    return (
        [
            jax.ShapeDtypeStruct((shards * piece.shape[0], piece.shape[1]), piece.dtype)
            for piece in pieces
        ]
        + [jax.ShapeDtypeStruct(rows.shape, rows.dtype) for rows in sent]
        + [
            jax.ShapeDtypeStruct((shards * each.shape[0], each.shape[1]), each.dtype)
            for each in shared
        ]
    )


def gather_call(
    shards, rows, tokens, cotangent, lengths, frequency, pieces, lents, gains, collective_id
):
    anywhere = pl.BlockSpec(memory_space=pl.ANY)
    inside = pl.BlockSpec(memory_space=pltpu.VMEM)
    count = len(pieces)
    packed = jax.ShapeDtypeStruct((2 * tokens.shape[0], tokens.shape[1]), tokens.dtype)
    results = pl.pallas_call(
        functools.partial(gather_kernel, shards, lents),
        out_shape=[
            *gather_shapes(shards, pieces, [packed], []),
            packed,
            *[jax.ShapeDtypeStruct((tokens.shape[0], 128), jnp.float32)] * 2,
            jax.ShapeDtypeStruct(rows.shape[::-1], rows.dtype),
            *[jax.ShapeDtypeStruct((1, tokens.shape[1]), jnp.float32)] * 2,
        ],
        in_specs=[
            *[inside] * 3,
            pl.BlockSpec(memory_space=pltpu.SMEM),
            inside,
            *[anywhere] * (count + 1),
        ],
        out_specs=[anywhere] * (count + 1) + [inside] * 6,
        scratch_shapes=[
            pltpu.VMEM(packed.shape, packed.dtype),
            pltpu.VMEM((8 * shards, 128), jnp.float32),
            *GatherAll.scratch(shards, count, 2),
        ],
        compiler_params=pltpu.CompilerParams(
            collective_id=collective_id, has_side_effects=True, vmem_limit_bytes=VMEM_LIMIT
        ),
    )(rows, tokens, cotangent, lengths, frequency, *pieces, gains)
    return results


class Reduce:
    def __init__(self, spot, lent, partial_ref, out_ref, refs, part=0, parts=1):
        self.spot, self.lent, self.partial, self.out = spot, lent, partial_ref, out_ref
        self.block_rows = partial_ref.shape[0] // spot.shards
        self.columns = partial_ref.shape[1]
        self.rows = self.block_rows // parts
        self.offset = part * self.rows
        self.unit = self.columns // 8
        self.kept = 8 - lent
        self.width = self.kept * self.unit
        (
            self.own,
            self.sib,
            self.got,
            self.own_far,
            self.sib_far,
            self.got_far,
            self.got_last,
        ) = refs[:7]
        sems = refs[7:]
        self.load_sem, self.load_far_sem = sems[0], sems[1]
        self.sib_sems, self.sib_far_sems = sems[2:4], sems[4:6]
        self.ring_sems, self.far_sems, self.last_sems = sems[6:8], sems[8:10], sems[10:12]
        self.out_sems = sems[12]

    @staticmethod
    def scratch(shards, lent, rows, columns):
        chips = shards // 2
        unit = columns // 8
        kept, lend = (8 - lent) * unit, lent * unit
        half = jnp.bfloat16
        buffers = [
            pltpu.VMEM((chips, rows, kept), half),
            pltpu.VMEM((chips, rows, kept), half),
            pltpu.VMEM((2, chips // 2, rows, kept), half),
            pltpu.VMEM((chips, rows, lend), half),
            pltpu.VMEM((chips, rows, lend), half),
            pltpu.VMEM((chips, rows, lend), half),
            pltpu.VMEM((rows, kept), half),
        ]
        sems = [DMA((chips,))] * 6 + [DMA((2, chips // 2))] * 2
        sems += [DMA((chips,))] * 2 + [DMA((1,))] * 2 + [DMA((2,))]
        return buffers + sems

    def owner(self, item, core):
        half = self.spot.half
        pair = (item + 1) // 2
        ahead = lax.rem(item, 2) == 1
        distance = half - pair
        place = jnp.where(ahead, self.spot.place + distance, self.spot.place - distance)
        return self.spot.block(place, core)

    def cut(self, item, core, first, count):
        columns = pl.ds(pl.multiple_of(first * self.unit, 128), count * self.unit)
        block = self.owner(item, core)
        first = pl.multiple_of(block * self.block_rows + self.offset, 16)
        return self.partial.at[pl.ds(first, self.rows), columns]

    def kept_cut(self, item, core):
        return self.cut(item, core, self.lent * self.spot.rep, self.kept)

    def lent_cut(self, item, core):
        return self.cut(item, core, self.kept * (1 - self.spot.rep), self.lent)

    def load(self, item):
        source = self.kept_cut(item, self.spot.core)
        return pltpu.make_async_copy(source, self.own.at[item], self.load_sem.at[item])

    def load_far(self, item):
        source = self.lent_cut(item, self.spot.core)
        return pltpu.make_async_copy(source, self.own_far.at[item], self.load_far_sem.at[item])

    def give(self, item):
        source = self.kept_cut(item, 1 - self.spot.core)
        target = (self.spot.rep, self.spot.sibling)
        return remote(source, self.sib.at[item], self.sib_sems, (item,), target)

    def give_far(self, item):
        source = self.lent_cut(item, 1 - self.spot.core)
        target = (self.spot.rep, self.spot.sibling)
        return remote(source, self.sib_far.at[item], self.sib_far_sems, (item,), target)

    def ring(self, way, step, short=False):
        item = 0 if short else 2 * step - 1 + way
        columns = pl.ds(way * self.width // 2, self.width // 2) if short else slice(None)
        return remote(
            self.own.at[item, :, columns],
            self.got.at[way, step, :, columns],
            self.ring_sems,
            (way, step),
            self.spot.ahead(way),
        )

    def far(self, item):
        target = (1 - self.spot.rep, self.spot.shard)
        return remote(
            self.own_far.at[item], self.got_far.at[item], self.far_sems, (item,), target
        )

    @staticmethod
    def out_shape(shards, lent, partial):
        rows, columns = partial.shape[0] // shards, partial.shape[1]
        return jax.ShapeDtypeStruct((2, rows, (8 - lent) * columns // 8), jnp.bfloat16)

    def last(self):
        target = (1 - self.spot.rep, self.spot.shard)
        source = self.own.at[self.spot.chips - 1]
        return remote(source, self.got_last, self.last_sems, (0,), target)

    def start(self, item):
        self.load_far(item).start()
        self.give_far(item).start()
        self.load(item).start()
        self.give(item).start()

    def tiles(self, width, body):
        chunk = width if width <= 768 else 512
        chunks = width // chunk

        def one(i, carry):
            tile, first = i // chunks, lax.rem(i, chunks) * chunk
            body(pl.ds(pl.multiple_of(tile * 16, 16), 16), first, chunk)
            return carry

        lax.fori_loop(0, self.rows // 16 * chunks, one, 0)

    def far_step(self, item):
        self.load_far(item).wait()
        self.give_far(item).wait_recv()

        def add(rows, first, count):
            at = pl.ds(pl.multiple_of(first, 128), count)
            total = self.own_far[item, rows, at].astype(jnp.float32)
            total += self.sib_far[item, rows, at].astype(jnp.float32)
            self.own_far[item, rows, at] = total.astype(jnp.bfloat16)

        self.tiles(self.lent * self.unit, add)
        self.far(item).start()

    def fold(self, item, extra=(), start=0, width=None):
        def add(rows, first, count):
            at = pl.ds(pl.multiple_of(start + first, 128), count)
            total = self.own[item, rows, at].astype(jnp.float32)
            total += self.sib[item, rows, at].astype(jnp.float32)
            for way, step in extra:
                total += self.got[way, step, rows, at].astype(jnp.float32)
            self.own[item, rows, at] = total.astype(jnp.bfloat16)

        self.tiles(self.width if width is None else width, add)

    def ready(self, item):
        self.load(item).wait()
        self.give(item).wait_recv()
        self.far(item).wait_recv()
        offset = self.spot.rep * (self.kept - self.lent) * self.unit

        def add(rows, first, count):
            at = pl.ds(pl.multiple_of(offset + first, 128), count)
            total = self.sib[item, rows, at].astype(jnp.float32)
            lent_at = pl.ds(pl.multiple_of(first, 128), count)
            total += self.got_far[item, rows, lent_at].astype(jnp.float32)
            self.sib[item, rows, at] = total.astype(jnp.bfloat16)

        self.tiles(self.lent * self.unit, add)

    def step(self, step):
        half, chips = self.spot.half, self.spot.chips

        @pl.when(step == 0)
        def _():
            self.ready(0)
            self.fold(0)
            for way in (0, 1):
                self.ring(way, 0, True).start()

        @pl.when((step > 0) & (step < half))
        def _():
            for way in (0, 1):
                item = 2 * step - 1 + way
                self.ready(item)

                @pl.when(step == 1)
                def _():
                    self.ring(way, 0, True).wait_recv()
                    middle = self.width // 2
                    self.fold(item, [(way, 0)], way * middle, middle)
                    self.fold(item, [], (1 - way) * middle, middle)

                @pl.when(step > 1)
                def _():
                    self.ring(way, step - 1).wait_recv()
                    self.fold(item, [(way, step - 1)])

                self.ring(way, step).start()

        @pl.when(step == half)
        def _():
            self.ready(chips - 1)
            for way in (0, 1):
                self.ring(way, half - 1).wait_recv()
            self.fold(chips - 1, [(0, half - 1), (1, half - 1)])
            self.last().start()

        @pl.when(step < half)
        def _():
            self.far_step(2 * step + 1)

            @pl.when(step < half - 1)
            def _():
                self.far_step(2 * step + 2)

    def finish(self):
        spot = self.spot
        rows = pl.ds(self.offset, self.rows)
        mine = pltpu.make_async_copy(
            self.own.at[spot.chips - 1], self.out.at[0, rows], self.out_sems.at[0]
        )
        mine.start()
        self.last().wait()
        theirs = pltpu.make_async_copy(
            self.got_last, self.out.at[1, rows], self.out_sems.at[1]
        )
        theirs.start()
        mine.wait()
        theirs.wait()

        def one(item, carry):
            self.give_far(item).wait_send()
            self.far(item).wait_send()
            self.give(item).wait_send()
            return carry

        lax.fori_loop(0, spot.chips, one, 0)
        for way in (0, 1):
            self.ring(way, 0, True).wait_send()

        def two(step, carry):
            for way in (0, 1):
                self.ring(way, step).wait_send()
            return carry

        lax.fori_loop(1, spot.half, two, 0)


class Tally:
    def __init__(self, spot, mine, out, refs):
        self.spot, self.mine, self.out = spot, mine, out
        self.got, self.half, self.other = refs[0:3]
        self.sems, self.own_sem, self.far_sems = refs[3:5], refs[5], refs[6:8]
        self.own = pltpu.make_async_copy(mine, self.got.at[spot.shard], self.own_sem)

    def copy(self, k):
        spot = self.spot
        target = lax.rem(spot.shard + k, spot.shards)
        return remote(self.mine, self.got.at[spot.shard], self.sems, (k,), (spot.rep, target))

    def far(self):
        target = (1 - self.spot.rep, self.spot.shard)
        return remote(self.half, self.other, self.far_sems, (0,), target)

    def start(self):
        def one(k, carry):
            self.copy(k).start()
            return carry

        lax.fori_loop(1, self.spot.shards, one, 0)
        self.own.start()

    def middle(self):
        def one(k, carry):
            self.copy(k).wait()
            return carry

        lax.fori_loop(1, self.spot.shards, one, 0)
        self.own.wait()

        def add(k, total):
            return total + self.got[k]

        self.half[...] = lax.fori_loop(0, self.spot.shards, add, jnp.zeros_like(self.half))
        self.far().start()

    def finish(self):
        self.far().wait()
        self.out[...] = self.half[...] + self.other[...]

    @staticmethod
    def scratch(shards, shape):
        full = jnp.float32
        return [
            pltpu.VMEM((shards, *shape), full),
            pltpu.VMEM(shape, full),
            pltpu.VMEM(shape, full),
            DMA((shards,)),
            DMA((shards,)),
            DMA,
            DMA((1,)),
            DMA((1,)),
        ]


def matmul(left, right, left_dim=1, right_dim=0):
    return lax.dot_general(
        left, right, (((left_dim,), (right_dim,)), ((), ())), preferred_element_type=jnp.float32
    )


def matmul_columns(out_ref, left, right_ref):
    def one(i, carry):
        at = pl.ds(pl.multiple_of(i * 512, 512), 512)
        part = matmul(left, right_ref[:, at].astype(jnp.bfloat16))
        out_ref[:, at] = part.astype(out_ref.dtype)
        return carry

    lax.fori_loop(0, out_ref.shape[1] // 512, one, 0)


def pick_rows(slot_column, slot_total):
    shape = (slot_column.shape[0], slot_total)
    return (slot_column == lax.broadcasted_iota(jnp.int32, shape, 1)).astype(jnp.bfloat16)


def place_rows(slot_row, slot_total):
    shape = (slot_total, slot_row.shape[1])
    return (slot_row == lax.broadcasted_iota(jnp.int32, shape, 0)).astype(jnp.bfloat16)


def assemble_kernel(rep_ref, *refs):
    raws, plain, sums_ref, refs = refs[:4], refs[4:6], refs[6], refs[7:]
    plain_outs, outs, root_ref, whole_ref = refs[:2], refs[2:9], refs[9], refs[10]
    square = jnp.sum(sums_ref[0:8, :], axis=1, keepdims=True)
    root = jnp.sqrt(square / (square[5:6, :] * plain_outs[0].shape[1]))
    row = lax.broadcasted_iota(jnp.int32, (8, 128), 0)
    lane = lax.broadcasted_iota(jnp.int32, (8, 128), 1)
    root_ref[...] = jnp.sum(jnp.where(row == lane, root, 0.0), axis=0, keepdims=True)
    for source, target in zip(plain, plain_outs, strict=True):
        target[...] = source[...]
    for raw_ref, out_ref in zip(raws, [*outs[:3], whole_ref], strict=True):
        kept = raw_ref.shape[2]
        columns = out_ref.shape[1]
        lent = columns - kept

        def write(low, high, raw_ref=raw_ref, out_ref=out_ref, kept=kept, lent=lent):
            def part(which, first, count):
                return raw_ref[which, :, first : first + count].astype(jnp.float32)

            out_ref[:, 0:lent] = part(low, 0, lent)
            if kept > lent:
                out_ref[:, lent:kept] = part(low, lent, kept - lent) + part(high, 0, kept - lent)
            out_ref[:, kept:] = part(high, kept - lent, lent)

        @pl.when(rep_ref[0, 0] == 0)
        def _(write=write):
            write(0, 1)

        @pl.when(rep_ref[0, 0] != 0)
        def _(write=write):
            write(1, 0)

    width = outs[3].shape[1]
    for i in range(4):
        outs[3 + i][...] = whole_ref[:, i * width : (i + 1) * width]


def assemble_call(rep, raws, plain, sums, shapes):
    def halves(array):
        *lead, rows, columns = array.shape
        return pl.BlockSpec(
            (*lead, rows // 2, columns), lambda i: (0,) * len(lead) + (i, 0)
        )

    root = jax.ShapeDtypeStruct((1, 128), jnp.float32)
    inputs = [*raws, *plain]
    largest = raws[-1]
    columns = sum(each.shape[1] for each in shapes[-4:])
    return pl.pallas_call(
        assemble_kernel,
        out_shape=[*shapes, root],
        grid=(2,),
        in_specs=[pl.BlockSpec(memory_space=pltpu.SMEM)]
        + [halves(each) for each in inputs]
        + [pl.BlockSpec(sums.shape, lambda i: (0, 0))],
        out_specs=[halves(each) for each in shapes]
        + [pl.BlockSpec(root.shape, lambda i: (0, 0))],
        scratch_shapes=[pltpu.VMEM((largest.shape[1] // 2, columns), jnp.float32)],
        compiler_params=pltpu.CompilerParams(vmem_limit_bytes=VMEM_LIMIT),
    )(rep, *inputs, sums)


def segment_of(index, lengths_ref):
    first = lengths_ref[0, 0]
    second = first + lengths_ref[0, 1]
    third = second + lengths_ref[0, 2]
    return (
        (index >= first).astype(jnp.int32)
        + (index >= second).astype(jnp.int32)
        + (index >= third).astype(jnp.int32)
    )


def angle_tables(lengths_ref, frequency_ref, cosine_ref, sine_ref):
    index = lax.broadcasted_iota(jnp.int32, (cosine_ref.shape[0], 1), 0)
    segment = segment_of(index, lengths_ref)
    begin = jnp.zeros_like(index)
    end = 0
    for i in range(3):
        end = end + lengths_ref[0, i]
        begin = jnp.where(segment == i + 1, end, begin)
    angle = (index - begin).astype(jnp.float32) * frequency_ref[...]
    lane = lax.broadcasted_iota(jnp.int32, angle.shape, 1)
    sine = jnp.sin(angle)
    cosine_ref[...] = jnp.cos(angle)
    sine_ref[...] = jnp.where(lane % 64 < 32, -sine, sine)


def gain_rows(gains_ref, share):
    shards = gains_ref.shape[0] // 8
    rows = []
    for which in (0, 1):
        parts = []
        for first in range(0, shards * share, 128):
            total = jnp.zeros((1, 128), jnp.float32)
            for lane in range(0, 128, share):
                at = (first + lane) // share * 8 + which
                part = gains_ref[at : at + 1, :]
                total += part if lane == 0 else pltpu.roll(part, lane, 1)
            parts.append(total)
        rows.append(jnp.concatenate(parts, axis=1))
    return rows


def pair_masks(columns_ref, rows_ref, lengths_ref, same_ref, hidden_ref):
    size = columns_ref.shape[0]
    shape = (size, size)
    key_id = lax.broadcasted_iota(jnp.int32, shape, 0)
    query_id = lax.broadcasted_iota(jnp.int32, shape, 1)
    key_column = lax.broadcasted_iota(jnp.int32, (size, 1), 0)
    query_row = lax.broadcasted_iota(jnp.int32, (1, size), 1)
    together = segment_of(key_column, lengths_ref) == segment_of(query_row, lengths_ref)
    seen = together & ((columns_ref[:, 3:4] > 0) | (key_id == query_id))
    same_ref[...] = (columns_ref[:, 2:3] == rows_ref[2:3, :]).astype(jnp.float32)
    hidden_ref[...] = jnp.where(seen, 0.0, masked_score)


def turn(values, cosine, sine):
    width = values.shape[1]
    lane = lax.broadcasted_iota(jnp.int32, values.shape, 1)
    other = jnp.where(
        lane % 64 < 32, pltpu.roll(values, width - 32, 1), pltpu.roll(values, 32, 1)
    )
    return values * cosine + other * sine


def head_lanes(values, head):
    lane = lax.broadcasted_iota(jnp.int32, values.shape, 1)
    return jnp.where((lane < 64) == (head == 0), values, jnp.zeros_like(values))


def project(input_ref, weight_refs, cosine_ref, sine_ref, out_ref, scale):
    width = weight_refs[0].shape[0]
    cosine = jnp.concatenate([cosine_ref[...]] * 2, axis=1)
    sine = jnp.concatenate([sine_ref[...]] * 2, axis=1)

    def one(i, carry):
        def columns(part):
            return pl.ds(pl.multiple_of(part * width + i * 256, 256), 256)

        at = pl.ds(pl.multiple_of(i * 256, 256), 256)
        query = matmul(input_ref[...], weight_refs[0][:, at])
        out_ref[:, columns(0)] = (turn(query, cosine, sine) * scale).astype(jnp.bfloat16)
        key = matmul(input_ref[...], weight_refs[1][:, at])
        out_ref[:, columns(1)] = turn(key, cosine, sine).astype(jnp.bfloat16)
        out_ref[:, columns(2)] = matmul(input_ref[...], weight_refs[2][:, at]).astype(
            jnp.bfloat16
        )
        return carry

    lax.fori_loop(0, width // 256, one, 0)


def attend_pair(pair, width, heads_ref, bias_ref, same_ref, hidden_ref, out_ref, log_ref):
    def columns(part):
        return pl.ds(pl.multiple_of(part * width + pair * 128, 128), 128)

    query, key, value = (heads_ref[:, columns(part)] for part in range(3))
    total = None
    for which in (0, 1):
        head = 2 * pair + which
        gap = bias_ref[0, head] - bias_ref[1, head]
        scores = matmul(head_lanes(key, which), query, 1, 1)
        scores = scores + same_ref[...] * gap + hidden_ref[...]
        top = jnp.max(scores, axis=0, keepdims=True)
        weights = jnp.exp(scores - top)
        weight_sum = jnp.sum(weights, axis=0, keepdims=True)
        log_ref[pl.ds(head, 1), :] = top + jnp.log(weight_sum)
        soft = (weights * (1.0 / weight_sum)).astype(jnp.bfloat16)
        part = matmul(head_lanes(value, which), soft, 0, 0)
        total = part if total is None else total + part
    out_ref[:, pl.ds(pl.multiple_of(pair * 128, 128), 128)] = total.T.astype(jnp.bfloat16)


def normed(values):
    factor = lax.rsqrt(jnp.mean(values * values, axis=-1, keepdims=True) + epsilon)
    return values * factor, factor


def forward_body(refs, between, loaded):
    (
        arrived_ref, columns_ref, rows_ref, lengths_ref, bias_ref, gain_ref,
        query_w_ref, key_w_ref, value_w_ref, cosine_ref, sine_ref,
        stream_ref, input_ref, heads_ref, out_ref, log_ref,
        same_ref, hidden_ref,
    ) = refs
    width = gain_ref.shape[1]
    scale = 1.0 / math.sqrt(64)
    pair_masks(columns_ref, rows_ref, lengths_ref, same_ref, hidden_ref)
    chosen = pick_rows(columns_ref[:, 1:2], arrived_ref.shape[0])
    loaded(0)
    matmul_columns(stream_ref, chosen, arrived_ref)
    stream = stream_ref[...].astype(jnp.float32)
    input_ref[...] = (normed(stream)[0] * gain_ref[...]).astype(jnp.bfloat16)
    weight_refs = (query_w_ref, key_w_ref, value_w_ref)
    for i in (1, 2, 3):
        loaded(i)
    project(input_ref, weight_refs, cosine_ref, sine_ref, heads_ref, scale)

    def one(pair, carry):
        between(pair)
        attend_pair(pair, width, heads_ref, bias_ref, same_ref, hidden_ref, out_ref, log_ref)
        return carry

    lax.fori_loop(0, width // 128, one, 0)


def fold_lanes(row):
    folded = row[:, 0:128]
    for i in range(1, row.shape[1] // 128):
        folded += row[:, i * 128 : (i + 1) * 128]
    return folded


def square_into(stats_ref, at, values, columns_ref):
    valid = (columns_ref[:, 3:4] > 0).astype(jnp.float32)
    across = jnp.sum(values * values * valid, axis=0, keepdims=True)
    stats_ref[at : at + 1, :] = fold_lanes(across)


def attend_back_pair(
    pair, width, scale, heads_ref, do_ref, bias_ref, log_ref, same_ref, hidden_ref, cosine_ref,
    sine_ref, grads_ref, bias_same_ref, bias_all_ref,
):
    half = jnp.bfloat16

    def columns(part):
        return pl.ds(pl.multiple_of(part * width + pair * 128, 128), 128)

    query, key, value = (heads_ref[:, columns(part)] for part in range(3))
    grad_out = do_ref[:, columns(0)]
    query_t = key_grad = value_grad = None
    for which in (0, 1):
        head = 2 * pair + which
        gap = bias_ref[0, head] - bias_ref[1, head]
        key_part = head_lanes(key, which)
        scores = matmul(key_part, query, 1, 1)
        scores = scores + same_ref[...] * gap + hidden_ref[...]
        soft = jnp.exp(scores - log_ref[pl.ds(head, 1), :])
        grad_soft = matmul(head_lanes(value, which), grad_out, 1, 1)
        inner = jnp.sum(soft * grad_soft, axis=0, keepdims=True)
        grad_scores = (soft * (grad_soft - inner)).astype(half)
        wide = grad_scores.astype(jnp.float32)
        bias_all_ref[pl.ds(head, 1), :] = jnp.sum(wide, axis=0, keepdims=True)
        bias_same_ref[pl.ds(head, 1), :] = jnp.sum(wide * same_ref[...], axis=0, keepdims=True)
        parts = (
            matmul(key_part, grad_scores, 0, 0),
            matmul(grad_scores, head_lanes(query, which)),
            matmul(soft.astype(half), head_lanes(grad_out, which)),
        )
        if which == 0:
            query_t, key_grad, value_grad = parts
        else:
            query_t, key_grad, value_grad = (
                query_t + parts[0],
                key_grad + parts[1],
                value_grad + parts[2],
            )
    cosine, sine = cosine_ref[...], -sine_ref[...]
    grads_ref[:, columns(0)] = (turn(query_t.T, cosine, sine) * scale).astype(half)
    grads_ref[:, columns(1)] = turn(key_grad, cosine, sine).astype(half)
    grads_ref[:, columns(2)] = value_grad.astype(half)


def feed_forward(refs, weights, gates_out, ups_out, hidden_out, scratch, saves, between):
    columns_ref, rows_ref, gain_ref, stream_ref, attended_ref, out_w_ref = refs[:6]
    packed_ref, middle_ref, input_ref, stats_ref = refs[6:]
    (
        gate_buf, up_buf, down_buf, gates_buf, ups_buf, hidden_buf, mlp_ref,
        load_sems, store_sems,
    ) = scratch
    tile = gate_buf.shape[2]
    tiles = gates_out.shape[1] // tile
    half = jnp.bfloat16

    def at(i):
        return pl.ds(pl.multiple_of(i * tile, tile), tile)

    def loads(i):
        slot = lax.rem(i, 2)
        return [
            pltpu.make_async_copy(weights[0].at[:, at(i)], gate_buf.at[slot], load_sems.at[slot, 0]),
            pltpu.make_async_copy(weights[1].at[:, at(i)], up_buf.at[slot], load_sems.at[slot, 1]),
            pltpu.make_async_copy(weights[2].at[at(i)], down_buf.at[slot], load_sems.at[slot, 2]),
        ]

    def stores(i):
        slot = lax.rem(i, 2)
        return [
            pltpu.make_async_copy(gates_buf.at[slot], gates_out.at[:, at(i)], store_sems.at[slot, 0]),
            pltpu.make_async_copy(ups_buf.at[slot], ups_out.at[:, at(i)], store_sems.at[slot, 1]),
            pltpu.make_async_copy(
                hidden_buf.at[slot], hidden_out.at[:, at(i)], store_sems.at[slot, 2]
            ),
        ]

    for copy in loads(0):
        copy.start()
    stats_ref[...] = jnp.zeros_like(stats_ref)
    stream = stream_ref[...].astype(jnp.float32)
    square_into(stats_ref, 0, stream, columns_ref)
    matmul_columns(mlp_ref, attended_ref[...], out_w_ref)
    attn_out = mlp_ref[...]
    square_into(stats_ref, 1, attn_out, columns_ref)
    middle = stream + attn_out
    square_into(stats_ref, 2, middle, columns_ref)
    middle_ref[...] = middle
    input_ref[...] = (normed(middle)[0] * gain_ref[...]).astype(half)
    for copy in saves:
        copy.start()
    mlp_ref[...] = jnp.zeros_like(mlp_ref)

    def one(i, carry):
        slot = lax.rem(i, 2)
        between(i)
        for copy in loads(i):
            copy.wait()

        @pl.when(i + 1 < tiles)
        def _():
            for copy in loads(i + 1):
                copy.start()

        @pl.when(i >= 2)
        def _():
            for copy in stores(i - 2):
                copy.wait()

        gate = matmul(input_ref[...], gate_buf[slot])
        up = matmul(input_ref[...], up_buf[slot])
        gates_buf[slot] = gate
        ups_buf[slot] = up
        hidden = (gate * jax.nn.sigmoid(gate) * up).astype(half)
        hidden_buf[slot] = hidden
        for copy in stores(i):
            copy.start()
        mlp_ref[...] += matmul(hidden, down_buf[slot])
        return carry

    lax.fori_loop(0, tiles, one, 0)
    valid = (columns_ref[:, 3:4] > 0).astype(jnp.float32)
    mlp_out = mlp_ref[...]
    result = middle_ref[...] + mlp_out
    placed = place_rows(rows_ref[1:2, :], packed_ref.shape[0])
    mlp_ref[...] = result
    matmul_columns(packed_ref, placed, mlp_ref)
    square_into(stats_ref, 3, mlp_out, columns_ref)
    square_into(stats_ref, 4, result, columns_ref)
    lane = lax.broadcasted_iota(jnp.int32, (valid.shape[0], 128), 1)
    stats_ref[5:6, :] = jnp.sum(jnp.where(lane == 0, valid, 0.0), axis=0, keepdims=True)
    for i in (tiles - 2, tiles - 1):
        for copy in stores(i):
            copy.wait()


def forward_gather_kernel(shards, lents, swap_count, compute_counts, *refs):
    ins, outs = compute_counts
    total = len(lents) + swap_count
    in_refs, refs = refs[: ins + total], refs[ins + total :]
    out_refs, refs = refs[: outs + total], refs[outs + total :]
    masks, out_w_buf, out_w_sem, feed_scratch, staged, sems, scratch = (
        refs[:2], refs[2], refs[3], refs[4:13], refs[13:24], refs[24:26], refs[26:],
    )
    work = GatherAll(
        Spot(shards), lents, swap_count, in_refs[ins:], out_refs[outs:], scratch
    )
    work.start()
    *attend_ins, gain_mlp_ref = in_refs[:ins]
    arriving, leaving = staged[:4], staged[4:]
    loads = [
        pltpu.make_async_copy(attend_ins[at], arriving[i], sems[0].at[i])
        for i, at in enumerate((0, 6, 7, 8))
    ]
    for copy in loads:
        copy.start()
    attend_ins[0], attend_ins[6:9] = arriving[0], arriving[1:4]
    attend_outs, feed_outs = leaving[:5], [*out_refs[5:9], *leaving[5:], out_refs[outs - 1]]
    saves = [
        pltpu.make_async_copy(leaving[i], out_refs[at], sems[1].at[i])
        for i, at in enumerate((0, 1, 2, 3, 4, 9, 10))
    ]
    pairs = attend_ins[5].shape[1] // 128

    tiles = out_refs[5].shape[1] // feed_scratch[0].shape[2]

    def between(pair):
        work.exchange(pair, pairs + tiles)
        work.steps(pair, pairs)

    forward_body(
        (*attend_ins, *attend_outs, *masks), between, lambda i: loads[i].wait()
    )
    for copy in saves[:5]:
        copy.start()
    work.finish_gathers()
    full_refs = out_refs[outs:]
    copy = pltpu.make_async_copy(full_refs[0], out_w_buf, out_w_sem)
    copy.start()
    copy.wait()
    gates_out, ups_out, hidden_out, *feed_outs = feed_outs
    feed_forward(
        (
            attend_ins[1], attend_ins[2], gain_mlp_ref, attend_outs[0], attend_outs[3], out_w_buf,
            *feed_outs,
        ),
        full_refs[1:4], gates_out, ups_out, hidden_out, feed_scratch, saves[5:],
        lambda i: work.exchange(pairs + i, pairs + tiles),
    )
    for copy in saves:
        copy.wait()
    for swap in work.swaps:
        swap.finish()


def forward_gather_call(
    shards, inputs, spaces, out_shape, out_specs, pieces, lents, sent, collective_id
):
    anywhere = pl.BlockSpec(memory_space=pl.ANY)
    tokens, width = out_shape[0].shape
    tile = 512
    half, full = jnp.bfloat16, jnp.float32
    counts = (len(inputs), len(out_shape))
    comm = len(pieces) + len(sent)
    results = pl.pallas_call(
        functools.partial(forward_gather_kernel, shards, lents, len(sent), counts),
        out_shape=[*out_shape, *gather_shapes(shards, pieces, sent, [])],
        in_specs=spaces + [anywhere] * comm,
        out_specs=out_specs + [anywhere] * comm,
        scratch_shapes=[
            pltpu.VMEM((tokens, tokens), full),
            pltpu.VMEM((tokens, tokens), full),
            pltpu.VMEM((width, width), half),
            DMA,
            pltpu.VMEM((2, width, tile), half),
            pltpu.VMEM((2, width, tile), half),
            pltpu.VMEM((2, tile, width), half),
            pltpu.VMEM((2, tokens, tile), full),
            pltpu.VMEM((2, tokens, tile), full),
            pltpu.VMEM((2, tokens, tile), half),
            pltpu.VMEM((tokens, width), full),
            DMA((2, 3)),
            DMA((2, 3)),
            *[pltpu.VMEM(inputs[at].shape, half) for at in (0, 6, 7, 8)],
            *[
                pltpu.VMEM(out_shape[at].shape, out_shape[at].dtype)
                for at in (0, 1, 2, 3, 4, 9, 10)
            ],
            DMA((4,)),
            DMA((7,)),
            *GatherAll.scratch(shards, len(pieces), len(sent)),
        ],
        compiler_params=pltpu.CompilerParams(
            collective_id=collective_id, has_side_effects=True, vmem_limit_bytes=VMEM_LIMIT
        ),
    )(*inputs, *pieces, *sent)
    first = len(out_shape)
    second = first + len(pieces)
    return results[:first], results[first:second], results[second:]


def input_grad_kernel(shards, lent, *refs):
    (
        columns_ref, rows_ref, lengths_ref, bias_ref, gain_mlp_ref, gain_attn_ref, middle_ref,
        out_w_ref, arrived_ref, heads_ref, log_ref, cosine_ref, sine_ref, stream_ref,
        query_w_ref, key_w_ref, value_w_ref, packed_out_ref, gates_ref, ups_ref, rows_mlp_ref,
        gate_w_ref, up_w_ref, down_w_ref,
        grads_ref, packed_ref, stats_ref, grad_down_ref,
        grad_gate_ref, grad_up_ref, home_ref, partial_ref,
        gates_buf, ups_buf, gate_buf, up_buf, down_buf, grad_gate_buf, grad_up_buf,
        back_ref, dh_ref, do_ref, same_ref, hidden_ref, bias_same_ref, bias_all_ref,
        load_sems, store_sems, weight_sems, send_sems, recv_sems, own_sem,
    ) = refs[:52]
    staged, in_sems, out_sem, refs = refs[52:59], refs[59], refs[60], refs[61:]
    arriving = [
        pltpu.make_async_copy(source, buffer, in_sems.at[i])
        for i, (source, buffer) in enumerate(
            zip(
                (arrived_ref, out_w_ref, middle_ref, heads_ref, cosine_ref, sine_ref, stream_ref),
                staged,
                strict=True,
            )
        )
    ]
    arrived_ref, out_w_ref, middle_ref, heads_ref, cosine_ref, sine_ref, stream_ref = staged
    saved_ref, grads_ref = grads_ref, refs[0]
    dy_ref, refs = refs[1], refs[2:]
    save = pltpu.make_async_copy(grads_ref, saved_ref, out_sem)
    spot = Spot(shards)
    swap = Swap(spot, packed_out_ref, home_ref, (send_sems, recv_sems), own_sem)
    reduces = [
        Reduce(spot, lent, partial_ref, grad_down_ref, refs[20 * g : 20 * g + 20], g, 2)
        for g in (0, 1)
    ]
    tile = gate_buf.shape[2]
    tiles = gates_ref.shape[1] // tile
    width = gain_attn_ref.shape[1]
    half = jnp.bfloat16

    def at(i):
        return pl.ds(pl.multiple_of(i * tile, tile), tile)

    def loads(i):
        slot = lax.rem(i, 2)
        pairs = [
            (gates_ref.at[:, at(i)], gates_buf),
            (ups_ref.at[:, at(i)], ups_buf),
            (gate_w_ref.at[:, at(i)], gate_buf),
            (up_w_ref.at[:, at(i)], up_buf),
            (down_w_ref.at[at(i)], down_buf),
        ]
        return [
            pltpu.make_async_copy(source, buffer.at[slot], load_sems.at[slot, j])
            for j, (source, buffer) in enumerate(pairs)
        ]

    def stores(i):
        slot = lax.rem(i, 2)
        pairs = [(grad_gate_buf, grad_gate_ref), (grad_up_buf, grad_up_ref)]
        return [
            pltpu.make_async_copy(buffer.at[slot], target.at[:, at(i)], store_sems.at[slot, j])
            for j, (buffer, target) in enumerate(pairs)
        ]

    def row_loads(i):
        slot = lax.rem(i, 2)
        return [
            pltpu.make_async_copy(
                rows_mlp_ref.at[:, at(i)], grad_gate_buf.at[slot], load_sems.at[slot, 0]
            )
        ]

    def row_stores(i):
        slot = lax.rem(i, 2)
        return [
            pltpu.make_async_copy(
                down_buf.at[slot], partial_ref.at[at(i)], store_sems.at[slot, 0]
            )
        ]

    pairs = width // 128
    slots = tiles + pairs
    steps = spot.half + 1

    def reduce_steps(slot):
        def one(step, carry):
            for reduce in reduces:
                reduce.step(step)
            return carry

        lax.fori_loop(slot * steps // slots, (slot + 1) * steps // slots, one, 0)

    greet(spot)
    for copy in [arriving[0], *row_loads(0), *arriving[1:]]:
        copy.start()
    chosen = pick_rows(columns_ref[:, 1:2], arrived_ref.shape[0])
    arriving[0].wait()
    matmul_columns(dy_ref, chosen, arrived_ref)

    def rows_step(i, carry):
        slot = lax.rem(i, 2)
        for copy in row_loads(i):
            copy.wait()

        @pl.when(i + 1 < tiles)
        def _():
            for copy in row_loads(i + 1):
                copy.start()

        @pl.when(i >= 2)
        def _():
            for copy in row_stores(i - 2):
                copy.wait()

        down_buf[slot] = matmul(grad_gate_buf[slot], dy_ref[...], 0, 0).astype(half)
        for copy in row_stores(i):
            copy.start()
        return carry

    lax.fori_loop(0, tiles, rows_step, 0)
    for i in (tiles - 2, tiles - 1):
        for copy in row_stores(i):
            copy.wait()
    for copy in loads(0):
        copy.start()

    def begin(item, carry):
        for reduce in reduces:
            reduce.start(item)
        return carry

    lax.fori_loop(0, spot.chips, begin, 0)
    back_ref[...] = jnp.zeros_like(back_ref)
    pair_masks(columns_ref, rows_ref, lengths_ref, same_ref, hidden_ref)
    for reduce in reduces:
        reduce.far_step(0)

    def one(i, carry):
        slot = lax.rem(i, 2)

        swap.start(i, slots)
        reduce_steps(i)
        for copy in loads(i):
            copy.wait()

        @pl.when(i + 1 < tiles)
        def _():
            for copy in loads(i + 1):
                copy.start()

        @pl.when(i >= 2)
        def _():
            for copy in stores(i - 2):
                copy.wait()

        gate, up = gates_buf[slot], ups_buf[slot]
        grad_hidden = matmul(dy_ref[...], down_buf[slot], 1, 1)
        sigmoid = jax.nn.sigmoid(gate)
        grad_gate = (grad_hidden * up * sigmoid * (1.0 + gate * (1.0 - sigmoid))).astype(half)
        grad_up = (grad_hidden * gate * sigmoid).astype(half)
        grad_gate_buf[slot] = grad_gate
        grad_up_buf[slot] = grad_up
        for copy in stores(i):
            copy.start()
        back_ref[...] += matmul(grad_gate, gate_buf[slot], 1, 1) + matmul(
            grad_up, up_buf[slot], 1, 1
        )
        return carry

    lax.fori_loop(0, tiles, one, 0)
    for copy in arriving[1:]:
        copy.wait()
    stats_ref[...] = jnp.zeros_like(stats_ref)

    def through_norm(values, grad, gain_ref, first):
        entry, factor = normed(values)
        gain_grad = jnp.sum(grad * entry, axis=0, keepdims=True)
        for i in range(width // 128):
            stats_ref[first + i : first + i + 1, :] = gain_grad[:, i * 128 : (i + 1) * 128]
        scaled = grad * gain_ref[...]
        inner = jnp.mean(scaled * entry, axis=-1, keepdims=True)
        return factor * (scaled - entry * inner)

    dh = dy_ref[...].astype(jnp.float32) + through_norm(
        middle_ref[...], back_ref[...], gain_mlp_ref, 0
    )
    dh_ref[...] = dh
    branch = dh.astype(half)
    grads_ref[:, pl.ds(3 * width, width)] = branch

    def back_out(i, carry):
        at = pl.ds(pl.multiple_of(i * 256, 256), 256)
        do_ref[:, at] = matmul(
            grads_ref[:, pl.ds(3 * width, width)], out_w_ref[at, :], 1, 1
        ).astype(half)
        return carry

    lax.fori_loop(0, width // 256, back_out, 0)
    scale = 1.0 / math.sqrt(64)
    for i in (tiles - 2, tiles - 1):
        for copy in stores(i):
            copy.wait()
    halves = [pl.ds(0, tile), pl.ds(tile, tile)]

    def weight_loads(source, buffer, which):
        return [
            pltpu.make_async_copy(source.at[:, columns], buffer.at[j], weight_sems.at[which, j])
            for j, columns in enumerate(halves)
        ]

    for copy in weight_loads(query_w_ref, gate_buf, 0) + weight_loads(key_w_ref, up_buf, 1):
        copy.start()

    def two(pair, carry):
        swap.start(tiles + pair, slots)
        reduce_steps(tiles + pair)
        attend_back_pair(
            pair, width, scale, heads_ref, do_ref, bias_ref, log_ref, same_ref, hidden_ref,
            cosine_ref, sine_ref, grads_ref, bias_same_ref, bias_all_ref,
        )
        return carry

    lax.fori_loop(0, width // 128, two, 0)
    save.start()
    heads = bias_all_ref.shape[0]
    lane = lax.broadcasted_iota(jnp.int32, (heads, 128), 1)
    row = lax.broadcasted_iota(jnp.int32, (heads, 128), 0)
    same = jnp.sum(bias_same_ref[...], axis=1, keepdims=True)
    other = jnp.sum(bias_all_ref[...], axis=1, keepdims=True) - same
    stats_ref[16:17, :] = jnp.sum(
        jnp.where(lane == row, same, 0.0) + jnp.where(lane == row + heads, other, 0.0),
        axis=0,
        keepdims=True,
    )
    def through(buffer, first):
        def one(j, carry):
            at = pl.ds(pl.multiple_of(first + j * tile, tile), tile)
            back_ref[...] += matmul(grads_ref[:, at], buffer[j], 1, 1)
            return carry

        lax.fori_loop(0, 2, one, 0)

    back_ref[...] = jnp.zeros_like(back_ref)

    for copy in weight_loads(query_w_ref, gate_buf, 0):
        copy.wait()
    through(gate_buf, 0)
    for copy in weight_loads(value_w_ref, gate_buf, 0):
        copy.start()
    for copy in weight_loads(key_w_ref, up_buf, 1):
        copy.wait()
    through(up_buf, width)
    for copy in weight_loads(value_w_ref, gate_buf, 0):
        copy.wait()
    through(gate_buf, 2 * width)
    grad_stream = dh_ref[...] + through_norm(
        stream_ref[...].astype(jnp.float32), back_ref[...], gain_attn_ref, 8
    )
    placed = place_rows(rows_ref[1:2, :], packed_ref.shape[0])
    dh_ref[...] = grad_stream
    matmul_columns(packed_ref, placed, dh_ref)
    save.wait()
    swap.finish()
    for reduce in reduces:
        reduce.finish()


def input_grad_call(shards, inputs, spaces, far_inputs, lent, collective_id):
    anywhere = pl.BlockSpec(memory_space=pl.ANY)
    inside = pl.BlockSpec(memory_space=pltpu.VMEM)
    packed, gates = far_inputs[3], far_inputs[4]
    tokens, hidden = gates.shape
    width = packed.shape[1]
    heads = inputs[10].shape[0]
    tile = 512
    assert 2 * tile == width
    half, full = jnp.bfloat16, jnp.float32
    vmem, shape = pltpu.VMEM, jax.ShapeDtypeStruct
    return pl.pallas_call(
        functools.partial(input_grad_kernel, shards, lent),
        out_shape=[
            shape((tokens, 4 * width), half),
            shape(packed.shape, half),
            shape((24, 128), full),
            Reduce.out_shape(shards, lent, shape((hidden, width), half)),
            shape((tokens, hidden), half),
            shape((tokens, hidden), half),
            shape(packed.shape, half),
            shape((hidden, width), half),
        ],
        in_specs=[*spaces, *[anywhere] * len(far_inputs)],
        out_specs=[anywhere] + [inside] * 2 + [anywhere] * 5,
        scratch_shapes=[
            vmem((2, tokens, tile), full),
            vmem((2, tokens, tile), full),
            vmem((2, width, tile), half),
            vmem((2, width, tile), half),
            vmem((2, tile, width), half),
            vmem((2, tokens, tile), half),
            vmem((2, tokens, tile), half),
            vmem((tokens, width), full),
            vmem((tokens, width), full),
            vmem((tokens, width), half),
            vmem((tokens, tokens), full),
            vmem((tokens, tokens), full),
            vmem((heads, tokens), full),
            vmem((heads, tokens), full),
            DMA((2, 5)),
            DMA((2, 2)),
            DMA((2, 2)),
            DMA((shards,)),
            DMA((shards,)),
            DMA,
            *[vmem(inputs[at].shape, inputs[at].dtype) for at in (8, 7, 6, 9, 11, 12, 13)],
            DMA((7,)),
            DMA,
            vmem((tokens, 4 * width), half),
            vmem((tokens, width), half),
            *Reduce.scratch(shards, lent, hidden // shards // 2, width) * 2,
        ],
        compiler_params=pltpu.CompilerParams(
            collective_id=collective_id, has_side_effects=True, vmem_limit_bytes=VMEM_LIMIT
        ),
    )(*inputs, *far_inputs)


def weight_grad_kernel(shards, lents, *refs):
    (
        columns_ref, input_attn_ref, attended_ref, input_mlp_ref, stats_forward_ref,
        stats_back_ref, home_out_ref, packed_ref, gate_ref, up_ref, entry_ref,
        grad_gate_ref, grad_up_ref, grad_in_ref, output_ref, input_grad_ref, sums_ref,
    ) = refs[:17]
    partials = refs[17:20]
    (
        attn_t_ref, attended_t_ref, mlp_t_ref, home_ref, stats_ref, tile_buf, part_buf,
        load_sems, store_sems, send_sems, recv_sems, own_sem,
    ) = refs[20:32]
    tally_refs, staged, in_sems, refs = refs[32:40], refs[40:44], refs[44], refs[45:]
    arriving = [
        pltpu.make_async_copy(source, buffer, in_sems.at[i])
        for i, (source, buffer) in enumerate(
            zip((input_mlp_ref, input_attn_ref, attended_ref, home_out_ref), staged, strict=True)
        )
    ]
    input_mlp_ref, input_attn_ref, attended_ref, home_out_ref = staged
    half, full = jnp.bfloat16, jnp.float32
    spot = Spot(shards)
    swap = Swap(spot, packed_ref, home_ref, (send_sems, recv_sems), own_sem)
    tally = Tally(spot, stats_ref, sums_ref, tally_refs)
    outputs = (grad_gate_ref, grad_up_ref, grad_in_ref)
    reduces = [
        Reduce(spot, lents[g], partials[g], outputs[g], refs[20 * g : 20 * g + 20])
        for g in range(3)
    ]
    steps = spot.half + 1
    parts = 5
    tile = tile_buf.shape[2]
    tiles = gate_ref.shape[1] // tile

    def at(i):
        return pl.ds(pl.multiple_of(i * tile, tile), tile)

    def product(source, lefts, partial, reduce):
        def load(i):
            slot = lax.rem(i, 2)
            return pltpu.make_async_copy(
                source.at[:, at(i)], tile_buf.at[slot], load_sems.at[slot]
            )

        def store(i):
            slot = lax.rem(i, 2)
            return pltpu.make_async_copy(
                part_buf.at[slot], partial.at[:, at(i)], store_sems.at[slot]
            )

        load(0).start()
        first = 0
        for left, count in lefts:

            def one(i, carry, left=left):
                slot = lax.rem(i, 2)
                load(i).wait()

                @pl.when(i + 1 < tiles)
                def _():
                    load(i + 1).start()

                @pl.when(i >= 2)
                def _():
                    store(i - 2).wait()

                part_buf[slot] = matmul(left[...], tile_buf[slot]).astype(half)
                store(i).start()
                return carry

            lax.fori_loop(first, first + count, one, 0)
            first += count
        for i in (tiles - 2, tiles - 1):
            store(i).wait()

        def begin(item, carry):
            reduce.start(item)
            return carry

        lax.fori_loop(0, spot.chips, begin, 0)
        reduce.far_step(0)

    greet(spot)
    swap.start(0, parts)
    for copy in arriving:
        copy.start()
    stats_ref[0:8, :] = stats_forward_ref[...]
    stats_ref[8:32, :] = stats_back_ref[...]
    tally.start()
    arriving[0].wait()
    mlp_t_ref[...] = input_mlp_ref[...].astype(full).T.astype(half)
    product(gate_ref, [(mlp_t_ref, tiles)], partials[0], reduces[0])
    swap.start(1, parts)
    product(up_ref, [(mlp_t_ref, tiles)], partials[1], reduces[1])
    swap.start(2, parts)
    chosen = pick_rows(columns_ref[:, 0:1], home_ref.shape[0])

    def ticks(tick, carry):
        reduces[0].step(tick)
        reduces[1].step(tick)

        @pl.when(tick < 2)
        def _():
            swap.start(3 + tick, parts)

        @pl.when(tick == 0)
        def _():
            for copy in arriving[1:]:
                copy.wait()
            attn_t_ref[...] = input_attn_ref[...].astype(full).T.astype(half)
            attended_t_ref[...] = attended_ref[...].astype(full).T.astype(half)
            product(
                entry_ref,
                [(attn_t_ref, tiles - tiles // 4), (attended_t_ref, tiles // 4)],
                partials[2],
                reduces[2],
            )

        @pl.when(tick == 1)
        def _():
            matmul_columns(output_ref, chosen, home_out_ref)
            tally.middle()

        reduces[2].step(tick)

        return carry

    lax.fori_loop(0, steps, ticks, 0)
    swap.finish()
    matmul_columns(input_grad_ref, chosen, home_ref)
    tally.finish()
    for reduce in reduces:
        reduce.finish()


def weight_grad_call(shards, inputs, far_inputs, lents, collective_id):
    tile = 512
    packed, hidden = far_inputs[0], far_inputs[1].shape[1]
    tokens, width = inputs[1].shape
    assert hidden == 4 * width
    half, full = jnp.bfloat16, jnp.float32
    shape = jax.ShapeDtypeStruct
    anywhere = pl.BlockSpec(memory_space=pl.ANY)
    inside = pl.BlockSpec(memory_space=pltpu.VMEM)
    scratch = []
    for lent in lents:
        scratch += Reduce.scratch(shards, lent, width // shards, hidden)
    results = pl.pallas_call(
        functools.partial(weight_grad_kernel, shards, lents),
        out_shape=[
            *[Reduce.out_shape(shards, lent, shape((width, hidden), half)) for lent in lents],
            shape((tokens, width), half),
            shape((tokens, width), half),
            shape((32, 128), full),
            *[shape((width, hidden), half)] * 3,
        ],
        in_specs=[inside]
        + [anywhere] * 3
        + [inside] * 2
        + [anywhere]
        + [anywhere] * len(far_inputs),
        out_specs=[anywhere] * 3 + [inside] * 3 + [anywhere] * 3,
        scratch_shapes=[
            *[pltpu.VMEM((width, tokens), half)] * 3,
            pltpu.VMEM(packed.shape, half),
            pltpu.VMEM((32, 128), full),
            pltpu.VMEM((2, tokens, tile), half),
            pltpu.VMEM((2, width, tile), half),
            DMA((2,)),
            DMA((2,)),
            DMA((shards,)),
            DMA((shards,)),
            DMA,
            *Tally.scratch(shards, (32, 128)),
            *[pltpu.VMEM(inputs[at].shape, half) for at in (3, 1, 2, 6)],
            DMA((4,)),
            *scratch,
        ],
        compiler_params=pltpu.CompilerParams(
            collective_id=collective_id, has_side_effects=True, vmem_limit_bytes=VMEM_LIMIT
        ),
    )(*inputs, *far_inputs)
    return results[:6]


def on_device(
    tokens,
    cotangent,
    send_slot,
    recv_slot,
    lengths,
    variate,
    valid_mask,
    norm_attn,
    w_query,
    w_key,
    w_value,
    w_out,
    variate_bias,
    norm_mlp,
    w_gate,
    w_up,
    w_down,
):
    shards = lax.axis_size("shard")
    tok_rows, width = tokens.shape
    slot_total = 2 * tok_rows
    heads = variate_bias.shape[1]
    half, full = jnp.bfloat16, jnp.float32
    share = width // shards
    indices = jnp.stack([send_slot, recv_slot, variate, valid_mask])
    rows = jnp.concatenate([indices, jnp.zeros_like(indices)])
    pair_count = width // heads // 2
    frequency = 1.0 / 10000.0 ** (np.arange(pair_count, dtype=np.float32) / pair_count)
    frequency = jnp.asarray(np.tile(frequency, 128 // pair_count)[None], full)
    gains = jnp.stack([norm_attn, norm_mlp]).astype(full)
    gains = jnp.pad(gains, ((0, 6), (0, 128 - share)))
    shape = jax.ShapeDtypeStruct
    packed_shape = shape((slot_total, width), half)
    token_shape = shape((tok_rows, width), half)
    *full_in, arrived_tokens, out_cotangent, cosine, sine, columns, gain_attn, gain_mlp = (
        gather_call(
            shards, rows, tokens, cotangent, lengths, frequency, [w_query, w_key, w_value],
            (4, 4, 4), gains, 1,
        )
    )
    inside = pl.BlockSpec(memory_space=pltpu.VMEM)
    anywhere = pl.BlockSpec(memory_space=pl.ANY)
    scalar = pl.BlockSpec(memory_space=pltpu.SMEM)
    hidden = w_gate.shape[1]
    (
        (
            stream, input_attn, head_rows, attended, logs,
            gates, ups, hidden_rows, packed, middle, input_mlp, stats_forward,
        ),
        (full_out, full_gate, full_up, full_down),
        (arrived_grads,),
    ) = forward_gather_call(
        shards,
        [
            arrived_tokens, columns, rows, lengths, variate_bias, gain_attn, *full_in,
            cosine, sine, gain_mlp,
        ],
        [anywhere] + [inside] * 2 + [scalar] * 2 + [inside] + [anywhere] * 3 + [inside] * 3,
        [
            token_shape,
            token_shape,
            shape((tok_rows, 3 * width), half),
            token_shape,
            shape((heads, tok_rows), full),
            shape((tok_rows, hidden), full),
            shape((tok_rows, hidden), full),
            shape((tok_rows, hidden), half),
            packed_shape,
            shape((tok_rows, width), full),
            token_shape,
            shape((8, 128), full),
        ],
        [anywhere] * 8 + [inside] + [anywhere] * 2 + [inside],
        [w_out, w_gate, w_up, w_down],
        (4, 4, 2, 2),
        [out_cotangent],
        2,
    )
    (
        entry_grads, packed_grad, stats_back, grad_down, grad_gates, grad_ups, home_out, _,
    ) = input_grad_call(
        shards,
        [
            columns, rows, lengths, variate_bias, gain_mlp, gain_attn, middle, full_out,
            arrived_grads, head_rows, logs, cosine, sine, stream,
        ],
        [inside] * 2
        + [scalar] * 2
        + [inside] * 2
        + [anywhere] * 4
        + [inside]
        + [anywhere] * 3,
        [*full_in, packed, gates, ups, hidden_rows, full_gate, full_up, full_down],
        4,
        3,
    )
    grad_gate, grad_up, grad_in, output, input_grad, sums = weight_grad_call(
        shards,
        [columns, input_attn, attended, input_mlp, stats_forward, stats_back, home_out],
        [packed_grad, grad_gates, grad_ups, entry_grads],
        (4, 2, 2),
        4,
    )
    rep = lax.axis_index("rep").astype(jnp.int32).reshape(1, 1)
    (
        output, input_grad, grad_gate, grad_up, grad_down,
        grad_query, grad_key, grad_value, grad_out, root_means,
    ) = assemble_call(
        rep,
        [grad_gate, grad_up, grad_down, grad_in],
        [output, input_grad],
        sums,
        [
            token_shape,
            token_shape,
            *[shape((share, hidden), full)] * 2,
            shape((hidden // shards, width), full),
            *[shape((share, width), full)] * 4,
        ],
    )
    root_means = root_means[0, :5]
    share_start = lax.axis_index("shard") * share
    grad_norm_mlp = lax.dynamic_slice_in_dim(sums[8:16].reshape(-1), share_start, share)
    grad_norm_attn = lax.dynamic_slice_in_dim(sums[16:24].reshape(-1), share_start, share)
    bias_grads = sums[24, : 2 * heads].reshape(2, heads)
    return (
        output,
        input_grad,
        grad_norm_attn,
        grad_query,
        grad_key,
        grad_value,
        grad_out,
        bias_grads,
        grad_norm_mlp,
        grad_gate,
        grad_up,
        grad_down,
        root_means,
    )


def solution(mesh):
    in_specs = (
        P(("rep", "shard"), None),
        P(("rep", "shard"), None),
        P(("rep", "shard")),
        P(("rep", "shard")),
        P(("rep", "shard"), None),
        P(("rep", "shard")),
        P(("rep", "shard")),
        P("shard"),
        P("shard", None),
        P("shard", None),
        P("shard", None),
        P("shard", None),
        P(),
        P("shard"),
        P("shard", None),
        P("shard", None),
        P("shard", None),
    )
    out_specs = (
        P(("rep", "shard"), None),
        P(("rep", "shard"), None),
        P("shard"),
        P("shard", None),
        P("shard", None),
        P("shard", None),
        P("shard", None),
        P(),
        P("shard"),
        P("shard", None),
        P("shard", None),
        P("shard", None),
        P(),
    )
    return jax.shard_map(
        on_device, mesh=mesh, in_specs=in_specs, out_specs=out_specs, check_vma=False
    )
```

```python
import functools
import math

import jax
import jax.numpy as jnp
import numpy as np
from jax import lax
from jax.experimental import pallas as pl
from jax.experimental.pallas import tpu as pltpu
from jax.sharding import PartitionSpec as P

MESH = pl.DeviceIdType.MESH
DMA = pltpu.SemaphoreType.DMA
epsilon = 1e-06
masked_score = -1e30
VMEM_LIMIT = 62 << 20


def ring_place(chip, chips):
    return jnp.where(chip % 2 == 0, chip // 2, chips - 1 - chip // 2)


def ring_chip(place, chips):
    wrapped = lax.rem(place + 2 * chips, chips)
    return jnp.where(wrapped < chips // 2, 2 * wrapped, 2 * (chips - 1 - wrapped) + 1)


class Spot:
    def __init__(self, shards):
        self.shards = shards
        self.chips = shards // 2
        self.half = self.chips // 2
        self.rep = lax.axis_index("rep")
        self.shard = lax.axis_index("shard")
        self.core = lax.rem(self.shard, 2)
        self.place = ring_place(self.shard // 2, self.chips)
        self.sibling = self.shard + 1 - 2 * self.core

    def block(self, place, core=None):
        return 2 * ring_chip(place, self.chips) + (self.core if core is None else core)

    def along(self, way, distance):
        return self.place - distance if way == 0 else self.place + distance

    def ahead(self, way):
        return (self.rep, self.block(self.along(way, -1)))


def greet(spot):
    barrier = pltpu.get_barrier_semaphore()

    def peer(k, carry):
        target = lax.rem(spot.shard + k, spot.shards)
        pl.semaphore_signal(barrier, inc=1, device_id=(spot.rep, target), device_id_type=MESH)
        return carry

    lax.fori_loop(1, spot.shards, peer, 0)
    pl.semaphore_signal(
        barrier, inc=1, device_id=(1 - spot.rep, spot.shard), device_id_type=MESH
    )
    pl.semaphore_wait(barrier, spot.shards)


def remote(src, dst, sems, at, target):
    return pltpu.make_async_remote_copy(
        src_ref=src,
        dst_ref=dst,
        send_sem=sems[0].at[at],
        recv_sem=sems[1].at[at],
        device_id=target,
        device_id_type=MESH,
    )


class Swap:
    def __init__(self, spot, source, arrived, sems, own_sem):
        self.spot, self.sems = spot, sems
        self.source, self.arrived = source, arrived
        self.capacity = arrived.shape[0] // spot.shards
        self.own = pltpu.make_async_copy(
            self.part(spot.shard), arrived.at[self.rows(spot.shard)], own_sem
        )

    def rows(self, shard):
        return pl.ds(pl.multiple_of(shard * self.capacity, 8), self.capacity)

    def part(self, shard):
        if self.source.shape[0] == self.capacity:
            return self.source
        return self.source.at[self.rows(shard)]

    def copy(self, k):
        spot = self.spot
        target = lax.rem(spot.shard + 7 * k, spot.shards)
        return remote(
            self.part(target),
            self.arrived.at[self.rows(spot.shard)],
            self.sems,
            (k,),
            (spot.rep, target),
        )

    def start(self, slot, slots):
        size = -(-self.spot.shards // slots)

        def one(k, carry):
            @pl.when(k == 0)
            def _():
                self.own.start()

            @pl.when(k > 0)
            def _():
                self.copy(k).start()

            return carry

        first = jnp.minimum(slot * size, self.spot.shards)
        lax.fori_loop(first, jnp.minimum(first + size, self.spot.shards), one, 0)

    def finish(self):
        def one(k, carry):
            self.copy(k).wait()
            return carry

        lax.fori_loop(1, self.spot.shards, one, 0)
        self.own.wait()


class Gather:
    def __init__(self, spot, lent, shard_ref, full_ref, sems):
        self.spot, self.lent, self.shard_ref, self.full_ref = spot, lent, shard_ref, full_ref
        self.rows = shard_ref.shape[0]
        self.unit = shard_ref.shape[1] // 8
        self.kept = 8 - lent
        self.ring_sems, self.near_sems, self.far_sems, self.far_near_sems = (
            sems[0:2],
            sems[2:4],
            sems[4:6],
            sems[6:8],
        )
        self.whole_sems, self.own_sem = sems[8:10], sems[10]

    def span(self, way, short):
        first, count = self.lent * self.spot.rep, self.kept
        if short:
            first, count = first + way * (count // 2), count // 2
        return pl.ds(pl.multiple_of(first * self.unit, 128), count * self.unit)

    def region(self, way, hop, short):
        block = self.spot.block(self.spot.along(way, hop))
        return self.full_ref.at[pl.ds(block * self.rows, self.rows), self.span(way, short)]

    def ring(self, way, hop, short, source=None):
        region = self.region(way, hop, short)
        return remote(
            region if source is None else source,
            region,
            self.ring_sems,
            (way, hop),
            self.spot.ahead(way),
        )

    def near(self, way, hop, short):
        region = self.region(way, hop + 1, short)
        target = (self.spot.rep, self.spot.sibling)
        return remote(region, region, self.near_sems, (way, hop), target)

    def lent_region(self, way, hop, owner):
        block = self.spot.block(self.spot.along(way, hop + 1))
        columns = pl.ds(
            pl.multiple_of(self.kept * owner * self.unit, 128), self.lent * self.unit
        )
        return self.full_ref.at[pl.ds(block * self.rows, self.rows), columns]

    def far(self, way, hop):
        region = self.lent_region(way, hop, self.spot.rep)
        target = (1 - self.spot.rep, self.spot.shard)
        return remote(region, region, self.far_sems, (way, hop), target)

    def far_near(self, way, hop):
        region = self.lent_region(way, hop, 1 - self.spot.rep)
        target = (self.spot.rep, self.spot.sibling)
        return remote(region, region, self.far_near_sems, (way, hop), target)

    def own(self):
        spot = self.spot
        mine = self.full_ref.at[pl.ds(spot.shard * self.rows, self.rows)]
        whole = remote(self.shard_ref, mine, self.whole_sems, (0,), (spot.rep, spot.sibling))
        return whole, pltpu.make_async_copy(self.shard_ref, mine, self.own_sem)

    def start(self):
        for way in (0, 1):
            self.ring(way, 0, False, self.shard_ref.at[:, self.span(way, False)]).start()
        for copy in self.own():
            copy.start()

    def step(self, hop):
        final = self.spot.half - 1

        @pl.when(hop < final)
        def _():
            for way in (0, 1):
                self.ring(way, hop, False).wait_recv()

                @pl.when(hop < final - 1)
                def _():
                    self.ring(way, hop + 1, False).start()

                @pl.when(hop == final - 1)
                def _():
                    self.ring(way, hop + 1, True).start()

            for way in (0, 1):
                self.far(way, hop).start()
                self.near(way, hop, False).start()

        @pl.when(hop == final)
        def _():
            for way in (0, 1):
                self.ring(way, hop, True).wait_recv()
            self.far(0, hop).start()
            for way in (0, 1):
                self.near(way, hop, True).start()

        @pl.when(hop > 0)
        def _():
            for way in (0, 1):
                self.relay(way, hop - 1)

    def relay(self, way, hop):
        self.far(way, hop).wait_recv()
        self.far_near(way, hop).start()

    def finish(self):
        final = self.spot.half - 1
        for copy in self.own():
            copy.wait()

        def one(hop, carry):
            for way in (0, 1):
                self.ring(way, hop, False).wait_send()
                self.near(way, hop, False).wait()
                self.far(way, hop).wait_send()
                self.far_near(way, hop).wait()
            return carry

        lax.fori_loop(0, final, one, 0)
        for way in (0, 1):
            self.ring(way, final, True).wait_send()
            self.near(way, final, True).wait()
        self.far(0, final).wait_send()
        self.far_near(0, final).wait()

    @staticmethod
    def scratch(half):
        return [DMA((2, half))] * 8 + [DMA((1,))] * 2 + [DMA]


class GatherAll:
    def __init__(self, spot, lents, swap_count, inputs, outputs, scratch):
        count = len(lents)
        self.spot = spot
        self.gathers = [
            Gather(spot, lents[g], inputs[g], outputs[g], scratch[11 * g : 11 * g + 11])
            for g in range(count)
        ]
        scratch = scratch[11 * count :]
        self.swaps = [
            Swap(
                spot,
                inputs[count + i],
                outputs[count + i],
                scratch[3 * i : 3 * i + 2],
                scratch[3 * i + 2],
            )
            for i in range(swap_count)
        ]

    def start(self):
        greet(self.spot)
        for gather in self.gathers:
            gather.start()

    def exchange(self, slot, slots):
        for swap in self.swaps:
            swap.start(slot, slots)

    def steps(self, slot, slots):
        def one(hop, carry):
            for gather in self.gathers:
                gather.step(hop)
            return carry

        half = self.spot.half
        lax.fori_loop(slot * half // slots, (slot + 1) * half // slots, one, 0)

    def finish_gathers(self):
        for gather in self.gathers:
            gather.relay(0, self.spot.half - 1)
        for gather in self.gathers:
            gather.finish()

    def finish(self):
        self.finish_gathers()
        for swap in self.swaps:
            swap.finish()

    @staticmethod
    def scratch(shards, count, swap_count):
        return Gather.scratch(shards // 4) * count + [
            DMA((shards,)),
            DMA((shards,)),
            DMA,
        ] * swap_count


def gather_kernel(shards, lents, *refs):
    spot = Spot(shards)
    rows_ref, tokens_ref, cotangent_ref, lengths_ref, frequency_ref = refs[:5]
    count = len(lents)
    pieces, gains_ref, refs = refs[5 : 5 + count], refs[5 + count], refs[6 + count :]
    outputs, packed_out, refs = refs[: count + 1], refs[count + 1], refs[count + 2 :]
    cosine_ref, sine_ref, columns_ref, *gain_refs = refs[:5]
    packed_ref, all_gains_ref, scratch = refs[5], refs[6], refs[7:]
    work = GatherAll(
        spot, lents, 2, [*pieces, packed_ref, gains_ref], [*outputs, all_gains_ref], scratch
    )
    work.start()
    chosen = place_rows(rows_ref[0:1, :], packed_ref.shape[0])
    matmul_columns(packed_ref, chosen, tokens_ref)

    def one(hop, carry):
        work.exchange(hop, spot.half)

        @pl.when(hop == 0)
        def _():
            matmul_columns(packed_out, chosen, cotangent_ref)
            angle_tables(lengths_ref, frequency_ref, cosine_ref, sine_ref)
            columns_ref[...] = rows_ref[...].T

        work.steps(hop, spot.half)
        return carry

    lax.fori_loop(0, spot.half, one, 0)
    work.finish()
    share = tokens_ref.shape[1] // shards
    for gain_ref, row in zip(gain_refs, gain_rows(all_gains_ref, share), strict=True):
        gain_ref[...] = row


def gather_shapes(shards, pieces, sent, shared):
    return (
        [
            jax.ShapeDtypeStruct((shards * piece.shape[0], piece.shape[1]), piece.dtype)
            for piece in pieces
        ]
        + [jax.ShapeDtypeStruct(rows.shape, rows.dtype) for rows in sent]
        + [
            jax.ShapeDtypeStruct((shards * each.shape[0], each.shape[1]), each.dtype)
            for each in shared
        ]
    )


def gather_call(
    shards, rows, tokens, cotangent, lengths, frequency, pieces, lents, gains, collective_id
):
    anywhere = pl.BlockSpec(memory_space=pl.ANY)
    inside = pl.BlockSpec(memory_space=pltpu.VMEM)
    count = len(pieces)
    packed = jax.ShapeDtypeStruct((2 * tokens.shape[0], tokens.shape[1]), tokens.dtype)
    results = pl.pallas_call(
        functools.partial(gather_kernel, shards, lents),
        out_shape=[
            *gather_shapes(shards, pieces, [packed], []),
            packed,
            *[jax.ShapeDtypeStruct((tokens.shape[0], 128), jnp.float32)] * 2,
            jax.ShapeDtypeStruct(rows.shape[::-1], rows.dtype),
            *[jax.ShapeDtypeStruct((1, tokens.shape[1]), jnp.float32)] * 2,
        ],
        in_specs=[
            *[inside] * 3,
            pl.BlockSpec(memory_space=pltpu.SMEM),
            inside,
            *[anywhere] * (count + 1),
        ],
        out_specs=[anywhere] * (count + 1) + [inside] * 6,
        scratch_shapes=[
            pltpu.VMEM(packed.shape, packed.dtype),
            pltpu.VMEM((8 * shards, 128), jnp.float32),
            *GatherAll.scratch(shards, count, 2),
        ],
        compiler_params=pltpu.CompilerParams(
            collective_id=collective_id, has_side_effects=True, vmem_limit_bytes=VMEM_LIMIT
        ),
    )(rows, tokens, cotangent, lengths, frequency, *pieces, gains)
    return results


class Reduce:
    def __init__(self, spot, lent, partial_ref, out_ref, refs, part=0, parts=1):
        self.spot, self.lent, self.partial, self.out = spot, lent, partial_ref, out_ref
        self.block_rows = partial_ref.shape[0] // spot.shards
        self.columns = partial_ref.shape[1]
        self.rows = self.block_rows // parts
        self.offset = part * self.rows
        self.unit = self.columns // 8
        self.kept = 8 - lent
        self.width = self.kept * self.unit
        (
            self.own,
            self.sib,
            self.got,
            self.own_far,
            self.sib_far,
            self.got_far,
            self.got_last,
        ) = refs[:7]
        sems = refs[7:]
        self.load_sem, self.load_far_sem = sems[0], sems[1]
        self.sib_sems, self.sib_far_sems = sems[2:4], sems[4:6]
        self.ring_sems, self.far_sems, self.last_sems = sems[6:8], sems[8:10], sems[10:12]
        self.out_sems = sems[12]

    @staticmethod
    def scratch(shards, lent, rows, columns):
        chips = shards // 2
        unit = columns // 8
        kept, lend = (8 - lent) * unit, lent * unit
        half = jnp.bfloat16
        buffers = [
            pltpu.VMEM((chips, rows, kept), half),
            pltpu.VMEM((chips, rows, kept), half),
            pltpu.VMEM((2, chips // 2, rows, kept), half),
            pltpu.VMEM((chips, rows, lend), half),
            pltpu.VMEM((chips, rows, lend), half),
            pltpu.VMEM((chips, rows, lend), half),
            pltpu.VMEM((rows, kept), half),
        ]
        sems = [DMA((chips,))] * 6 + [DMA((2, chips // 2))] * 2
        sems += [DMA((chips,))] * 2 + [DMA((1,))] * 2 + [DMA((2,))]
        return buffers + sems

    def owner(self, item, core):
        half = self.spot.half
        pair = (item + 1) // 2
        ahead = lax.rem(item, 2) == 1
        distance = half - pair
        place = jnp.where(ahead, self.spot.place + distance, self.spot.place - distance)
        return self.spot.block(place, core)

    def cut(self, item, core, first, count):
        columns = pl.ds(pl.multiple_of(first * self.unit, 128), count * self.unit)
        block = self.owner(item, core)
        first = pl.multiple_of(block * self.block_rows + self.offset, 16)
        return self.partial.at[pl.ds(first, self.rows), columns]

    def kept_cut(self, item, core):
        return self.cut(item, core, self.lent * self.spot.rep, self.kept)

    def lent_cut(self, item, core):
        return self.cut(item, core, self.kept * (1 - self.spot.rep), self.lent)

    def load(self, item):
        source = self.kept_cut(item, self.spot.core)
        return pltpu.make_async_copy(source, self.own.at[item], self.load_sem.at[item])

    def load_far(self, item):
        source = self.lent_cut(item, self.spot.core)
        return pltpu.make_async_copy(source, self.own_far.at[item], self.load_far_sem.at[item])

    def give(self, item):
        source = self.kept_cut(item, 1 - self.spot.core)
        target = (self.spot.rep, self.spot.sibling)
        return remote(source, self.sib.at[item], self.sib_sems, (item,), target)

    def give_far(self, item):
        source = self.lent_cut(item, 1 - self.spot.core)
        target = (self.spot.rep, self.spot.sibling)
        return remote(source, self.sib_far.at[item], self.sib_far_sems, (item,), target)

    def ring(self, way, step, short=False):
        item = 0 if short else 2 * step - 1 + way
        columns = pl.ds(way * self.width // 2, self.width // 2) if short else slice(None)
        return remote(
            self.own.at[item, :, columns],
            self.got.at[way, step, :, columns],
            self.ring_sems,
            (way, step),
            self.spot.ahead(way),
        )

    def far(self, item):
        target = (1 - self.spot.rep, self.spot.shard)
        return remote(
            self.own_far.at[item], self.got_far.at[item], self.far_sems, (item,), target
        )

    @staticmethod
    def out_shape(shards, lent, partial):
        rows, columns = partial.shape[0] // shards, partial.shape[1]
        return jax.ShapeDtypeStruct((2, rows, (8 - lent) * columns // 8), jnp.bfloat16)

    def last(self):
        target = (1 - self.spot.rep, self.spot.shard)
        source = self.own.at[self.spot.chips - 1]
        return remote(source, self.got_last, self.last_sems, (0,), target)

    def start(self, item):
        self.load_far(item).start()
        self.give_far(item).start()
        self.load(item).start()
        self.give(item).start()

    def tiles(self, width, body):
        chunk = width if width <= 768 else 512
        chunks = width // chunk

        def one(i, carry):
            tile, first = i // chunks, lax.rem(i, chunks) * chunk
            body(pl.ds(pl.multiple_of(tile * 16, 16), 16), first, chunk)
            return carry

        lax.fori_loop(0, self.rows // 16 * chunks, one, 0)

    def far_step(self, item):
        self.load_far(item).wait()
        self.give_far(item).wait_recv()

        def add(rows, first, count):
            at = pl.ds(pl.multiple_of(first, 128), count)
            total = self.own_far[item, rows, at].astype(jnp.float32)
            total += self.sib_far[item, rows, at].astype(jnp.float32)
            self.own_far[item, rows, at] = total.astype(jnp.bfloat16)

        self.tiles(self.lent * self.unit, add)
        self.far(item).start()

    def fold(self, item, extra=(), start=0, width=None):
        def add(rows, first, count):
            at = pl.ds(pl.multiple_of(start + first, 128), count)
            total = self.own[item, rows, at].astype(jnp.float32)
            total += self.sib[item, rows, at].astype(jnp.float32)
            for way, step in extra:
                total += self.got[way, step, rows, at].astype(jnp.float32)
            self.own[item, rows, at] = total.astype(jnp.bfloat16)

        self.tiles(self.width if width is None else width, add)

    def ready(self, item):
        self.load(item).wait()
        self.give(item).wait_recv()
        self.far(item).wait_recv()
        offset = self.spot.rep * (self.kept - self.lent) * self.unit

        def add(rows, first, count):
            at = pl.ds(pl.multiple_of(offset + first, 128), count)
            total = self.sib[item, rows, at].astype(jnp.float32)
            lent_at = pl.ds(pl.multiple_of(first, 128), count)
            total += self.got_far[item, rows, lent_at].astype(jnp.float32)
            self.sib[item, rows, at] = total.astype(jnp.bfloat16)

        self.tiles(self.lent * self.unit, add)

    def step(self, step):
        half, chips = self.spot.half, self.spot.chips

        @pl.when(step == 0)
        def _():
            self.ready(0)
            self.fold(0)
            for way in (0, 1):
                self.ring(way, 0, True).start()

        @pl.when((step > 0) & (step < half))
        def _():
            for way in (0, 1):
                item = 2 * step - 1 + way
                self.ready(item)

                @pl.when(step == 1)
                def _():
                    self.ring(way, 0, True).wait_recv()
                    middle = self.width // 2
                    self.fold(item, [(way, 0)], way * middle, middle)
                    self.fold(item, [], (1 - way) * middle, middle)

                @pl.when(step > 1)
                def _():
                    self.ring(way, step - 1).wait_recv()
                    self.fold(item, [(way, step - 1)])

                self.ring(way, step).start()

        @pl.when(step == half)
        def _():
            self.ready(chips - 1)
            for way in (0, 1):
                self.ring(way, half - 1).wait_recv()
            self.fold(chips - 1, [(0, half - 1), (1, half - 1)])
            self.last().start()

        @pl.when(step < half)
        def _():
            self.far_step(2 * step + 1)

            @pl.when(step < half - 1)
            def _():
                self.far_step(2 * step + 2)

    def finish(self):
        spot = self.spot
        rows = pl.ds(self.offset, self.rows)
        mine = pltpu.make_async_copy(
            self.own.at[spot.chips - 1], self.out.at[0, rows], self.out_sems.at[0]
        )
        mine.start()
        self.last().wait()
        theirs = pltpu.make_async_copy(
            self.got_last, self.out.at[1, rows], self.out_sems.at[1]
        )
        theirs.start()
        mine.wait()
        theirs.wait()

        def one(item, carry):
            self.give_far(item).wait_send()
            self.far(item).wait_send()
            self.give(item).wait_send()
            return carry

        lax.fori_loop(0, spot.chips, one, 0)
        for way in (0, 1):
            self.ring(way, 0, True).wait_send()

        def two(step, carry):
            for way in (0, 1):
                self.ring(way, step).wait_send()
            return carry

        lax.fori_loop(1, spot.half, two, 0)


class Tally:
    def __init__(self, spot, mine, out, refs):
        self.spot, self.mine, self.out = spot, mine, out
        self.got, self.half, self.other = refs[0:3]
        self.sems, self.own_sem, self.far_sems = refs[3:5], refs[5], refs[6:8]
        self.own = pltpu.make_async_copy(mine, self.got.at[spot.shard], self.own_sem)

    def copy(self, k):
        spot = self.spot
        target = lax.rem(spot.shard + k, spot.shards)
        return remote(self.mine, self.got.at[spot.shard], self.sems, (k,), (spot.rep, target))

    def far(self):
        target = (1 - self.spot.rep, self.spot.shard)
        return remote(self.half, self.other, self.far_sems, (0,), target)

    def start(self):
        def one(k, carry):
            self.copy(k).start()
            return carry

        lax.fori_loop(1, self.spot.shards, one, 0)
        self.own.start()

    def middle(self):
        def one(k, carry):
            self.copy(k).wait()
            return carry

        lax.fori_loop(1, self.spot.shards, one, 0)
        self.own.wait()

        def add(k, total):
            return total + self.got[k]

        self.half[...] = lax.fori_loop(0, self.spot.shards, add, jnp.zeros_like(self.half))
        self.far().start()

    def finish(self):
        self.far().wait()
        self.out[...] = self.half[...] + self.other[...]

    @staticmethod
    def scratch(shards, shape):
        full = jnp.float32
        return [
            pltpu.VMEM((shards, *shape), full),
            pltpu.VMEM(shape, full),
            pltpu.VMEM(shape, full),
            DMA((shards,)),
            DMA((shards,)),
            DMA,
            DMA((1,)),
            DMA((1,)),
        ]


def matmul(left, right, left_dim=1, right_dim=0):
    return lax.dot_general(
        left, right, (((left_dim,), (right_dim,)), ((), ())), preferred_element_type=jnp.float32
    )


def matmul_columns(out_ref, left, right_ref):
    def one(i, carry):
        at = pl.ds(pl.multiple_of(i * 512, 512), 512)
        part = matmul(left, right_ref[:, at].astype(jnp.bfloat16))
        out_ref[:, at] = part.astype(out_ref.dtype)
        return carry

    lax.fori_loop(0, out_ref.shape[1] // 512, one, 0)


def pick_rows(slot_column, slot_total):
    shape = (slot_column.shape[0], slot_total)
    return (slot_column == lax.broadcasted_iota(jnp.int32, shape, 1)).astype(jnp.bfloat16)


def place_rows(slot_row, slot_total):
    shape = (slot_total, slot_row.shape[1])
    return (slot_row == lax.broadcasted_iota(jnp.int32, shape, 0)).astype(jnp.bfloat16)


def assemble_kernel(rep_ref, *refs):
    raws, plain, sums_ref, refs = refs[:4], refs[4:6], refs[6], refs[7:]
    plain_outs, outs, root_ref, whole_ref = refs[:2], refs[2:9], refs[9], refs[10]
    square = jnp.sum(sums_ref[0:8, :], axis=1, keepdims=True)
    root = jnp.sqrt(square / (square[5:6, :] * plain_outs[0].shape[1]))
    row = lax.broadcasted_iota(jnp.int32, (8, 128), 0)
    lane = lax.broadcasted_iota(jnp.int32, (8, 128), 1)
    root_ref[...] = jnp.sum(jnp.where(row == lane, root, 0.0), axis=0, keepdims=True)
    for source, target in zip(plain, plain_outs, strict=True):
        target[...] = source[...]
    for raw_ref, out_ref in zip(raws, [*outs[:3], whole_ref], strict=True):
        kept = raw_ref.shape[2]
        columns = out_ref.shape[1]
        lent = columns - kept

        def write(low, high, raw_ref=raw_ref, out_ref=out_ref, kept=kept, lent=lent):
            def part(which, first, count):
                return raw_ref[which, :, first : first + count].astype(jnp.float32)

            out_ref[:, 0:lent] = part(low, 0, lent)
            if kept > lent:
                out_ref[:, lent:kept] = part(low, lent, kept - lent) + part(high, 0, kept - lent)
            out_ref[:, kept:] = part(high, kept - lent, lent)

        @pl.when(rep_ref[0, 0] == 0)
        def _(write=write):
            write(0, 1)

        @pl.when(rep_ref[0, 0] != 0)
        def _(write=write):
            write(1, 0)

    width = outs[3].shape[1]
    for i in range(4):
        outs[3 + i][...] = whole_ref[:, i * width : (i + 1) * width]


def assemble_call(rep, raws, plain, sums, shapes):
    def halves(array):
        *lead, rows, columns = array.shape
        return pl.BlockSpec(
            (*lead, rows // 2, columns), lambda i: (0,) * len(lead) + (i, 0)
        )

    root = jax.ShapeDtypeStruct((1, 128), jnp.float32)
    inputs = [*raws, *plain]
    largest = raws[-1]
    columns = sum(each.shape[1] for each in shapes[-4:])
    return pl.pallas_call(
        assemble_kernel,
        out_shape=[*shapes, root],
        grid=(2,),
        in_specs=[pl.BlockSpec(memory_space=pltpu.SMEM)]
        + [halves(each) for each in inputs]
        + [pl.BlockSpec(sums.shape, lambda i: (0, 0))],
        out_specs=[halves(each) for each in shapes]
        + [pl.BlockSpec(root.shape, lambda i: (0, 0))],
        scratch_shapes=[pltpu.VMEM((largest.shape[1] // 2, columns), jnp.float32)],
        compiler_params=pltpu.CompilerParams(vmem_limit_bytes=VMEM_LIMIT),
    )(rep, *inputs, sums)


def segment_of(index, lengths_ref):
    first = lengths_ref[0, 0]
    second = first + lengths_ref[0, 1]
    third = second + lengths_ref[0, 2]
    return (
        (index >= first).astype(jnp.int32)
        + (index >= second).astype(jnp.int32)
        + (index >= third).astype(jnp.int32)
    )


def angle_tables(lengths_ref, frequency_ref, cosine_ref, sine_ref):
    index = lax.broadcasted_iota(jnp.int32, (cosine_ref.shape[0], 1), 0)
    segment = segment_of(index, lengths_ref)
    begin = jnp.zeros_like(index)
    end = 0
    for i in range(3):
        end = end + lengths_ref[0, i]
        begin = jnp.where(segment == i + 1, end, begin)
    angle = (index - begin).astype(jnp.float32) * frequency_ref[...]
    lane = lax.broadcasted_iota(jnp.int32, angle.shape, 1)
    sine = jnp.sin(angle)
    cosine_ref[...] = jnp.cos(angle)
    sine_ref[...] = jnp.where(lane % 64 < 32, -sine, sine)


def gain_rows(gains_ref, share):
    shards = gains_ref.shape[0] // 8
    rows = []
    for which in (0, 1):
        parts = []
        for first in range(0, shards * share, 128):
            total = jnp.zeros((1, 128), jnp.float32)
            for lane in range(0, 128, share):
                at = (first + lane) // share * 8 + which
                part = gains_ref[at : at + 1, :]
                total += part if lane == 0 else pltpu.roll(part, lane, 1)
            parts.append(total)
        rows.append(jnp.concatenate(parts, axis=1))
    return rows


def pair_masks(columns_ref, rows_ref, lengths_ref, same_ref, hidden_ref):
    size = columns_ref.shape[0]
    shape = (size, size)
    key_id = lax.broadcasted_iota(jnp.int32, shape, 0)
    query_id = lax.broadcasted_iota(jnp.int32, shape, 1)
    key_column = lax.broadcasted_iota(jnp.int32, (size, 1), 0)
    query_row = lax.broadcasted_iota(jnp.int32, (1, size), 1)
    together = segment_of(key_column, lengths_ref) == segment_of(query_row, lengths_ref)
    seen = together & ((columns_ref[:, 3:4] > 0) | (key_id == query_id))
    same_ref[...] = (columns_ref[:, 2:3] == rows_ref[2:3, :]).astype(jnp.float32)
    hidden_ref[...] = jnp.where(seen, 0.0, masked_score)


def turn(values, cosine, sine):
    width = values.shape[1]
    lane = lax.broadcasted_iota(jnp.int32, values.shape, 1)
    other = jnp.where(
        lane % 64 < 32, pltpu.roll(values, width - 32, 1), pltpu.roll(values, 32, 1)
    )
    return values * cosine + other * sine


def head_lanes(values, head):
    lane = lax.broadcasted_iota(jnp.int32, values.shape, 1)
    return jnp.where((lane < 64) == (head == 0), values, jnp.zeros_like(values))


def project(input_ref, weight_refs, cosine_ref, sine_ref, out_ref, scale):
    width = weight_refs[0].shape[0]
    cosine = jnp.concatenate([cosine_ref[...]] * 2, axis=1)
    sine = jnp.concatenate([sine_ref[...]] * 2, axis=1)

    def one(i, carry):
        def columns(part):
            return pl.ds(pl.multiple_of(part * width + i * 256, 256), 256)

        at = pl.ds(pl.multiple_of(i * 256, 256), 256)
        query = matmul(input_ref[...], weight_refs[0][:, at])
        out_ref[:, columns(0)] = (turn(query, cosine, sine) * scale).astype(jnp.bfloat16)
        key = matmul(input_ref[...], weight_refs[1][:, at])
        out_ref[:, columns(1)] = turn(key, cosine, sine).astype(jnp.bfloat16)
        out_ref[:, columns(2)] = matmul(input_ref[...], weight_refs[2][:, at]).astype(
            jnp.bfloat16
        )
        return carry

    lax.fori_loop(0, width // 256, one, 0)


def attend_pair(pair, width, heads_ref, bias_ref, same_ref, hidden_ref, out_ref, log_ref):
    def columns(part):
        return pl.ds(pl.multiple_of(part * width + pair * 128, 128), 128)

    query, key, value = (heads_ref[:, columns(part)] for part in range(3))
    total = None
    for which in (0, 1):
        head = 2 * pair + which
        gap = bias_ref[0, head] - bias_ref[1, head]
        scores = matmul(head_lanes(key, which), query, 1, 1)
        scores = scores + same_ref[...] * gap + hidden_ref[...]
        top = jnp.max(scores, axis=0, keepdims=True)
        weights = jnp.exp(scores - top)
        weight_sum = jnp.sum(weights, axis=0, keepdims=True)
        log_ref[pl.ds(head, 1), :] = top + jnp.log(weight_sum)
        soft = (weights * (1.0 / weight_sum)).astype(jnp.bfloat16)
        part = matmul(head_lanes(value, which), soft, 0, 0)
        total = part if total is None else total + part
    out_ref[:, pl.ds(pl.multiple_of(pair * 128, 128), 128)] = total.T.astype(jnp.bfloat16)


def normed(values):
    factor = lax.rsqrt(jnp.mean(values * values, axis=-1, keepdims=True) + epsilon)
    return values * factor, factor


def forward_body(refs, between, loaded):
    (
        arrived_ref, columns_ref, rows_ref, lengths_ref, bias_ref, gain_ref,
        query_w_ref, key_w_ref, value_w_ref, cosine_ref, sine_ref,
        stream_ref, input_ref, heads_ref, out_ref, log_ref,
        same_ref, hidden_ref,
    ) = refs
    width = gain_ref.shape[1]
    scale = 1.0 / math.sqrt(64)
    pair_masks(columns_ref, rows_ref, lengths_ref, same_ref, hidden_ref)
    chosen = pick_rows(columns_ref[:, 1:2], arrived_ref.shape[0])
    loaded(0)
    matmul_columns(stream_ref, chosen, arrived_ref)
    stream = stream_ref[...].astype(jnp.float32)
    input_ref[...] = (normed(stream)[0] * gain_ref[...]).astype(jnp.bfloat16)
    weight_refs = (query_w_ref, key_w_ref, value_w_ref)
    for i in (1, 2, 3):
        loaded(i)
    project(input_ref, weight_refs, cosine_ref, sine_ref, heads_ref, scale)

    def one(pair, carry):
        between(pair)
        attend_pair(pair, width, heads_ref, bias_ref, same_ref, hidden_ref, out_ref, log_ref)
        return carry

    lax.fori_loop(0, width // 128, one, 0)


def fold_lanes(row):
    folded = row[:, 0:128]
    for i in range(1, row.shape[1] // 128):
        folded += row[:, i * 128 : (i + 1) * 128]
    return folded


def square_into(stats_ref, at, values, columns_ref):
    valid = (columns_ref[:, 3:4] > 0).astype(jnp.float32)
    across = jnp.sum(values * values * valid, axis=0, keepdims=True)
    stats_ref[at : at + 1, :] = fold_lanes(across)


def attend_back_pair(
    pair, width, scale, heads_ref, do_ref, bias_ref, log_ref, same_ref, hidden_ref, cosine_ref,
    sine_ref, grads_ref, bias_same_ref, bias_all_ref,
):
    half = jnp.bfloat16

    def columns(part):
        return pl.ds(pl.multiple_of(part * width + pair * 128, 128), 128)

    query, key, value = (heads_ref[:, columns(part)] for part in range(3))
    grad_out = do_ref[:, columns(0)]
    query_t = key_grad = value_grad = None
    for which in (0, 1):
        head = 2 * pair + which
        gap = bias_ref[0, head] - bias_ref[1, head]
        key_part = head_lanes(key, which)
        scores = matmul(key_part, query, 1, 1)
        scores = scores + same_ref[...] * gap + hidden_ref[...]
        soft = jnp.exp(scores - log_ref[pl.ds(head, 1), :])
        grad_soft = matmul(head_lanes(value, which), grad_out, 1, 1)
        inner = jnp.sum(soft * grad_soft, axis=0, keepdims=True)
        grad_scores = (soft * (grad_soft - inner)).astype(half)
        wide = grad_scores.astype(jnp.float32)
        bias_all_ref[pl.ds(head, 1), :] = jnp.sum(wide, axis=0, keepdims=True)
        bias_same_ref[pl.ds(head, 1), :] = jnp.sum(wide * same_ref[...], axis=0, keepdims=True)
        parts = (
            matmul(key_part, grad_scores, 0, 0),
            matmul(grad_scores, head_lanes(query, which)),
            matmul(soft.astype(half), head_lanes(grad_out, which)),
        )
        if which == 0:
            query_t, key_grad, value_grad = parts
        else:
            query_t, key_grad, value_grad = (
                query_t + parts[0],
                key_grad + parts[1],
                value_grad + parts[2],
            )
    cosine, sine = cosine_ref[...], -sine_ref[...]
    grads_ref[:, columns(0)] = (turn(query_t.T, cosine, sine) * scale).astype(half)
    grads_ref[:, columns(1)] = turn(key_grad, cosine, sine).astype(half)
    grads_ref[:, columns(2)] = value_grad.astype(half)


def feed_forward(refs, weights, gates_out, ups_out, hidden_out, scratch, saves, between):
    columns_ref, rows_ref, gain_ref, stream_ref, attended_ref, out_w_ref = refs[:6]
    packed_ref, middle_ref, input_ref, stats_ref = refs[6:]
    (
        gate_buf, up_buf, down_buf, gates_buf, ups_buf, hidden_buf, mlp_ref,
        load_sems, store_sems,
    ) = scratch
    tile = gate_buf.shape[2]
    tiles = gates_out.shape[1] // tile
    half = jnp.bfloat16

    def at(i):
        return pl.ds(pl.multiple_of(i * tile, tile), tile)

    def loads(i):
        slot = lax.rem(i, 2)
        return [
            pltpu.make_async_copy(weights[0].at[:, at(i)], gate_buf.at[slot], load_sems.at[slot, 0]),
            pltpu.make_async_copy(weights[1].at[:, at(i)], up_buf.at[slot], load_sems.at[slot, 1]),
            pltpu.make_async_copy(weights[2].at[at(i)], down_buf.at[slot], load_sems.at[slot, 2]),
        ]

    def stores(i):
        slot = lax.rem(i, 2)
        return [
            pltpu.make_async_copy(gates_buf.at[slot], gates_out.at[:, at(i)], store_sems.at[slot, 0]),
            pltpu.make_async_copy(ups_buf.at[slot], ups_out.at[:, at(i)], store_sems.at[slot, 1]),
            pltpu.make_async_copy(
                hidden_buf.at[slot], hidden_out.at[:, at(i)], store_sems.at[slot, 2]
            ),
        ]

    for copy in loads(0):
        copy.start()
    stats_ref[...] = jnp.zeros_like(stats_ref)
    stream = stream_ref[...].astype(jnp.float32)
    square_into(stats_ref, 0, stream, columns_ref)
    matmul_columns(mlp_ref, attended_ref[...], out_w_ref)
    attn_out = mlp_ref[...]
    square_into(stats_ref, 1, attn_out, columns_ref)
    middle = stream + attn_out
    square_into(stats_ref, 2, middle, columns_ref)
    middle_ref[...] = middle
    input_ref[...] = (normed(middle)[0] * gain_ref[...]).astype(half)
    for copy in saves:
        copy.start()
    mlp_ref[...] = jnp.zeros_like(mlp_ref)

    def one(i, carry):
        slot = lax.rem(i, 2)
        between(i)
        for copy in loads(i):
            copy.wait()

        @pl.when(i + 1 < tiles)
        def _():
            for copy in loads(i + 1):
                copy.start()

        @pl.when(i >= 2)
        def _():
            for copy in stores(i - 2):
                copy.wait()

        gate = matmul(input_ref[...], gate_buf[slot])
        up = matmul(input_ref[...], up_buf[slot])
        gates_buf[slot] = gate
        ups_buf[slot] = up
        hidden = (gate * jax.nn.sigmoid(gate) * up).astype(half)
        hidden_buf[slot] = hidden
        for copy in stores(i):
            copy.start()
        mlp_ref[...] += matmul(hidden, down_buf[slot])
        return carry

    lax.fori_loop(0, tiles, one, 0)
    valid = (columns_ref[:, 3:4] > 0).astype(jnp.float32)
    mlp_out = mlp_ref[...]
    result = middle_ref[...] + mlp_out
    placed = place_rows(rows_ref[1:2, :], packed_ref.shape[0])
    mlp_ref[...] = result
    matmul_columns(packed_ref, placed, mlp_ref)
    square_into(stats_ref, 3, mlp_out, columns_ref)
    square_into(stats_ref, 4, result, columns_ref)
    lane = lax.broadcasted_iota(jnp.int32, (valid.shape[0], 128), 1)
    stats_ref[5:6, :] = jnp.sum(jnp.where(lane == 0, valid, 0.0), axis=0, keepdims=True)
    for i in (tiles - 2, tiles - 1):
        for copy in stores(i):
            copy.wait()


def forward_gather_kernel(shards, lents, swap_count, compute_counts, *refs):
    ins, outs = compute_counts
    total = len(lents) + swap_count
    in_refs, refs = refs[: ins + total], refs[ins + total :]
    out_refs, refs = refs[: outs + total], refs[outs + total :]
    masks, out_w_buf, out_w_sem, feed_scratch, staged, sems, scratch = (
        refs[:2], refs[2], refs[3], refs[4:13], refs[13:24], refs[24:26], refs[26:],
    )
    work = GatherAll(
        Spot(shards), lents, swap_count, in_refs[ins:], out_refs[outs:], scratch
    )
    work.start()
    *attend_ins, gain_mlp_ref = in_refs[:ins]
    arriving, leaving = staged[:4], staged[4:]
    loads = [
        pltpu.make_async_copy(attend_ins[at], arriving[i], sems[0].at[i])
        for i, at in enumerate((0, 6, 7, 8))
    ]
    for copy in loads:
        copy.start()
    attend_ins[0], attend_ins[6:9] = arriving[0], arriving[1:4]
    attend_outs, feed_outs = leaving[:5], [*out_refs[5:9], *leaving[5:], out_refs[outs - 1]]
    saves = [
        pltpu.make_async_copy(leaving[i], out_refs[at], sems[1].at[i])
        for i, at in enumerate((0, 1, 2, 3, 4, 9, 10))
    ]
    pairs = attend_ins[5].shape[1] // 128

    tiles = out_refs[5].shape[1] // feed_scratch[0].shape[2]

    def between(pair):
        work.exchange(pair, pairs + tiles)
        work.steps(pair, pairs)

    forward_body(
        (*attend_ins, *attend_outs, *masks), between, lambda i: loads[i].wait()
    )
    for copy in saves[:5]:
        copy.start()
    work.finish_gathers()
    full_refs = out_refs[outs:]
    copy = pltpu.make_async_copy(full_refs[0], out_w_buf, out_w_sem)
    copy.start()
    copy.wait()
    gates_out, ups_out, hidden_out, *feed_outs = feed_outs
    feed_forward(
        (
            attend_ins[1], attend_ins[2], gain_mlp_ref, attend_outs[0], attend_outs[3], out_w_buf,
            *feed_outs,
        ),
        full_refs[1:4], gates_out, ups_out, hidden_out, feed_scratch, saves[5:],
        lambda i: work.exchange(pairs + i, pairs + tiles),
    )
    for copy in saves:
        copy.wait()
    for swap in work.swaps:
        swap.finish()


def forward_gather_call(
    shards, inputs, spaces, out_shape, out_specs, pieces, lents, sent, collective_id
):
    anywhere = pl.BlockSpec(memory_space=pl.ANY)
    tokens, width = out_shape[0].shape
    tile = 512
    half, full = jnp.bfloat16, jnp.float32
    counts = (len(inputs), len(out_shape))
    comm = len(pieces) + len(sent)
    results = pl.pallas_call(
        functools.partial(forward_gather_kernel, shards, lents, len(sent), counts),
        out_shape=[*out_shape, *gather_shapes(shards, pieces, sent, [])],
        in_specs=spaces + [anywhere] * comm,
        out_specs=out_specs + [anywhere] * comm,
        scratch_shapes=[
            pltpu.VMEM((tokens, tokens), full),
            pltpu.VMEM((tokens, tokens), full),
            pltpu.VMEM((width, width), half),
            DMA,
            pltpu.VMEM((2, width, tile), half),
            pltpu.VMEM((2, width, tile), half),
            pltpu.VMEM((2, tile, width), half),
            pltpu.VMEM((2, tokens, tile), full),
            pltpu.VMEM((2, tokens, tile), full),
            pltpu.VMEM((2, tokens, tile), half),
            pltpu.VMEM((tokens, width), full),
            DMA((2, 3)),
            DMA((2, 3)),
            *[pltpu.VMEM(inputs[at].shape, half) for at in (0, 6, 7, 8)],
            *[
                pltpu.VMEM(out_shape[at].shape, out_shape[at].dtype)
                for at in (0, 1, 2, 3, 4, 9, 10)
            ],
            DMA((4,)),
            DMA((7,)),
            *GatherAll.scratch(shards, len(pieces), len(sent)),
        ],
        compiler_params=pltpu.CompilerParams(
            collective_id=collective_id, has_side_effects=True, vmem_limit_bytes=VMEM_LIMIT
        ),
    )(*inputs, *pieces, *sent)
    first = len(out_shape)
    second = first + len(pieces)
    return results[:first], results[first:second], results[second:]


def input_grad_kernel(shards, lent, *refs):
    (
        columns_ref, rows_ref, lengths_ref, bias_ref, gain_mlp_ref, gain_attn_ref, middle_ref,
        out_w_ref, arrived_ref, heads_ref, log_ref, cosine_ref, sine_ref, stream_ref,
        query_w_ref, key_w_ref, value_w_ref, packed_out_ref, gates_ref, ups_ref, rows_mlp_ref,
        gate_w_ref, up_w_ref, down_w_ref,
        grads_ref, packed_ref, stats_ref, grad_down_ref,
        grad_gate_ref, grad_up_ref, home_ref, partial_ref,
        gates_buf, ups_buf, gate_buf, up_buf, down_buf, grad_gate_buf, grad_up_buf,
        back_ref, dh_ref, do_ref, same_ref, hidden_ref, bias_same_ref, bias_all_ref,
        load_sems, store_sems, weight_sems, send_sems, recv_sems, own_sem,
    ) = refs[:52]
    staged, in_sems, out_sem, refs = refs[52:59], refs[59], refs[60], refs[61:]
    arriving = [
        pltpu.make_async_copy(source, buffer, in_sems.at[i])
        for i, (source, buffer) in enumerate(
            zip(
                (arrived_ref, out_w_ref, middle_ref, heads_ref, cosine_ref, sine_ref, stream_ref),
                staged,
                strict=True,
            )
        )
    ]
    arrived_ref, out_w_ref, middle_ref, heads_ref, cosine_ref, sine_ref, stream_ref = staged
    saved_ref, grads_ref = grads_ref, refs[0]
    dy_ref, refs = refs[1], refs[2:]
    save = pltpu.make_async_copy(grads_ref, saved_ref, out_sem)
    spot = Spot(shards)
    swap = Swap(spot, packed_out_ref, home_ref, (send_sems, recv_sems), own_sem)
    reduces = [
        Reduce(spot, lent, partial_ref, grad_down_ref, refs[20 * g : 20 * g + 20], g, 2)
        for g in (0, 1)
    ]
    tile = gate_buf.shape[2]
    tiles = gates_ref.shape[1] // tile
    width = gain_attn_ref.shape[1]
    half = jnp.bfloat16

    def at(i):
        return pl.ds(pl.multiple_of(i * tile, tile), tile)

    def loads(i):
        slot = lax.rem(i, 2)
        pairs = [
            (gates_ref.at[:, at(i)], gates_buf),
            (ups_ref.at[:, at(i)], ups_buf),
            (gate_w_ref.at[:, at(i)], gate_buf),
            (up_w_ref.at[:, at(i)], up_buf),
            (down_w_ref.at[at(i)], down_buf),
        ]
        return [
            pltpu.make_async_copy(source, buffer.at[slot], load_sems.at[slot, j])
            for j, (source, buffer) in enumerate(pairs)
        ]

    def stores(i):
        slot = lax.rem(i, 2)
        pairs = [(grad_gate_buf, grad_gate_ref), (grad_up_buf, grad_up_ref)]
        return [
            pltpu.make_async_copy(buffer.at[slot], target.at[:, at(i)], store_sems.at[slot, j])
            for j, (buffer, target) in enumerate(pairs)
        ]

    def row_loads(i):
        slot = lax.rem(i, 2)
        return [
            pltpu.make_async_copy(
                rows_mlp_ref.at[:, at(i)], grad_gate_buf.at[slot], load_sems.at[slot, 0]
            )
        ]

    def row_stores(i):
        slot = lax.rem(i, 2)
        return [
            pltpu.make_async_copy(
                down_buf.at[slot], partial_ref.at[at(i)], store_sems.at[slot, 0]
            )
        ]

    pairs = width // 128
    slots = tiles + pairs
    steps = spot.half + 1

    def reduce_steps(slot):
        def one(step, carry):
            for reduce in reduces:
                reduce.step(step)
            return carry

        lax.fori_loop(slot * steps // slots, (slot + 1) * steps // slots, one, 0)

    greet(spot)
    for copy in [arriving[0], *row_loads(0), *arriving[1:]]:
        copy.start()
    early = slots // 4
    for slot in range(early):
        swap.start(slot, slots)
    chosen = pick_rows(columns_ref[:, 1:2], arrived_ref.shape[0])
    arriving[0].wait()
    matmul_columns(dy_ref, chosen, arrived_ref)

    def rows_step(i, carry):
        slot = lax.rem(i, 2)
        for copy in row_loads(i):
            copy.wait()

        @pl.when(i + 1 < tiles)
        def _():
            for copy in row_loads(i + 1):
                copy.start()

        @pl.when(i >= 2)
        def _():
            for copy in row_stores(i - 2):
                copy.wait()

        down_buf[slot] = matmul(grad_gate_buf[slot], dy_ref[...], 0, 0).astype(half)
        for copy in row_stores(i):
            copy.start()
        return carry

    lax.fori_loop(0, tiles, rows_step, 0)
    for i in (tiles - 2, tiles - 1):
        for copy in row_stores(i):
            copy.wait()
    for copy in loads(0):
        copy.start()

    def begin(item, carry):
        for reduce in reduces:
            reduce.start(item)
        return carry

    lax.fori_loop(0, spot.chips, begin, 0)
    back_ref[...] = jnp.zeros_like(back_ref)
    pair_masks(columns_ref, rows_ref, lengths_ref, same_ref, hidden_ref)
    for reduce in reduces:
        reduce.far_step(0)

    def one(i, carry):
        slot = lax.rem(i, 2)

        swap.start(early + i, slots)
        reduce_steps(i)
        for copy in loads(i):
            copy.wait()

        @pl.when(i + 1 < tiles)
        def _():
            for copy in loads(i + 1):
                copy.start()

        @pl.when(i >= 2)
        def _():
            for copy in stores(i - 2):
                copy.wait()

        gate, up = gates_buf[slot], ups_buf[slot]
        grad_hidden = matmul(dy_ref[...], down_buf[slot], 1, 1)
        sigmoid = jax.nn.sigmoid(gate)
        grad_gate = (grad_hidden * up * sigmoid * (1.0 + gate * (1.0 - sigmoid))).astype(half)
        grad_up = (grad_hidden * gate * sigmoid).astype(half)
        grad_gate_buf[slot] = grad_gate
        grad_up_buf[slot] = grad_up
        for copy in stores(i):
            copy.start()
        back_ref[...] += matmul(grad_gate, gate_buf[slot], 1, 1) + matmul(
            grad_up, up_buf[slot], 1, 1
        )
        return carry

    lax.fori_loop(0, tiles, one, 0)
    for copy in arriving[1:]:
        copy.wait()
    stats_ref[...] = jnp.zeros_like(stats_ref)

    def through_norm(values, grad, gain_ref, first):
        entry, factor = normed(values)
        gain_grad = jnp.sum(grad * entry, axis=0, keepdims=True)
        for i in range(width // 128):
            stats_ref[first + i : first + i + 1, :] = gain_grad[:, i * 128 : (i + 1) * 128]
        scaled = grad * gain_ref[...]
        inner = jnp.mean(scaled * entry, axis=-1, keepdims=True)
        return factor * (scaled - entry * inner)

    dh = dy_ref[...].astype(jnp.float32) + through_norm(
        middle_ref[...], back_ref[...], gain_mlp_ref, 0
    )
    dh_ref[...] = dh
    branch = dh.astype(half)
    grads_ref[:, pl.ds(3 * width, width)] = branch

    def back_out(i, carry):
        at = pl.ds(pl.multiple_of(i * 256, 256), 256)
        do_ref[:, at] = matmul(
            grads_ref[:, pl.ds(3 * width, width)], out_w_ref[at, :], 1, 1
        ).astype(half)
        return carry

    lax.fori_loop(0, width // 256, back_out, 0)
    scale = 1.0 / math.sqrt(64)
    for i in (tiles - 2, tiles - 1):
        for copy in stores(i):
            copy.wait()
    halves = [pl.ds(0, tile), pl.ds(tile, tile)]

    def weight_loads(source, buffer, which):
        return [
            pltpu.make_async_copy(source.at[:, columns], buffer.at[j], weight_sems.at[which, j])
            for j, columns in enumerate(halves)
        ]

    for copy in weight_loads(query_w_ref, gate_buf, 0) + weight_loads(key_w_ref, up_buf, 1):
        copy.start()

    def two(pair, carry):
        swap.start(early + tiles + pair, slots)
        reduce_steps(tiles + pair)
        attend_back_pair(
            pair, width, scale, heads_ref, do_ref, bias_ref, log_ref, same_ref, hidden_ref,
            cosine_ref, sine_ref, grads_ref, bias_same_ref, bias_all_ref,
        )
        return carry

    lax.fori_loop(0, width // 128, two, 0)
    save.start()
    heads = bias_all_ref.shape[0]
    lane = lax.broadcasted_iota(jnp.int32, (heads, 128), 1)
    row = lax.broadcasted_iota(jnp.int32, (heads, 128), 0)
    same = jnp.sum(bias_same_ref[...], axis=1, keepdims=True)
    other = jnp.sum(bias_all_ref[...], axis=1, keepdims=True) - same
    stats_ref[16:17, :] = jnp.sum(
        jnp.where(lane == row, same, 0.0) + jnp.where(lane == row + heads, other, 0.0),
        axis=0,
        keepdims=True,
    )
    def through(buffer, first):
        def one(j, carry):
            at = pl.ds(pl.multiple_of(first + j * tile, tile), tile)
            back_ref[...] += matmul(grads_ref[:, at], buffer[j], 1, 1)
            return carry

        lax.fori_loop(0, 2, one, 0)

    back_ref[...] = jnp.zeros_like(back_ref)

    for copy in weight_loads(query_w_ref, gate_buf, 0):
        copy.wait()
    through(gate_buf, 0)
    for copy in weight_loads(value_w_ref, gate_buf, 0):
        copy.start()
    for copy in weight_loads(key_w_ref, up_buf, 1):
        copy.wait()
    through(up_buf, width)
    for copy in weight_loads(value_w_ref, gate_buf, 0):
        copy.wait()
    through(gate_buf, 2 * width)
    grad_stream = dh_ref[...] + through_norm(
        stream_ref[...].astype(jnp.float32), back_ref[...], gain_attn_ref, 8
    )
    placed = place_rows(rows_ref[1:2, :], packed_ref.shape[0])
    dh_ref[...] = grad_stream
    matmul_columns(packed_ref, placed, dh_ref)
    save.wait()
    swap.finish()
    for reduce in reduces:
        reduce.finish()


def input_grad_call(shards, inputs, spaces, far_inputs, lent, collective_id):
    anywhere = pl.BlockSpec(memory_space=pl.ANY)
    inside = pl.BlockSpec(memory_space=pltpu.VMEM)
    packed, gates = far_inputs[3], far_inputs[4]
    tokens, hidden = gates.shape
    width = packed.shape[1]
    heads = inputs[10].shape[0]
    tile = 512
    assert 2 * tile == width
    half, full = jnp.bfloat16, jnp.float32
    vmem, shape = pltpu.VMEM, jax.ShapeDtypeStruct
    return pl.pallas_call(
        functools.partial(input_grad_kernel, shards, lent),
        out_shape=[
            shape((tokens, 4 * width), half),
            shape(packed.shape, half),
            shape((24, 128), full),
            Reduce.out_shape(shards, lent, shape((hidden, width), half)),
            shape((tokens, hidden), half),
            shape((tokens, hidden), half),
            shape(packed.shape, half),
            shape((hidden, width), half),
        ],
        in_specs=[*spaces, *[anywhere] * len(far_inputs)],
        out_specs=[anywhere] + [inside] * 2 + [anywhere] * 5,
        scratch_shapes=[
            vmem((2, tokens, tile), full),
            vmem((2, tokens, tile), full),
            vmem((2, width, tile), half),
            vmem((2, width, tile), half),
            vmem((2, tile, width), half),
            vmem((2, tokens, tile), half),
            vmem((2, tokens, tile), half),
            vmem((tokens, width), full),
            vmem((tokens, width), full),
            vmem((tokens, width), half),
            vmem((tokens, tokens), full),
            vmem((tokens, tokens), full),
            vmem((heads, tokens), full),
            vmem((heads, tokens), full),
            DMA((2, 5)),
            DMA((2, 2)),
            DMA((2, 2)),
            DMA((shards,)),
            DMA((shards,)),
            DMA,
            *[vmem(inputs[at].shape, inputs[at].dtype) for at in (8, 7, 6, 9, 11, 12, 13)],
            DMA((7,)),
            DMA,
            vmem((tokens, 4 * width), half),
            vmem((tokens, width), half),
            *Reduce.scratch(shards, lent, hidden // shards // 2, width) * 2,
        ],
        compiler_params=pltpu.CompilerParams(
            collective_id=collective_id, has_side_effects=True, vmem_limit_bytes=VMEM_LIMIT
        ),
    )(*inputs, *far_inputs)


def weight_grad_kernel(shards, lents, *refs):
    (
        columns_ref, input_attn_ref, attended_ref, input_mlp_ref, stats_forward_ref,
        stats_back_ref, home_out_ref, packed_ref, gate_ref, up_ref, entry_ref,
        grad_gate_ref, grad_up_ref, grad_in_ref, output_ref, input_grad_ref, sums_ref,
    ) = refs[:17]
    partials = refs[17:20]
    (
        attn_t_ref, attended_t_ref, mlp_t_ref, home_ref, stats_ref, tile_buf, part_buf,
        load_sems, store_sems, send_sems, recv_sems, own_sem,
    ) = refs[20:32]
    tally_refs, staged, in_sems, refs = refs[32:40], refs[40:44], refs[44], refs[45:]
    arriving = [
        pltpu.make_async_copy(source, buffer, in_sems.at[i])
        for i, (source, buffer) in enumerate(
            zip((input_mlp_ref, input_attn_ref, attended_ref, home_out_ref), staged, strict=True)
        )
    ]
    input_mlp_ref, input_attn_ref, attended_ref, home_out_ref = staged
    half, full = jnp.bfloat16, jnp.float32
    spot = Spot(shards)
    swap = Swap(spot, packed_ref, home_ref, (send_sems, recv_sems), own_sem)
    tally = Tally(spot, stats_ref, sums_ref, tally_refs)
    outputs = (grad_gate_ref, grad_up_ref, grad_in_ref)
    reduces = [
        Reduce(spot, lents[g], partials[g], outputs[g], refs[20 * g : 20 * g + 20])
        for g in range(3)
    ]
    steps = spot.half + 1
    parts = 5
    tile = tile_buf.shape[2]
    tiles = gate_ref.shape[1] // tile

    def at(i):
        return pl.ds(pl.multiple_of(i * tile, tile), tile)

    def product(source, lefts, partial, reduce):
        def load(i):
            slot = lax.rem(i, 2)
            return pltpu.make_async_copy(
                source.at[:, at(i)], tile_buf.at[slot], load_sems.at[slot]
            )

        def store(i):
            slot = lax.rem(i, 2)
            return pltpu.make_async_copy(
                part_buf.at[slot], partial.at[:, at(i)], store_sems.at[slot]
            )

        load(0).start()
        first = 0
        for left, count in lefts:

            def one(i, carry, left=left):
                slot = lax.rem(i, 2)
                load(i).wait()

                @pl.when(i + 1 < tiles)
                def _():
                    load(i + 1).start()

                @pl.when(i >= 2)
                def _():
                    store(i - 2).wait()

                part_buf[slot] = matmul(left[...], tile_buf[slot]).astype(half)
                store(i).start()
                return carry

            lax.fori_loop(first, first + count, one, 0)
            first += count
        for i in (tiles - 2, tiles - 1):
            store(i).wait()

        def begin(item, carry):
            reduce.start(item)
            return carry

        lax.fori_loop(0, spot.chips, begin, 0)
        reduce.far_step(0)

    greet(spot)
    swap.start(0, parts)
    for copy in arriving:
        copy.start()
    stats_ref[0:8, :] = stats_forward_ref[...]
    stats_ref[8:32, :] = stats_back_ref[...]
    tally.start()
    arriving[0].wait()
    mlp_t_ref[...] = input_mlp_ref[...].astype(full).T.astype(half)
    product(gate_ref, [(mlp_t_ref, tiles)], partials[0], reduces[0])
    swap.start(1, parts)
    product(up_ref, [(mlp_t_ref, tiles)], partials[1], reduces[1])
    swap.start(2, parts)
    chosen = pick_rows(columns_ref[:, 0:1], home_ref.shape[0])

    def ticks(tick, carry):
        reduces[0].step(tick)
        reduces[1].step(tick)

        @pl.when(tick < 2)
        def _():
            swap.start(3 + tick, parts)

        @pl.when(tick == 0)
        def _():
            for copy in arriving[1:]:
                copy.wait()
            attn_t_ref[...] = input_attn_ref[...].astype(full).T.astype(half)
            attended_t_ref[...] = attended_ref[...].astype(full).T.astype(half)
            product(
                entry_ref,
                [(attn_t_ref, tiles - tiles // 4), (attended_t_ref, tiles // 4)],
                partials[2],
                reduces[2],
            )

        @pl.when(tick == 1)
        def _():
            matmul_columns(output_ref, chosen, home_out_ref)
            tally.middle()

        reduces[2].step(tick)

        return carry

    lax.fori_loop(0, steps, ticks, 0)
    swap.finish()
    matmul_columns(input_grad_ref, chosen, home_ref)
    tally.finish()
    for reduce in reduces:
        reduce.finish()


def weight_grad_call(shards, inputs, far_inputs, lents, collective_id):
    tile = 512
    packed, hidden = far_inputs[0], far_inputs[1].shape[1]
    tokens, width = inputs[1].shape
    assert hidden == 4 * width
    half, full = jnp.bfloat16, jnp.float32
    shape = jax.ShapeDtypeStruct
    anywhere = pl.BlockSpec(memory_space=pl.ANY)
    inside = pl.BlockSpec(memory_space=pltpu.VMEM)
    scratch = []
    for lent in lents:
        scratch += Reduce.scratch(shards, lent, width // shards, hidden)
    results = pl.pallas_call(
        functools.partial(weight_grad_kernel, shards, lents),
        out_shape=[
            *[Reduce.out_shape(shards, lent, shape((width, hidden), half)) for lent in lents],
            shape((tokens, width), half),
            shape((tokens, width), half),
            shape((32, 128), full),
            *[shape((width, hidden), half)] * 3,
        ],
        in_specs=[inside]
        + [anywhere] * 3
        + [inside] * 2
        + [anywhere]
        + [anywhere] * len(far_inputs),
        out_specs=[anywhere] * 3 + [inside] * 3 + [anywhere] * 3,
        scratch_shapes=[
            *[pltpu.VMEM((width, tokens), half)] * 3,
            pltpu.VMEM(packed.shape, half),
            pltpu.VMEM((32, 128), full),
            pltpu.VMEM((2, tokens, tile), half),
            pltpu.VMEM((2, width, tile), half),
            DMA((2,)),
            DMA((2,)),
            DMA((shards,)),
            DMA((shards,)),
            DMA,
            *Tally.scratch(shards, (32, 128)),
            *[pltpu.VMEM(inputs[at].shape, half) for at in (3, 1, 2, 6)],
            DMA((4,)),
            *scratch,
        ],
        compiler_params=pltpu.CompilerParams(
            collective_id=collective_id, has_side_effects=True, vmem_limit_bytes=VMEM_LIMIT
        ),
    )(*inputs, *far_inputs)
    return results[:6]


def on_device(
    tokens,
    cotangent,
    send_slot,
    recv_slot,
    lengths,
    variate,
    valid_mask,
    norm_attn,
    w_query,
    w_key,
    w_value,
    w_out,
    variate_bias,
    norm_mlp,
    w_gate,
    w_up,
    w_down,
):
    shards = lax.axis_size("shard")
    tok_rows, width = tokens.shape
    slot_total = 2 * tok_rows
    heads = variate_bias.shape[1]
    half, full = jnp.bfloat16, jnp.float32
    share = width // shards
    indices = jnp.stack([send_slot, recv_slot, variate, valid_mask])
    rows = jnp.concatenate([indices, jnp.zeros_like(indices)])
    pair_count = width // heads // 2
    frequency = 1.0 / 10000.0 ** (np.arange(pair_count, dtype=np.float32) / pair_count)
    frequency = jnp.asarray(np.tile(frequency, 128 // pair_count)[None], full)
    gains = jnp.stack([norm_attn, norm_mlp]).astype(full)
    gains = jnp.pad(gains, ((0, 6), (0, 128 - share)))
    shape = jax.ShapeDtypeStruct
    packed_shape = shape((slot_total, width), half)
    token_shape = shape((tok_rows, width), half)
    *full_in, arrived_tokens, out_cotangent, cosine, sine, columns, gain_attn, gain_mlp = (
        gather_call(
            shards, rows, tokens, cotangent, lengths, frequency, [w_query, w_key, w_value],
            (4, 4, 4), gains, 1,
        )
    )
    inside = pl.BlockSpec(memory_space=pltpu.VMEM)
    anywhere = pl.BlockSpec(memory_space=pl.ANY)
    scalar = pl.BlockSpec(memory_space=pltpu.SMEM)
    hidden = w_gate.shape[1]
    (
        (
            stream, input_attn, head_rows, attended, logs,
            gates, ups, hidden_rows, packed, middle, input_mlp, stats_forward,
        ),
        (full_out, full_gate, full_up, full_down),
        (arrived_grads,),
    ) = forward_gather_call(
        shards,
        [
            arrived_tokens, columns, rows, lengths, variate_bias, gain_attn, *full_in,
            cosine, sine, gain_mlp,
        ],
        [anywhere] + [inside] * 2 + [scalar] * 2 + [inside] + [anywhere] * 3 + [inside] * 3,
        [
            token_shape,
            token_shape,
            shape((tok_rows, 3 * width), half),
            token_shape,
            shape((heads, tok_rows), full),
            shape((tok_rows, hidden), full),
            shape((tok_rows, hidden), full),
            shape((tok_rows, hidden), half),
            packed_shape,
            shape((tok_rows, width), full),
            token_shape,
            shape((8, 128), full),
        ],
        [anywhere] * 8 + [inside] + [anywhere] * 2 + [inside],
        [w_out, w_gate, w_up, w_down],
        (4, 4, 2, 2),
        [out_cotangent],
        2,
    )
    (
        entry_grads, packed_grad, stats_back, grad_down, grad_gates, grad_ups, home_out, _,
    ) = input_grad_call(
        shards,
        [
            columns, rows, lengths, variate_bias, gain_mlp, gain_attn, middle, full_out,
            arrived_grads, head_rows, logs, cosine, sine, stream,
        ],
        [inside] * 2
        + [scalar] * 2
        + [inside] * 2
        + [anywhere] * 4
        + [inside]
        + [anywhere] * 3,
        [*full_in, packed, gates, ups, hidden_rows, full_gate, full_up, full_down],
        4,
        3,
    )
    grad_gate, grad_up, grad_in, output, input_grad, sums = weight_grad_call(
        shards,
        [columns, input_attn, attended, input_mlp, stats_forward, stats_back, home_out],
        [packed_grad, grad_gates, grad_ups, entry_grads],
        (4, 2, 2),
        4,
    )
    rep = lax.axis_index("rep").astype(jnp.int32).reshape(1, 1)
    (
        output, input_grad, grad_gate, grad_up, grad_down,
        grad_query, grad_key, grad_value, grad_out, root_means,
    ) = assemble_call(
        rep,
        [grad_gate, grad_up, grad_down, grad_in],
        [output, input_grad],
        sums,
        [
            token_shape,
            token_shape,
            *[shape((share, hidden), full)] * 2,
            shape((hidden // shards, width), full),
            *[shape((share, width), full)] * 4,
        ],
    )
    root_means = root_means[0, :5]
    share_start = lax.axis_index("shard") * share
    grad_norm_mlp = lax.dynamic_slice_in_dim(sums[8:16].reshape(-1), share_start, share)
    grad_norm_attn = lax.dynamic_slice_in_dim(sums[16:24].reshape(-1), share_start, share)
    bias_grads = sums[24, : 2 * heads].reshape(2, heads)
    return (
        output,
        input_grad,
        grad_norm_attn,
        grad_query,
        grad_key,
        grad_value,
        grad_out,
        bias_grads,
        grad_norm_mlp,
        grad_gate,
        grad_up,
        grad_down,
        root_means,
    )


def solution(mesh):
    in_specs = (
        P(("rep", "shard"), None),
        P(("rep", "shard"), None),
        P(("rep", "shard")),
        P(("rep", "shard")),
        P(("rep", "shard"), None),
        P(("rep", "shard")),
        P(("rep", "shard")),
        P("shard"),
        P("shard", None),
        P("shard", None),
        P("shard", None),
        P("shard", None),
        P(),
        P("shard"),
        P("shard", None),
        P("shard", None),
        P("shard", None),
    )
    out_specs = (
        P(("rep", "shard"), None),
        P(("rep", "shard"), None),
        P("shard"),
        P("shard", None),
        P("shard", None),
        P("shard", None),
        P("shard", None),
        P(),
        P("shard"),
        P("shard", None),
        P("shard", None),
        P("shard", None),
        P(),
    )
    return jax.shard_map(
        on_device, mesh=mesh, in_specs=in_specs, out_specs=out_specs, check_vma=False
    )
```
